32 devices in a mesh: wide: 16 (over z, x, core), seq: 2 (over y).
Axes of the slice: x: 2, y: 2, z: 4, core: 2. Of those that a mesh axis runs over, the one named last changes fastest.
Arguments:
- tokens: bfloat16 [32, 1024, 768], P('wide', 'seq'), may hold values from -6 to 6
- time_embed: float32 [32, 768], P('wide'), may hold values from -6 to 6
- segment_ids: int32 [32, 1024], P('wide', 'seq'), may hold values from 0 to 4, as said below
- pad_mask: int32 [32, 1024], P('wide', 'seq'), may hold values 0 or 1
- out_grad: bfloat16 [32, 1024, 768], P('wide', 'seq'), may hold values from -6 to 6
- qkv_weight: bfloat16 [2, 768, 2304], P(None, 'wide'), may hold values from -0.21875 to 0.21875
- out_weight: bfloat16 [2, 768, 768], P(None, 'wide'), may hold values from -1.25 to 1.25
- up_weight: bfloat16 [2, 768, 3072], P(None, 'wide'), may hold values from -0.21875 to 0.21875
- down_weight: bfloat16 [2, 3072, 768], P(None, 'wide'), may hold values from -0.109375 to 0.109375
- norm_gains: bfloat16 [2, 2, 768], P(None, None, 'wide'), may hold values from 0.5 to 1.5
- bias_rows: bfloat16 [2, 6, 768], P(None, None, 'wide'), may hold values from -1.75 to 1.75
- up_bias: bfloat16 [2, 3072], P(None, 'wide'), may hold values from -1.75 to 1.75
Outputs:
- output: float32 [32, 1024, 768], P('wide', 'seq')
- input_gradient: float32 [32, 1024, 768], P('wide', 'seq')
- qkv_weight_gradient: float32 [2, 768, 2304], P(None, 'wide')
- out_weight_gradient: float32 [2, 768, 768], P(None, 'wide')
- up_weight_gradient: float32 [2, 768, 3072], P(None, 'wide')
- down_weight_gradient: float32 [2, 3072, 768], P(None, 'wide')
- norm_gains_gradient: float32 [2, 2, 768], P(None, None, 'wide')
- bias_rows_gradient: float32 [2, 6, 768], P(None, None, 'wide')
- up_bias_gradient: float32 [2, 3072], P(None, 'wide')
The draws below stay inside these ranges and needn't reach their ends.
Inputs may be any that keep to these rules, and one draw needn't show every extreme that they name: `segment_ids`: in each sequence the ids never fall along positions, are 0 at the first token and 4 at the last; one document of every sequence covers positions 384 to 639.
All inputs are finite; a program needn't handle non-finite values. No bound on the sum of `pad_mask` on one device may be relied on, other than what follows from the above.
Results may differ from the reference program's by a relative error of at most 0.011.
Values may be sent and summed in bfloat16 or wider, within the bound.
No kernel may reach another device: no remote copies, remote signals or barrier semaphores. Data moves between devices by JAX's collectives and lax.ppermute only.
A program may use at most 320 MiB of HBM per device.

```python
import jax
import jax.numpy as jnp
from jax import lax

D = 768
H = 12
HEAD_SIZE = 64
FF = 3072
LEN = 1024
LAYERS = 2
SEQS = 32
DOCS = 4


def draw_segment_ids(key, part):
    span = 3 * LEN // 4 - 1
    picks = jax.random.randint(key, (SEQS, DOCS), 0, span)
    cuts = 1 + picks + jnp.where(picks >= 3 * LEN // 8 - 1, LEN // 4, 0)
    positions = jnp.arange(LEN)
    below = (cuts[:, None, :] <= positions[None, :, None]).astype(jnp.int32)
    return jnp.sum(below, axis=-1).astype(jnp.int32)


def touch_ends(entries, rng, smallest, high):
    spot = [jax.random.randint(jax.random.fold_in(rng, axis), (), 0, length) for axis, length in enumerate(entries.shape)]
    widest = entries.shape.index(max(entries.shape))
    next_to = spot[:widest] + [(spot[widest] + 1) % entries.shape[widest]] + spot[widest + 1:]
    return entries.at[tuple(spot)].set(smallest).at[tuple(next_to)].set(high)


def block_levels(key, extent, shards, smallest, largest):
    def one(dim, shards_of):
        draws = jax.random.uniform(jax.random.fold_in(jax.random.fold_in(key, 6), dim), (shards_of,), jnp.float32, smallest / len(shards), largest / len(shards))
        return jnp.repeat(jnp.exp(draws), extent[dim] // shards_of).reshape((-1,) + (1,) * (len(extent) - dim - 1))

    factor_of = one(*shards[0])
    for cut in shards[1:]:
        factor_of = factor_of * one(*cut)
    return factor_of


def noise(own_key, extent, width, bound, pieces=(), held_as=jnp.bfloat16):
    gain = block_levels(own_key, extent, pieces, -0.22, 0.18) if pieces else 1.0
    values = jax.random.normal(own_key, extent, jnp.float32) * width * gain
    return jnp.minimum(jnp.maximum(values, -bound), bound).astype(held_as)


def setup_inputs(seed: int = 0) -> dict:
    key_of = jax.random.split(jax.random.key(seed), 13)
    return {
        "tokens": noise(key_of[0], (SEQS, LEN, D), 1.0, 6.0, ((0, 16), (1, 2))),
        "time_embed": noise(key_of[1], (SEQS, D), 1.0, 6.0, ((0, 16),), jnp.float32),
        "segment_ids": draw_segment_ids(jax.random.fold_in(key_of[12], 71), 0),
        "pad_mask": touch_ends((jax.random.randint(key_of[3], (SEQS, LEN), 0, 8) < 7).astype(jnp.int32), jax.random.fold_in(key_of[3], 1), 0, 1),
        "out_grad": noise(key_of[4], (SEQS, LEN, D), 1.0, 6.0, ((0, 16), (1, 2))),
        "qkv_weight": noise(key_of[5], (LAYERS, D, 3 * D), D ** -0.5, 0.21875, ((1, 16),)),
        "out_weight": noise(key_of[6], (LAYERS, D, D), (D // 32) ** -0.5, 1.25, ((1, 16),)),
        "up_weight": noise(key_of[7], (LAYERS, D, FF), D ** -0.5, 0.21875, ((1, 16),)),
        "down_weight": noise(key_of[8], (LAYERS, FF, D), FF ** -0.5, 0.109375, ((1, 16),)),
        "norm_gains": jnp.clip(1.0 + 0.1 * jax.random.normal(key_of[9], (LAYERS, 2, D), jnp.float32), 0.5, 1.5).astype(jnp.bfloat16),
        "bias_rows": noise(key_of[10], (LAYERS, 6, D), 0.3, 1.75, ((2, 16),)),
        "up_bias": noise(key_of[11], (LAYERS, FF), 0.3, 1.75, ((1, 16),)),
    }


@jax.custom_vjp
def lower_precision(v):
    return lax.optimization_barrier(v.astype(jnp.bfloat16)).astype(jnp.float32)

@jax.custom_vjp
def low_back(v):
    return v

def low_keep(v):
    return (lower_precision(v), None)

def low_pass(kept, grad):
    return (grad,)

def back_keep(v):
    return (v, None)

def back_low(kept, grad):
    return (lower_precision(grad),)
lower_precision.defvjp(low_keep, low_pass)
low_back.defvjp(back_keep, back_low)
epsilon = 1e-05
negative_fill = -1000000000.0

def rounded(value):
    return low_back(lower_precision(value))

def product(left, right):
    return jnp.dot(left, right, precision=lax.Precision.HIGHEST, preferred_element_type=jnp.float32)

def layer_norm(hidden, scale_gain, offset):
    center = hidden - lax.optimization_barrier(jnp.mean(hidden, axis=-1, keepdims=True))
    spread = lax.optimization_barrier(jnp.mean(center * center, axis=-1, keepdims=True))
    return center * lax.rsqrt(spread + epsilon) * scale_gain + offset

def head_attention(query_rows, key_portion, value_portion, allowed):
    attention_scores = jnp.einsum('yuf,yzf->yuz', query_rows, key_portion, precision=lax.Precision.HIGHEST) * HEAD_SIZE ** (-0.5)
    attention_scores = jnp.where(allowed, low_back(attention_scores), negative_fill)
    row_max = lax.optimization_barrier(jnp.max(attention_scores, axis=-1, keepdims=True))
    weights_exp = jnp.exp(attention_scores - row_max)
    attention_probs = weights_exp / lax.optimization_barrier(jnp.sum(weights_exp, axis=-1, keepdims=True))
    return jnp.einsum('xev,xvm->xem', lower_precision(attention_probs), value_portion, precision=lax.Precision.HIGHEST)

def attention(query_rows, key_portion, value_portion, allowed):

    def split_heads(tensor):
        return tensor.reshape(tensor.shape[0], tensor.shape[1], H, HEAD_SIZE).transpose(2, 0, 1, 3)
    block = jax.checkpoint(lambda head_parts: head_attention(head_parts[0], head_parts[1], head_parts[2], allowed))
    head_outputs = lax.map(block, (split_heads(query_rows), split_heads(key_portion), split_heads(value_portion)))
    return head_outputs.transpose(1, 2, 0, 3).reshape(query_rows.shape)

def layer_apply(hidden, params, allowed):
    qkv_weight, out_weight, up_weight, down_weight, norm_gains, bias_rows, up_bias = params
    normed = lower_precision(layer_norm(hidden, norm_gains[0], bias_rows[0]))
    projected = product(normed, qkv_weight)
    query_rows = rounded(projected[..., 0:D] + bias_rows[1])
    key_portion = rounded(projected[..., D:2 * D])
    value_portion = rounded(projected[..., 2 * D:3 * D] + bias_rows[2])
    attended = rounded(attention(query_rows, key_portion, value_portion, allowed))
    middle = hidden + low_back(product(attended, out_weight) + bias_rows[3])
    second_normed = lower_precision(layer_norm(middle, norm_gains[1], bias_rows[4]))
    pre_activation = low_back(product(second_normed, up_weight) + up_bias)
    activated = lower_precision(jax.nn.gelu(pre_activation, approximate=True))
    return middle + low_back(product(activated, down_weight) + bias_rows[5])

def reference(tokens, time_embed, segment_ids, pad_mask, out_grad, qkv_weight, out_weight, up_weight, down_weight, norm_gains, bias_rows, up_bias):
    weights = tuple((array.astype(jnp.float32) for array in (qkv_weight, out_weight, up_weight, down_weight, norm_gains, bias_rows, up_bias)))
    group = 4
    count = tokens.shape[0] // group
    positions = jnp.arange(LEN)
    diagonal = positions[:, None] == positions[None, :]

    def regroup(array):
        return array.reshape((count, group) + array.shape[1:])

    def per_group(totals, items):
        block_tokens, block_time, block_ids, block_pad, block_cotangent = items
        allowed = (block_ids[:, :, None] == block_ids[:, None, :]) & ((block_pad[:, None, :] == 1) | diagonal[None])

        def forward(inputs, params):
            hidden = inputs + block_time[:, None, :]
            for layer_index in range(LAYERS):
                hidden = layer_apply(hidden, tuple((array[layer_index] for array in params)), allowed)
            return hidden
        result, pull = jax.vjp(forward, block_tokens.astype(jnp.float32), weights)
        input_part, weight_parts = pull(block_cotangent.astype(jnp.float32))
        totals = tuple((total + part for total, part in zip(totals, weight_parts)))
        return (totals, (result, input_part))
    start = tuple((jnp.zeros_like(array) for array in weights))
    totals, (results, input_parts) = lax.scan(per_group, start, (regroup(tokens), regroup(time_embed), regroup(segment_ids), regroup(pad_mask), regroup(out_grad)))
    return (results.reshape(tokens.shape), input_parts.reshape(tokens.shape), totals[0], totals[1], totals[2], totals[3], totals[4], totals[5], totals[6])
```

```python
import functools

import jax
import jax.numpy as jnp
from jax import lax
from jax.experimental import pallas as pl
from jax.experimental.pallas import tpu as pltpu
from jax.sharding import PartitionSpec as P

HEAD_SIZE = 64
PAIR = 2 * HEAD_SIZE
FORWARD_ROWS = 512
BACKWARD_ROWS = 256

epsilon = 1e-05
masked_bias = -1e30
half = jnp.bfloat16
single = jnp.float32


def contract(left, right, left_dim, right_dim):
    return lax.dot_general(
        left, right, (((left_dim,), (right_dim,)), ((), ())), preferred_element_type=jnp.float32
    )


def first_head_lanes():
    return lax.broadcasted_iota(jnp.int32, (1, PAIR), 1) < HEAD_SIZE


def one_head_of(pair, head):
    lanes = first_head_lanes()
    keep = lanes if head == 0 else jnp.logical_not(lanes)
    return jnp.where(keep, pair, jnp.zeros_like(pair))


def attend_kernel(query_ref, key_ref, value_ref, bias_ref, out_ref, total_ref, *, rows):
    keys = key_ref[...]
    values = value_ref[...]
    scale = jnp.asarray(HEAD_SIZE ** (-0.5), half)
    for start in range(0, keys.shape[0], rows):
        window = pl.ds(start, rows)
        queries = query_ref[window, :] * scale
        bias = bias_ref[:, window]
        attended = []
        for head in range(2):
            scores = contract(keys, one_head_of(queries, head), 1, 1) + bias
            top = jnp.max(scores, axis=0, keepdims=True)
            weights = jnp.exp(scores - top)
            total = jnp.sum(weights, axis=0, keepdims=True)
            mixed = contract(values, weights.astype(half), 0, 0) * (1.0 / total)
            attended.append(mixed[HEAD_SIZE * head : HEAD_SIZE * (head + 1)])
            total_ref[head : head + 1, window] = top + jnp.log(total)
        out_ref[window, :] = jnp.concatenate(attended, 0).T.astype(half)


def attend_forward(packed, bias):
    length = packed.shape[0]
    features = packed.shape[1] // 3
    pairs = features // PAIR
    columns = lambda part: pl.BlockSpec((length, PAIR), lambda i: (0, part * pairs + i))
    return pl.pallas_call(
        functools.partial(attend_kernel, rows=FORWARD_ROWS),
        grid=(pairs,),
        in_specs=[
            columns(0),
            columns(1),
            columns(2),
            pl.BlockSpec((length, length), lambda i: (0, 0)),
        ],
        out_specs=[columns(0), pl.BlockSpec((None, 2, length), lambda i: (i, 0, 0))],
        out_shape=[
            jax.ShapeDtypeStruct((length, features), half),
            jax.ShapeDtypeStruct((pairs, 2, length), single),
        ],
        compiler_params=pltpu.CompilerParams(vmem_limit_bytes=56 << 20),
        cost_estimate=pl.CostEstimate(
            flops=4 * length * length * features * 4,
            bytes_accessed=8 * length * features,
            transcendentals=length * length * features // HEAD_SIZE,
        ),
        name="attend_forward",
    )(packed, packed, packed, bias)


def attend_grad_kernel(
    query_ref,
    key_ref,
    value_ref,
    bias_ref,
    upstream_ref,
    total_ref,
    attended_ref,
    out_ref,
    key_sum,
    value_sum,
    *,
    rows,
):
    pair = pl.program_id(0)
    features = out_ref.shape[1] // 3
    keys = key_ref[...]
    values = value_ref[...]
    scale = HEAD_SIZE ** (-0.5)
    for start in range(0, keys.shape[0], rows):
        window = pl.ds(start, rows)
        queries = query_ref[window, :] * jnp.asarray(scale, half)
        upstream = upstream_ref[window, :]
        product = (upstream.astype(single) * attended_ref[window, :].astype(single)).T
        bias = bias_ref[:, window]
        query_grads, key_grad, value_grad = [], 0.0, 0.0
        for head in range(2):
            head_queries = one_head_of(queries, head)
            head_upstream = one_head_of(upstream, head)
            inner = jnp.sum(
                product[HEAD_SIZE * head : HEAD_SIZE * (head + 1)], axis=0, keepdims=True
            )
            scores = contract(keys, head_queries, 1, 1) + bias
            weights = jnp.exp(scores - total_ref[head : head + 1, window])
            weight_grads = contract(values, head_upstream, 1, 1)
            score_grads = (weights * (weight_grads - inner)).astype(half)
            value_grad = value_grad + contract(weights.astype(half), head_upstream, 1, 0)
            key_grad = key_grad + contract(score_grads, head_queries, 1, 0)
            query_grads.append(
                contract(keys, score_grads, 0, 0)[HEAD_SIZE * head : HEAD_SIZE * (head + 1)]
            )
        out_ref[window, pl.ds(pl.multiple_of(pair * PAIR, PAIR), PAIR)] = (
            jnp.concatenate(query_grads, 0).T * scale
        ).astype(half)
        if start == 0:
            key_sum[...] = key_grad
            value_sum[...] = value_grad
        else:
            key_sum[...] += key_grad
            value_sum[...] += value_grad
    out_ref[:, pl.ds(pl.multiple_of(features + pair * PAIR, PAIR), PAIR)] = key_sum[...].astype(
        half
    )
    out_ref[:, pl.ds(pl.multiple_of(2 * features + pair * PAIR, PAIR), PAIR)] = value_sum[
        ...
    ].astype(half)


def attend_backward(packed, bias, upstream, totals, attended):
    length = packed.shape[0]
    features = packed.shape[1] // 3
    pairs = features // PAIR
    columns = lambda part: pl.BlockSpec((length, PAIR), lambda i: (0, part * pairs + i))
    return pl.pallas_call(
        functools.partial(attend_grad_kernel, rows=BACKWARD_ROWS),
        grid=(pairs,),
        in_specs=[
            columns(0),
            columns(1),
            columns(2),
            pl.BlockSpec((length, length), lambda i: (0, 0)),
            columns(0),
            pl.BlockSpec((None, 2, length), lambda i: (i, 0, 0)),
            columns(0),
        ],
        out_specs=pl.BlockSpec((length, 3 * features), lambda i: (0, 0)),
        out_shape=jax.ShapeDtypeStruct((length, 3 * features), half),
        scratch_shapes=[pltpu.VMEM((length, PAIR), single)] * 2,
        compiler_params=pltpu.CompilerParams(vmem_limit_bytes=56 << 20),
        cost_estimate=pl.CostEstimate(
            flops=10 * length * length * features * 4,
            bytes_accessed=16 * length * features,
            transcendentals=length * length * features // HEAD_SIZE,
        ),
        name="attend_backward",
    )(packed, packed, packed, bias, upstream, totals, attended)


def layer_norm(hidden, scale_gain, offset):
    center = hidden - jnp.mean(hidden, axis=-1, keepdims=True)
    spread = jnp.mean(center * center, axis=-1, keepdims=True)
    return center * lax.rsqrt(spread + epsilon) * scale_gain + offset


def layer_norm_grad(hidden, scale_gain, upstream):
    center = hidden - jnp.mean(hidden, axis=-1, keepdims=True)
    inverse = lax.rsqrt(jnp.mean(center * center, axis=-1, keepdims=True) + epsilon)
    normal = center * inverse
    scaled = upstream * scale_gain
    slope = jnp.mean(scaled, axis=-1, keepdims=True)
    tilt = jnp.mean(scaled * normal, axis=-1, keepdims=True)
    return (
        inverse * (scaled - slope - normal * tilt),
        jnp.sum(upstream * normal, axis=0),
        jnp.sum(upstream, axis=0),
    )


def layer_forward(hidden, matrices, rows, bias):
    qkv_weight, out_weight, up_weight, down_weight = matrices
    gains, offsets, up_bias = rows
    normed = layer_norm(hidden, gains[0], offsets[0]).astype(half)
    shift = jnp.concatenate([offsets[1], jnp.zeros_like(offsets[1]), offsets[2]])
    packed = (contract(normed, qkv_weight, 1, 0) + shift).astype(half)
    attended, totals = attend_forward(packed, bias)
    middle = hidden + (contract(attended, out_weight, 1, 0) + offsets[3])
    second = layer_norm(middle, gains[1], offsets[4]).astype(half)
    pre_activation = contract(second, up_weight, 1, 0) + up_bias
    activated = jax.nn.gelu(pre_activation, approximate=True).astype(half)
    result = middle + (contract(activated, down_weight, 1, 0) + offsets[5])
    return (
        result,
        (hidden, normed, packed, totals, attended, middle, second, pre_activation, activated),
    )


def per_device(
    tokens,
    time_embed,
    segment_ids,
    pad_mask,
    out_grad,
    qkv_weight,
    out_weight,
    up_weight,
    down_weight,
    norm_gains,
    bias_rows,
    up_bias,
):
    layers = qkv_weight.shape[0]
    features = tokens.shape[2]
    groups = lax.axis_size("wide")
    swap = [(0, 1), (1, 0)]

    def whole_sequence(part):
        return lax.all_to_all(part, "seq", split_axis=0, concat_axis=1, tiled=True)[0]

    marks = whole_sequence(jnp.stack([segment_ids, pad_mask], axis=2))
    my_tokens = whole_sequence(tokens)
    my_upstream = whole_sequence(out_grad)
    my_time = lax.dynamic_index_in_dim(time_embed, lax.axis_index("seq"), 0, keepdims=True)

    sources = (qkv_weight, out_weight, up_weight, down_weight)
    small = jnp.concatenate(
        [norm_gains.reshape(-1), bias_rows.reshape(-1), up_bias.reshape(-1)]
    )
    matrices = [[None] * 4 for _ in range(layers)]
    matrices[0][0] = lax.all_gather(qkv_weight[0], "wide", axis=0, tiled=True)
    small_whole = lax.all_gather(small, "wide", axis=0, tiled=False)
    for layer in range(layers):
        for index, source in enumerate(sources):
            if matrices[layer][index] is None:
                matrices[layer][index] = lax.all_gather(
                    source[layer], "wide", axis=0, tiled=True
                )
    cut_gains = norm_gains.size
    cut_rows = cut_gains + bias_rows.size

    def whole_rows(part, count):
        parts = part.reshape(groups, layers, count, -1)
        return parts.transpose(1, 2, 0, 3).reshape(layers, count, -1).astype(single)

    all_gains = whole_rows(small_whole[:, :cut_gains], norm_gains.shape[1])
    all_offsets = whole_rows(small_whole[:, cut_gains:cut_rows], bias_rows.shape[1])
    all_up_bias = whole_rows(small_whole[:, cut_rows:], 1)[:, 0]

    doc, pad = marks[:, 0], marks[:, 1]
    positions = jnp.arange(doc.shape[0])
    allowed = (doc[:, None] == doc[None, :]) & (
        (pad[:, None] == 1) | (positions[:, None] == positions[None, :])
    )
    bias = jnp.where(allowed, 0.0, masked_bias)

    hidden = my_tokens.astype(single) + my_time
    saved = []
    for layer in range(layers):
        rows = (all_gains[layer], all_offsets[layer], all_up_bias[layer])
        hidden, kept = layer_forward(hidden, matrices[layer], rows, bias)
        saved.append(kept)

    def split_back(result):
        parts = result.reshape(2, -1, features).astype(half)
        return lax.all_to_all(parts, "seq", split_axis=0, concat_axis=0, tiled=True)

    output = split_back(hidden).astype(single)

    def scatter(term):
        share = lax.psum_scatter(term.astype(half), "wide", scatter_dimension=0, tiled=True)
        other = lax.ppermute(share, "seq", swap)
        return share.astype(single) + other.astype(single)

    gradient = my_upstream.astype(single)
    weight_grads = [None] * layers
    small_grads = [None] * layers
    for layer in range(layers - 1, -1, -1):
        qkv_full, out_full, up_full, down_full = matrices[layer]
        gains = all_gains[layer]
        (hidden, normed, packed, totals, attended, middle, second, pre_activation, activated) = (
            saved[layer]
        )
        branch = gradient.astype(half)
        down_share = scatter(contract(activated, branch, 0, 0))
        down_bias_grad = jnp.sum(branch, axis=0, dtype=single)
        activated_grad = contract(branch, down_full, 1, 1)
        pull = jax.vjp(lambda value: jax.nn.gelu(value, approximate=True), pre_activation)[1]
        upper = pull(activated_grad)[0].astype(half)
        up_share = scatter(contract(second, upper, 0, 0))
        up_bias_grad = jnp.sum(upper, axis=0, dtype=single)
        second_grad = contract(upper, up_full, 1, 1)
        middle_part, second_gain, second_offset = layer_norm_grad(middle, gains[1], second_grad)
        middle_grad = gradient + middle_part
        attention_grad = middle_grad.astype(half)
        out_share = scatter(contract(attended, attention_grad, 0, 0))
        out_bias_grad = jnp.sum(attention_grad, axis=0, dtype=single)
        upstream = contract(attention_grad, out_full, 1, 1).astype(half)
        packed_grad = attend_backward(packed, bias, upstream, totals, attended)
        qkv_share = scatter(contract(normed, packed_grad, 0, 0))
        column_sums = jnp.sum(packed_grad, axis=0, dtype=single)
        normed_grad = contract(packed_grad, qkv_full, 1, 1)
        hidden_part, first_gain, first_offset = layer_norm_grad(hidden, gains[0], normed_grad)
        gradient = middle_grad + hidden_part
        weight_grads[layer] = (qkv_share, out_share, up_share, down_share)
        small_grads[layer] = (
            jnp.stack([first_gain, second_gain]),
            jnp.stack(
                [
                    first_offset,
                    column_sums[:features],
                    column_sums[2 * features :],
                    out_bias_grad,
                    second_offset,
                    down_bias_grad,
                ]
            ),
            up_bias_grad,
        )
    input_grad = split_back(gradient).astype(single)

    def by_owner(parts):
        stacked = jnp.stack(parts)
        stacked = stacked.reshape(layers, -1, groups, stacked.shape[-1] // groups)
        return stacked.transpose(2, 0, 1, 3).reshape(groups, -1)

    owned = jnp.concatenate(
        [by_owner([small_grads[layer][part] for layer in range(layers)]) for part in range(3)],
        axis=1,
    )
    owned = lax.psum_scatter(owned, "wide", scatter_dimension=0, tiled=True)[0]
    owned = owned + lax.ppermute(owned, "seq", swap)
    stacked = [
        jnp.stack([weight_grads[layer][part] for layer in range(layers)]) for part in range(4)
    ]
    return (
        output,
        input_grad,
        *stacked,
        owned[:cut_gains].reshape(norm_gains.shape),
        owned[cut_gains:cut_rows].reshape(bias_rows.shape),
        owned[cut_rows:].reshape(up_bias.shape),
    )


def solution(mesh):
    tokens_spec = P("wide", "seq", None)
    matrix_spec = P(None, "wide", None)
    rows_spec = P(None, None, "wide")
    return jax.shard_map(
        per_device,
        mesh=mesh,
        in_specs=(
            tokens_spec,
            P("wide", None),
            P("wide", "seq"),
            P("wide", "seq"),
            tokens_spec,
            matrix_spec,
            matrix_spec,
            matrix_spec,
            matrix_spec,
            rows_spec,
            rows_spec,
            P(None, "wide"),
        ),
        out_specs=(
            tokens_spec,
            tokens_spec,
            matrix_spec,
            matrix_spec,
            matrix_spec,
            matrix_spec,
            rows_spec,
            rows_spec,
            P(None, "wide"),
        ),
        check_vma=False,
    )
```

```python
import functools

import jax
import jax.numpy as jnp
from jax import lax
from jax.experimental import pallas as pl
from jax.experimental.pallas import tpu as pltpu
from jax.sharding import PartitionSpec as P

HEAD_SIZE = 64
PAIR = 2 * HEAD_SIZE
FORWARD_ROWS = 512
BACKWARD_ROWS = 256

epsilon = 1e-05
masked_bias = -1e30
half = jnp.bfloat16
single = jnp.float32


def contract(left, right, left_dim, right_dim):
    return lax.dot_general(
        left, right, (((left_dim,), (right_dim,)), ((), ())), preferred_element_type=jnp.float32
    )


def first_head_lanes():
    return lax.broadcasted_iota(jnp.int32, (1, PAIR), 1) < HEAD_SIZE


def one_head_of(pair, head):
    lanes = first_head_lanes()
    keep = lanes if head == 0 else jnp.logical_not(lanes)
    return jnp.where(keep, pair, jnp.zeros_like(pair))


def attend_kernel(query_ref, key_ref, value_ref, bias_ref, out_ref, total_ref, *, rows):
    keys = key_ref[...]
    values = value_ref[...]
    scale = jnp.asarray(HEAD_SIZE ** (-0.5), half)
    for start in range(0, keys.shape[0], rows):
        window = pl.ds(start, rows)
        queries = query_ref[window, :] * scale
        bias = bias_ref[:, window]
        attended = []
        for head in range(2):
            scores = contract(keys, one_head_of(queries, head), 1, 1) + bias
            top = jnp.max(scores, axis=0, keepdims=True)
            weights = jnp.exp(scores - top)
            total = jnp.sum(weights, axis=0, keepdims=True)
            mixed = contract(values, weights.astype(half), 0, 0) * (1.0 / total)
            attended.append(mixed[HEAD_SIZE * head : HEAD_SIZE * (head + 1)])
            total_ref[head : head + 1, window] = top + jnp.log(total)
        out_ref[window, :] = jnp.concatenate(attended, 0).T.astype(half)


def attend_forward(packed, bias):
    length = packed.shape[0]
    features = packed.shape[1] // 3
    pairs = features // PAIR
    columns = lambda part: pl.BlockSpec((length, PAIR), lambda i: (0, part * pairs + i))
    return pl.pallas_call(
        functools.partial(attend_kernel, rows=FORWARD_ROWS),
        grid=(pairs,),
        in_specs=[
            columns(0),
            columns(1),
            columns(2),
            pl.BlockSpec((length, length), lambda i: (0, 0)),
        ],
        out_specs=[columns(0), pl.BlockSpec((None, 2, length), lambda i: (i, 0, 0))],
        out_shape=[
            jax.ShapeDtypeStruct((length, features), half),
            jax.ShapeDtypeStruct((pairs, 2, length), single),
        ],
        compiler_params=pltpu.CompilerParams(vmem_limit_bytes=56 << 20),
        cost_estimate=pl.CostEstimate(
            flops=4 * length * length * features * 4,
            bytes_accessed=8 * length * features,
            transcendentals=length * length * features // HEAD_SIZE,
        ),
        name="attend_forward",
    )(packed, packed, packed, bias)


def attend_grad_kernel(
    query_ref,
    key_ref,
    value_ref,
    bias_ref,
    upstream_ref,
    total_ref,
    attended_ref,
    out_ref,
    key_sum,
    value_sum,
    *,
    rows,
):
    pair = pl.program_id(0)
    features = out_ref.shape[1] // 3
    keys = key_ref[...]
    values = value_ref[...]
    scale = HEAD_SIZE ** (-0.5)
    for start in range(0, keys.shape[0], rows):
        window = pl.ds(start, rows)
        queries = query_ref[window, :] * jnp.asarray(scale, half)
        upstream = upstream_ref[window, :]
        product = (upstream.astype(single) * attended_ref[window, :].astype(single)).T
        bias = bias_ref[:, window]
        query_grads, key_grad, value_grad = [], 0.0, 0.0
        for head in range(2):
            head_queries = one_head_of(queries, head)
            head_upstream = one_head_of(upstream, head)
            inner = jnp.sum(
                product[HEAD_SIZE * head : HEAD_SIZE * (head + 1)], axis=0, keepdims=True
            )
            scores = contract(keys, head_queries, 1, 1) + bias
            weights = jnp.exp(scores - total_ref[head : head + 1, window])
            weight_grads = contract(values, head_upstream, 1, 1)
            score_grads = (weights * (weight_grads - inner)).astype(half)
            value_grad = value_grad + contract(weights.astype(half), head_upstream, 1, 0)
            key_grad = key_grad + contract(score_grads, head_queries, 1, 0)
            query_grads.append(
                contract(keys, score_grads, 0, 0)[HEAD_SIZE * head : HEAD_SIZE * (head + 1)]
            )
        out_ref[window, pl.ds(pl.multiple_of(pair * PAIR, PAIR), PAIR)] = (
            jnp.concatenate(query_grads, 0).T * scale
        ).astype(half)
        if start == 0:
            key_sum[...] = key_grad
            value_sum[...] = value_grad
        else:
            key_sum[...] += key_grad
            value_sum[...] += value_grad
    out_ref[:, pl.ds(pl.multiple_of(features + pair * PAIR, PAIR), PAIR)] = key_sum[...].astype(
        half
    )
    out_ref[:, pl.ds(pl.multiple_of(2 * features + pair * PAIR, PAIR), PAIR)] = value_sum[
        ...
    ].astype(half)


def attend_backward(packed, bias, upstream, totals, attended):
    length = packed.shape[0]
    features = packed.shape[1] // 3
    pairs = features // PAIR
    columns = lambda part: pl.BlockSpec((length, PAIR), lambda i: (0, part * pairs + i))
    return pl.pallas_call(
        functools.partial(attend_grad_kernel, rows=BACKWARD_ROWS),
        grid=(pairs,),
        in_specs=[
            columns(0),
            columns(1),
            columns(2),
            pl.BlockSpec((length, length), lambda i: (0, 0)),
            columns(0),
            pl.BlockSpec((None, 2, length), lambda i: (i, 0, 0)),
            columns(0),
        ],
        out_specs=pl.BlockSpec((length, 3 * features), lambda i: (0, 0)),
        out_shape=jax.ShapeDtypeStruct((length, 3 * features), half),
        scratch_shapes=[pltpu.VMEM((length, PAIR), single)] * 2,
        compiler_params=pltpu.CompilerParams(vmem_limit_bytes=56 << 20),
        cost_estimate=pl.CostEstimate(
            flops=10 * length * length * features * 4,
            bytes_accessed=16 * length * features,
            transcendentals=length * length * features // HEAD_SIZE,
        ),
        name="attend_backward",
    )(packed, packed, packed, bias, upstream, totals, attended)


def layer_norm(hidden, scale_gain, offset):
    center = hidden - jnp.mean(hidden, axis=-1, keepdims=True)
    spread = jnp.mean(center * center, axis=-1, keepdims=True)
    return center * lax.rsqrt(spread + epsilon) * scale_gain + offset


def layer_norm_grad(hidden, scale_gain, upstream):
    center = hidden - jnp.mean(hidden, axis=-1, keepdims=True)
    inverse = lax.rsqrt(jnp.mean(center * center, axis=-1, keepdims=True) + epsilon)
    normal = center * inverse
    scaled = upstream * scale_gain
    slope = jnp.mean(scaled, axis=-1, keepdims=True)
    tilt = jnp.mean(scaled * normal, axis=-1, keepdims=True)
    return (
        inverse * (scaled - slope - normal * tilt),
        jnp.sum(upstream * normal, axis=0),
        jnp.sum(upstream, axis=0),
    )


def layer_forward(hidden, matrices, rows, bias):
    qkv_weight, out_weight, up_weight, down_weight = matrices
    gains, offsets, up_bias = rows
    normed = layer_norm(hidden, gains[0], offsets[0]).astype(half)
    shift = jnp.concatenate([offsets[1], jnp.zeros_like(offsets[1]), offsets[2]])
    packed = (contract(normed, qkv_weight, 1, 0) + shift).astype(half)
    attended, totals = attend_forward(packed, bias)
    middle = hidden + (contract(attended, out_weight, 1, 0) + offsets[3])
    second = layer_norm(middle, gains[1], offsets[4]).astype(half)
    pre_activation = contract(second, up_weight, 1, 0) + up_bias
    activated = jax.nn.gelu(pre_activation, approximate=True).astype(half)
    result = middle + (contract(activated, down_weight, 1, 0) + offsets[5])
    return (
        result,
        (hidden, normed, packed, totals, attended, middle, second, pre_activation, activated),
    )


def per_device(
    tokens,
    time_embed,
    segment_ids,
    pad_mask,
    out_grad,
    qkv_weight,
    out_weight,
    up_weight,
    down_weight,
    norm_gains,
    bias_rows,
    up_bias,
):
    layers = qkv_weight.shape[0]
    features = tokens.shape[2]
    groups = lax.axis_size("wide")
    swap = [(0, 1), (1, 0)]

    def whole_sequence(part):
        return lax.all_to_all(part, "seq", split_axis=0, concat_axis=1, tiled=True)[0]

    marks = whole_sequence(jnp.stack([segment_ids, pad_mask], axis=2))
    my_tokens = whole_sequence(tokens)
    my_upstream = whole_sequence(out_grad)
    my_time = lax.dynamic_index_in_dim(time_embed, lax.axis_index("seq"), 0, keepdims=True)

    sources = (qkv_weight, out_weight, up_weight, down_weight)
    small = jnp.concatenate(
        [norm_gains.reshape(-1), bias_rows.reshape(-1), up_bias.reshape(-1)]
    )
    matrices = [[None] * 4 for _ in range(layers)]
    side = small.reshape(qkv_weight.shape[1], -1)
    side_width = side.shape[1]
    side = jnp.pad(side, ((0, 0), (0, -side_width % PAIR)))
    first_whole = lax.all_gather(
        jnp.concatenate([qkv_weight[0], side], axis=1), "wide", axis=0, tiled=True
    )
    matrices[0][0] = first_whole[:, : qkv_weight.shape[2]]
    small_whole = first_whole[:, qkv_weight.shape[2] :][:, :side_width].reshape(groups, -1)
    for layer in range(layers):
        for index, source in enumerate(sources):
            if matrices[layer][index] is None:
                matrices[layer][index] = lax.all_gather(
                    source[layer], "wide", axis=0, tiled=True
                )
    cut_gains = norm_gains.size
    cut_rows = cut_gains + bias_rows.size

    def whole_rows(part, count):
        parts = part.reshape(groups, layers, count, -1)
        return parts.transpose(1, 2, 0, 3).reshape(layers, count, -1).astype(single)

    all_gains = whole_rows(small_whole[:, :cut_gains], norm_gains.shape[1])
    all_offsets = whole_rows(small_whole[:, cut_gains:cut_rows], bias_rows.shape[1])
    all_up_bias = whole_rows(small_whole[:, cut_rows:], 1)[:, 0]

    doc, pad = marks[:, 0], marks[:, 1]
    positions = jnp.arange(doc.shape[0])
    allowed = (doc[:, None] == doc[None, :]) & (
        (pad[:, None] == 1) | (positions[:, None] == positions[None, :])
    )
    bias = jnp.where(allowed, 0.0, masked_bias)

    hidden = my_tokens.astype(single) + my_time
    saved = []
    for layer in range(layers):
        rows = (all_gains[layer], all_offsets[layer], all_up_bias[layer])
        hidden, kept = layer_forward(hidden, matrices[layer], rows, bias)
        saved.append(kept)

    def split_back(result):
        parts = result.reshape(2, -1, features).astype(half)
        return lax.all_to_all(parts, "seq", split_axis=0, concat_axis=0, tiled=True)

    output = split_back(hidden)

    core = lax.axis_index("wide") & 1
    row_unit = qkv_weight.shape[1]
    pair_up = lambda bit: [(index, index ^ bit) for index in range(groups)]

    def column_half(array, which):
        count = array.shape[1] // 2
        return lax.dynamic_slice_in_dim(array, which * count, count, axis=1)

    def core_terms(left, right):
        return contract(left, column_half(right, 1 - core), 0, 0).astype(half)

    def merge_cores(left, right, received):
        kept = contract(left, column_half(right, core), 0, 0) + received.astype(single)
        kept = kept.astype(half)
        pieces = kept.shape[0] // (groups * row_unit)
        kept = kept.reshape(groups // 2, 2, pieces, row_unit, kept.shape[1])
        return [kept[:, :, piece] for piece in range(pieces)]

    def side_of(array, which, axis):
        return lax.dynamic_index_in_dim(array, which, axis, keepdims=False)

    def reduce_group(terms):
        place = lax.axis_index("seq")
        pieces, counts = [], []
        arrived = yield [lax.ppermute(core_terms(*term), "wide", pair_up(1)) for term in terms]
        for (left, right), received in zip(terms, arrived):
            merged = merge_cores(left, right, received)
            counts.append((len(merged), merged[0].shape[-1]))
            pieces += merged
        sent = jnp.concatenate([side_of(piece, 1 - place, 1) for piece in pieces], axis=-1)
        kept = jnp.concatenate([side_of(piece, place, 1) for piece in pieces], axis=-1)
        (received,) = yield [lax.ppermute(sent, "seq", swap)]
        current = (kept.astype(single) + received.astype(single)).astype(half)
        bit = 2
        while bit < groups:
            current = current.reshape(-1, 2, row_unit, current.shape[-1])
            mine = (lax.axis_index("wide") >> (bit.bit_length() - 1)) & 1
            sent = side_of(current, 1 - mine, 1)
            (received,) = yield [lax.ppermute(sent, "wide", pair_up(bit))]
            kept = side_of(current, mine, 1)
            current = (kept.astype(single) + received.astype(single)).astype(half)
            bit *= 2
        current = current.reshape(row_unit, -1)
        (other,) = yield [lax.ppermute(current, "seq", swap)]
        same = place == core
        owned = jnp.where(same, current, other)
        passed = jnp.where(same, other, current)
        (received,) = yield [lax.ppermute(passed, "wide", pair_up(1))]
        low = jnp.where(core == 0, owned, received)
        high = jnp.where(core == 0, received, owned)
        shares, start = [], 0
        for count, width in counts:
            rows = []
            for _ in range(count):
                window = slice(start, start + width)
                rows.append(jnp.concatenate([low[:, window], high[:, window]], axis=1))
                start += width
            shares.append(jnp.concatenate(rows, axis=0).astype(single))
        return shares

    weight_grads = [[None] * 4 for _ in range(layers)]
    running = []

    def begin(layer, parts, terms):
        steps = reduce_group(terms)
        running.append([layer, parts, steps, next(steps)])

    def advance(main):
        if not running:
            return main
        flying = [entry[3] for entry in running]
        main, flying = lax.optimization_barrier((main, flying))
        for entry, arrived in zip(list(running), flying):
            layer, parts, steps, _ = entry
            try:
                entry[3] = steps.send(arrived)
            except StopIteration as stop:
                for part, share in zip(parts, stop.value):
                    weight_grads[layer][part] = share
                running.remove(entry)
        return main

    gradient = my_upstream.astype(single)
    small_grads = [None] * layers
    for layer in range(layers - 1, -1, -1):
        qkv_full, out_full, up_full, down_full = matrices[layer]
        gains = all_gains[layer]
        (hidden, normed, packed, totals, attended, middle, second, pre_activation, activated) = (
            saved[layer]
        )
        branch = gradient.astype(half)
        down_bias_grad = jnp.sum(branch, axis=0, dtype=single)
        activated_grad = contract(branch, down_full, 1, 1)
        pull = jax.vjp(lambda value: jax.nn.gelu(value, approximate=True), pre_activation)[1]
        upper = pull(activated_grad)[0].astype(half)
        upper = advance(upper)
        first_batch = ((3, 2), ((activated, branch), (second, upper)))
        if layer:
            begin(layer, *first_batch)
        up_bias_grad = jnp.sum(upper, axis=0, dtype=single)
        second_grad = contract(upper, up_full, 1, 1)
        middle_part, second_gain, second_offset = layer_norm_grad(middle, gains[1], second_grad)
        middle_grad = gradient + middle_part
        attention_grad = middle_grad.astype(half)
        out_bias_grad = jnp.sum(attention_grad, axis=0, dtype=single)
        attention_grad = advance(attention_grad)
        if not layer:
            begin(layer, (3, 2, 1), first_batch[1] + ((attended, attention_grad),))
        upstream = contract(attention_grad, out_full, 1, 1).astype(half)
        if not layer:
            upstream = advance(upstream)
        if layer == layers - 1:
            upstream, output = lax.optimization_barrier((upstream, output))
            output = output.astype(single)
        packed_grad = attend_backward(packed, bias, upstream, totals, attended)
        packed_grad = advance(packed_grad)
        if layer:
            begin(layer, (0, 1), ((normed, packed_grad), (attended, attention_grad)))
        else:
            begin(layer, (0,), ((normed, packed_grad),))
        column_sums = jnp.sum(packed_grad, axis=0, dtype=single)
        normed_grad = contract(packed_grad, qkv_full, 1, 1)
        hidden_part, first_gain, first_offset = layer_norm_grad(hidden, gains[0], normed_grad)
        gradient = advance(middle_grad + hidden_part)
        small_grads[layer] = (
            jnp.stack([first_gain, second_gain]),
            jnp.stack(
                [
                    first_offset,
                    column_sums[:features],
                    column_sums[2 * features :],
                    out_bias_grad,
                    second_offset,
                    down_bias_grad,
                ]
            ),
            up_bias_grad,
        )
    input_grad = split_back(gradient)
    while running:
        input_grad = advance(input_grad)
    input_grad = input_grad.astype(single)

    def by_owner(parts):
        stacked = jnp.stack(parts)
        stacked = stacked.reshape(layers, -1, groups, stacked.shape[-1] // groups)
        return stacked.transpose(2, 0, 1, 3).reshape(groups, -1)

    owned = jnp.concatenate(
        [by_owner([small_grads[layer][part] for layer in range(layers)]) for part in range(3)],
        axis=1,
    )
    owned = lax.psum_scatter(owned, "wide", scatter_dimension=0, tiled=True)[0]
    owned = owned + lax.ppermute(owned, "seq", swap)
    stacked = [
        jnp.stack([weight_grads[layer][part] for layer in range(layers)]) for part in range(4)
    ]
    return (
        output,
        input_grad,
        *stacked,
        owned[:cut_gains].reshape(norm_gains.shape),
        owned[cut_gains:cut_rows].reshape(bias_rows.shape),
        owned[cut_rows:].reshape(up_bias.shape),
    )


def solution(mesh):
    tokens_spec = P("wide", "seq", None)
    matrix_spec = P(None, "wide", None)
    rows_spec = P(None, None, "wide")
    return jax.shard_map(
        per_device,
        mesh=mesh,
        in_specs=(
            tokens_spec,
            P("wide", None),
            P("wide", "seq"),
            P("wide", "seq"),
            tokens_spec,
            matrix_spec,
            matrix_spec,
            matrix_spec,
            matrix_spec,
            rows_spec,
            rows_spec,
            P(None, "wide"),
        ),
        out_specs=(
            tokens_spec,
            tokens_spec,
            matrix_spec,
            matrix_spec,
            matrix_spec,
            matrix_spec,
            rows_spec,
            rows_spec,
            P(None, "wide"),
        ),
        check_vma=False,
    )
```

```python
import functools

import jax
import jax.numpy as jnp
from jax import lax
from jax.experimental import pallas as pl
from jax.experimental.pallas import tpu as pltpu
from jax.sharding import PartitionSpec as P

HEAD_SIZE = 64
PAIR = 2 * HEAD_SIZE
FORWARD_ROWS = 512
BACKWARD_ROWS = 256

epsilon = 1e-05
masked_bias = -1e30
half = jnp.bfloat16
single = jnp.float32


def contract(left, right, left_dim, right_dim):
    return lax.dot_general(
        left, right, (((left_dim,), (right_dim,)), ((), ())), preferred_element_type=jnp.float32
    )


def first_head_lanes():
    return lax.broadcasted_iota(jnp.int32, (1, PAIR), 1) < HEAD_SIZE


def one_head_of(pair, head):
    lanes = first_head_lanes()
    keep = lanes if head == 0 else jnp.logical_not(lanes)
    return jnp.where(keep, pair, jnp.zeros_like(pair))


def attend_kernel(query_ref, key_ref, value_ref, bias_ref, out_ref, total_ref, *, rows):
    keys = key_ref[...]
    values = value_ref[...]
    scale = jnp.asarray(HEAD_SIZE ** (-0.5), half)
    for start in range(0, keys.shape[0], rows):
        window = pl.ds(start, rows)
        queries = query_ref[window, :] * scale
        bias = bias_ref[:, window]
        attended = []
        for head in range(2):
            scores = contract(keys, one_head_of(queries, head), 1, 1) + bias
            top = jnp.max(scores, axis=0, keepdims=True)
            weights = jnp.exp(scores - top)
            total = jnp.sum(weights, axis=0, keepdims=True)
            mixed = contract(values, weights.astype(half), 0, 0) * (1.0 / total)
            attended.append(mixed[HEAD_SIZE * head : HEAD_SIZE * (head + 1)])
            total_ref[head : head + 1, window] = top + jnp.log(total)
        out_ref[window, :] = jnp.concatenate(attended, 0).T.astype(half)


def attend_forward(packed, bias):
    length = packed.shape[0]
    features = packed.shape[1] // 3
    pairs = features // PAIR
    columns = lambda part: pl.BlockSpec((length, PAIR), lambda i: (0, part * pairs + i))
    return pl.pallas_call(
        functools.partial(attend_kernel, rows=FORWARD_ROWS),
        grid=(pairs,),
        in_specs=[
            columns(0),
            columns(1),
            columns(2),
            pl.BlockSpec((length, length), lambda i: (0, 0)),
        ],
        out_specs=[columns(0), pl.BlockSpec((None, 2, length), lambda i: (i, 0, 0))],
        out_shape=[
            jax.ShapeDtypeStruct((length, features), half),
            jax.ShapeDtypeStruct((pairs, 2, length), single),
        ],
        compiler_params=pltpu.CompilerParams(vmem_limit_bytes=56 << 20),
        cost_estimate=pl.CostEstimate(
            flops=4 * length * length * features * 4,
            bytes_accessed=8 * length * features,
            transcendentals=length * length * features // HEAD_SIZE,
        ),
        name="attend_forward",
    )(packed, packed, packed, bias)


def attend_grad_kernel(
    query_ref,
    key_ref,
    value_ref,
    bias_ref,
    upstream_ref,
    total_ref,
    attended_ref,
    out_ref,
    key_sum,
    value_sum,
    *,
    rows,
):
    pair = pl.program_id(0)
    features = out_ref.shape[1] // 3
    keys = key_ref[...]
    values = value_ref[...]
    scale = HEAD_SIZE ** (-0.5)
    for start in range(0, keys.shape[0], rows):
        window = pl.ds(start, rows)
        queries = query_ref[window, :] * jnp.asarray(scale, half)
        upstream = upstream_ref[window, :]
        product = (upstream.astype(single) * attended_ref[window, :].astype(single)).T
        bias = bias_ref[:, window]
        query_grads, key_grad, value_grad = [], 0.0, 0.0
        for head in range(2):
            head_queries = one_head_of(queries, head)
            head_upstream = one_head_of(upstream, head)
            inner = jnp.sum(
                product[HEAD_SIZE * head : HEAD_SIZE * (head + 1)], axis=0, keepdims=True
            )
            scores = contract(keys, head_queries, 1, 1) + bias
            weights = jnp.exp(scores - total_ref[head : head + 1, window])
            weight_grads = contract(values, head_upstream, 1, 1)
            score_grads = (weights * (weight_grads - inner)).astype(half)
            value_grad = value_grad + contract(weights.astype(half), head_upstream, 1, 0)
            key_grad = key_grad + contract(score_grads, head_queries, 1, 0)
            query_grads.append(
                contract(keys, score_grads, 0, 0)[HEAD_SIZE * head : HEAD_SIZE * (head + 1)]
            )
        out_ref[window, pl.ds(pl.multiple_of(pair * PAIR, PAIR), PAIR)] = (
            jnp.concatenate(query_grads, 0).T * scale
        ).astype(half)
        if start == 0:
            key_sum[...] = key_grad
            value_sum[...] = value_grad
        else:
            key_sum[...] += key_grad
            value_sum[...] += value_grad
    out_ref[:, pl.ds(pl.multiple_of(features + pair * PAIR, PAIR), PAIR)] = key_sum[...].astype(
        half
    )
    out_ref[:, pl.ds(pl.multiple_of(2 * features + pair * PAIR, PAIR), PAIR)] = value_sum[
        ...
    ].astype(half)


def attend_backward(packed, bias, upstream, totals, attended):
    length = packed.shape[0]
    features = packed.shape[1] // 3
    pairs = features // PAIR
    columns = lambda part: pl.BlockSpec((length, PAIR), lambda i: (0, part * pairs + i))
    return pl.pallas_call(
        functools.partial(attend_grad_kernel, rows=BACKWARD_ROWS),
        grid=(pairs,),
        in_specs=[
            columns(0),
            columns(1),
            columns(2),
            pl.BlockSpec((length, length), lambda i: (0, 0)),
            columns(0),
            pl.BlockSpec((None, 2, length), lambda i: (i, 0, 0)),
            columns(0),
        ],
        out_specs=pl.BlockSpec((length, 3 * features), lambda i: (0, 0)),
        out_shape=jax.ShapeDtypeStruct((length, 3 * features), half),
        scratch_shapes=[pltpu.VMEM((length, PAIR), single)] * 2,
        compiler_params=pltpu.CompilerParams(vmem_limit_bytes=56 << 20),
        cost_estimate=pl.CostEstimate(
            flops=10 * length * length * features * 4,
            bytes_accessed=16 * length * features,
            transcendentals=length * length * features // HEAD_SIZE,
        ),
        name="attend_backward",
    )(packed, packed, packed, bias, upstream, totals, attended)


def place_pieces(pieces, out_shape, targets, indices):
    def kernel(index_ref, *refs):
        sources, out_ref, semaphores = refs[: len(pieces)], refs[-2], refs[-1]
        copies = [
            pltpu.make_async_copy(
                source, out_ref.at[target(index_ref)], semaphores.at[number]
            )
            for number, (source, target) in enumerate(zip(sources, targets))
        ]
        for copy in copies:
            copy.start()
        for copy in copies:
            copy.wait()

    size = 2 * 2
    for extent in out_shape:
        size *= extent
    anywhere = pl.BlockSpec(memory_space=pl.ANY)
    return pl.pallas_call(
        kernel,
        in_specs=[pl.BlockSpec(memory_space=pltpu.SMEM)] + [anywhere] * len(pieces),
        out_specs=anywhere,
        out_shape=jax.ShapeDtypeStruct(out_shape, pieces[0].dtype),
        scratch_shapes=[pltpu.SemaphoreType.DMA((len(pieces),))],
        cost_estimate=pl.CostEstimate(flops=0, bytes_accessed=size, transcendentals=0),
        name="place_pieces",
    )(indices, *pieces)


def layer_norm(hidden, scale_gain, offset):
    center = hidden - jnp.mean(hidden, axis=-1, keepdims=True)
    spread = jnp.mean(center * center, axis=-1, keepdims=True)
    return center * lax.rsqrt(spread + epsilon) * scale_gain + offset


def layer_norm_grad(hidden, scale_gain, upstream):
    center = hidden - jnp.mean(hidden, axis=-1, keepdims=True)
    inverse = lax.rsqrt(jnp.mean(center * center, axis=-1, keepdims=True) + epsilon)
    normal = center * inverse
    scaled = upstream * scale_gain
    slope = jnp.mean(scaled, axis=-1, keepdims=True)
    tilt = jnp.mean(scaled * normal, axis=-1, keepdims=True)
    return (
        inverse * (scaled - slope - normal * tilt),
        jnp.sum(upstream * normal, axis=0),
        jnp.sum(upstream, axis=0),
    )


def per_device(
    tokens,
    time_embed,
    segment_ids,
    pad_mask,
    out_grad,
    qkv_weight,
    out_weight,
    up_weight,
    down_weight,
    norm_gains,
    bias_rows,
    up_bias,
):
    layers = qkv_weight.shape[0]
    features = tokens.shape[2]
    groups = lax.axis_size("wide")
    swap = [(0, 1), (1, 0)]

    def whole_sequence(part):
        return lax.all_to_all(part, "seq", split_axis=0, concat_axis=1, tiled=True)[0]

    core = lax.axis_index("wide") & 1
    place = lax.axis_index("seq")
    indices = jnp.stack([core, place]).astype(jnp.int32)
    row_unit = qkv_weight.shape[1]
    pair_up = lambda bit: [(index, index ^ bit) for index in range(groups)]
    bit_of = lambda bit: (lax.axis_index("wide") >> (bit.bit_length() - 1)) & 1
    running = []

    def begin(steps, finish):
        running.append([steps, finish, next(steps)])

    def advance(main):
        if not running:
            return main
        main, flying = lax.optimization_barrier((main, [entry[2] for entry in running]))
        for entry, arrived in zip(list(running), flying):
            try:
                entry[2] = entry[0].send(arrived)
            except StopIteration as stop:
                entry[1](stop.value)
                running.remove(entry)
        return main

    def side_of(array, which, axis):
        return lax.dynamic_index_in_dim(array, which, axis, keepdims=False)

    def gather_steps(shard, split_rows):
        rows, columns = shard.shape
        if split_rows:
            rows //= 2
            mine = side_of(shard.reshape(2, rows, columns), place, 0)
        else:
            columns //= 2
            mine = lax.dynamic_slice_in_dim(shard, place * columns, columns, axis=1)
        current = mine[None]
        bit = groups // 2
        while bit > 1:
            (received,) = yield [lax.ppermute(current, "wide", pair_up(bit))]
            count = current.shape[0]
            current = place_pieces(
                [current, received],
                (count, 2, rows, columns),
                [lambda ref: (slice(None), ref[0]), lambda ref: (slice(None), 1 - ref[0])],
                bit_of(bit).reshape(1).astype(jnp.int32),
            ).reshape(2 * count, rows, columns)
            bit //= 2
        (beside,) = yield [lax.ppermute(current, "seq", swap)]
        passed = yield [lax.ppermute(part, "wide", pair_up(1)) for part in (current, beside)]
        count = current.shape[0]

        def target(own_core, own_place):
            def where(ref):
                which_core = ref[0] if own_core else 1 - ref[0]
                which_place = ref[1] if own_place else 1 - ref[1]
                if split_rows:
                    return (slice(None), which_core, which_place)
                start = pl.multiple_of(which_place * columns, columns)
                return (slice(None), which_core, slice(None), pl.ds(start, columns))

            return where

        whole = place_pieces(
            [current, beside, *passed],
            (count, 2, 2, rows, columns) if split_rows else (count, 2, rows, 2 * columns),
            [target(True, True), target(True, False), target(False, True), target(False, False)],
            indices,
        )
        return whole.reshape(-1, shard.shape[1])

    my_tokens = whole_sequence(tokens)
    marks = whole_sequence(jnp.stack([segment_ids, pad_mask], axis=2))
    my_time = lax.dynamic_index_in_dim(time_embed, place, 0, keepdims=True)

    small = jnp.concatenate(
        [norm_gains.reshape(-1), bias_rows.reshape(-1), up_bias.reshape(-1)]
    )
    side = small.reshape(row_unit, -1)
    side_width = side.shape[1]
    side = jnp.pad(side, ((0, 0), (0, -side_width % PAIR)))
    cuts = [0]
    for source in (qkv_weight, out_weight, up_weight):
        cuts.append(cuts[-1] + source.shape[2])

    def beside_each_other(layer, *more):
        parts = [qkv_weight[layer], out_weight[layer], up_weight[layer], *more]
        return jnp.concatenate(parts, axis=1)

    def split_matrices(joined):
        return [joined[:, low:high] for low, high in zip(cuts, cuts[1:])]

    first_whole = lax.all_gather(beside_each_other(0, side), "wide", axis=0, tiled=True)
    first_down = lax.all_gather(down_weight[0], "wide", axis=0, tiled=True)
    matrices = [None] * layers
    matrices[0] = split_matrices(first_whole) + [first_down]
    small_whole = first_whole[:, cuts[-1] :][:, :side_width].reshape(groups, -1)
    cut_gains = norm_gains.size
    cut_rows = cut_gains + bias_rows.size

    def whole_rows(part, count):
        parts = part.reshape(groups, layers, count, -1)
        return parts.transpose(1, 2, 0, 3).reshape(layers, count, -1).astype(single)

    all_gains = whole_rows(small_whole[:, :cut_gains], norm_gains.shape[1])
    all_offsets = whole_rows(small_whole[:, cut_gains:cut_rows], bias_rows.shape[1])
    all_up_bias = whole_rows(small_whole[:, cut_rows:], 1)[:, 0]

    doc, pad = marks[:, 0], marks[:, 1]
    positions = jnp.arange(doc.shape[0])
    allowed = (doc[:, None] == doc[None, :]) & (
        (pad[:, None] == 1) | (positions[:, None] == positions[None, :])
    )
    bias = jnp.where(allowed, 0.0, masked_bias)

    joined = {}
    downs = {}
    for layer in range(1, layers):
        begin(
            gather_steps(beside_each_other(layer), False),
            functools.partial(joined.__setitem__, layer),
        )
    bit = groups // 2
    while bit > 1:
        my_tokens = advance(my_tokens)
        bit //= 2
    hidden = my_tokens.astype(single) + my_time
    saved = []
    for layer in range(layers):
        if layer:
            matrices[layer] = split_matrices(joined[layer]) + [None]
        qkv_full, out_full, up_full, down_full = matrices[layer]
        gains, offsets = all_gains[layer], all_offsets[layer]
        before = hidden
        normed = layer_norm(hidden, gains[0], offsets[0]).astype(half)
        shift = jnp.concatenate([offsets[1], jnp.zeros_like(offsets[1]), offsets[2]])
        packed = (contract(normed, qkv_full, 1, 0) + shift).astype(half)
        if layer:
            packed = advance(packed)
        attended, totals = attend_forward(packed, bias)
        attended = advance(attended)
        if layer == 0:
            for later in range(1, layers):
                begin(
                    gather_steps(down_weight[later], True),
                    functools.partial(downs.__setitem__, later),
                )
            attended, out_grad = lax.optimization_barrier((attended, out_grad))
            my_upstream = whole_sequence(out_grad)
        middle = hidden + (contract(attended, out_full, 1, 0) + offsets[3])
        second = layer_norm(middle, gains[1], offsets[4]).astype(half)
        if layer:
            second = advance(second)
        pre_activation = contract(second, up_full, 1, 0) + all_up_bias[layer]
        activated = jax.nn.gelu(pre_activation, approximate=True).astype(half)
        activated = advance(activated)
        if layer:
            while layer not in downs:
                activated = advance(activated)
            matrices[layer][3] = down_full = downs[layer]
        hidden = middle + (contract(activated, down_full, 1, 0) + offsets[5])
        if layer < layers - 1:
            while layer + 1 not in joined:
                hidden = advance(hidden)
            hidden = advance(hidden)
        saved.append(
            (before, normed, packed, totals, attended, middle, second, pre_activation, activated)
        )

    def split_back(result):
        parts = result.reshape(2, -1, features).astype(half)
        return lax.all_to_all(parts, "seq", split_axis=0, concat_axis=0, tiled=True)

    output = split_back(hidden)

    def column_half(array, which):
        count = array.shape[1] // 2
        return lax.dynamic_slice_in_dim(array, which * count, count, axis=1)

    def total_of(addends):
        return functools.reduce(jnp.add, [addend.astype(single) for addend in addends])

    def owner_blocks(array):
        pieces = array.shape[0] // (groups * row_unit)
        array = array.reshape(groups // 2, 2, pieces, row_unit, array.shape[1])
        return [array[:, :, piece] for piece in range(pieces)]

    def reduce_group(terms):
        sent = [contract(left, column_half(right, 1 - core), 0, 0).astype(half) for left, right in terms]
        sent = [lax.ppermute(part, "wide", pair_up(1)) for part in sent]
        kept = [contract(left, column_half(right, core), 0, 0).astype(half) for left, right in terms]
        arrived = yield sent
        counts, blocks = [], ([], [])
        for own, other in zip(kept, arrived):
            own_blocks, other_blocks = owner_blocks(own), owner_blocks(other)
            counts.append((len(own_blocks), own.shape[1]))
            for pair in zip(own_blocks, other_blocks):
                for side in range(2):
                    which = place if side == 0 else 1 - place
                    chosen = [side_of(part, which, 1) for part in pair]
                    blocks[side].append(total_of(chosen).astype(half))
        (received,) = yield [lax.ppermute(jnp.concatenate(blocks[1], axis=-1), "seq", swap)]
        addends = [jnp.concatenate(blocks[0], axis=-1), received]
        width = received.shape[-1]
        bit = 2
        while bit < groups:
            views = [addend.reshape(-1, 2, row_unit, width) for addend in addends]
            mine = bit_of(bit)
            sent = total_of([side_of(view, 1 - mine, 1) for view in views]).astype(half)
            (received,) = yield [lax.ppermute(sent, "wide", pair_up(bit))]
            addends = [side_of(view, mine, 1) for view in views] + [received]
            bit *= 2
        current = total_of(addends).astype(half).reshape(row_unit, width)
        (other,) = yield [lax.ppermute(current, "seq", swap)]
        same = place == core
        owned = jnp.where(same, current, other)
        (received,) = yield [lax.ppermute(jnp.where(same, other, current), "wide", pair_up(1))]
        low = jnp.where(core == 0, owned, received)
        high = jnp.where(core == 0, received, owned)
        shares, start = [], 0
        for count, each in counts:
            rows = []
            for _ in range(count):
                window = slice(start, start + each)
                rows.append(jnp.concatenate([low[:, window], high[:, window]], axis=1))
                start += each
            shares.append(jnp.concatenate(rows, axis=0).astype(single))
        return shares

    def reduce_small(array):
        bit = 1
        while bit < groups:
            view = array.reshape(-1, 2, array.shape[-1])
            mine = bit_of(bit)
            sent = side_of(view, 1 - mine, 1)
            (received,) = yield [lax.ppermute(sent, "wide", pair_up(bit))]
            array = side_of(view, mine, 1) + received
            bit *= 2
        (received,) = yield [lax.ppermute(array, "seq", swap)]
        return (array + received)[0]

    weight_grads = [[None] * 4 for _ in range(layers)]

    def begin_group(layer, parts, terms):
        def finish(shares):
            for part, share in zip(parts, shares):
                weight_grads[layer][part] = share

        begin(reduce_group(terms), finish)

    gradient = my_upstream.astype(single)
    small_grads = [None] * layers
    for layer in range(layers - 1, -1, -1):
        qkv_full, out_full, up_full, down_full = matrices[layer]
        gains = all_gains[layer]
        (hidden, normed, packed, totals, attended, middle, second, pre_activation, activated) = (
            saved[layer]
        )
        branch = gradient.astype(half)
        down_bias_grad = jnp.sum(branch, axis=0, dtype=single)
        activated_grad = contract(branch, down_full, 1, 1)
        pull = jax.vjp(lambda value: jax.nn.gelu(value, approximate=True), pre_activation)[1]
        upper = pull(activated_grad)[0].astype(half)
        upper = advance(upper)
        first_batch = ((3, 2), ((activated, branch), (second, upper)))
        if layer:
            begin_group(layer, *first_batch)
        up_bias_grad = jnp.sum(upper, axis=0, dtype=single)
        second_grad = contract(upper, up_full, 1, 1)
        middle_part, second_gain, second_offset = layer_norm_grad(middle, gains[1], second_grad)
        middle_grad = gradient + middle_part
        attention_grad = middle_grad.astype(half)
        out_bias_grad = jnp.sum(attention_grad, axis=0, dtype=single)
        attention_grad = advance(attention_grad)
        if not layer:
            begin_group(layer, (3, 2, 1), first_batch[1] + ((attended, attention_grad),))
        upstream = contract(attention_grad, out_full, 1, 1).astype(half)
        if not layer:
            upstream = advance(upstream)
        if layer == layers - 1:
            upstream, output = lax.optimization_barrier((upstream, output))
            output = output.astype(single)
        packed_grad = attend_backward(packed, bias, upstream, totals, attended)
        packed_grad = advance(packed_grad)
        if layer:
            begin_group(layer, (0, 1), ((normed, packed_grad), (attended, attention_grad)))
        else:
            begin_group(layer, (0,), ((normed, packed_grad),))
        column_sums = jnp.sum(packed_grad, axis=0, dtype=single)
        normed_grad = contract(packed_grad, qkv_full, 1, 1)
        hidden_part, first_gain, first_offset = layer_norm_grad(hidden, gains[0], normed_grad)
        gradient = advance(middle_grad + hidden_part)
        small_grads[layer] = (
            jnp.stack([first_gain, second_gain]),
            jnp.stack(
                [
                    first_offset,
                    column_sums[:features],
                    column_sums[2 * features :],
                    out_bias_grad,
                    second_offset,
                    down_bias_grad,
                ]
            ),
            up_bias_grad,
        )
    def by_owner(parts):
        stacked = jnp.stack(parts)
        stacked = stacked.reshape(layers, -1, groups, stacked.shape[-1] // groups)
        return stacked.transpose(2, 0, 1, 3).reshape(groups, -1)

    owned = jnp.concatenate(
        [by_owner([small_grads[layer][part] for layer in range(layers)]) for part in range(3)],
        axis=1,
    )
    small_result = []
    begin(reduce_small(owned), small_result.append)
    input_grad = split_back(gradient)
    while running:
        input_grad = advance(input_grad)
    input_grad = input_grad.astype(single)
    owned = small_result[0]
    stacked = [
        jnp.stack([weight_grads[layer][part] for layer in range(layers)]) for part in range(4)
    ]
    return (
        output,
        input_grad,
        *stacked,
        owned[:cut_gains].reshape(norm_gains.shape),
        owned[cut_gains:cut_rows].reshape(bias_rows.shape),
        owned[cut_rows:].reshape(up_bias.shape),
    )


def solution(mesh):
    tokens_spec = P("wide", "seq", None)
    matrix_spec = P(None, "wide", None)
    rows_spec = P(None, None, "wide")
    return jax.shard_map(
        per_device,
        mesh=mesh,
        in_specs=(
            tokens_spec,
            P("wide", None),
            P("wide", "seq"),
            P("wide", "seq"),
            tokens_spec,
            matrix_spec,
            matrix_spec,
            matrix_spec,
            matrix_spec,
            rows_spec,
            rows_spec,
            P(None, "wide"),
        ),
        out_specs=(
            tokens_spec,
            tokens_spec,
            matrix_spec,
            matrix_spec,
            matrix_spec,
            matrix_spec,
            rows_spec,
            rows_spec,
            P(None, "wide"),
        ),
        check_vma=False,
    )
```

```python
import functools

import jax
import jax.numpy as jnp
from jax import lax
from jax.experimental import pallas as pl
from jax.experimental.pallas import tpu as pltpu
from jax.sharding import PartitionSpec as P

HEAD_SIZE = 64
PAIR = 2 * HEAD_SIZE
FORWARD_ROWS = 512
BACKWARD_ROWS = 256

epsilon = 1e-05
masked_bias = -1e30
half = jnp.bfloat16
single = jnp.float32


def contract(left, right, left_dim, right_dim):
    return lax.dot_general(
        left, right, (((left_dim,), (right_dim,)), ((), ())), preferred_element_type=jnp.float32
    )


def first_head_lanes():
    return lax.broadcasted_iota(jnp.int32, (1, PAIR), 1) < HEAD_SIZE


def one_head_of(pair, head):
    lanes = first_head_lanes()
    keep = lanes if head == 0 else jnp.logical_not(lanes)
    return jnp.where(keep, pair, jnp.zeros_like(pair))


def attend_kernel(query_ref, key_ref, value_ref, bias_ref, out_ref, total_ref, *, rows):
    keys = key_ref[...]
    values = value_ref[...]
    scale = jnp.asarray(HEAD_SIZE ** (-0.5), half)
    for start in range(0, keys.shape[0], rows):
        window = pl.ds(start, rows)
        queries = query_ref[window, :] * scale
        bias = bias_ref[:, window]
        attended = []
        for head in range(2):
            scores = contract(keys, one_head_of(queries, head), 1, 1) + bias
            top = jnp.max(scores, axis=0, keepdims=True)
            weights = jnp.exp(scores - top)
            total = jnp.sum(weights, axis=0, keepdims=True)
            mixed = contract(values, weights.astype(half), 0, 0) * (1.0 / total)
            attended.append(mixed[HEAD_SIZE * head : HEAD_SIZE * (head + 1)])
            total_ref[head : head + 1, window] = top + jnp.log(total)
        out_ref[window, :] = jnp.concatenate(attended, 0).T.astype(half)


def attend_forward(packed, bias):
    length = packed.shape[0]
    features = packed.shape[1] // 3
    pairs = features // PAIR
    columns = lambda part: pl.BlockSpec((length, PAIR), lambda i: (0, part * pairs + i))
    return pl.pallas_call(
        functools.partial(attend_kernel, rows=FORWARD_ROWS),
        grid=(pairs,),
        in_specs=[
            columns(0),
            columns(1),
            columns(2),
            pl.BlockSpec((length, length), lambda i: (0, 0)),
        ],
        out_specs=[columns(0), pl.BlockSpec((None, 2, length), lambda i: (i, 0, 0))],
        out_shape=[
            jax.ShapeDtypeStruct((length, features), half),
            jax.ShapeDtypeStruct((pairs, 2, length), single),
        ],
        compiler_params=pltpu.CompilerParams(vmem_limit_bytes=56 << 20),
        cost_estimate=pl.CostEstimate(
            flops=4 * length * length * features * 4,
            bytes_accessed=8 * length * features,
            transcendentals=length * length * features // HEAD_SIZE,
        ),
        name="attend_forward",
    )(packed, packed, packed, bias)


def attend_grad_kernel(
    query_ref,
    key_ref,
    value_ref,
    bias_ref,
    upstream_ref,
    total_ref,
    attended_ref,
    out_ref,
    key_sum,
    value_sum,
    *,
    rows,
):
    pair = pl.program_id(0)
    features = out_ref.shape[1] // 3
    keys = key_ref[...]
    values = value_ref[...]
    scale = HEAD_SIZE ** (-0.5)
    for start in range(0, keys.shape[0], rows):
        window = pl.ds(start, rows)
        queries = query_ref[window, :] * jnp.asarray(scale, half)
        upstream = upstream_ref[window, :]
        product = (upstream.astype(single) * attended_ref[window, :].astype(single)).T
        bias = bias_ref[:, window]
        query_grads, key_grad, value_grad = [], 0.0, 0.0
        for head in range(2):
            head_queries = one_head_of(queries, head)
            head_upstream = one_head_of(upstream, head)
            inner = jnp.sum(
                product[HEAD_SIZE * head : HEAD_SIZE * (head + 1)], axis=0, keepdims=True
            )
            scores = contract(keys, head_queries, 1, 1) + bias
            weights = jnp.exp(scores - total_ref[head : head + 1, window])
            weight_grads = contract(values, head_upstream, 1, 1)
            score_grads = (weights * (weight_grads - inner)).astype(half)
            value_grad = value_grad + contract(weights.astype(half), head_upstream, 1, 0)
            key_grad = key_grad + contract(score_grads, head_queries, 1, 0)
            query_grads.append(
                contract(keys, score_grads, 0, 0)[HEAD_SIZE * head : HEAD_SIZE * (head + 1)]
            )
        out_ref[window, pl.ds(pl.multiple_of(pair * PAIR, PAIR), PAIR)] = (
            jnp.concatenate(query_grads, 0).T * scale
        ).astype(half)
        if start == 0:
            key_sum[...] = key_grad
            value_sum[...] = value_grad
        else:
            key_sum[...] += key_grad
            value_sum[...] += value_grad
    out_ref[:, pl.ds(pl.multiple_of(features + pair * PAIR, PAIR), PAIR)] = key_sum[...].astype(
        half
    )
    out_ref[:, pl.ds(pl.multiple_of(2 * features + pair * PAIR, PAIR), PAIR)] = value_sum[
        ...
    ].astype(half)


def attend_backward(packed, bias, upstream, totals, attended):
    length = packed.shape[0]
    features = packed.shape[1] // 3
    pairs = features // PAIR
    columns = lambda part: pl.BlockSpec((length, PAIR), lambda i: (0, part * pairs + i))
    return pl.pallas_call(
        functools.partial(attend_grad_kernel, rows=BACKWARD_ROWS),
        grid=(pairs,),
        in_specs=[
            columns(0),
            columns(1),
            columns(2),
            pl.BlockSpec((length, length), lambda i: (0, 0)),
            columns(0),
            pl.BlockSpec((None, 2, length), lambda i: (i, 0, 0)),
            columns(0),
        ],
        out_specs=pl.BlockSpec((length, 3 * features), lambda i: (0, 0)),
        out_shape=jax.ShapeDtypeStruct((length, 3 * features), half),
        scratch_shapes=[pltpu.VMEM((length, PAIR), single)] * 2,
        compiler_params=pltpu.CompilerParams(vmem_limit_bytes=56 << 20),
        cost_estimate=pl.CostEstimate(
            flops=10 * length * length * features * 4,
            bytes_accessed=16 * length * features,
            transcendentals=length * length * features // HEAD_SIZE,
        ),
        name="attend_backward",
    )(packed, packed, packed, bias, upstream, totals, attended)


def place_pieces(pieces, out_shape, targets, indices):
    def kernel(index_ref, *refs):
        sources, out_ref, semaphores = refs[: len(pieces)], refs[-2], refs[-1]
        copies = [
            pltpu.make_async_copy(
                source, out_ref.at[target(index_ref)], semaphores.at[number]
            )
            for number, (source, target) in enumerate(zip(sources, targets))
        ]
        for copy in copies:
            copy.start()
        for copy in copies:
            copy.wait()

    size = 2 * 2
    for extent in out_shape:
        size *= extent
    anywhere = pl.BlockSpec(memory_space=pl.ANY)
    return pl.pallas_call(
        kernel,
        in_specs=[pl.BlockSpec(memory_space=pltpu.SMEM)] + [anywhere] * len(pieces),
        out_specs=pl.BlockSpec(memory_space=pltpu.VMEM),
        out_shape=jax.ShapeDtypeStruct(out_shape, pieces[0].dtype),
        scratch_shapes=[pltpu.SemaphoreType.DMA((len(pieces),))],
        compiler_params=pltpu.CompilerParams(vmem_limit_bytes=32 << 20),
        cost_estimate=pl.CostEstimate(flops=0, bytes_accessed=size, transcendentals=0),
        name="place_pieces",
    )(indices, *pieces)


def layer_norm(hidden, scale_gain, offset):
    center = hidden - jnp.mean(hidden, axis=-1, keepdims=True)
    spread = jnp.mean(center * center, axis=-1, keepdims=True)
    return center * lax.rsqrt(spread + epsilon) * scale_gain + offset


def layer_norm_grad(hidden, scale_gain, upstream):
    center = hidden - jnp.mean(hidden, axis=-1, keepdims=True)
    inverse = lax.rsqrt(jnp.mean(center * center, axis=-1, keepdims=True) + epsilon)
    normal = center * inverse
    scaled = upstream * scale_gain
    slope = jnp.mean(scaled, axis=-1, keepdims=True)
    tilt = jnp.mean(scaled * normal, axis=-1, keepdims=True)
    return (
        inverse * (scaled - slope - normal * tilt),
        jnp.sum(upstream * normal, axis=0),
        jnp.sum(upstream, axis=0),
    )


def per_device(
    tokens,
    time_embed,
    segment_ids,
    pad_mask,
    out_grad,
    qkv_weight,
    out_weight,
    up_weight,
    down_weight,
    norm_gains,
    bias_rows,
    up_bias,
):
    layers = qkv_weight.shape[0]
    features = tokens.shape[2]
    groups = lax.axis_size("wide")
    swap = [(0, 1), (1, 0)]

    def whole_sequence(part):
        return lax.all_to_all(part, "seq", split_axis=0, concat_axis=1, tiled=True)[0]

    core = lax.axis_index("wide") & 1
    place = lax.axis_index("seq")
    indices = jnp.stack([core, place]).astype(jnp.int32)
    row_unit = qkv_weight.shape[1]
    pair_up = lambda bit: [(index, index ^ bit) for index in range(groups)]
    bit_of = lambda bit: (lax.axis_index("wide") >> (bit.bit_length() - 1)) & 1
    running = []

    def begin(steps, finish):
        running.append([steps, finish, next(steps)])

    def advance(main):
        if not running:
            return main
        main, flying = lax.optimization_barrier((main, [entry[2] for entry in running]))
        for entry, arrived in zip(list(running), flying):
            try:
                entry[2] = entry[0].send(arrived)
            except StopIteration as stop:
                entry[1](stop.value)
                running.remove(entry)
        return main

    def side_of(array, which, axis):
        return lax.dynamic_index_in_dim(array, which, axis, keepdims=False)

    def gather_steps(shard, split_rows):
        rows, columns = shard.shape
        if split_rows:
            rows //= 2
            mine = side_of(shard.reshape(2, rows, columns), place, 0)
        else:
            columns //= 2
            mine = lax.dynamic_slice_in_dim(shard, place * columns, columns, axis=1)
        current = mine[None]
        bit = groups // 2
        while bit > 1:
            (received,) = yield [lax.ppermute(current, "wide", pair_up(bit))]
            count = current.shape[0]
            current = place_pieces(
                [current, received],
                (count, 2, rows, columns),
                [lambda ref: (slice(None), ref[0]), lambda ref: (slice(None), 1 - ref[0])],
                bit_of(bit).reshape(1).astype(jnp.int32),
            ).reshape(2 * count, rows, columns)
            bit //= 2
        (beside,) = yield [lax.ppermute(current, "seq", swap)]
        passed = yield [lax.ppermute(part, "wide", pair_up(1)) for part in (current, beside)]
        count = current.shape[0]

        def target(own_core, own_place):
            def where(ref):
                which_core = ref[0] if own_core else 1 - ref[0]
                which_place = ref[1] if own_place else 1 - ref[1]
                if split_rows:
                    return (slice(None), which_core, which_place)
                start = pl.multiple_of(which_place * columns, columns)
                return (slice(None), which_core, slice(None), pl.ds(start, columns))

            return where

        whole = place_pieces(
            [current, beside, *passed],
            (count, 2, 2, rows, columns) if split_rows else (count, 2, rows, 2 * columns),
            [target(True, True), target(True, False), target(False, True), target(False, False)],
            indices,
        )
        return whole.reshape(-1, shard.shape[1])

    my_tokens = whole_sequence(tokens)
    marks = whole_sequence(jnp.stack([segment_ids, pad_mask], axis=2))
    my_time = lax.dynamic_index_in_dim(time_embed, place, 0, keepdims=True)

    small = jnp.concatenate(
        [norm_gains.reshape(-1), bias_rows.reshape(-1), up_bias.reshape(-1)]
    )
    side = small.reshape(row_unit, -1)
    side_width = side.shape[1]
    side = jnp.pad(side, ((0, 0), (0, -side_width % PAIR)))
    cuts = [0]
    for source in (qkv_weight, out_weight, up_weight):
        cuts.append(cuts[-1] + source.shape[2])

    def beside_each_other(layer, *more):
        parts = [qkv_weight[layer], out_weight[layer], up_weight[layer], *more]
        return jnp.concatenate(parts, axis=1)

    def split_matrices(joined):
        return [joined[:, low:high] for low, high in zip(cuts, cuts[1:])]

    first_whole = lax.all_gather(beside_each_other(0, side), "wide", axis=0, tiled=True)
    first_down = lax.all_gather(down_weight[0], "wide", axis=0, tiled=True)
    matrices = [None] * layers
    matrices[0] = split_matrices(first_whole) + [first_down]
    small_whole = first_whole[:, cuts[-1] :][:, :side_width].reshape(groups, -1)
    cut_gains = norm_gains.size
    cut_rows = cut_gains + bias_rows.size

    def whole_rows(part, count):
        parts = part.reshape(groups, layers, count, -1)
        return parts.transpose(1, 2, 0, 3).reshape(layers, count, -1).astype(single)

    all_gains = whole_rows(small_whole[:, :cut_gains], norm_gains.shape[1])
    all_offsets = whole_rows(small_whole[:, cut_gains:cut_rows], bias_rows.shape[1])
    all_up_bias = whole_rows(small_whole[:, cut_rows:], 1)[:, 0]

    doc, pad = marks[:, 0], marks[:, 1]
    positions = jnp.arange(doc.shape[0])
    allowed = (doc[:, None] == doc[None, :]) & (
        (pad[:, None] == 1) | (positions[:, None] == positions[None, :])
    )
    bias = jnp.where(allowed, 0.0, masked_bias)

    joined = {}
    downs = {}
    for layer in range(1, layers):
        begin(
            gather_steps(beside_each_other(layer), False),
            functools.partial(joined.__setitem__, layer),
        )
    bit = groups // 2
    while bit > 1:
        my_tokens = advance(my_tokens)
        bit //= 2
    hidden = my_tokens.astype(single) + my_time
    saved = []
    for layer in range(layers):
        if layer:
            matrices[layer] = split_matrices(joined[layer]) + [None]
        qkv_full, out_full, up_full, down_full = matrices[layer]
        gains, offsets = all_gains[layer], all_offsets[layer]
        before = hidden
        normed = layer_norm(hidden, gains[0], offsets[0]).astype(half)
        shift = jnp.concatenate([offsets[1], jnp.zeros_like(offsets[1]), offsets[2]])
        packed = (contract(normed, qkv_full, 1, 0) + shift).astype(half)
        if layer:
            packed = advance(packed)
        attended, totals = attend_forward(packed, bias)
        attended = advance(attended)
        if layer == 0:
            for later in range(1, layers):
                begin(
                    gather_steps(down_weight[later], True),
                    functools.partial(downs.__setitem__, later),
                )
            attended, out_grad = lax.optimization_barrier((attended, out_grad))
            my_upstream = whole_sequence(out_grad)
        middle = hidden + (contract(attended, out_full, 1, 0) + offsets[3])
        second = layer_norm(middle, gains[1], offsets[4]).astype(half)
        if layer:
            second = advance(second)
        pre_activation = contract(second, up_full, 1, 0) + all_up_bias[layer]
        activated = jax.nn.gelu(pre_activation, approximate=True).astype(half)
        activated = advance(activated)
        if layer:
            while layer not in downs:
                activated = advance(activated)
            matrices[layer][3] = down_full = downs[layer]
        hidden = middle + (contract(activated, down_full, 1, 0) + offsets[5])
        if layer < layers - 1:
            while layer + 1 not in joined:
                hidden = advance(hidden)
            hidden = advance(hidden)
        saved.append(
            (before, normed, packed, totals, attended, middle, second, pre_activation, activated)
        )

    def split_back(result):
        parts = result.reshape(2, -1, features).astype(half)
        return lax.all_to_all(parts, "seq", split_axis=0, concat_axis=0, tiled=True)

    output = split_back(hidden)

    def column_half(array, which):
        count = array.shape[1] // 2
        return lax.dynamic_slice_in_dim(array, which * count, count, axis=1)

    def total_of(addends):
        return functools.reduce(jnp.add, [addend.astype(single) for addend in addends])

    def owner_blocks(array):
        pieces = array.shape[0] // (groups * row_unit)
        array = array.reshape(groups // 2, 2, pieces, row_unit, array.shape[1])
        return [array[:, :, piece] for piece in range(pieces)]

    def reduce_group(terms):
        sent = [contract(left, column_half(right, 1 - core), 0, 0).astype(half) for left, right in terms]
        sent = [lax.ppermute(part, "wide", pair_up(1)) for part in sent]
        kept = [contract(left, column_half(right, core), 0, 0).astype(half) for left, right in terms]
        arrived = yield sent
        counts, blocks = [], ([], [])
        for own, other in zip(kept, arrived):
            own_blocks, other_blocks = owner_blocks(own), owner_blocks(other)
            counts.append((len(own_blocks), own.shape[1]))
            for pair in zip(own_blocks, other_blocks):
                for side in range(2):
                    which = place if side == 0 else 1 - place
                    chosen = [side_of(part, which, 1) for part in pair]
                    blocks[side].append(total_of(chosen).astype(half))
        (received,) = yield [lax.ppermute(jnp.concatenate(blocks[1], axis=-1), "seq", swap)]
        addends = [jnp.concatenate(blocks[0], axis=-1), received]
        width = received.shape[-1]
        bit = 2
        while bit < groups:
            views = [addend.reshape(-1, 2, row_unit, width) for addend in addends]
            mine = bit_of(bit)
            sent = total_of([side_of(view, 1 - mine, 1) for view in views]).astype(half)
            (received,) = yield [lax.ppermute(sent, "wide", pair_up(bit))]
            addends = [side_of(view, mine, 1) for view in views] + [received]
            bit *= 2
        current = total_of(addends).astype(half).reshape(row_unit, width)
        (other,) = yield [lax.ppermute(current, "seq", swap)]
        same = place == core
        owned = jnp.where(same, current, other)
        (received,) = yield [lax.ppermute(jnp.where(same, other, current), "wide", pair_up(1))]
        low = jnp.where(core == 0, owned, received)
        high = jnp.where(core == 0, received, owned)
        shares, start = [], 0
        for count, each in counts:
            rows = []
            for _ in range(count):
                window = slice(start, start + each)
                rows.append(jnp.concatenate([low[:, window], high[:, window]], axis=1))
                start += each
            shares.append(jnp.concatenate(rows, axis=0).astype(single))
        return shares

    def reduce_small(array):
        bit = 1
        while bit < groups:
            view = array.reshape(-1, 2, array.shape[-1])
            mine = bit_of(bit)
            sent = side_of(view, 1 - mine, 1)
            (received,) = yield [lax.ppermute(sent, "wide", pair_up(bit))]
            array = side_of(view, mine, 1) + received
            bit *= 2
        (received,) = yield [lax.ppermute(array, "seq", swap)]
        return (array + received)[0]

    weight_grads = [[None] * 4 for _ in range(layers)]

    def begin_group(layer, parts, terms):
        def finish(shares):
            for part, share in zip(parts, shares):
                weight_grads[layer][part] = share

        begin(reduce_group(terms), finish)

    gradient = my_upstream.astype(single)
    small_grads = [None] * layers
    for layer in range(layers - 1, -1, -1):
        qkv_full, out_full, up_full, down_full = matrices[layer]
        gains = all_gains[layer]
        (hidden, normed, packed, totals, attended, middle, second, pre_activation, activated) = (
            saved[layer]
        )
        branch = gradient.astype(half)
        down_bias_grad = jnp.sum(branch, axis=0, dtype=single)
        activated_grad = contract(branch, down_full, 1, 1)
        pull = jax.vjp(lambda value: jax.nn.gelu(value, approximate=True), pre_activation)[1]
        upper = pull(activated_grad)[0].astype(half)
        upper = advance(upper)
        first_batch = ((3, 2), ((activated, branch), (second, upper)))
        if layer:
            begin_group(layer, *first_batch)
        up_bias_grad = jnp.sum(upper, axis=0, dtype=single)
        second_grad = contract(upper, up_full, 1, 1)
        middle_part, second_gain, second_offset = layer_norm_grad(middle, gains[1], second_grad)
        middle_grad = gradient + middle_part
        attention_grad = middle_grad.astype(half)
        out_bias_grad = jnp.sum(attention_grad, axis=0, dtype=single)
        attention_grad = advance(attention_grad)
        if not layer:
            begin_group(layer, (3, 2, 1), first_batch[1] + ((attended, attention_grad),))
        upstream = contract(attention_grad, out_full, 1, 1).astype(half)
        if not layer:
            upstream = advance(upstream)
        if layer == layers - 1:
            upstream, output = lax.optimization_barrier((upstream, output))
            output = output.astype(single)
        packed_grad = attend_backward(packed, bias, upstream, totals, attended)
        packed_grad = advance(packed_grad)
        if layer:
            begin_group(layer, (0, 1), ((normed, packed_grad), (attended, attention_grad)))
        else:
            begin_group(layer, (0,), ((normed, packed_grad),))
        column_sums = jnp.sum(packed_grad, axis=0, dtype=single)
        normed_grad = contract(packed_grad, qkv_full, 1, 1)
        hidden_part, first_gain, first_offset = layer_norm_grad(hidden, gains[0], normed_grad)
        gradient = advance(middle_grad + hidden_part)
        small_grads[layer] = (
            jnp.stack([first_gain, second_gain]),
            jnp.stack(
                [
                    first_offset,
                    column_sums[:features],
                    column_sums[2 * features :],
                    out_bias_grad,
                    second_offset,
                    down_bias_grad,
                ]
            ),
            up_bias_grad,
        )
    def by_owner(parts):
        stacked = jnp.stack(parts)
        stacked = stacked.reshape(layers, -1, groups, stacked.shape[-1] // groups)
        return stacked.transpose(2, 0, 1, 3).reshape(groups, -1)

    owned = jnp.concatenate(
        [by_owner([small_grads[layer][part] for layer in range(layers)]) for part in range(3)],
        axis=1,
    )
    small_result = []
    begin(reduce_small(owned), small_result.append)
    input_grad = split_back(gradient)
    while running:
        input_grad = advance(input_grad)
    input_grad = input_grad.astype(single)
    owned = small_result[0]
    stacked = [
        jnp.stack([weight_grads[layer][part] for layer in range(layers)]) for part in range(4)
    ]
    return (
        output,
        input_grad,
        *stacked,
        owned[:cut_gains].reshape(norm_gains.shape),
        owned[cut_gains:cut_rows].reshape(bias_rows.shape),
        owned[cut_rows:].reshape(up_bias.shape),
    )


def solution(mesh):
    tokens_spec = P("wide", "seq", None)
    matrix_spec = P(None, "wide", None)
    rows_spec = P(None, None, "wide")
    return jax.shard_map(
        per_device,
        mesh=mesh,
        in_specs=(
            tokens_spec,
            P("wide", None),
            P("wide", "seq"),
            P("wide", "seq"),
            tokens_spec,
            matrix_spec,
            matrix_spec,
            matrix_spec,
            matrix_spec,
            rows_spec,
            rows_spec,
            P(None, "wide"),
        ),
        out_specs=(
            tokens_spec,
            tokens_spec,
            matrix_spec,
            matrix_spec,
            matrix_spec,
            matrix_spec,
            rows_spec,
            rows_spec,
            P(None, "wide"),
        ),
        check_vma=False,
    )
```

```python
import functools

import jax
import jax.numpy as jnp
from jax import lax
from jax.experimental import pallas as pl
from jax.experimental.pallas import tpu as pltpu
from jax.sharding import PartitionSpec as P

HEAD_SIZE = 64
PAIR = 2 * HEAD_SIZE
FORWARD_ROWS = 512
BACKWARD_ROWS = 256
ROW_TILE = 256
FF_CHUNK = 1024

epsilon = 1e-05
masked_bias = -1e30
half = jnp.bfloat16
single = jnp.float32


def estimate(flops, size):
    return pl.CostEstimate(flops=flops // 16, bytes_accessed=size // 16, transcendentals=0)


def contract(left, right, left_dim, right_dim):
    return lax.dot_general(
        left, right, (((left_dim,), (right_dim,)), ((), ())), preferred_element_type=jnp.float32
    )


def first_head_lanes():
    return lax.broadcasted_iota(jnp.int32, (1, PAIR), 1) < HEAD_SIZE


def one_head_of(pair, head):
    lanes = first_head_lanes()
    keep = lanes if head == 0 else jnp.logical_not(lanes)
    return jnp.where(keep, pair, jnp.zeros_like(pair))


def attend_kernel(query_ref, key_ref, value_ref, bias_ref, out_ref, total_ref, *, rows):
    keys = key_ref[...]
    values = value_ref[...]
    scale = jnp.asarray(HEAD_SIZE ** (-0.5), half)
    for start in range(0, keys.shape[0], rows):
        window = pl.ds(start, rows)
        queries = query_ref[window, :] * scale
        bias = bias_ref[:, window]
        attended = []
        for head in range(2):
            scores = contract(keys, one_head_of(queries, head), 1, 1) + bias
            top = jnp.max(scores, axis=0, keepdims=True)
            weights = jnp.exp(scores - top)
            total = jnp.sum(weights, axis=0, keepdims=True)
            mixed = contract(values, weights.astype(half), 0, 0) * (1.0 / total)
            attended.append(mixed[HEAD_SIZE * head : HEAD_SIZE * (head + 1)])
            total_ref[head : head + 1, window] = top + jnp.log(total)
        out_ref[window, :] = jnp.concatenate(attended, 0).T.astype(half)


def attend_forward(packed, bias):
    length = packed.shape[0]
    features = packed.shape[1] // 3
    pairs = features // PAIR
    columns = lambda part: pl.BlockSpec((length, PAIR), lambda i: (0, part * pairs + i))
    return pl.pallas_call(
        functools.partial(attend_kernel, rows=FORWARD_ROWS),
        grid=(pairs,),
        in_specs=[
            columns(0),
            columns(1),
            columns(2),
            pl.BlockSpec((length, length), lambda i: (0, 0)),
        ],
        out_specs=[columns(0), pl.BlockSpec((None, 2, length), lambda i: (i, 0, 0))],
        out_shape=[
            jax.ShapeDtypeStruct((length, features), half),
            jax.ShapeDtypeStruct((pairs, 2, length), single),
        ],
        compiler_params=pltpu.CompilerParams(vmem_limit_bytes=56 << 20),
        cost_estimate=estimate(16 * length * length * features, 8 * length * features),
        name="attend_forward",
    )(packed, packed, packed, bias)


def attend_grad_kernel(
    query_ref,
    key_ref,
    value_ref,
    bias_ref,
    upstream_ref,
    total_ref,
    attended_ref,
    out_ref,
    key_sum,
    value_sum,
    *,
    rows,
):
    pair = pl.program_id(0)
    features = out_ref.shape[1] // 3
    keys = key_ref[...]
    values = value_ref[...]
    scale = HEAD_SIZE ** (-0.5)
    for start in range(0, keys.shape[0], rows):
        window = pl.ds(start, rows)
        queries = query_ref[window, :] * jnp.asarray(scale, half)
        upstream = upstream_ref[window, :]
        product = (upstream.astype(single) * attended_ref[window, :].astype(single)).T
        bias = bias_ref[:, window]
        query_grads, key_grad, value_grad = [], 0.0, 0.0
        for head in range(2):
            head_queries = one_head_of(queries, head)
            head_upstream = one_head_of(upstream, head)
            inner = jnp.sum(
                product[HEAD_SIZE * head : HEAD_SIZE * (head + 1)], axis=0, keepdims=True
            )
            scores = contract(keys, head_queries, 1, 1) + bias
            weights = jnp.exp(scores - total_ref[head : head + 1, window])
            weight_grads = contract(values, head_upstream, 1, 1)
            score_grads = (weights * (weight_grads - inner)).astype(half)
            value_grad = value_grad + contract(weights.astype(half), head_upstream, 1, 0)
            key_grad = key_grad + contract(score_grads, head_queries, 1, 0)
            query_grads.append(
                contract(keys, score_grads, 0, 0)[HEAD_SIZE * head : HEAD_SIZE * (head + 1)]
            )
        out_ref[window, pl.ds(pl.multiple_of(pair * PAIR, PAIR), PAIR)] = (
            jnp.concatenate(query_grads, 0).T * scale
        ).astype(half)
        if start == 0:
            key_sum[...] = key_grad
            value_sum[...] = value_grad
        else:
            key_sum[...] += key_grad
            value_sum[...] += value_grad
    out_ref[:, pl.ds(pl.multiple_of(features + pair * PAIR, PAIR), PAIR)] = key_sum[...].astype(
        half
    )
    out_ref[:, pl.ds(pl.multiple_of(2 * features + pair * PAIR, PAIR), PAIR)] = value_sum[
        ...
    ].astype(half)


def attend_backward(packed, bias, upstream, totals, attended):
    length = packed.shape[0]
    features = packed.shape[1] // 3
    pairs = features // PAIR
    columns = lambda part: pl.BlockSpec((length, PAIR), lambda i: (0, part * pairs + i))
    return pl.pallas_call(
        functools.partial(attend_grad_kernel, rows=BACKWARD_ROWS),
        grid=(pairs,),
        in_specs=[
            columns(0),
            columns(1),
            columns(2),
            pl.BlockSpec((length, length), lambda i: (0, 0)),
            columns(0),
            pl.BlockSpec((None, 2, length), lambda i: (i, 0, 0)),
            columns(0),
        ],
        out_specs=pl.BlockSpec((length, 3 * features), lambda i: (0, 0)),
        out_shape=jax.ShapeDtypeStruct((length, 3 * features), half),
        scratch_shapes=[pltpu.VMEM((length, PAIR), single)] * 2,
        compiler_params=pltpu.CompilerParams(vmem_limit_bytes=56 << 20),
        cost_estimate=estimate(40 * length * length * features, 16 * length * features),
        name="attend_backward",
    )(packed, packed, packed, bias, upstream, totals, attended)


def place_pieces(pieces, out_shape, targets, indices):
    def kernel(index_ref, *refs):
        sources, out_ref, semaphores = refs[: len(pieces)], refs[-2], refs[-1]
        copies = [
            pltpu.make_async_copy(
                source, out_ref.at[target(index_ref)], semaphores.at[number]
            )
            for number, (source, target) in enumerate(zip(sources, targets))
        ]
        for copy in copies:
            copy.start()
        for copy in copies:
            copy.wait()

    size = 2 * 2
    for extent in out_shape:
        size *= extent
    anywhere = pl.BlockSpec(memory_space=pl.ANY)
    return pl.pallas_call(
        kernel,
        in_specs=[pl.BlockSpec(memory_space=pltpu.SMEM)] + [anywhere] * len(pieces),
        out_specs=pl.BlockSpec(memory_space=pltpu.VMEM),
        out_shape=jax.ShapeDtypeStruct(out_shape, pieces[0].dtype),
        scratch_shapes=[pltpu.SemaphoreType.DMA((len(pieces),))],
        compiler_params=pltpu.CompilerParams(vmem_limit_bytes=32 << 20),
        cost_estimate=estimate(0, size),
        name="place_pieces",
    )(indices, *pieces)


def normal_of(hidden):
    center = hidden - jnp.mean(hidden, axis=-1, keepdims=True)
    inverse = lax.rsqrt(jnp.mean(center * center, axis=-1, keepdims=True) + epsilon)
    return center * inverse, inverse


def norm_pull(normal, inverse, gain, upstream):
    scaled = upstream * gain
    slope = jnp.mean(scaled, axis=-1, keepdims=True)
    tilt = jnp.mean(scaled * normal, axis=-1, keepdims=True)
    return inverse * (scaled - slope - normal * tilt)


def column_sum(array):
    return jnp.sum(array, axis=0, keepdims=True)


def tile_of(columns):
    return pl.BlockSpec((ROW_TILE, columns), lambda i: (i, 0))


def resident(shape, *index):
    place = index or (0,) * len(shape)
    return pl.BlockSpec(shape, lambda i: place, pipeline_mode=pl.Buffered(1))


def row_tiled(kernel, name, length, in_specs, out_specs, out_shape, operands, flops):
    size = sum(operand.size * operand.dtype.itemsize for operand in operands)
    size += sum(shape.size * jnp.dtype(shape.dtype).itemsize for shape in out_shape)
    return pl.pallas_call(
        kernel,
        grid=(length // ROW_TILE,),
        in_specs=in_specs,
        out_specs=out_specs,
        out_shape=out_shape,
        compiler_params=pltpu.CompilerParams(vmem_limit_bytes=56 << 20),
        cost_estimate=estimate(flops, size),
        name=name,
    )(*operands)


def project_kernel(hidden_ref, gains_ref, offsets_ref, weight_ref, normed_ref, packed_ref):
    features = hidden_ref.shape[1]
    normal, _ = normal_of(hidden_ref[...])
    normed = (normal * gains_ref[0:1] + offsets_ref[0:1]).astype(half)
    normed_ref[...] = normed
    for part in range(3):
        window = slice(part * features, (part + 1) * features)
        product = contract(normed, weight_ref[:, window], 1, 0)
        if part != 1:
            row = 1 if part == 0 else 2
            product = product + offsets_ref[row : row + 1]
        packed_ref[:, window] = product.astype(half)


def project(hidden, gains, offsets, joined):
    length, features = hidden.shape
    return row_tiled(
        project_kernel,
        "project",
        length,
        [
            tile_of(features),
            resident(gains.shape),
            resident(offsets.shape),
            resident((features, 3 * features)),
        ],
        [tile_of(features), tile_of(3 * features)],
        [
            jax.ShapeDtypeStruct((length, features), half),
            jax.ShapeDtypeStruct((length, 3 * features), half),
        ],
        (hidden, gains, offsets, joined),
        6 * length * features * features,
    )


def feed_kernel(
    attended_ref,
    hidden_ref,
    gains_ref,
    offsets_ref,
    up_bias_ref,
    out_weight_ref,
    up_ref,
    down_ref,
    middle_ref,
    second_ref,
    activated_ref,
    slope_ref,
    result_ref,
):
    hidden_units = up_ref.shape[1]
    middle = hidden_ref[...] + (
        contract(attended_ref[...], out_weight_ref[...], 1, 0) + offsets_ref[3:4]
    )
    middle_ref[...] = middle
    normal, _ = normal_of(middle)
    second = (normal * gains_ref[1:2] + offsets_ref[4:5]).astype(half)
    second_ref[...] = second
    result = middle + offsets_ref[5:6]
    rate = 0.7978845608028654
    for start in range(0, hidden_units, FF_CHUNK):
        window = slice(start, start + FF_CHUNK)
        value = contract(second, up_ref[:, window], 1, 0) + up_bias_ref[:, window]
        square = value * value
        bent = jnp.tanh(value * (rate + (rate * 0.044715) * square))
        opened = 0.5 + 0.5 * bent
        activated = (value * opened).astype(half)
        activated_ref[:, window] = activated
        curve = (value * (0.5 * rate + (1.5 * rate * 0.044715) * square)) * (1.0 - bent * bent)
        slope_ref[:, window] = (opened + curve).astype(half)
        result = result + contract(activated, down_ref[window, :], 1, 0)
    result_ref[...] = result.astype(result_ref.dtype)


def feed(attended, hidden, gains, offsets, up_bias, joined, down, result_type):
    length, features = hidden.shape
    units = down.shape[0]
    out_place = 3
    up_place = 4 * features // units
    shape = jax.ShapeDtypeStruct
    return row_tiled(
        feed_kernel,
        "feed",
        length,
        [
            tile_of(features),
            tile_of(features),
            resident(gains.shape),
            resident(offsets.shape),
            resident(up_bias.shape),
            resident((features, features), 0, out_place),
            resident((features, units), 0, up_place),
            resident(down.shape),
        ],
        [tile_of(features), tile_of(features), tile_of(units), tile_of(units), tile_of(features)],
        [
            shape((length, features), single),
            shape((length, features), half),
            shape((length, units), half),
            shape((length, units), half),
            shape((length, features), result_type),
        ],
        (attended, hidden, gains, offsets, up_bias, joined, joined, down),
        2 * length * features * (features + 2 * units),
    )


def feed_grad_kernel(
    gradient_ref,
    slope_ref,
    middle_ref,
    gains_ref,
    out_weight_ref,
    up_ref,
    down_ref,
    branch_ref,
    upper_ref,
    middle_grad_ref,
    attention_grad_ref,
    upstream_ref,
    sums_ref,
    unit_sums_ref,
):
    units = up_ref.shape[1]

    @pl.when(pl.program_id(0) == 0)
    def _():
        sums_ref[...] = jnp.zeros_like(sums_ref)
        unit_sums_ref[...] = jnp.zeros_like(unit_sums_ref)

    gradient = gradient_ref[...].astype(single)
    branch = gradient.astype(half)
    branch_ref[...] = branch
    sums_ref[0:1] += column_sum(branch.astype(single))
    second_grad = jnp.zeros(gradient.shape, single)
    for start in range(0, units, FF_CHUNK):
        window = slice(start, start + FF_CHUNK)
        pulled = contract(branch, down_ref[window, :], 1, 1) * slope_ref[:, window].astype(single)
        upper = pulled.astype(half)
        upper_ref[:, window] = upper
        unit_sums_ref[:, window] += column_sum(upper.astype(single))
        second_grad = second_grad + contract(upper, up_ref[:, window], 1, 1)
    normal, inverse = normal_of(middle_ref[...])
    middle_grad = gradient + norm_pull(normal, inverse, gains_ref[1:2], second_grad)
    sums_ref[1:2] += column_sum(second_grad * normal)
    sums_ref[2:3] += column_sum(second_grad)
    middle_grad_ref[...] = middle_grad
    attention_grad = middle_grad.astype(half)
    attention_grad_ref[...] = attention_grad
    sums_ref[3:4] += column_sum(attention_grad.astype(single))
    upstream_ref[...] = contract(attention_grad, out_weight_ref[...], 1, 1).astype(half)


def feed_grad(gradient, slope, middle, gains, joined, down):
    length, features = middle.shape
    units = down.shape[0]
    shape = jax.ShapeDtypeStruct
    return row_tiled(
        feed_grad_kernel,
        "feed_grad",
        length,
        [
            tile_of(features),
            tile_of(units),
            tile_of(features),
            resident(gains.shape),
            resident((features, features), 0, 3),
            resident((features, units), 0, 4 * features // units),
            resident(down.shape),
        ],
        [
            tile_of(features),
            tile_of(units),
            tile_of(features),
            tile_of(features),
            tile_of(features),
            resident((8, features)),
            resident((1, units)),
        ],
        [
            shape((length, features), half),
            shape((length, units), half),
            shape((length, features), single),
            shape((length, features), half),
            shape((length, features), half),
            shape((8, features), single),
            shape((1, units), single),
        ],
        (gradient, slope, middle, gains, joined, joined, down),
        2 * length * features * (features + 2 * units),
    )


def project_grad_kernel(
    packed_grad_ref, hidden_ref, middle_grad_ref, gains_ref, weight_ref, result_ref, sums_ref
):
    features = hidden_ref.shape[1]

    @pl.when(pl.program_id(0) == 0)
    def _():
        sums_ref[...] = jnp.zeros_like(sums_ref)

    packed_grad = packed_grad_ref[...]
    normed_grad = contract(packed_grad, weight_ref[...], 1, 1)
    normal, inverse = normal_of(hidden_ref[...])
    result = middle_grad_ref[...] + norm_pull(normal, inverse, gains_ref[0:1], normed_grad)
    result_ref[...] = result.astype(result_ref.dtype)
    sums_ref[0:1] += column_sum(normed_grad * normal)
    sums_ref[1:2] += column_sum(normed_grad)
    sums_ref[2:3] += column_sum(packed_grad[:, :features].astype(single))
    sums_ref[3:4] += column_sum(packed_grad[:, 2 * features :].astype(single))


def project_grad(packed_grad, hidden, middle_grad, gains, joined, result_type):
    length, features = hidden.shape
    shape = jax.ShapeDtypeStruct
    return row_tiled(
        project_grad_kernel,
        "project_grad",
        length,
        [
            tile_of(3 * features),
            tile_of(features),
            tile_of(features),
            resident(gains.shape),
            resident((features, 3 * features)),
        ],
        [tile_of(features), resident((8, features))],
        [shape((length, features), result_type), shape((8, features), single)],
        (packed_grad, hidden, middle_grad, gains, joined),
        6 * length * features * features,
    )


def term_blocks(terms, core, groups, row_unit):
    pieces = [left.shape[1] // (groups * row_unit) for left, _ in terms]
    widths = [right.shape[1] // 2 for _, right in terms]
    total = sum(count * width for count, width in zip(pieces, widths))
    chips = groups // 2
    out_shape = (chips, 2, row_unit, total)
    if row_unit % 16:
        columns = []
        for (left, right), count, width in zip(terms, pieces, widths):
            part = contract(left, right, 0, 0).astype(half)
            part = part.reshape(chips, 2, count, row_unit, 2, width).transpose(2, 1, 0, 4, 3, 5)
            columns += [part[piece] for piece in range(count)]
        whole = jnp.concatenate(columns, axis=-1)
        return [
            lax.dynamic_index_in_dim(whole, which, 0, keepdims=False) for which in (1 - core, core)
        ]
    number = len(terms)

    def kernel(core_ref, *refs):
        sources = refs[: 2 * number]
        other_ref, own_ref = refs[2 * number : 2 * number + 2]
        buffers = refs[2 * number + 2 : 4 * number + 2]
        semaphores = refs[4 * number + 2]
        first_core = core_ref[0] == 0
        copies = [
            pltpu.make_async_copy(source, buffer, semaphores.at[index])
            for index, (source, buffer) in enumerate(zip(sources, buffers))
        ]
        for copy in copies:
            copy.start()
        start = 0
        for index, (count, width) in enumerate(zip(pieces, widths)):
            copies[2 * index].wait()
            copies[2 * index + 1].wait()
            left, right = buffers[2 * index], buffers[2 * index + 1]
            rows = groups * row_unit
            step = max(size for size in (768, 640, 512, 384, 256, 128) if width % size == 0)
            held = chips // count
            for turn in range(count):
                turned = left[:, turn * rows : (turn + 1) * rows].T
                some = slice(turn * held, (turn + 1) * held)
                for low in range(0, 2 * width, step):
                    product = contract(turned, right[:, low : low + step], 1, 0).astype(half)
                    product = product.reshape(held, 2, count, row_unit, step)
                    side, inside = divmod(low, width)
                    for piece in range(count):
                        lanes = start + piece * width + inside
                        lanes = slice(lanes, lanes + step)
                        even, odd = product[:, 0, piece], product[:, 1, piece]
                        other_ref[some, side, :, lanes] = jnp.where(first_core, odd, even)
                        own_ref[some, side, :, lanes] = jnp.where(first_core, even, odd)
            start += count * width

    anywhere = pl.BlockSpec(memory_space=pl.ANY)
    operands = [operand for term in terms for operand in term]
    size = sum(operand.size for operand in operands) * 2
    flops = sum(2 * left.size * right.shape[1] for left, right in terms)
    shape = jax.ShapeDtypeStruct(out_shape, half)
    return pl.pallas_call(
        kernel,
        in_specs=[pl.BlockSpec(memory_space=pltpu.SMEM)] + [anywhere] * len(operands),
        out_specs=[pl.BlockSpec(memory_space=pltpu.VMEM)] * 2,
        out_shape=[shape, shape],
        scratch_shapes=[pltpu.VMEM(operand.shape, half) for operand in operands]
        + [pltpu.SemaphoreType.DMA((len(operands),))],
        compiler_params=pltpu.CompilerParams(vmem_limit_bytes=60 << 20),
        cost_estimate=estimate(flops, size + 4 * shape.size),
        name="term_blocks",
    )(core.reshape(1).astype(jnp.int32), *operands)


def per_device(
    tokens,
    time_embed,
    segment_ids,
    pad_mask,
    out_grad,
    qkv_weight,
    out_weight,
    up_weight,
    down_weight,
    norm_gains,
    bias_rows,
    up_bias,
):
    layers = qkv_weight.shape[0]
    features = tokens.shape[2]
    groups = lax.axis_size("wide")
    swap = [(0, 1), (1, 0)]

    def whole_sequence(part):
        return lax.all_to_all(part, "seq", split_axis=0, concat_axis=1, tiled=True)[0]

    core = lax.axis_index("wide") & 1
    place = lax.axis_index("seq")
    indices = jnp.stack([core, place]).astype(jnp.int32)
    row_unit = qkv_weight.shape[1]
    pair_up = lambda bit: [(index, index ^ bit) for index in range(groups)]
    bit_of = lambda bit: (lax.axis_index("wide") >> (bit.bit_length() - 1)) & 1
    running = []

    def begin(steps, finish):
        entry = [steps, finish, next(steps), None]
        running.append(entry)
        return entry

    def launch(main, entries):
        fresh = [entry for entry in entries if entry in running and entry[3] is None]
        if fresh:
            sends = [[sent for sent, _, _ in entry[2]] for entry in fresh]
            main, sends = lax.optimization_barrier((main, sends))
            for entry, sent in zip(fresh, sends):
                entry[3] = [
                    lax.ppermute(part, axis, pairs)
                    for part, (_, axis, pairs) in zip(sent, entry[2])
                ]
        return main

    def advance(main, *only):
        chosen = [entry for entry in only or list(running) if entry in running]
        main = launch(main, chosen)
        if not chosen:
            return main
        main, flying = lax.optimization_barrier((main, [entry[3] for entry in chosen]))
        for entry, arrived in zip(chosen, flying):
            entry[3] = None
            try:
                entry[2] = entry[0].send(arrived)
            except StopIteration as stop:
                entry[1](stop.value)
                running.remove(entry)
        return launch(main, chosen)

    def side_of(array, which, axis):
        return lax.dynamic_index_in_dim(array, which, axis, keepdims=False)

    def gather_steps(shard, split_rows):
        rows, columns = shard.shape
        if split_rows:
            rows //= 2
            mine = side_of(shard.reshape(2, rows, columns), place, 0)
        else:
            columns //= 2
            mine = lax.dynamic_slice_in_dim(shard, place * columns, columns, axis=1)
        current = mine[None]
        bit = groups // 2
        while bit > 1:
            (received,) = yield [(current, "wide", pair_up(bit))]
            count = current.shape[0]
            current = place_pieces(
                [current, received],
                (count, 2, rows, columns),
                [lambda ref: (slice(None), ref[0]), lambda ref: (slice(None), 1 - ref[0])],
                bit_of(bit).reshape(1).astype(jnp.int32),
            ).reshape(2 * count, rows, columns)
            bit //= 2
        (beside,) = yield [(current, "seq", swap)]
        passed = yield [(part, "wide", pair_up(1)) for part in (current, beside)]
        count = current.shape[0]

        def target(own_core, own_place):
            def where(ref):
                which_core = ref[0] if own_core else 1 - ref[0]
                which_place = ref[1] if own_place else 1 - ref[1]
                if split_rows:
                    return (slice(None), which_core, which_place)
                start = pl.multiple_of(which_place * columns, columns)
                return (slice(None), which_core, slice(None), pl.ds(start, columns))

            return where

        whole = place_pieces(
            [current, beside, *passed],
            (count, 2, 2, rows, columns) if split_rows else (count, 2, rows, 2 * columns),
            [target(True, True), target(True, False), target(False, True), target(False, False)],
            indices,
        )
        return whole.reshape(-1, shard.shape[1])

    my_tokens = whole_sequence(tokens)
    marks = whole_sequence(jnp.stack([segment_ids, pad_mask], axis=2))
    my_time = lax.dynamic_index_in_dim(time_embed, place, 0, keepdims=True)

    small = jnp.concatenate(
        [norm_gains.reshape(-1), bias_rows.reshape(-1), up_bias.reshape(-1)]
    )
    side = small.reshape(row_unit, -1)
    side_width = side.shape[1]
    side = jnp.pad(side, ((0, 0), (0, -side_width % PAIR)))
    cuts = [0]
    for source in (qkv_weight, out_weight, up_weight):
        cuts.append(cuts[-1] + source.shape[2])

    def beside_each_other(layer, *more):
        parts = [qkv_weight[layer], out_weight[layer], up_weight[layer], *more]
        return jnp.concatenate(parts, axis=1)

    first_whole = lax.all_gather(beside_each_other(0, side), "wide", axis=0, tiled=True)
    first_down = lax.all_gather(down_weight[0], "wide", axis=0, tiled=True)
    matrices = [None] * layers
    matrices[0] = (first_whole, first_down)
    small_whole = first_whole[:, cuts[-1] :][:, :side_width].reshape(groups, -1)
    cut_gains = norm_gains.size
    cut_rows = cut_gains + bias_rows.size

    def whole_rows(part, count):
        parts = part.reshape(groups, layers, count, -1)
        return parts.transpose(1, 2, 0, 3).reshape(layers, count, -1).astype(single)

    all_gains = whole_rows(small_whole[:, :cut_gains], norm_gains.shape[1])
    all_offsets = whole_rows(small_whole[:, cut_gains:cut_rows], bias_rows.shape[1])
    all_up_bias = whole_rows(small_whole[:, cut_rows:], 1)[:, 0]

    doc, pad = marks[:, 0], marks[:, 1]
    positions = jnp.arange(doc.shape[0])
    allowed = (doc[:, None] == doc[None, :]) & (
        (pad[:, None] == 1) | (positions[:, None] == positions[None, :])
    )
    bias = jnp.where(allowed, 0.0, masked_bias)

    joined = {}
    downs = {}
    for layer in range(1, layers):
        begin(
            gather_steps(beside_each_other(layer), False),
            functools.partial(joined.__setitem__, layer),
        )
    bit = groups // 2
    while bit > 1:
        my_tokens = advance(my_tokens)
        bit //= 2
    hidden = my_tokens.astype(single) + my_time
    saved = []
    for layer in range(layers):
        whole = joined[layer] if layer else first_whole
        gains, offsets = all_gains[layer], all_offsets[layer]
        before = hidden
        normed, packed = project(hidden, gains, offsets, whole)
        if layer:
            packed = advance(packed)
        attended, totals = attend_forward(packed, bias)
        attended = advance(attended)
        if layer == 0:
            for later in range(1, layers):
                begin(
                    gather_steps(down_weight[later], True),
                    functools.partial(downs.__setitem__, later),
                )
            attended = launch(attended, list(running))
            attended, out_grad = lax.optimization_barrier((attended, out_grad))
            my_upstream = whole_sequence(out_grad)
        else:
            while layer not in downs:
                attended = advance(attended)
        down = downs[layer] if layer else first_down
        matrices[layer] = (whole, down)
        middle, second, activated, slope, hidden = feed(
            attended,
            hidden,
            gains,
            offsets,
            all_up_bias[layer][None],
            whole,
            down,
            single if layer < layers - 1 else half,
        )
        if layer < layers - 1:
            while layer + 1 not in joined:
                hidden = advance(hidden)
            hidden = advance(hidden)
        saved.append((before, normed, packed, totals, attended, middle, second, activated, slope))

    def split_back(result):
        parts = result.reshape(2, -1, features).astype(half)
        return lax.all_to_all(parts, "seq", split_axis=0, concat_axis=0, tiled=True)

    output = split_back(hidden)

    def total_of(addends):
        return functools.reduce(jnp.add, [addend.astype(single) for addend in addends])

    chip_bits = [1 << number for number in range(groups.bit_length() - 2, 0, -1)]

    def reduce_group(terms, spread):
        other, own = term_blocks(terms, core, groups, row_unit)
        counts = [(left.shape[1] // (groups * row_unit), right.shape[1] // 2) for left, right in terms]
        (received,) = yield [(other, "wide", pair_up(1))]
        width = own.shape[-1]
        axes = chip_bits + ["seq"]
        addends = [part.reshape((2,) * len(axes) + (row_unit, width)) for part in (own, received)]
        for stage in (["seq"] if spread else []) + chip_bits[::-1]:
            axis = axes.index(stage)
            mine = place if stage == "seq" else bit_of(stage)
            sent = total_of([side_of(part, 1 - mine, axis) for part in addends]).astype(half)
            if stage == "seq":
                (received,) = yield [(sent, "seq", swap)]
            else:
                (received,) = yield [(sent, "wide", pair_up(stage))]
            addends = [side_of(part, mine, axis) for part in addends] + [received]
            axes.remove(stage)
        current = total_of(addends).astype(half)
        (received,) = yield [(current, "seq", swap)]
        if spread:
            low = jnp.where(place == 0, current, received).astype(single)
            high = jnp.where(place == 0, received, current).astype(single)
        else:
            low, high = current.astype(single) + received.astype(single)
        shares, start = [], 0
        for count, each in counts:
            rows = []
            for _ in range(count):
                window = slice(start, start + each)
                rows.append(jnp.concatenate([low[:, window], high[:, window]], axis=1))
                start += each
            shares.append(jnp.concatenate(rows, axis=0))
        return shares

    def reduce_small(array):
        bit = 1
        while bit < groups:
            view = array.reshape(-1, 2, array.shape[-1])
            mine = bit_of(bit)
            sent = side_of(view, 1 - mine, 1)
            (received,) = yield [(sent, "wide", pair_up(bit))]
            array = side_of(view, mine, 1) + received
            bit *= 2
        (received,) = yield [(array, "seq", swap)]
        return (array + received)[0]

    weight_grads = [[None] * 4 for _ in range(layers)]

    def begin_group(spread, *named):
        def finish(shares):
            for (layer, part, _), share in zip(named, shares):
                weight_grads[layer][part] = share

        return begin(reduce_group([term for _, _, term in named], spread), finish)

    gradient = my_upstream
    small_grads = [None] * layers
    waiting = []
    for layer in range(layers - 1, -1, -1):
        whole, down = matrices[layer]
        gains = all_gains[layer]
        hidden, normed, packed, totals, attended, middle, second, activated, slope = saved[layer]
        early = None
        if layer < layers - 1:
            branch = gradient.astype(half)
            early = begin_group(True, *waiting, (layer, 3, (activated, branch)))
            gradient = launch(gradient, [early])
            waiting = []
        branch, upper, middle_grad, attention_grad, upstream, sums, unit_sums = feed_grad(
            gradient, slope, middle, gains, whole, down
        )
        upstream = advance(upstream)
        named = [(layer, 2, (second, upper)), (layer, 1, (attended, attention_grad))]
        if early is None:
            named = [(layer, 3, (activated, branch))] + named
        entry = begin_group(False, *named)
        upstream = launch(upstream, [entry])
        if layer == 0:
            upstream = advance(upstream, entry)
        packed_grad = attend_backward(packed, bias, upstream, totals, attended)
        if layer == layers - 1:
            packed_grad, output = lax.optimization_barrier((packed_grad, output))
            output = output.astype(single)
        packed_grad = advance(packed_grad)
        last = (layer, 0, (normed, packed_grad))
        if layer:
            waiting = [last]
        else:
            entry = begin_group(False, last)
            packed_grad = advance(packed_grad, entry)
        gradient, more_sums = project_grad(
            packed_grad, hidden, middle_grad, gains, whole, single if layer else half
        )
        small_grads[layer] = (
            jnp.stack([more_sums[0], sums[1]]),
            jnp.stack([more_sums[1], more_sums[2], more_sums[3], sums[3], sums[2], sums[0]]),
            unit_sums[0],
        )

    def by_owner(parts):
        stacked = jnp.stack(parts)
        stacked = stacked.reshape(layers, -1, groups, stacked.shape[-1] // groups)
        return stacked.transpose(2, 0, 1, 3).reshape(groups, -1)

    owned = jnp.concatenate(
        [by_owner([small_grads[layer][part] for layer in range(layers)]) for part in range(3)],
        axis=1,
    )
    small_result = []
    begin(reduce_small(owned), small_result.append)
    input_grad = split_back(gradient)
    while running:
        input_grad = advance(input_grad)
    input_grad = input_grad.astype(single)
    owned = small_result[0]
    stacked = [
        jnp.stack([weight_grads[layer][part] for layer in range(layers)]) for part in range(4)
    ]
    return (
        output,
        input_grad,
        *stacked,
        owned[:cut_gains].reshape(norm_gains.shape),
        owned[cut_gains:cut_rows].reshape(bias_rows.shape),
        owned[cut_rows:].reshape(up_bias.shape),
    )


def solution(mesh):
    tokens_spec = P("wide", "seq", None)
    matrix_spec = P(None, "wide", None)
    rows_spec = P(None, None, "wide")
    return jax.shard_map(
        per_device,
        mesh=mesh,
        in_specs=(
            tokens_spec,
            P("wide", None),
            P("wide", "seq"),
            P("wide", "seq"),
            tokens_spec,
            matrix_spec,
            matrix_spec,
            matrix_spec,
            matrix_spec,
            rows_spec,
            rows_spec,
            P(None, "wide"),
        ),
        out_specs=(
            tokens_spec,
            tokens_spec,
            matrix_spec,
            matrix_spec,
            matrix_spec,
            matrix_spec,
            rows_spec,
            rows_spec,
            P(None, "wide"),
        ),
        check_vma=False,
    )
```

```python
import functools

import jax
import jax.numpy as jnp
from jax import lax
from jax.experimental import pallas as pl
from jax.experimental.pallas import tpu as pltpu
from jax.sharding import PartitionSpec as P

HEAD_SIZE = 64
PAIR = 2 * HEAD_SIZE
FORWARD_ROWS = 512
BACKWARD_ROWS = 256
ROW_TILE = 256
FF_CHUNK = 1024

epsilon = 1e-05
masked_bias = -1e30
half = jnp.bfloat16
single = jnp.float32


def estimate(flops, size):
    return pl.CostEstimate(flops=flops // 16, bytes_accessed=size // 16, transcendentals=0)


def contract(left, right, left_dim, right_dim):
    return lax.dot_general(
        left, right, (((left_dim,), (right_dim,)), ((), ())), preferred_element_type=jnp.float32
    )


def first_head_lanes():
    return lax.broadcasted_iota(jnp.int32, (1, PAIR), 1) < HEAD_SIZE


def one_head_of(pair, head):
    lanes = first_head_lanes()
    keep = lanes if head == 0 else jnp.logical_not(lanes)
    return jnp.where(keep, pair, jnp.zeros_like(pair))


def attend_kernel(query_ref, key_ref, value_ref, bias_ref, out_ref, total_ref, *, rows):
    keys = key_ref[...]
    values = value_ref[...]
    scale = jnp.asarray(HEAD_SIZE ** (-0.5), half)
    for start in range(0, keys.shape[0], rows):
        window = pl.ds(start, rows)
        queries = query_ref[window, :] * scale
        bias = bias_ref[:, window]
        attended = []
        for head in range(2):
            scores = contract(keys, one_head_of(queries, head), 1, 1) + bias
            top = jnp.max(scores, axis=0, keepdims=True)
            weights = jnp.exp(scores - top)
            total = jnp.sum(weights, axis=0, keepdims=True)
            mixed = contract(values, weights.astype(half), 0, 0) * (1.0 / total)
            attended.append(mixed[HEAD_SIZE * head : HEAD_SIZE * (head + 1)])
            total_ref[head : head + 1, window] = top + jnp.log(total)
        out_ref[window, :] = jnp.concatenate(attended, 0).T.astype(half)


def attend_forward(packed, bias):
    length = packed.shape[0]
    features = packed.shape[1] // 3
    pairs = features // PAIR
    columns = lambda part: pl.BlockSpec((length, PAIR), lambda i: (0, part * pairs + i))
    return pl.pallas_call(
        functools.partial(attend_kernel, rows=FORWARD_ROWS),
        grid=(pairs,),
        in_specs=[
            columns(0),
            columns(1),
            columns(2),
            pl.BlockSpec((length, length), lambda i: (0, 0)),
        ],
        out_specs=[columns(0), pl.BlockSpec((None, 2, length), lambda i: (i, 0, 0))],
        out_shape=[
            jax.ShapeDtypeStruct((length, features), half),
            jax.ShapeDtypeStruct((pairs, 2, length), single),
        ],
        compiler_params=pltpu.CompilerParams(vmem_limit_bytes=56 << 20),
        cost_estimate=estimate(16 * length * length * features, 8 * length * features),
        name="attend_forward",
    )(packed, packed, packed, bias)


def attend_grad_kernel(
    query_ref,
    key_ref,
    value_ref,
    bias_ref,
    upstream_ref,
    total_ref,
    attended_ref,
    out_ref,
    key_sum,
    value_sum,
    *,
    rows,
):
    pair = pl.program_id(0)
    features = out_ref.shape[1] // 3
    keys = key_ref[...]
    values = value_ref[...]
    scale = HEAD_SIZE ** (-0.5)
    for start in range(0, keys.shape[0], rows):
        window = pl.ds(start, rows)
        queries = query_ref[window, :] * jnp.asarray(scale, half)
        upstream = upstream_ref[window, :]
        product = (upstream.astype(single) * attended_ref[window, :].astype(single)).T
        bias = bias_ref[:, window]
        query_grads, key_grad, value_grad = [], 0.0, 0.0
        for head in range(2):
            head_queries = one_head_of(queries, head)
            head_upstream = one_head_of(upstream, head)
            inner = jnp.sum(
                product[HEAD_SIZE * head : HEAD_SIZE * (head + 1)], axis=0, keepdims=True
            )
            scores = contract(keys, head_queries, 1, 1) + bias
            weights = jnp.exp(scores - total_ref[head : head + 1, window])
            weight_grads = contract(values, head_upstream, 1, 1)
            score_grads = (weights * (weight_grads - inner)).astype(half)
            value_grad = value_grad + contract(weights.astype(half), head_upstream, 1, 0)
            key_grad = key_grad + contract(score_grads, head_queries, 1, 0)
            query_grads.append(
                contract(keys, score_grads, 0, 0)[HEAD_SIZE * head : HEAD_SIZE * (head + 1)]
            )
        out_ref[window, pl.ds(pl.multiple_of(pair * PAIR, PAIR), PAIR)] = (
            jnp.concatenate(query_grads, 0).T * scale
        ).astype(half)
        if start == 0:
            key_sum[...] = key_grad
            value_sum[...] = value_grad
        else:
            key_sum[...] += key_grad
            value_sum[...] += value_grad
    out_ref[:, pl.ds(pl.multiple_of(features + pair * PAIR, PAIR), PAIR)] = key_sum[...].astype(
        half
    )
    out_ref[:, pl.ds(pl.multiple_of(2 * features + pair * PAIR, PAIR), PAIR)] = value_sum[
        ...
    ].astype(half)


def attend_backward(packed, bias, upstream, totals, attended):
    length = packed.shape[0]
    features = packed.shape[1] // 3
    pairs = features // PAIR
    columns = lambda part: pl.BlockSpec((length, PAIR), lambda i: (0, part * pairs + i))
    return pl.pallas_call(
        functools.partial(attend_grad_kernel, rows=BACKWARD_ROWS),
        grid=(pairs,),
        in_specs=[
            columns(0),
            columns(1),
            columns(2),
            pl.BlockSpec((length, length), lambda i: (0, 0)),
            columns(0),
            pl.BlockSpec((None, 2, length), lambda i: (i, 0, 0)),
            columns(0),
        ],
        out_specs=pl.BlockSpec((length, 3 * features), lambda i: (0, 0)),
        out_shape=jax.ShapeDtypeStruct((length, 3 * features), half),
        scratch_shapes=[pltpu.VMEM((length, PAIR), single)] * 2,
        compiler_params=pltpu.CompilerParams(vmem_limit_bytes=56 << 20),
        cost_estimate=estimate(40 * length * length * features, 16 * length * features),
        name="attend_backward",
    )(packed, packed, packed, bias, upstream, totals, attended)


def place_pieces(pieces, out_shape, targets, indices):
    def kernel(index_ref, *refs):
        sources, out_ref, semaphores = refs[: len(pieces)], refs[-2], refs[-1]
        copies = [
            pltpu.make_async_copy(
                source, out_ref.at[target(index_ref)], semaphores.at[number]
            )
            for number, (source, target) in enumerate(zip(sources, targets))
        ]
        for copy in copies:
            copy.start()
        for copy in copies:
            copy.wait()

    size = 2 * 2
    for extent in out_shape:
        size *= extent
    anywhere = pl.BlockSpec(memory_space=pl.ANY)
    return pl.pallas_call(
        kernel,
        in_specs=[pl.BlockSpec(memory_space=pltpu.SMEM)] + [anywhere] * len(pieces),
        out_specs=pl.BlockSpec(memory_space=pltpu.VMEM),
        out_shape=jax.ShapeDtypeStruct(out_shape, pieces[0].dtype),
        scratch_shapes=[pltpu.SemaphoreType.DMA((len(pieces),))],
        compiler_params=pltpu.CompilerParams(vmem_limit_bytes=32 << 20),
        cost_estimate=estimate(0, size),
        name="place_pieces",
    )(indices, *pieces)


def normal_of(hidden):
    center = hidden - jnp.mean(hidden, axis=-1, keepdims=True)
    inverse = lax.rsqrt(jnp.mean(center * center, axis=-1, keepdims=True) + epsilon)
    return center * inverse, inverse


def norm_pull(normal, inverse, gain, upstream):
    scaled = upstream * gain
    slope = jnp.mean(scaled, axis=-1, keepdims=True)
    tilt = jnp.mean(scaled * normal, axis=-1, keepdims=True)
    return inverse * (scaled - slope - normal * tilt)


def column_sum(array):
    return jnp.sum(array, axis=0, keepdims=True)


def tile_of(columns):
    return pl.BlockSpec((ROW_TILE, columns), lambda i: (i, 0))


def resident(shape, *index):
    place = index or (0,) * len(shape)
    return pl.BlockSpec(shape, lambda i: place, pipeline_mode=pl.Buffered(1))


def row_tiled(kernel, name, length, in_specs, out_specs, out_shape, operands, flops):
    size = sum(operand.size * operand.dtype.itemsize for operand in operands)
    size += sum(shape.size * jnp.dtype(shape.dtype).itemsize for shape in out_shape)
    return pl.pallas_call(
        kernel,
        grid=(length // ROW_TILE,),
        in_specs=in_specs,
        out_specs=out_specs,
        out_shape=out_shape,
        compiler_params=pltpu.CompilerParams(vmem_limit_bytes=56 << 20),
        cost_estimate=estimate(flops, size),
        name=name,
    )(*operands)


def project_kernel(hidden_ref, gains_ref, offsets_ref, weight_ref, normed_ref, packed_ref):
    features = hidden_ref.shape[1]
    normal, _ = normal_of(hidden_ref[...])
    normed = (normal * gains_ref[0:1] + offsets_ref[0:1]).astype(half)
    normed_ref[...] = normed
    for part in range(3):
        window = slice(part * features, (part + 1) * features)
        product = contract(normed, weight_ref[:, window], 1, 0)
        if part != 1:
            row = 1 if part == 0 else 2
            product = product + offsets_ref[row : row + 1]
        packed_ref[:, window] = product.astype(half)


def project(hidden, gains, offsets, joined):
    length, features = hidden.shape
    return row_tiled(
        project_kernel,
        "project",
        length,
        [
            tile_of(features),
            resident(gains.shape),
            resident(offsets.shape),
            resident((features, 3 * features)),
        ],
        [tile_of(features), tile_of(3 * features)],
        [
            jax.ShapeDtypeStruct((length, features), half),
            jax.ShapeDtypeStruct((length, 3 * features), half),
        ],
        (hidden, gains, offsets, joined),
        6 * length * features * features,
    )


def feed_kernel(
    attended_ref,
    hidden_ref,
    gains_ref,
    offsets_ref,
    up_bias_ref,
    out_weight_ref,
    up_ref,
    down_ref,
    middle_ref,
    second_ref,
    activated_ref,
    slope_ref,
    result_ref,
):
    hidden_units = up_ref.shape[1]
    middle = hidden_ref[...] + (
        contract(attended_ref[...], out_weight_ref[...], 1, 0) + offsets_ref[3:4]
    )
    middle_ref[...] = middle
    normal, _ = normal_of(middle)
    second = (normal * gains_ref[1:2] + offsets_ref[4:5]).astype(half)
    second_ref[...] = second
    result = middle + offsets_ref[5:6]
    rate = 0.7978845608028654
    for start in range(0, hidden_units, FF_CHUNK):
        window = slice(start, start + FF_CHUNK)
        value = contract(second, up_ref[:, window], 1, 0) + up_bias_ref[:, window]
        square = value * value
        bent = jnp.tanh(value * (rate + (rate * 0.044715) * square))
        opened = 0.5 + 0.5 * bent
        activated = (value * opened).astype(half)
        activated_ref[:, window] = activated
        curve = (value * (0.5 * rate + (1.5 * rate * 0.044715) * square)) * (1.0 - bent * bent)
        slope_ref[:, window] = (opened + curve).astype(half)
        result = result + contract(activated, down_ref[window, :], 1, 0)
    result_ref[...] = result.astype(result_ref.dtype)


def feed(attended, hidden, gains, offsets, up_bias, joined, up, down, result_type):
    length, features = hidden.shape
    units = down.shape[0]
    up_array, up_place = up
    shape = jax.ShapeDtypeStruct
    return row_tiled(
        feed_kernel,
        "feed",
        length,
        [
            tile_of(features),
            tile_of(features),
            resident(gains.shape),
            resident(offsets.shape),
            resident(up_bias.shape),
            resident((features, features), 0, 3),
            resident((features, units), 0, up_place),
            resident(down.shape),
        ],
        [tile_of(features), tile_of(features), tile_of(units), tile_of(units), tile_of(features)],
        [
            shape((length, features), single),
            shape((length, features), half),
            shape((length, units), half),
            shape((length, units), half),
            shape((length, features), result_type),
        ],
        (attended, hidden, gains, offsets, up_bias, joined, up_array, down),
        2 * length * features * (features + 2 * units),
    )


def feed_grad_kernel(
    gradient_ref,
    slope_ref,
    middle_ref,
    gains_ref,
    out_weight_ref,
    up_ref,
    down_ref,
    branch_ref,
    upper_ref,
    middle_grad_ref,
    attention_grad_ref,
    upstream_ref,
    sums_ref,
    unit_sums_ref,
):
    units = up_ref.shape[1]

    @pl.when(pl.program_id(0) == 0)
    def _():
        sums_ref[...] = jnp.zeros_like(sums_ref)
        unit_sums_ref[...] = jnp.zeros_like(unit_sums_ref)

    gradient = gradient_ref[...].astype(single)
    branch = gradient.astype(half)
    branch_ref[...] = branch
    sums_ref[0:1] += column_sum(branch.astype(single))
    second_grad = jnp.zeros(gradient.shape, single)
    for start in range(0, units, FF_CHUNK):
        window = slice(start, start + FF_CHUNK)
        pulled = contract(branch, down_ref[window, :], 1, 1) * slope_ref[:, window].astype(single)
        upper = pulled.astype(half)
        upper_ref[:, window] = upper
        unit_sums_ref[:, window] += column_sum(upper.astype(single))
        second_grad = second_grad + contract(upper, up_ref[:, window], 1, 1)
    normal, inverse = normal_of(middle_ref[...])
    middle_grad = gradient + norm_pull(normal, inverse, gains_ref[1:2], second_grad)
    sums_ref[1:2] += column_sum(second_grad * normal)
    sums_ref[2:3] += column_sum(second_grad)
    middle_grad_ref[...] = middle_grad
    attention_grad = middle_grad.astype(half)
    attention_grad_ref[...] = attention_grad
    sums_ref[3:4] += column_sum(attention_grad.astype(single))
    upstream_ref[...] = contract(attention_grad, out_weight_ref[...], 1, 1).astype(half)


def feed_grad(gradient, slope, middle, gains, joined, up, down):
    up_array, up_place = up
    length, features = middle.shape
    units = down.shape[0]
    shape = jax.ShapeDtypeStruct
    return row_tiled(
        feed_grad_kernel,
        "feed_grad",
        length,
        [
            tile_of(features),
            tile_of(units),
            tile_of(features),
            resident(gains.shape),
            resident((features, features), 0, 3),
            resident((features, units), 0, up_place),
            resident(down.shape),
        ],
        [
            tile_of(features),
            tile_of(units),
            tile_of(features),
            tile_of(features),
            tile_of(features),
            resident((8, features)),
            resident((1, units)),
        ],
        [
            shape((length, features), half),
            shape((length, units), half),
            shape((length, features), single),
            shape((length, features), half),
            shape((length, features), half),
            shape((8, features), single),
            shape((1, units), single),
        ],
        (gradient, slope, middle, gains, joined, up_array, down),
        2 * length * features * (features + 2 * units),
    )


def project_grad_kernel(
    packed_grad_ref, hidden_ref, middle_grad_ref, gains_ref, weight_ref, result_ref, sums_ref
):
    features = hidden_ref.shape[1]

    @pl.when(pl.program_id(0) == 0)
    def _():
        sums_ref[...] = jnp.zeros_like(sums_ref)

    packed_grad = packed_grad_ref[...]
    normed_grad = contract(packed_grad, weight_ref[...], 1, 1)
    normal, inverse = normal_of(hidden_ref[...])
    result = middle_grad_ref[...] + norm_pull(normal, inverse, gains_ref[0:1], normed_grad)
    result_ref[...] = result.astype(result_ref.dtype)
    sums_ref[0:1] += column_sum(normed_grad * normal)
    sums_ref[1:2] += column_sum(normed_grad)
    sums_ref[2:3] += column_sum(packed_grad[:, :features].astype(single))
    sums_ref[3:4] += column_sum(packed_grad[:, 2 * features :].astype(single))


def project_grad(packed_grad, hidden, middle_grad, gains, joined, result_type):
    length, features = hidden.shape
    shape = jax.ShapeDtypeStruct
    return row_tiled(
        project_grad_kernel,
        "project_grad",
        length,
        [
            tile_of(3 * features),
            tile_of(features),
            tile_of(features),
            resident(gains.shape),
            resident((features, 3 * features)),
        ],
        [tile_of(features), resident((8, features))],
        [shape((length, features), result_type), shape((8, features), single)],
        (packed_grad, hidden, middle_grad, gains, joined),
        6 * length * features * features,
    )


def term_blocks(terms, core, groups, row_unit, by_core):
    pieces = [left.shape[1] // (groups * row_unit) for left, _ in terms]
    widths = [right.shape[1] // (2 if by_core else 1) for _, right in terms]
    total = sum(count * width for count, width in zip(pieces, widths))
    chips = groups // 2
    out_shape = (chips, 2, row_unit, total) if by_core else (groups, row_unit, total)
    outputs = 2 if by_core else 1
    if row_unit % 16:
        columns = []
        for (left, right), count, width in zip(terms, pieces, widths):
            part = contract(left, right, 0, 0).astype(half)
            part = part.reshape(chips, 2, count, row_unit, -1, width).transpose(2, 1, 0, 4, 3, 5)
            columns += [part[piece] for piece in range(count)]
        whole = jnp.concatenate(columns, axis=-1)
        if not by_core:
            return [whole[:, :, 0].swapaxes(0, 1).reshape(out_shape)]
        return [
            lax.dynamic_index_in_dim(whole, which, 0, keepdims=False) for which in (1 - core, core)
        ]
    number = len(terms)

    def kernel(core_ref, *refs):
        sources = refs[: 2 * number]
        outs = refs[2 * number : 2 * number + outputs]
        buffers = refs[2 * number + outputs : 4 * number + outputs]
        semaphores = refs[4 * number + outputs]
        first_core = core_ref[0] == 0
        copies = [
            pltpu.make_async_copy(source, buffer, semaphores.at[index])
            for index, (source, buffer) in enumerate(zip(sources, buffers))
        ]
        for copy in copies:
            copy.start()
        start = 0
        for index, (count, width) in enumerate(zip(pieces, widths)):
            copies[2 * index].wait()
            copies[2 * index + 1].wait()
            left, right = buffers[2 * index], buffers[2 * index + 1]
            rows = groups * row_unit
            step = max(size for size in (768, 640, 512, 384, 256, 128) if width % size == 0)
            held = chips // count
            for turn in range(count):
                turned = left[:, turn * rows : (turn + 1) * rows].T
                some = slice(turn * held, (turn + 1) * held)
                for low in range(0, right.shape[1], step):
                    product = contract(turned, right[:, low : low + step], 1, 0).astype(half)
                    product = product.reshape(held, 2, count, row_unit, step)
                    side, inside = divmod(low, width)
                    for piece in range(count):
                        lanes = start + piece * width + inside
                        lanes = slice(lanes, lanes + step)
                        even, odd = product[:, 0, piece], product[:, 1, piece]
                        if by_core:
                            outs[0][some, side, :, lanes] = jnp.where(first_core, odd, even)
                            outs[1][some, side, :, lanes] = jnp.where(first_core, even, odd)
                        else:
                            for chip in range(held):
                                owner = 2 * (turn * held + chip)
                                outs[0][owner, :, lanes] = even[chip]
                                outs[0][owner + 1, :, lanes] = odd[chip]
            start += count * width

    anywhere = pl.BlockSpec(memory_space=pl.ANY)
    operands = [operand for term in terms for operand in term]
    size = sum(operand.size for operand in operands) * 2
    flops = sum(2 * left.size * right.shape[1] for left, right in terms)
    shape = jax.ShapeDtypeStruct(out_shape, half)
    return pl.pallas_call(
        kernel,
        in_specs=[pl.BlockSpec(memory_space=pltpu.SMEM)] + [anywhere] * len(operands),
        out_specs=[pl.BlockSpec(memory_space=pltpu.VMEM)] * outputs,
        out_shape=[shape] * outputs,
        scratch_shapes=[pltpu.VMEM(operand.shape, half) for operand in operands]
        + [pltpu.SemaphoreType.DMA((len(operands),))],
        compiler_params=pltpu.CompilerParams(vmem_limit_bytes=60 << 20),
        cost_estimate=estimate(flops, size + 2 * outputs * shape.size),
        name="term_blocks",
    )(core.reshape(1).astype(jnp.int32), *operands)


def per_device(
    tokens,
    time_embed,
    segment_ids,
    pad_mask,
    out_grad,
    qkv_weight,
    out_weight,
    up_weight,
    down_weight,
    norm_gains,
    bias_rows,
    up_bias,
):
    layers = qkv_weight.shape[0]
    features = tokens.shape[2]
    groups = lax.axis_size("wide")
    swap = [(0, 1), (1, 0)]

    def whole_sequence(part):
        return lax.all_to_all(part, "seq", split_axis=0, concat_axis=1, tiled=True)[0]

    core = lax.axis_index("wide") & 1
    place = lax.axis_index("seq")
    indices = jnp.stack([core, place]).astype(jnp.int32)
    row_unit = qkv_weight.shape[1]

    def across(bit):
        pairs = [(index, index ^ bit) for index in range(groups)]
        return lambda part: lax.ppermute(part, "wide", pairs)

    def beside_seq(part):
        return lax.ppermute(part, "seq", swap)

    def to_owners(part):
        return lax.psum_scatter(part, "wide", scatter_dimension=0, tiled=True)

    bit_of = lambda bit: (lax.axis_index("wide") >> (bit.bit_length() - 1)) & 1
    running = []

    def begin(steps, finish):
        entry = [steps, finish, next(steps), None]
        running.append(entry)
        return entry

    def launch(main, entries):
        fresh = [entry for entry in entries if entry in running and entry[3] is None]
        if fresh:
            sends = [[sent for sent, _ in entry[2]] for entry in fresh]
            main, sends = lax.optimization_barrier((main, sends))
            for entry, sent in zip(fresh, sends):
                entry[3] = [pass_on(part) for part, (_, pass_on) in zip(sent, entry[2])]
        return main

    def advance(main, *only):
        chosen = [entry for entry in only or list(running) if entry in running]
        main = launch(main, chosen)
        if not chosen:
            return main
        main, flying = lax.optimization_barrier((main, [entry[3] for entry in chosen]))
        for entry, arrived in zip(chosen, flying):
            entry[3] = None
            try:
                entry[2] = entry[0].send(arrived)
            except StopIteration as stop:
                entry[1](stop.value)
                running.remove(entry)
        return launch(main, chosen)

    def side_of(array, which, axis):
        return lax.dynamic_index_in_dim(array, which, axis, keepdims=False)

    chip_bits = [1 << number for number in range(groups.bit_length() - 2, 0, -1)]

    def join(current, received, which):
        lead = current.shape[0]
        joined = place_pieces(
            [current, received],
            (lead, 2) + current.shape[1:],
            [lambda ref: (slice(None), ref[0]), lambda ref: (slice(None), 1 - ref[0])],
            which.reshape(1).astype(jnp.int32),
        )
        return joined.reshape((2 * lead,) + current.shape[1:])

    def gather_columns(shard):
        rows, columns = shard.shape[0], shard.shape[1] // 2
        current = lax.dynamic_slice_in_dim(shard, place * columns, columns, axis=1)[None]
        for bit in chip_bits:
            (received,) = yield [(current, across(bit))]
            current = join(current, received, bit_of(bit))
        (aside,) = yield [(current, beside_seq)]
        passed = yield [(part, across(1)) for part in (current, aside)]

        def target(own_core, own_place):
            def where(ref):
                which_core = ref[0] if own_core else 1 - ref[0]
                which_place = ref[1] if own_place else 1 - ref[1]
                start = pl.multiple_of(which_place * columns, columns)
                return (slice(None), which_core, slice(None), pl.ds(start, columns))

            return where

        return place_pieces(
            [current, aside, *passed],
            (current.shape[0], 2, rows, 2 * columns),
            [target(True, True), target(True, False), target(False, True), target(False, False)],
            indices,
        ).reshape(-1, 2 * columns)

    def gather_rows(shard):
        rows, columns = shard.shape[0] // 2, shard.shape[1]
        current = side_of(shard.reshape(2, rows, columns), place, 0)[None]
        for bit in chip_bits[:-1]:
            (received,) = yield [(current, across(bit))]
            current = join(current, received, bit_of(bit))
        (received,) = yield [(current, beside_seq)]
        current = join(current, received, place).reshape(-1, 2 * rows, columns)
        for bit in chip_bits[-1:] + [1]:
            (received,) = yield [(current, across(bit))]
            current = join(current, received, bit_of(bit))
        return current.reshape(-1, columns)

    marks = whole_sequence(jnp.stack([segment_ids, pad_mask], axis=2))
    tokens, marks = lax.optimization_barrier((tokens, marks))
    my_tokens = whole_sequence(tokens)

    small = jnp.concatenate(
        [norm_gains.reshape(-1), bias_rows.reshape(-1), up_bias.reshape(-1)]
    )
    side = small.reshape(row_unit, -1)
    side_width = side.shape[1]
    side = jnp.pad(side, ((0, 0), (0, -side_width % PAIR)))
    joined_parts = [jnp.concatenate([qkv_weight[0], out_weight[0], side], axis=1)]
    for layer in range(1, layers):
        parts = [qkv_weight[layer], out_weight[layer], up_weight[layer]]
        joined_parts.append(jnp.concatenate(parts, axis=1))
    joined = [lax.all_gather(part, "wide", axis=0, tiled=True) for part in joined_parts]
    small_whole = joined[0][:, -side.shape[1] :][:, :side_width].reshape(groups, -1)
    cut_gains = norm_gains.size
    cut_rows = cut_gains + bias_rows.size

    def whole_rows(part, count):
        parts = part.reshape(groups, layers, count, -1)
        return parts.transpose(1, 2, 0, 3).reshape(layers, count, -1).astype(single)

    all_gains = whole_rows(small_whole[:, :cut_gains], norm_gains.shape[1])
    all_offsets = whole_rows(small_whole[:, cut_gains:cut_rows], bias_rows.shape[1])
    all_up_bias = whole_rows(small_whole[:, cut_rows:], 1)[:, 0]

    doc, pad = marks[:, 0], marks[:, 1]
    positions = jnp.arange(doc.shape[0])
    allowed = (doc[:, None] == doc[None, :]) & (
        (pad[:, None] == 1) | (positions[:, None] == positions[None, :])
    )
    bias = jnp.where(allowed, 0.0, masked_bias)

    matrices = [None] * layers
    ups, downs = {}, {}
    fetches = [
        begin(gather_columns(up_weight[0]), functools.partial(ups.__setitem__, 0)),
        begin(gather_rows(down_weight[0]), functools.partial(downs.__setitem__, 0)),
    ]
    for _ in chip_bits:
        time_embed = advance(time_embed, *fetches)
    my_time = lax.dynamic_index_in_dim(time_embed, place, 0, keepdims=True)
    hidden = my_tokens.astype(single) + my_time
    saved = []
    for layer in range(layers):
        whole = joined[layer]
        gains, offsets = all_gains[layer], all_offsets[layer]
        before = hidden
        normed, packed = project(hidden, gains, offsets, whole)
        if layer == layers - 1:
            packed, out_grad = lax.optimization_barrier((packed, out_grad))
            my_upstream = whole_sequence(out_grad)
        packed = advance(packed, *fetches)
        attended, totals = attend_forward(packed, bias)
        attended = advance(attended, *fetches)
        while running:
            attended = advance(attended, *fetches)
        up = (whole, 4 * features // up_bias.shape[1] // groups) if layer else (ups[0], 0)
        matrices[layer] = (whole, up, downs[layer])
        fetches = []
        if layer < layers - 1:
            fetches = [
                begin(
                    gather_rows(down_weight[layer + 1]),
                    functools.partial(downs.__setitem__, layer + 1),
                )
            ]
            attended = launch(attended, fetches)
        middle, second, activated, slope, hidden = feed(
            attended,
            hidden,
            gains,
            offsets,
            all_up_bias[layer][None],
            whole,
            up,
            downs[layer],
            single if layer < layers - 1 else half,
        )
        for _ in chip_bits:
            hidden = advance(hidden, *fetches)
        saved.append((before, normed, packed, totals, attended, middle, second, activated, slope))

    def split_back(result):
        parts = result.reshape(2, -1, features).astype(half)
        return lax.all_to_all(parts, "seq", split_axis=0, concat_axis=0, tiled=True)

    output = split_back(hidden)

    def total_of(addends):
        return functools.reduce(jnp.add, [addend.astype(single) for addend in addends])

    def shares_of(terms, low, high):
        shares, start = [], 0
        for left, right in terms:
            rows, each = [], right.shape[1] // 2
            if high is None:
                each *= 2
            for _ in range(left.shape[1] // (groups * row_unit)):
                window = slice(start, start + each)
                if high is None:
                    rows.append(low[:, window])
                else:
                    rows.append(jnp.concatenate([low[:, window], high[:, window]], axis=1))
                start += each
            shares.append(jnp.concatenate(rows, axis=0))
        return shares

    def scatter_group(terms):
        (whole,) = term_blocks(terms, core, groups, row_unit, False)
        whole = whole.reshape(groups * row_unit, -1)
        (share,) = yield [(whole, to_owners)]
        (received,) = yield [(share, beside_seq)]
        return shares_of(terms, share.astype(single) + received.astype(single), None)

    def reduce_group(terms):
        other, own = term_blocks(terms, core, groups, row_unit, True)
        (received,) = yield [(other, across(1))]
        shape = (2,) * len(chip_bits) + (2, row_unit, own.shape[-1])
        addends = [part.reshape(shape) for part in (own, received)]
        axis = len(chip_bits) - 1
        for bit in chip_bits[::-1]:
            mine = bit_of(bit)
            sent = total_of([side_of(part, 1 - mine, axis) for part in addends]).astype(half)
            (received,) = yield [(sent, across(bit))]
            addends = [side_of(part, mine, axis) for part in addends] + [received]
            axis -= 1
        current = total_of(addends).astype(half)
        (received,) = yield [(current, beside_seq)]
        low, high = current.astype(single) + received.astype(single)
        return shares_of(terms, low, high)

    def reduce_small(array):
        bit = 1
        while bit < groups:
            view = array.reshape(-1, 2, array.shape[-1])
            mine = bit_of(bit)
            sent = side_of(view, 1 - mine, 1)
            (received,) = yield [(sent, across(bit))]
            array = side_of(view, mine, 1) + received
            bit *= 2
        (received,) = yield [(array, beside_seq)]
        return (array + received)[0]

    weight_grads = [[None] * 4 for _ in range(layers)]

    def begin_group(steps, layer, named):
        def finish(shares):
            for (part, _), share in zip(named, shares):
                weight_grads[layer][part] = share

        return begin(steps([term for _, term in named]), finish)

    gradient = my_upstream
    small_grads = [None] * layers
    held = []
    for layer in range(layers - 1, -1, -1):
        whole, up, down = matrices[layer]
        gains = all_gains[layer]
        hidden, normed, packed, totals, attended, middle, second, activated, slope = saved[layer]
        steps = scatter_group if layer else reduce_group
        if not layer:
            first = begin_group(steps, layer, [(3, (activated, gradient.astype(half)))])
            gradient = launch(gradient, [first])
        branch, upper, middle_grad, attention_grad, upstream, sums, unit_sums = feed_grad(
            gradient, slope, middle, gains, whole, up, down
        )
        named = [(2, (second, upper)), (1, (attended, attention_grad))]
        if layer:
            held.append(begin_group(steps, layer, [(3, (activated, branch))] + named))
            upstream = launch(upstream, held[-1:])
        else:
            second_group = begin_group(steps, layer, named)
            upstream = launch(upstream, [second_group])
            upstream = advance(upstream, first)
            upstream = advance(upstream, second_group)
        packed_grad = attend_backward(packed, bias, upstream, totals, attended)
        if layer == layers - 1:
            packed_grad, output = lax.optimization_barrier((packed_grad, output))
            output = output.astype(single)
        named = [(0, (normed, packed_grad))]
        if layer:
            held.append(begin_group(steps, layer, named))
            packed_grad = launch(packed_grad, held[-1:])
        else:
            packed_grad = advance(packed_grad, first, second_group, *held[:1])
            last_group = begin_group(steps, layer, named)
            packed_grad = launch(packed_grad, [last_group])
            packed_grad = advance(packed_grad, first)
            packed_grad = advance(packed_grad, last_group)
        gradient, more_sums = project_grad(
            packed_grad, hidden, middle_grad, gains, whole, single if layer else half
        )
        if not layer:
            gradient = advance(gradient, first, second_group, last_group, *held[:1])
        small_grads[layer] = (
            jnp.stack([more_sums[0], sums[1]]),
            jnp.stack([more_sums[1], more_sums[2], more_sums[3], sums[3], sums[2], sums[0]]),
            unit_sums[0],
        )

    def by_owner(parts):
        stacked = jnp.stack(parts)
        stacked = stacked.reshape(layers, -1, groups, stacked.shape[-1] // groups)
        return stacked.transpose(2, 0, 1, 3).reshape(groups, -1)

    owned = jnp.concatenate(
        [by_owner([small_grads[layer][part] for layer in range(layers)]) for part in range(3)],
        axis=1,
    )
    small_result = []
    begin(reduce_small(owned), small_result.append)
    input_grad = split_back(gradient)
    while running:
        input_grad = advance(input_grad)
    input_grad = input_grad.astype(single)
    owned = small_result[0]
    stacked = [
        jnp.stack([weight_grads[layer][part] for layer in range(layers)]) for part in range(4)
    ]
    return (
        output,
        input_grad,
        *stacked,
        owned[:cut_gains].reshape(norm_gains.shape),
        owned[cut_gains:cut_rows].reshape(bias_rows.shape),
        owned[cut_rows:].reshape(up_bias.shape),
    )


def solution(mesh):
    tokens_spec = P("wide", "seq", None)
    matrix_spec = P(None, "wide", None)
    rows_spec = P(None, None, "wide")
    return jax.shard_map(
        per_device,
        mesh=mesh,
        in_specs=(
            tokens_spec,
            P("wide", None),
            P("wide", "seq"),
            P("wide", "seq"),
            tokens_spec,
            matrix_spec,
            matrix_spec,
            matrix_spec,
            matrix_spec,
            rows_spec,
            rows_spec,
            P(None, "wide"),
        ),
        out_specs=(
            tokens_spec,
            tokens_spec,
            matrix_spec,
            matrix_spec,
            matrix_spec,
            matrix_spec,
            rows_spec,
            rows_spec,
            P(None, "wide"),
        ),
        check_vma=False,
    )
```

```python
import functools

import jax
import jax.numpy as jnp
from jax import lax
from jax.experimental import pallas as pl
from jax.experimental.pallas import tpu as pltpu
from jax.sharding import PartitionSpec as P

HEAD_SIZE = 64
PAIR = 2 * HEAD_SIZE
FORWARD_ROWS = 512
BACKWARD_ROWS = 256
ROW_TILE = 256
FF_CHUNK = 1024

epsilon = 1e-05
masked_bias = -1e30
half = jnp.bfloat16
single = jnp.float32


def estimate(flops, size):
    return pl.CostEstimate(flops=flops // 16, bytes_accessed=size // 16, transcendentals=0)


def contract(left, right, left_dim, right_dim):
    return lax.dot_general(
        left, right, (((left_dim,), (right_dim,)), ((), ())), preferred_element_type=jnp.float32
    )


def first_head_lanes():
    return lax.broadcasted_iota(jnp.int32, (1, PAIR), 1) < HEAD_SIZE


def one_head_of(pair, head):
    lanes = first_head_lanes()
    keep = lanes if head == 0 else jnp.logical_not(lanes)
    return jnp.where(keep, pair, jnp.zeros_like(pair))


def attend_kernel(query_ref, key_ref, value_ref, bias_ref, out_ref, total_ref, *, rows):
    keys = key_ref[...]
    values = value_ref[...]
    scale = jnp.asarray(HEAD_SIZE ** (-0.5), half)
    for start in range(0, keys.shape[0], rows):
        window = pl.ds(start, rows)
        queries = query_ref[window, :] * scale
        bias = bias_ref[:, window]
        attended = []
        for head in range(2):
            scores = contract(keys, one_head_of(queries, head), 1, 1) + bias
            top = jnp.max(scores, axis=0, keepdims=True)
            weights = jnp.exp(scores - top)
            total = jnp.sum(weights, axis=0, keepdims=True)
            mixed = contract(values, weights.astype(half), 0, 0) * (1.0 / total)
            attended.append(mixed[HEAD_SIZE * head : HEAD_SIZE * (head + 1)])
            total_ref[head : head + 1, window] = top + jnp.log(total)
        out_ref[window, :] = jnp.concatenate(attended, 0).T.astype(half)


def attend_forward(packed, bias):
    length = packed.shape[0]
    features = packed.shape[1] // 3
    pairs = features // PAIR
    columns = lambda part: pl.BlockSpec((length, PAIR), lambda i: (0, part * pairs + i))
    return pl.pallas_call(
        functools.partial(attend_kernel, rows=FORWARD_ROWS),
        grid=(pairs,),
        in_specs=[
            columns(0),
            columns(1),
            columns(2),
            pl.BlockSpec((length, length), lambda i: (0, 0)),
        ],
        out_specs=[columns(0), pl.BlockSpec((None, 2, length), lambda i: (i, 0, 0))],
        out_shape=[
            jax.ShapeDtypeStruct((length, features), half),
            jax.ShapeDtypeStruct((pairs, 2, length), single),
        ],
        compiler_params=pltpu.CompilerParams(vmem_limit_bytes=56 << 20),
        cost_estimate=estimate(16 * length * length * features, 8 * length * features),
        name="attend_forward",
    )(packed, packed, packed, bias)


def attend_grad_kernel(
    query_ref,
    key_ref,
    value_ref,
    bias_ref,
    upstream_ref,
    total_ref,
    attended_ref,
    out_ref,
    key_sum,
    value_sum,
    *,
    rows,
):
    pair = pl.program_id(0)
    features = out_ref.shape[1] // 3
    keys = key_ref[...]
    values = value_ref[...]
    scale = HEAD_SIZE ** (-0.5)
    for start in range(0, keys.shape[0], rows):
        window = pl.ds(start, rows)
        queries = query_ref[window, :] * jnp.asarray(scale, half)
        upstream = upstream_ref[window, :]
        product = (upstream.astype(single) * attended_ref[window, :].astype(single)).T
        bias = bias_ref[:, window]
        query_grads, key_grad, value_grad = [], 0.0, 0.0
        for head in range(2):
            head_queries = one_head_of(queries, head)
            head_upstream = one_head_of(upstream, head)
            inner = jnp.sum(
                product[HEAD_SIZE * head : HEAD_SIZE * (head + 1)], axis=0, keepdims=True
            )
            scores = contract(keys, head_queries, 1, 1) + bias
            weights = jnp.exp(scores - total_ref[head : head + 1, window])
            weight_grads = contract(values, head_upstream, 1, 1)
            score_grads = (weights * (weight_grads - inner)).astype(half)
            value_grad = value_grad + contract(weights.astype(half), head_upstream, 1, 0)
            key_grad = key_grad + contract(score_grads, head_queries, 1, 0)
            query_grads.append(
                contract(keys, score_grads, 0, 0)[HEAD_SIZE * head : HEAD_SIZE * (head + 1)]
            )
        out_ref[window, pl.ds(pl.multiple_of(pair * PAIR, PAIR), PAIR)] = (
            jnp.concatenate(query_grads, 0).T * scale
        ).astype(half)
        if start == 0:
            key_sum[...] = key_grad
            value_sum[...] = value_grad
        else:
            key_sum[...] += key_grad
            value_sum[...] += value_grad
    out_ref[:, pl.ds(pl.multiple_of(features + pair * PAIR, PAIR), PAIR)] = key_sum[...].astype(
        half
    )
    out_ref[:, pl.ds(pl.multiple_of(2 * features + pair * PAIR, PAIR), PAIR)] = value_sum[
        ...
    ].astype(half)


def attend_backward(packed, bias, upstream, totals, attended):
    length = packed.shape[0]
    features = packed.shape[1] // 3
    pairs = features // PAIR
    columns = lambda part: pl.BlockSpec((length, PAIR), lambda i: (0, part * pairs + i))
    return pl.pallas_call(
        functools.partial(attend_grad_kernel, rows=BACKWARD_ROWS),
        grid=(pairs,),
        in_specs=[
            columns(0),
            columns(1),
            columns(2),
            pl.BlockSpec((length, length), lambda i: (0, 0)),
            columns(0),
            pl.BlockSpec((None, 2, length), lambda i: (i, 0, 0)),
            columns(0),
        ],
        out_specs=pl.BlockSpec((length, 3 * features), lambda i: (0, 0)),
        out_shape=jax.ShapeDtypeStruct((length, 3 * features), half),
        scratch_shapes=[pltpu.VMEM((length, PAIR), single)] * 2,
        compiler_params=pltpu.CompilerParams(vmem_limit_bytes=56 << 20),
        cost_estimate=estimate(40 * length * length * features, 16 * length * features),
        name="attend_backward",
    )(packed, packed, packed, bias, upstream, totals, attended)


def place_pieces(pieces, out_shape, targets, indices):
    def kernel(index_ref, *refs):
        sources, out_ref, semaphores = refs[: len(pieces)], refs[-2], refs[-1]
        copies = [
            pltpu.make_async_copy(
                source, out_ref.at[target(index_ref)], semaphores.at[number]
            )
            for number, (source, target) in enumerate(zip(sources, targets))
        ]
        for copy in copies:
            copy.start()
        for copy in copies:
            copy.wait()

    size = 2 * 2
    for extent in out_shape:
        size *= extent
    anywhere = pl.BlockSpec(memory_space=pl.ANY)
    return pl.pallas_call(
        kernel,
        in_specs=[pl.BlockSpec(memory_space=pltpu.SMEM)] + [anywhere] * len(pieces),
        out_specs=pl.BlockSpec(memory_space=pltpu.VMEM),
        out_shape=jax.ShapeDtypeStruct(out_shape, pieces[0].dtype),
        scratch_shapes=[pltpu.SemaphoreType.DMA((len(pieces),))],
        compiler_params=pltpu.CompilerParams(vmem_limit_bytes=32 << 20),
        cost_estimate=estimate(0, size),
        name="place_pieces",
    )(indices, *pieces)


def normal_of(hidden):
    center = hidden - jnp.mean(hidden, axis=-1, keepdims=True)
    inverse = lax.rsqrt(jnp.mean(center * center, axis=-1, keepdims=True) + epsilon)
    return center * inverse, inverse


def norm_pull(normal, inverse, gain, upstream):
    scaled = upstream * gain
    slope = jnp.mean(scaled, axis=-1, keepdims=True)
    tilt = jnp.mean(scaled * normal, axis=-1, keepdims=True)
    return inverse * (scaled - slope - normal * tilt)


def column_sum(array):
    return jnp.sum(array, axis=0, keepdims=True)


def tile_of(columns):
    return pl.BlockSpec((ROW_TILE, columns), lambda i: (i, 0))


def resident(shape, *index):
    place = index or (0,) * len(shape)
    return pl.BlockSpec(shape, lambda i: place, pipeline_mode=pl.Buffered(1))


def row_tiled(kernel, name, length, in_specs, out_specs, out_shape, operands, flops):
    size = sum(operand.size * operand.dtype.itemsize for operand in operands)
    size += sum(shape.size * jnp.dtype(shape.dtype).itemsize for shape in out_shape)
    return pl.pallas_call(
        kernel,
        grid=(length // ROW_TILE,),
        in_specs=in_specs,
        out_specs=out_specs,
        out_shape=out_shape,
        compiler_params=pltpu.CompilerParams(vmem_limit_bytes=56 << 20),
        cost_estimate=estimate(flops, size),
        name=name,
    )(*operands)


def project_kernel(hidden_ref, gains_ref, offsets_ref, weight_ref, normed_ref, packed_ref):
    features = hidden_ref.shape[1]
    normal, _ = normal_of(hidden_ref[...])
    normed = (normal * gains_ref[0:1] + offsets_ref[0:1]).astype(half)
    normed_ref[...] = normed
    for part in range(3):
        window = slice(part * features, (part + 1) * features)
        product = contract(normed, weight_ref[:, window], 1, 0)
        if part != 1:
            row = 1 if part == 0 else 2
            product = product + offsets_ref[row : row + 1]
        packed_ref[:, window] = product.astype(half)


def project(hidden, gains, offsets, joined):
    length, features = hidden.shape
    return row_tiled(
        project_kernel,
        "project",
        length,
        [
            tile_of(features),
            resident(gains.shape),
            resident(offsets.shape),
            resident((features, 3 * features)),
        ],
        [tile_of(features), tile_of(3 * features)],
        [
            jax.ShapeDtypeStruct((length, features), half),
            jax.ShapeDtypeStruct((length, 3 * features), half),
        ],
        (hidden, gains, offsets, joined),
        6 * length * features * features,
    )


def feed_kernel(
    attended_ref,
    hidden_ref,
    gains_ref,
    offsets_ref,
    up_bias_ref,
    out_weight_ref,
    up_ref,
    down_ref,
    middle_ref,
    second_ref,
    activated_ref,
    slope_ref,
    result_ref,
):
    hidden_units = up_ref.shape[1]
    middle = hidden_ref[...] + (
        contract(attended_ref[...], out_weight_ref[...], 1, 0) + offsets_ref[3:4]
    )
    middle_ref[...] = middle
    normal, _ = normal_of(middle)
    second = (normal * gains_ref[1:2] + offsets_ref[4:5]).astype(half)
    second_ref[...] = second
    result = middle + offsets_ref[5:6]
    rate = 0.7978845608028654
    for start in range(0, hidden_units, FF_CHUNK):
        window = slice(start, start + FF_CHUNK)
        value = contract(second, up_ref[:, window], 1, 0) + up_bias_ref[:, window]
        square = value * value
        bent = jnp.tanh(value * (rate + (rate * 0.044715) * square))
        opened = 0.5 + 0.5 * bent
        activated = (value * opened).astype(half)
        activated_ref[:, window] = activated
        curve = (value * (0.5 * rate + (1.5 * rate * 0.044715) * square)) * (1.0 - bent * bent)
        slope_ref[:, window] = (opened + curve).astype(half)
        result = result + contract(activated, down_ref[window, :], 1, 0)
    result_ref[...] = result.astype(result_ref.dtype)


def feed(attended, hidden, gains, offsets, up_bias, joined, up, down, result_type):
    length, features = hidden.shape
    units = down.shape[0]
    up_array, up_place = up
    shape = jax.ShapeDtypeStruct
    return row_tiled(
        feed_kernel,
        "feed",
        length,
        [
            tile_of(features),
            tile_of(features),
            resident(gains.shape),
            resident(offsets.shape),
            resident(up_bias.shape),
            resident((features, features), 0, 3),
            resident((features, units), 0, up_place),
            resident(down.shape),
        ],
        [tile_of(features), tile_of(features), tile_of(units), tile_of(units), tile_of(features)],
        [
            shape((length, features), single),
            shape((length, features), half),
            shape((length, units), half),
            shape((length, units), half),
            shape((length, features), result_type),
        ],
        (attended, hidden, gains, offsets, up_bias, joined, up_array, down),
        2 * length * features * (features + 2 * units),
    )


def feed_grad_kernel(
    gradient_ref,
    slope_ref,
    middle_ref,
    gains_ref,
    out_weight_ref,
    up_ref,
    down_ref,
    branch_ref,
    upper_ref,
    middle_grad_ref,
    attention_grad_ref,
    upstream_ref,
    sums_ref,
    unit_sums_ref,
):
    units = up_ref.shape[1]

    @pl.when(pl.program_id(0) == 0)
    def _():
        sums_ref[...] = jnp.zeros_like(sums_ref)
        unit_sums_ref[...] = jnp.zeros_like(unit_sums_ref)

    gradient = gradient_ref[...].astype(single)
    branch = gradient.astype(half)
    branch_ref[...] = branch
    sums_ref[0:1] += column_sum(branch.astype(single))
    second_grad = jnp.zeros(gradient.shape, single)
    for start in range(0, units, FF_CHUNK):
        window = slice(start, start + FF_CHUNK)
        pulled = contract(branch, down_ref[window, :], 1, 1) * slope_ref[:, window].astype(single)
        upper = pulled.astype(half)
        upper_ref[:, window] = upper
        unit_sums_ref[:, window] += column_sum(upper.astype(single))
        second_grad = second_grad + contract(upper, up_ref[:, window], 1, 1)
    normal, inverse = normal_of(middle_ref[...])
    middle_grad = gradient + norm_pull(normal, inverse, gains_ref[1:2], second_grad)
    sums_ref[1:2] += column_sum(second_grad * normal)
    sums_ref[2:3] += column_sum(second_grad)
    middle_grad_ref[...] = middle_grad
    attention_grad = middle_grad.astype(half)
    attention_grad_ref[...] = attention_grad
    sums_ref[3:4] += column_sum(attention_grad.astype(single))
    upstream_ref[...] = contract(attention_grad, out_weight_ref[...], 1, 1).astype(half)


def feed_grad(gradient, slope, middle, gains, joined, up, down):
    up_array, up_place = up
    length, features = middle.shape
    units = down.shape[0]
    shape = jax.ShapeDtypeStruct
    return row_tiled(
        feed_grad_kernel,
        "feed_grad",
        length,
        [
            tile_of(features),
            tile_of(units),
            tile_of(features),
            resident(gains.shape),
            resident((features, features), 0, 3),
            resident((features, units), 0, up_place),
            resident(down.shape),
        ],
        [
            tile_of(features),
            tile_of(units),
            tile_of(features),
            tile_of(features),
            tile_of(features),
            resident((8, features)),
            resident((1, units)),
        ],
        [
            shape((length, features), half),
            shape((length, units), half),
            shape((length, features), single),
            shape((length, features), half),
            shape((length, features), half),
            shape((8, features), single),
            shape((1, units), single),
        ],
        (gradient, slope, middle, gains, joined, up_array, down),
        2 * length * features * (features + 2 * units),
    )


def project_grad_kernel(
    packed_grad_ref, hidden_ref, middle_grad_ref, gains_ref, weight_ref, result_ref, sums_ref
):
    features = hidden_ref.shape[1]

    @pl.when(pl.program_id(0) == 0)
    def _():
        sums_ref[...] = jnp.zeros_like(sums_ref)

    packed_grad = packed_grad_ref[...]
    normed_grad = contract(packed_grad, weight_ref[...], 1, 1)
    normal, inverse = normal_of(hidden_ref[...])
    result = middle_grad_ref[...] + norm_pull(normal, inverse, gains_ref[0:1], normed_grad)
    result_ref[...] = result.astype(result_ref.dtype)
    sums_ref[0:1] += column_sum(normed_grad * normal)
    sums_ref[1:2] += column_sum(normed_grad)
    sums_ref[2:3] += column_sum(packed_grad[:, :features].astype(single))
    sums_ref[3:4] += column_sum(packed_grad[:, 2 * features :].astype(single))


def project_grad(packed_grad, hidden, middle_grad, gains, joined, result_type):
    length, features = hidden.shape
    shape = jax.ShapeDtypeStruct
    return row_tiled(
        project_grad_kernel,
        "project_grad",
        length,
        [
            tile_of(3 * features),
            tile_of(features),
            tile_of(features),
            resident(gains.shape),
            resident((features, 3 * features)),
        ],
        [tile_of(features), resident((8, features))],
        [shape((length, features), result_type), shape((8, features), single)],
        (packed_grad, hidden, middle_grad, gains, joined),
        6 * length * features * features,
    )


def term_blocks(terms, core, groups, row_unit, by_core):
    pieces = [left.shape[1] // (groups * row_unit) for left, _ in terms]
    widths = [right.shape[1] // (2 if by_core else 1) for _, right in terms]
    total = sum(count * width for count, width in zip(pieces, widths))
    chips = groups // 2
    out_shape = (chips, 2, row_unit, total) if by_core else (groups, row_unit, total)
    outputs = 2 if by_core else 1
    if row_unit % 16:
        columns = []
        for (left, right), count, width in zip(terms, pieces, widths):
            part = contract(left, right, 0, 0).astype(half)
            part = part.reshape(chips, 2, count, row_unit, -1, width).transpose(2, 1, 0, 4, 3, 5)
            columns += [part[piece] for piece in range(count)]
        whole = jnp.concatenate(columns, axis=-1)
        if not by_core:
            return [whole[:, :, 0].swapaxes(0, 1).reshape(out_shape)]
        return [
            lax.dynamic_index_in_dim(whole, which, 0, keepdims=False) for which in (1 - core, core)
        ]
    number = len(terms)

    def kernel(core_ref, *refs):
        sources = refs[: 2 * number]
        outs = refs[2 * number : 2 * number + outputs]
        buffers = refs[2 * number + outputs : 4 * number + outputs]
        semaphores = refs[4 * number + outputs]
        first_core = core_ref[0] == 0
        copies = [
            pltpu.make_async_copy(source, buffer, semaphores.at[index])
            for index, (source, buffer) in enumerate(zip(sources, buffers))
        ]
        for copy in copies:
            copy.start()
        start = 0
        for index, (count, width) in enumerate(zip(pieces, widths)):
            copies[2 * index].wait()
            copies[2 * index + 1].wait()
            left, right = buffers[2 * index], buffers[2 * index + 1]
            rows = groups * row_unit
            step = max(size for size in (768, 640, 512, 384, 256, 128) if width % size == 0)
            held = chips // count
            for turn in range(count):
                turned = left[:, turn * rows : (turn + 1) * rows].T
                some = slice(turn * held, (turn + 1) * held)
                for low in range(0, right.shape[1], step):
                    product = contract(turned, right[:, low : low + step], 1, 0).astype(half)
                    product = product.reshape(held, 2, count, row_unit, step)
                    side, inside = divmod(low, width)
                    for piece in range(count):
                        lanes = start + piece * width + inside
                        lanes = slice(lanes, lanes + step)
                        even, odd = product[:, 0, piece], product[:, 1, piece]
                        if by_core:
                            outs[0][some, side, :, lanes] = jnp.where(first_core, odd, even)
                            outs[1][some, side, :, lanes] = jnp.where(first_core, even, odd)
                        else:
                            for chip in range(held):
                                owner = 2 * (turn * held + chip)
                                outs[0][owner, :, lanes] = even[chip]
                                outs[0][owner + 1, :, lanes] = odd[chip]
            start += count * width

    anywhere = pl.BlockSpec(memory_space=pl.ANY)
    operands = [operand for term in terms for operand in term]
    size = sum(operand.size for operand in operands) * 2
    flops = sum(2 * left.size * right.shape[1] for left, right in terms)
    shape = jax.ShapeDtypeStruct(out_shape, half)
    return pl.pallas_call(
        kernel,
        in_specs=[pl.BlockSpec(memory_space=pltpu.SMEM)] + [anywhere] * len(operands),
        out_specs=[pl.BlockSpec(memory_space=pltpu.VMEM)] * outputs,
        out_shape=[shape] * outputs,
        scratch_shapes=[pltpu.VMEM(operand.shape, half) for operand in operands]
        + [pltpu.SemaphoreType.DMA((len(operands),))],
        compiler_params=pltpu.CompilerParams(vmem_limit_bytes=60 << 20),
        cost_estimate=estimate(flops, size + 2 * outputs * shape.size),
        name="term_blocks",
    )(core.reshape(1).astype(jnp.int32), *operands)


def per_device(
    tokens,
    time_embed,
    segment_ids,
    pad_mask,
    out_grad,
    qkv_weight,
    out_weight,
    up_weight,
    down_weight,
    norm_gains,
    bias_rows,
    up_bias,
):
    layers = qkv_weight.shape[0]
    features = tokens.shape[2]
    groups = lax.axis_size("wide")
    swap = [(0, 1), (1, 0)]

    def whole_sequence(part):
        return lax.all_to_all(part, "seq", split_axis=0, concat_axis=1, tiled=True)[0]

    core = lax.axis_index("wide") & 1
    place = lax.axis_index("seq")
    indices = jnp.stack([core, place]).astype(jnp.int32)
    row_unit = qkv_weight.shape[1]

    def across(bit):
        pairs = [(index, index ^ bit) for index in range(groups)]
        return lambda part: lax.ppermute(part, "wide", pairs)

    def beside_seq(part):
        return lax.ppermute(part, "seq", swap)

    def to_owners(part):
        return lax.psum_scatter(part, "wide", scatter_dimension=0, tiled=True)

    bit_of = lambda bit: (lax.axis_index("wide") >> (bit.bit_length() - 1)) & 1
    running = []

    def begin(steps, finish):
        entry = [steps, finish, next(steps), None]
        running.append(entry)
        return entry

    def launch(main, entries):
        fresh = [entry for entry in entries if entry in running and entry[3] is None]
        if fresh:
            sends = [[sent for sent, _ in entry[2]] for entry in fresh]
            main, sends = lax.optimization_barrier((main, sends))
            for entry, sent in zip(fresh, sends):
                entry[3] = [pass_on(part) for part, (_, pass_on) in zip(sent, entry[2])]
        return main

    def advance(main, *only):
        chosen = [entry for entry in only or list(running) if entry in running]
        main = launch(main, chosen)
        if not chosen:
            return main
        main, flying = lax.optimization_barrier((main, [entry[3] for entry in chosen]))
        for entry, arrived in zip(chosen, flying):
            entry[3] = None
            try:
                entry[2] = entry[0].send(arrived)
            except StopIteration as stop:
                entry[1](stop.value)
                running.remove(entry)
        return launch(main, chosen)

    def side_of(array, which, axis):
        return lax.dynamic_index_in_dim(array, which, axis, keepdims=False)

    chip_bits = [1 << number for number in range(groups.bit_length() - 2, 0, -1)]

    def join(current, received, which):
        lead = current.shape[0]
        joined = place_pieces(
            [current, received],
            (lead, 2) + current.shape[1:],
            [lambda ref: (slice(None), ref[0]), lambda ref: (slice(None), 1 - ref[0])],
            which.reshape(1).astype(jnp.int32),
        )
        return joined.reshape((2 * lead,) + current.shape[1:])

    def gather_columns(shard):
        rows, columns = shard.shape[0], shard.shape[1] // 2
        current = lax.dynamic_slice_in_dim(shard, place * columns, columns, axis=1)[None]
        for bit in chip_bits:
            (received,) = yield [(current, across(bit))]
            current = join(current, received, bit_of(bit))
        (aside,) = yield [(current, beside_seq)]
        passed = yield [(part, across(1)) for part in (current, aside)]

        def target(own_core, own_place):
            def where(ref):
                which_core = ref[0] if own_core else 1 - ref[0]
                which_place = ref[1] if own_place else 1 - ref[1]
                start = pl.multiple_of(which_place * columns, columns)
                return (slice(None), which_core, slice(None), pl.ds(start, columns))

            return where

        return place_pieces(
            [current, aside, *passed],
            (current.shape[0], 2, rows, 2 * columns),
            [target(True, True), target(True, False), target(False, True), target(False, False)],
            indices,
        ).reshape(-1, 2 * columns)

    def gather_rows(shard):
        rows, columns = shard.shape[0] // 2, shard.shape[1]
        current = side_of(shard.reshape(2, rows, columns), place, 0)[None]
        for bit in chip_bits[:-1]:
            (received,) = yield [(current, across(bit))]
            current = join(current, received, bit_of(bit))
        (received,) = yield [(current, beside_seq)]
        current = join(current, received, place).reshape(-1, 2 * rows, columns)
        for bit in chip_bits[-1:] + [1]:
            (received,) = yield [(current, across(bit))]
            current = join(current, received, bit_of(bit))
        return current.reshape(-1, columns)

    marks = whole_sequence(jnp.stack([segment_ids, pad_mask], axis=2))
    tokens, marks = lax.optimization_barrier((tokens, marks))
    my_tokens = whole_sequence(tokens)

    small = jnp.concatenate(
        [norm_gains.reshape(-1), bias_rows.reshape(-1), up_bias.reshape(-1)]
    )
    side = small.reshape(row_unit, -1)
    side_width = side.shape[1]
    side = jnp.pad(side, ((0, 0), (0, -side_width % PAIR)))
    joined_parts = [jnp.concatenate([qkv_weight[0], out_weight[0], side], axis=1)]
    for layer in range(1, layers):
        parts = [qkv_weight[layer], out_weight[layer], up_weight[layer]]
        joined_parts.append(jnp.concatenate(parts, axis=1))
    joined = [lax.all_gather(part, "wide", axis=0, tiled=True) for part in joined_parts]
    small_whole = joined[0][:, -side.shape[1] :][:, :side_width].reshape(groups, -1)
    cut_gains = norm_gains.size
    cut_rows = cut_gains + bias_rows.size

    def whole_rows(part, count):
        parts = part.reshape(groups, layers, count, -1)
        return parts.transpose(1, 2, 0, 3).reshape(layers, count, -1).astype(single)

    all_gains = whole_rows(small_whole[:, :cut_gains], norm_gains.shape[1])
    all_offsets = whole_rows(small_whole[:, cut_gains:cut_rows], bias_rows.shape[1])
    all_up_bias = whole_rows(small_whole[:, cut_rows:], 1)[:, 0]

    doc, pad = marks[:, 0], marks[:, 1]
    positions = jnp.arange(doc.shape[0])
    allowed = (doc[:, None] == doc[None, :]) & (
        (pad[:, None] == 1) | (positions[:, None] == positions[None, :])
    )
    bias = jnp.where(allowed, 0.0, masked_bias)

    matrices = [None] * layers
    ups, downs = {}, {}
    fetches = [
        begin(gather_columns(up_weight[0]), functools.partial(ups.__setitem__, 0)),
        begin(gather_rows(down_weight[0]), functools.partial(downs.__setitem__, 0)),
    ]
    for _ in chip_bits[1:]:
        time_embed = advance(time_embed, *fetches)
    my_time = lax.dynamic_index_in_dim(time_embed, place, 0, keepdims=True)
    hidden = my_tokens.astype(single) + my_time
    saved = []
    for layer in range(layers):
        whole = joined[layer]
        gains, offsets = all_gains[layer], all_offsets[layer]
        before = hidden
        normed, packed = project(hidden, gains, offsets, whole)
        if layer == layers - 1:
            packed, out_grad = lax.optimization_barrier((packed, out_grad))
            my_upstream = whole_sequence(out_grad)
        packed = advance(packed, *fetches)
        attended, totals = attend_forward(packed, bias)
        attended = advance(attended, *fetches)
        while running:
            attended = advance(attended, *fetches)
        up = (whole, 4 * features // up_bias.shape[1] // groups) if layer else (ups[0], 0)
        matrices[layer] = (whole, up, downs[layer])
        fetches = []
        if layer < layers - 1:
            fetches = [
                begin(
                    gather_rows(down_weight[layer + 1]),
                    functools.partial(downs.__setitem__, layer + 1),
                )
            ]
            attended = launch(attended, fetches)
        middle, second, activated, slope, hidden = feed(
            attended,
            hidden,
            gains,
            offsets,
            all_up_bias[layer][None],
            whole,
            up,
            downs[layer],
            single if layer < layers - 1 else half,
        )
        for _ in chip_bits:
            hidden = advance(hidden, *fetches)
        saved.append((before, normed, packed, totals, attended, middle, second, activated, slope))

    def split_back(result):
        parts = result.reshape(2, -1, features).astype(half)
        return lax.all_to_all(parts, "seq", split_axis=0, concat_axis=0, tiled=True)

    output = split_back(hidden)

    def total_of(addends):
        return functools.reduce(jnp.add, [addend.astype(single) for addend in addends])

    def shares_of(terms, low, high):
        shares, start = [], 0
        for left, right in terms:
            rows, each = [], right.shape[1] // 2
            if high is None:
                each *= 2
            for _ in range(left.shape[1] // (groups * row_unit)):
                window = slice(start, start + each)
                if high is None:
                    rows.append(low[:, window])
                else:
                    rows.append(jnp.concatenate([low[:, window], high[:, window]], axis=1))
                start += each
            shares.append(jnp.concatenate(rows, axis=0))
        return shares

    def scatter_group(terms):
        (whole,) = term_blocks(terms, core, groups, row_unit, False)
        whole = whole.reshape(groups * row_unit, -1)
        (share,) = yield [(whole, to_owners)]
        (received,) = yield [(share, beside_seq)]
        return shares_of(terms, share.astype(single) + received.astype(single), None)

    def reduce_group(terms):
        other, own = term_blocks(terms, core, groups, row_unit, True)
        (received,) = yield [(other, across(1))]
        shape = (2,) * len(chip_bits) + (2, row_unit, own.shape[-1])
        addends = [part.reshape(shape) for part in (own, received)]
        axis = len(chip_bits) - 1
        for bit in chip_bits[::-1]:
            mine = bit_of(bit)
            sent = total_of([side_of(part, 1 - mine, axis) for part in addends]).astype(half)
            (received,) = yield [(sent, across(bit))]
            addends = [side_of(part, mine, axis) for part in addends] + [received]
            axis -= 1
        current = total_of(addends).astype(half)
        (received,) = yield [(current, beside_seq)]
        low, high = current.astype(single) + received.astype(single)
        return shares_of(terms, low, high)

    def reduce_small(array):
        bit = 1
        while bit < groups:
            view = array.reshape(-1, 2, array.shape[-1])
            mine = bit_of(bit)
            sent = side_of(view, 1 - mine, 1)
            (received,) = yield [(sent, across(bit))]
            array = side_of(view, mine, 1) + received
            bit *= 2
        (received,) = yield [(array, beside_seq)]
        return (array + received)[0]

    weight_grads = [[None] * 4 for _ in range(layers)]

    def begin_group(steps, layer, named):
        def finish(shares):
            for (part, _), share in zip(named, shares):
                weight_grads[layer][part] = share

        return begin(steps([term for _, term in named]), finish)

    gradient = my_upstream
    small_grads = [None] * layers
    held = []
    for layer in range(layers - 1, -1, -1):
        whole, up, down = matrices[layer]
        gains = all_gains[layer]
        hidden, normed, packed, totals, attended, middle, second, activated, slope = saved[layer]
        steps = scatter_group if layer else reduce_group
        branch, upper, middle_grad, attention_grad, upstream, sums, unit_sums = feed_grad(
            gradient, slope, middle, gains, whole, up, down
        )
        named = [(2, (second, upper)), (1, (attended, attention_grad))]
        if layer:
            held.append(begin_group(steps, layer, [(3, (activated, branch))] + named))
            upstream = launch(upstream, held[-1:])
        else:
            upstream = advance(upstream, first_group)
            upper, upstream = lax.optimization_barrier((upper, upstream))
            named = [(2, (second, upper)), (1, (attended, attention_grad))]
            second_group = begin_group(steps, layer, named)
            upstream = launch(upstream, [second_group])
            upstream = advance(upstream, second_group)
        packed_grad = attend_backward(packed, bias, upstream, totals, attended)
        if layer == layers - 1:
            packed_grad, output = lax.optimization_barrier((packed_grad, output))
            output = output.astype(single)
        named = [(0, (normed, packed_grad))]
        if not layer:
            packed_grad = advance(packed_grad, first_group, second_group, *held[:1])
            last_group = begin_group(steps, layer, named)
            packed_grad = launch(packed_grad, [last_group])
            packed_grad = advance(packed_grad, last_group)
        gradient, more_sums = project_grad(
            packed_grad, hidden, middle_grad, gains, whole, single if layer else half
        )
        if layer == 1:
            below = (saved[0][7], gradient.astype(half))
            first_group = begin_group(reduce_group, 0, [(3, below)])
            gradient = launch(gradient, [first_group])
        if layer:
            held.append(begin_group(steps, layer, named))
            gradient = launch(gradient, held[-1:])
        if layer == 1:
            gradient = advance(gradient, first_group)
        if not layer:
            gradient = advance(gradient, first_group, second_group, *held)
            gradient = advance(gradient, last_group)
        small_grads[layer] = (
            jnp.stack([more_sums[0], sums[1]]),
            jnp.stack([more_sums[1], more_sums[2], more_sums[3], sums[3], sums[2], sums[0]]),
            unit_sums[0],
        )

    def by_owner(parts):
        stacked = jnp.stack(parts)
        stacked = stacked.reshape(layers, -1, groups, stacked.shape[-1] // groups)
        return stacked.transpose(2, 0, 1, 3).reshape(groups, -1)

    owned = jnp.concatenate(
        [by_owner([small_grads[layer][part] for layer in range(layers)]) for part in range(3)],
        axis=1,
    )
    small_result = []
    begin(reduce_small(owned), small_result.append)
    input_grad = split_back(gradient)
    while running:
        input_grad = advance(input_grad)
    input_grad = input_grad.astype(single)
    owned = small_result[0]
    stacked = [
        jnp.stack([weight_grads[layer][part] for layer in range(layers)]) for part in range(4)
    ]
    return (
        output,
        input_grad,
        *stacked,
        owned[:cut_gains].reshape(norm_gains.shape),
        owned[cut_gains:cut_rows].reshape(bias_rows.shape),
        owned[cut_rows:].reshape(up_bias.shape),
    )


def solution(mesh):
    tokens_spec = P("wide", "seq", None)
    matrix_spec = P(None, "wide", None)
    rows_spec = P(None, None, "wide")
    return jax.shard_map(
        per_device,
        mesh=mesh,
        in_specs=(
            tokens_spec,
            P("wide", None),
            P("wide", "seq"),
            P("wide", "seq"),
            tokens_spec,
            matrix_spec,
            matrix_spec,
            matrix_spec,
            matrix_spec,
            rows_spec,
            rows_spec,
            P(None, "wide"),
        ),
        out_specs=(
            tokens_spec,
            tokens_spec,
            matrix_spec,
            matrix_spec,
            matrix_spec,
            matrix_spec,
            rows_spec,
            rows_spec,
            P(None, "wide"),
        ),
        check_vma=False,
    )
```

```python
import functools

import jax
import jax.numpy as jnp
from jax import lax
from jax.experimental import pallas as pl
from jax.experimental.pallas import tpu as pltpu
from jax.sharding import PartitionSpec as P

HEAD_SIZE = 64
PAIR = 2 * HEAD_SIZE
FORWARD_ROWS = 512
BACKWARD_ROWS = 256
ROW_TILE = 256
FF_CHUNK = 1024

epsilon = 1e-05
masked_bias = -1e30
half = jnp.bfloat16
single = jnp.float32


def estimate(flops, size):
    return pl.CostEstimate(flops=flops // 16, bytes_accessed=size // 16, transcendentals=0)


def contract(left, right, left_dim, right_dim):
    return lax.dot_general(
        left, right, (((left_dim,), (right_dim,)), ((), ())), preferred_element_type=jnp.float32
    )


def first_head_lanes():
    return lax.broadcasted_iota(jnp.int32, (1, PAIR), 1) < HEAD_SIZE


def one_head_of(pair, head):
    lanes = first_head_lanes()
    keep = lanes if head == 0 else jnp.logical_not(lanes)
    return jnp.where(keep, pair, jnp.zeros_like(pair))


def attend_kernel(query_ref, key_ref, value_ref, bias_ref, out_ref, total_ref, *, rows):
    keys = key_ref[...]
    values = value_ref[...]
    scale = jnp.asarray(HEAD_SIZE ** (-0.5), half)
    for start in range(0, keys.shape[0], rows):
        window = pl.ds(start, rows)
        queries = query_ref[window, :] * scale
        bias = bias_ref[:, window]
        attended = []
        for head in range(2):
            scores = contract(keys, one_head_of(queries, head), 1, 1) + bias
            top = jnp.max(scores, axis=0, keepdims=True)
            weights = jnp.exp(scores - top)
            total = jnp.sum(weights, axis=0, keepdims=True)
            mixed = contract(values, weights.astype(half), 0, 0) * (1.0 / total)
            attended.append(mixed[HEAD_SIZE * head : HEAD_SIZE * (head + 1)])
            total_ref[head : head + 1, window] = top + jnp.log(total)
        out_ref[window, :] = jnp.concatenate(attended, 0).T.astype(half)


def attend_forward(packed, bias):
    length = packed.shape[0]
    features = packed.shape[1] // 3
    pairs = features // PAIR
    columns = lambda part: pl.BlockSpec((length, PAIR), lambda i: (0, part * pairs + i))
    return pl.pallas_call(
        functools.partial(attend_kernel, rows=FORWARD_ROWS),
        grid=(pairs,),
        in_specs=[
            columns(0),
            columns(1),
            columns(2),
            pl.BlockSpec((length, length), lambda i: (0, 0)),
        ],
        out_specs=[columns(0), pl.BlockSpec((None, 2, length), lambda i: (i, 0, 0))],
        out_shape=[
            jax.ShapeDtypeStruct((length, features), half),
            jax.ShapeDtypeStruct((pairs, 2, length), single),
        ],
        compiler_params=pltpu.CompilerParams(vmem_limit_bytes=56 << 20),
        cost_estimate=estimate(16 * length * length * features, 8 * length * features),
        name="attend_forward",
    )(packed, packed, packed, bias)


def attend_grad_kernel(
    query_ref,
    key_ref,
    value_ref,
    bias_ref,
    upstream_ref,
    total_ref,
    attended_ref,
    out_ref,
    key_sum,
    value_sum,
    *,
    rows,
):
    pair = pl.program_id(0)
    features = out_ref.shape[1] // 3
    keys = key_ref[...]
    values = value_ref[...]
    scale = HEAD_SIZE ** (-0.5)
    for start in range(0, keys.shape[0], rows):
        window = pl.ds(start, rows)
        queries = query_ref[window, :] * jnp.asarray(scale, half)
        upstream = upstream_ref[window, :]
        product = (upstream.astype(single) * attended_ref[window, :].astype(single)).T
        bias = bias_ref[:, window]
        query_grads, key_grad, value_grad = [], 0.0, 0.0
        for head in range(2):
            head_queries = one_head_of(queries, head)
            head_upstream = one_head_of(upstream, head)
            inner = jnp.sum(
                product[HEAD_SIZE * head : HEAD_SIZE * (head + 1)], axis=0, keepdims=True
            )
            scores = contract(keys, head_queries, 1, 1) + bias
            weights = jnp.exp(scores - total_ref[head : head + 1, window])
            weight_grads = contract(values, head_upstream, 1, 1)
            score_grads = (weights * (weight_grads - inner)).astype(half)
            value_grad = value_grad + contract(weights.astype(half), head_upstream, 1, 0)
            key_grad = key_grad + contract(score_grads, head_queries, 1, 0)
            query_grads.append(
                contract(keys, score_grads, 0, 0)[HEAD_SIZE * head : HEAD_SIZE * (head + 1)]
            )
        out_ref[window, pl.ds(pl.multiple_of(pair * PAIR, PAIR), PAIR)] = (
            jnp.concatenate(query_grads, 0).T * scale
        ).astype(half)
        if start == 0:
            key_sum[...] = key_grad
            value_sum[...] = value_grad
        else:
            key_sum[...] += key_grad
            value_sum[...] += value_grad
    out_ref[:, pl.ds(pl.multiple_of(features + pair * PAIR, PAIR), PAIR)] = key_sum[...].astype(
        half
    )
    out_ref[:, pl.ds(pl.multiple_of(2 * features + pair * PAIR, PAIR), PAIR)] = value_sum[
        ...
    ].astype(half)


def attend_backward(packed, bias, upstream, totals, attended):
    length = packed.shape[0]
    features = packed.shape[1] // 3
    pairs = features // PAIR
    columns = lambda part: pl.BlockSpec((length, PAIR), lambda i: (0, part * pairs + i))
    return pl.pallas_call(
        functools.partial(attend_grad_kernel, rows=BACKWARD_ROWS),
        grid=(pairs,),
        in_specs=[
            columns(0),
            columns(1),
            columns(2),
            pl.BlockSpec((length, length), lambda i: (0, 0)),
            columns(0),
            pl.BlockSpec((None, 2, length), lambda i: (i, 0, 0)),
            columns(0),
        ],
        out_specs=pl.BlockSpec((length, 3 * features), lambda i: (0, 0)),
        out_shape=jax.ShapeDtypeStruct((length, 3 * features), half),
        scratch_shapes=[pltpu.VMEM((length, PAIR), single)] * 2,
        compiler_params=pltpu.CompilerParams(vmem_limit_bytes=56 << 20),
        cost_estimate=estimate(40 * length * length * features, 16 * length * features),
        name="attend_backward",
    )(packed, packed, packed, bias, upstream, totals, attended)


def place_pieces(pieces, out_shape, targets, indices):
    def kernel(index_ref, *refs):
        sources, out_ref, semaphores = refs[: len(pieces)], refs[-2], refs[-1]
        copies = [
            pltpu.make_async_copy(
                source, out_ref.at[target(index_ref)], semaphores.at[number]
            )
            for number, (source, target) in enumerate(zip(sources, targets))
        ]
        for copy in copies:
            copy.start()
        for copy in copies:
            copy.wait()

    size = 2 * 2
    for extent in out_shape:
        size *= extent
    anywhere = pl.BlockSpec(memory_space=pl.ANY)
    return pl.pallas_call(
        kernel,
        in_specs=[pl.BlockSpec(memory_space=pltpu.SMEM)] + [anywhere] * len(pieces),
        out_specs=pl.BlockSpec(memory_space=pltpu.VMEM),
        out_shape=jax.ShapeDtypeStruct(out_shape, pieces[0].dtype),
        scratch_shapes=[pltpu.SemaphoreType.DMA((len(pieces),))],
        compiler_params=pltpu.CompilerParams(vmem_limit_bytes=32 << 20),
        cost_estimate=estimate(0, size),
        name="place_pieces",
    )(indices, *pieces)


def normal_of(hidden):
    center = hidden - jnp.mean(hidden, axis=-1, keepdims=True)
    inverse = lax.rsqrt(jnp.mean(center * center, axis=-1, keepdims=True) + epsilon)
    return center * inverse, inverse


def norm_pull(normal, inverse, gain, upstream):
    scaled = upstream * gain
    slope = jnp.mean(scaled, axis=-1, keepdims=True)
    tilt = jnp.mean(scaled * normal, axis=-1, keepdims=True)
    return inverse * (scaled - slope - normal * tilt)


def column_sum(array):
    return jnp.sum(array, axis=0, keepdims=True)


def tile_of(columns):
    return pl.BlockSpec((ROW_TILE, columns), lambda i: (i, 0))


def resident(shape, *index):
    place = index or (0,) * len(shape)
    return pl.BlockSpec(shape, lambda i: place, pipeline_mode=pl.Buffered(1))


def row_tiled(kernel, name, length, in_specs, out_specs, out_shape, operands, flops):
    size = sum(operand.size * operand.dtype.itemsize for operand in operands)
    size += sum(shape.size * jnp.dtype(shape.dtype).itemsize for shape in out_shape)
    return pl.pallas_call(
        kernel,
        grid=(length // ROW_TILE,),
        in_specs=in_specs,
        out_specs=out_specs,
        out_shape=out_shape,
        compiler_params=pltpu.CompilerParams(vmem_limit_bytes=56 << 20),
        cost_estimate=estimate(flops, size),
        name=name,
    )(*operands)


def project_kernel(hidden_ref, gains_ref, offsets_ref, weight_ref, normed_ref, packed_ref):
    features = hidden_ref.shape[1]
    normal, _ = normal_of(hidden_ref[...])
    normed = (normal * gains_ref[0:1] + offsets_ref[0:1]).astype(half)
    normed_ref[...] = normed
    for part in range(3):
        window = slice(part * features, (part + 1) * features)
        product = contract(normed, weight_ref[:, window], 1, 0)
        if part != 1:
            row = 1 if part == 0 else 2
            product = product + offsets_ref[row : row + 1]
        packed_ref[:, window] = product.astype(half)


def project(hidden, gains, offsets, joined):
    length, features = hidden.shape
    return row_tiled(
        project_kernel,
        "project",
        length,
        [
            tile_of(features),
            resident(gains.shape),
            resident(offsets.shape),
            resident((features, 3 * features)),
        ],
        [tile_of(features), tile_of(3 * features)],
        [
            jax.ShapeDtypeStruct((length, features), half),
            jax.ShapeDtypeStruct((length, 3 * features), half),
        ],
        (hidden, gains, offsets, joined),
        6 * length * features * features,
    )


def feed_kernel(
    attended_ref,
    hidden_ref,
    gains_ref,
    offsets_ref,
    up_bias_ref,
    out_weight_ref,
    up_ref,
    down_ref,
    middle_ref,
    second_ref,
    activated_ref,
    slope_ref,
    result_ref,
):
    hidden_units = up_ref.shape[1]
    middle = hidden_ref[...] + (
        contract(attended_ref[...], out_weight_ref[...], 1, 0) + offsets_ref[3:4]
    )
    middle_ref[...] = middle
    normal, _ = normal_of(middle)
    second = (normal * gains_ref[1:2] + offsets_ref[4:5]).astype(half)
    second_ref[...] = second
    result = middle + offsets_ref[5:6]
    rate = 0.7978845608028654
    for start in range(0, hidden_units, FF_CHUNK):
        window = slice(start, start + FF_CHUNK)
        value = contract(second, up_ref[:, window], 1, 0) + up_bias_ref[:, window]
        square = value * value
        bent = jnp.tanh(value * (rate + (rate * 0.044715) * square))
        opened = 0.5 + 0.5 * bent
        activated = (value * opened).astype(half)
        activated_ref[:, window] = activated
        curve = (value * (0.5 * rate + (1.5 * rate * 0.044715) * square)) * (1.0 - bent * bent)
        slope_ref[:, window] = (opened + curve).astype(half)
        result = result + contract(activated, down_ref[window, :], 1, 0)
    result_ref[...] = result.astype(result_ref.dtype)


def feed(attended, hidden, gains, offsets, up_bias, joined, up, down, result_type):
    length, features = hidden.shape
    units = down.shape[0]
    up_array, up_place = up
    shape = jax.ShapeDtypeStruct
    return row_tiled(
        feed_kernel,
        "feed",
        length,
        [
            tile_of(features),
            tile_of(features),
            resident(gains.shape),
            resident(offsets.shape),
            resident(up_bias.shape),
            resident((features, features), 0, 3),
            resident((features, units), 0, up_place),
            resident(down.shape),
        ],
        [tile_of(features), tile_of(features), tile_of(units), tile_of(units), tile_of(features)],
        [
            shape((length, features), single),
            shape((length, features), half),
            shape((length, units), half),
            shape((length, units), half),
            shape((length, features), result_type),
        ],
        (attended, hidden, gains, offsets, up_bias, joined, up_array, down),
        2 * length * features * (features + 2 * units),
    )


def feed_grad_kernel(
    gradient_ref,
    slope_ref,
    middle_ref,
    gains_ref,
    out_weight_ref,
    up_ref,
    down_ref,
    branch_ref,
    upper_ref,
    middle_grad_ref,
    attention_grad_ref,
    upstream_ref,
    sums_ref,
    unit_sums_ref,
):
    units = up_ref.shape[1]

    @pl.when(pl.program_id(0) == 0)
    def _():
        sums_ref[...] = jnp.zeros_like(sums_ref)
        unit_sums_ref[...] = jnp.zeros_like(unit_sums_ref)

    gradient = gradient_ref[...].astype(single)
    branch = gradient.astype(half)
    branch_ref[...] = branch
    sums_ref[0:1] += column_sum(branch.astype(single))
    second_grad = jnp.zeros(gradient.shape, single)
    for start in range(0, units, FF_CHUNK):
        window = slice(start, start + FF_CHUNK)
        pulled = contract(branch, down_ref[window, :], 1, 1) * slope_ref[:, window].astype(single)
        upper = pulled.astype(half)
        upper_ref[:, window] = upper
        unit_sums_ref[:, window] += column_sum(upper.astype(single))
        second_grad = second_grad + contract(upper, up_ref[:, window], 1, 1)
    normal, inverse = normal_of(middle_ref[...])
    middle_grad = gradient + norm_pull(normal, inverse, gains_ref[1:2], second_grad)
    sums_ref[1:2] += column_sum(second_grad * normal)
    sums_ref[2:3] += column_sum(second_grad)
    middle_grad_ref[...] = middle_grad
    attention_grad = middle_grad.astype(half)
    attention_grad_ref[...] = attention_grad
    sums_ref[3:4] += column_sum(attention_grad.astype(single))
    upstream_ref[...] = contract(attention_grad, out_weight_ref[...], 1, 1).astype(half)


def feed_grad(gradient, slope, middle, gains, joined, up, down):
    up_array, up_place = up
    length, features = middle.shape
    units = down.shape[0]
    shape = jax.ShapeDtypeStruct
    return row_tiled(
        feed_grad_kernel,
        "feed_grad",
        length,
        [
            tile_of(features),
            tile_of(units),
            tile_of(features),
            resident(gains.shape),
            resident((features, features), 0, 3),
            resident((features, units), 0, up_place),
            resident(down.shape),
        ],
        [
            tile_of(features),
            tile_of(units),
            tile_of(features),
            tile_of(features),
            tile_of(features),
            resident((8, features)),
            resident((1, units)),
        ],
        [
            shape((length, features), half),
            shape((length, units), half),
            shape((length, features), single),
            shape((length, features), half),
            shape((length, features), half),
            shape((8, features), single),
            shape((1, units), single),
        ],
        (gradient, slope, middle, gains, joined, up_array, down),
        2 * length * features * (features + 2 * units),
    )


def project_grad_kernel(
    packed_grad_ref, hidden_ref, middle_grad_ref, gains_ref, weight_ref, *out_refs
):
    sums_ref = out_refs[-1]
    features = hidden_ref.shape[1]

    @pl.when(pl.program_id(0) == 0)
    def _():
        sums_ref[...] = jnp.zeros_like(sums_ref)

    packed_grad = packed_grad_ref[...]
    normed_grad = contract(packed_grad, weight_ref[...], 1, 1)
    normal, inverse = normal_of(hidden_ref[...])
    result = middle_grad_ref[...] + norm_pull(normal, inverse, gains_ref[0:1], normed_grad)
    for result_ref in out_refs[:-1]:
        result_ref[...] = result.astype(result_ref.dtype)
    sums_ref[0:1] += column_sum(normed_grad * normal)
    sums_ref[1:2] += column_sum(normed_grad)
    sums_ref[2:3] += column_sum(packed_grad[:, :features].astype(single))
    sums_ref[3:4] += column_sum(packed_grad[:, 2 * features :].astype(single))


def project_grad(packed_grad, hidden, middle_grad, gains, joined, result_types):
    length, features = hidden.shape
    shape = jax.ShapeDtypeStruct
    return row_tiled(
        project_grad_kernel,
        "project_grad",
        length,
        [
            tile_of(3 * features),
            tile_of(features),
            tile_of(features),
            resident(gains.shape),
            resident((features, 3 * features)),
        ],
        [tile_of(features) for _ in result_types] + [resident((8, features))],
        [shape((length, features), result_type) for result_type in result_types]
        + [shape((8, features), single)],
        (packed_grad, hidden, middle_grad, gains, joined),
        6 * length * features * features,
    )


def term_blocks(terms, core, groups, row_unit, by_core):
    pieces = [left.shape[1] // (groups * row_unit) for left, _ in terms]
    widths = [right.shape[1] // (2 if by_core else 1) for _, right in terms]
    total = sum(count * width for count, width in zip(pieces, widths))
    chips = groups // 2
    out_shape = (chips, 2, row_unit, total) if by_core else (groups, row_unit, total)
    outputs = 2 if by_core else 1
    if row_unit % 16:
        columns = []
        for (left, right), count, width in zip(terms, pieces, widths):
            part = contract(left, right, 0, 0).astype(half)
            part = part.reshape(chips, 2, count, row_unit, -1, width).transpose(2, 1, 0, 4, 3, 5)
            columns += [part[piece] for piece in range(count)]
        whole = jnp.concatenate(columns, axis=-1)
        if not by_core:
            return [whole[:, :, 0].swapaxes(0, 1).reshape(out_shape)]
        return [
            lax.dynamic_index_in_dim(whole, which, 0, keepdims=False) for which in (1 - core, core)
        ]
    number = len(terms)

    def kernel(core_ref, *refs):
        sources = refs[: 2 * number]
        outs = refs[2 * number : 2 * number + outputs]
        buffers = refs[2 * number + outputs : 4 * number + outputs]
        semaphores = refs[4 * number + outputs]
        first_core = core_ref[0] == 0
        copies = [
            pltpu.make_async_copy(source, buffer, semaphores.at[index])
            for index, (source, buffer) in enumerate(zip(sources, buffers))
        ]
        for copy in copies:
            copy.start()
        start = 0
        for index, (count, width) in enumerate(zip(pieces, widths)):
            copies[2 * index].wait()
            copies[2 * index + 1].wait()
            left, right = buffers[2 * index], buffers[2 * index + 1]
            rows = groups * row_unit
            step = max(size for size in (768, 640, 512, 384, 256, 128) if width % size == 0)
            held = chips // count
            for turn in range(count):
                turned = left[:, turn * rows : (turn + 1) * rows].T
                some = slice(turn * held, (turn + 1) * held)
                for low in range(0, right.shape[1], step):
                    product = contract(turned, right[:, low : low + step], 1, 0).astype(half)
                    product = product.reshape(held, 2, count, row_unit, step)
                    side, inside = divmod(low, width)
                    for piece in range(count):
                        lanes = start + piece * width + inside
                        lanes = slice(lanes, lanes + step)
                        even, odd = product[:, 0, piece], product[:, 1, piece]
                        if by_core:
                            outs[0][some, side, :, lanes] = jnp.where(first_core, odd, even)
                            outs[1][some, side, :, lanes] = jnp.where(first_core, even, odd)
                        else:
                            for chip in range(held):
                                owner = 2 * (turn * held + chip)
                                outs[0][owner, :, lanes] = even[chip]
                                outs[0][owner + 1, :, lanes] = odd[chip]
            start += count * width

    anywhere = pl.BlockSpec(memory_space=pl.ANY)
    operands = [operand for term in terms for operand in term]
    size = sum(operand.size for operand in operands) * 2
    flops = sum(2 * left.size * right.shape[1] for left, right in terms)
    shape = jax.ShapeDtypeStruct(out_shape, half)
    return pl.pallas_call(
        kernel,
        in_specs=[pl.BlockSpec(memory_space=pltpu.SMEM)] + [anywhere] * len(operands),
        out_specs=[pl.BlockSpec(memory_space=pltpu.VMEM)] * outputs,
        out_shape=[shape] * outputs,
        scratch_shapes=[pltpu.VMEM(operand.shape, half) for operand in operands]
        + [pltpu.SemaphoreType.DMA((len(operands),))],
        compiler_params=pltpu.CompilerParams(vmem_limit_bytes=60 << 20),
        cost_estimate=estimate(flops, size + 2 * outputs * shape.size),
        name="term_blocks",
    )(core.reshape(1).astype(jnp.int32), *operands)


def per_device(
    tokens,
    time_embed,
    segment_ids,
    pad_mask,
    out_grad,
    qkv_weight,
    out_weight,
    up_weight,
    down_weight,
    norm_gains,
    bias_rows,
    up_bias,
):
    layers = qkv_weight.shape[0]
    features = tokens.shape[2]
    groups = lax.axis_size("wide")
    swap = [(0, 1), (1, 0)]

    def whole_sequence(part):
        return lax.all_to_all(part, "seq", split_axis=0, concat_axis=1, tiled=True)[0]

    core = lax.axis_index("wide") & 1
    place = lax.axis_index("seq")
    indices = jnp.stack([core, place]).astype(jnp.int32)
    row_unit = qkv_weight.shape[1]

    def across(bit):
        pairs = [(index, index ^ bit) for index in range(groups)]
        return lambda part: lax.ppermute(part, "wide", pairs)

    def beside_seq(part):
        return lax.ppermute(part, "seq", swap)

    def to_owners(part):
        return lax.psum_scatter(part, "wide", scatter_dimension=0, tiled=True)

    bit_of = lambda bit: (lax.axis_index("wide") >> (bit.bit_length() - 1)) & 1
    running = []

    def begin(steps, finish):
        entry = [steps, finish, next(steps), None]
        running.append(entry)
        return entry

    def launch(main, entries):
        fresh = [entry for entry in entries if entry in running and entry[3] is None]
        if fresh:
            sends = [[sent for sent, _ in entry[2]] for entry in fresh]
            main, sends = lax.optimization_barrier((main, sends))
            for entry, sent in zip(fresh, sends):
                entry[3] = [pass_on(part) for part, (_, pass_on) in zip(sent, entry[2])]
        return main

    def advance(main, *only):
        chosen = [entry for entry in only or list(running) if entry in running]
        main = launch(main, chosen)
        if not chosen:
            return main
        main, flying = lax.optimization_barrier((main, [entry[3] for entry in chosen]))
        for entry, arrived in zip(chosen, flying):
            entry[3] = None
            try:
                entry[2] = entry[0].send(arrived)
            except StopIteration as stop:
                entry[1](stop.value)
                running.remove(entry)
        return launch(main, chosen)

    def side_of(array, which, axis):
        return lax.dynamic_index_in_dim(array, which, axis, keepdims=False)

    chip_bits = [1 << number for number in range(groups.bit_length() - 2, 0, -1)]

    def join(current, received, which):
        lead = current.shape[0]
        joined = place_pieces(
            [current, received],
            (lead, 2) + current.shape[1:],
            [lambda ref: (slice(None), ref[0]), lambda ref: (slice(None), 1 - ref[0])],
            which.reshape(1).astype(jnp.int32),
        )
        return joined.reshape((2 * lead,) + current.shape[1:])

    def gather_columns(shard):
        rows, columns = shard.shape[0], shard.shape[1] // 2
        current = lax.dynamic_slice_in_dim(shard, place * columns, columns, axis=1)[None]
        for bit in chip_bits:
            (received,) = yield [(current, across(bit))]
            current = join(current, received, bit_of(bit))
        (aside,) = yield [(current, beside_seq)]
        passed = yield [(part, across(1)) for part in (current, aside)]

        def target(own_core, own_place):
            def where(ref):
                which_core = ref[0] if own_core else 1 - ref[0]
                which_place = ref[1] if own_place else 1 - ref[1]
                start = pl.multiple_of(which_place * columns, columns)
                return (slice(None), which_core, slice(None), pl.ds(start, columns))

            return where

        return place_pieces(
            [current, aside, *passed],
            (current.shape[0], 2, rows, 2 * columns),
            [target(True, True), target(True, False), target(False, True), target(False, False)],
            indices,
        ).reshape(-1, 2 * columns)

    def gather_rows(shard):
        rows, columns = shard.shape[0] // 2, shard.shape[1]
        current = side_of(shard.reshape(2, rows, columns), place, 0)[None]
        for bit in chip_bits[:-1]:
            (received,) = yield [(current, across(bit))]
            current = join(current, received, bit_of(bit))
        (received,) = yield [(current, beside_seq)]
        current = join(current, received, place).reshape(-1, 2 * rows, columns)
        for bit in chip_bits[-1:] + [1]:
            (received,) = yield [(current, across(bit))]
            current = join(current, received, bit_of(bit))
        return current.reshape(-1, columns)

    marks = whole_sequence(jnp.stack([segment_ids, pad_mask], axis=2))
    tokens, marks = lax.optimization_barrier((tokens, marks))
    my_tokens = whole_sequence(tokens)

    small = jnp.concatenate(
        [norm_gains.reshape(-1), bias_rows.reshape(-1), up_bias.reshape(-1)]
    )
    side = small.reshape(row_unit, -1)
    side_width = side.shape[1]
    side = jnp.pad(side, ((0, 0), (0, -side_width % PAIR)))
    joined_parts = [jnp.concatenate([qkv_weight[0], out_weight[0], side], axis=1)]
    for layer in range(1, layers):
        parts = [qkv_weight[layer], out_weight[layer], up_weight[layer]]
        joined_parts.append(jnp.concatenate(parts, axis=1))
    joined = [lax.all_gather(part, "wide", axis=0, tiled=True) for part in joined_parts]
    downs = {
        layer: lax.all_gather(down_weight[layer], "wide", axis=0, tiled=True)
        for layer in range(1, layers)
    }
    small_whole = joined[0][:, -side.shape[1] :][:, :side_width].reshape(groups, -1)
    cut_gains = norm_gains.size
    cut_rows = cut_gains + bias_rows.size

    def whole_rows(part, count):
        parts = part.reshape(groups, layers, count, -1)
        return parts.transpose(1, 2, 0, 3).reshape(layers, count, -1).astype(single)

    all_gains = whole_rows(small_whole[:, :cut_gains], norm_gains.shape[1])
    all_offsets = whole_rows(small_whole[:, cut_gains:cut_rows], bias_rows.shape[1])
    all_up_bias = whole_rows(small_whole[:, cut_rows:], 1)[:, 0]

    doc, pad = marks[:, 0], marks[:, 1]
    positions = jnp.arange(doc.shape[0])
    allowed = (doc[:, None] == doc[None, :]) & (
        (pad[:, None] == 1) | (positions[:, None] == positions[None, :])
    )
    bias = jnp.where(allowed, 0.0, masked_bias)

    matrices = [None] * layers
    ups = {}
    fetches = [
        begin(gather_columns(up_weight[0]), functools.partial(ups.__setitem__, 0)),
        begin(gather_rows(down_weight[0]), functools.partial(downs.__setitem__, 0)),
    ]
    for _ in chip_bits[1:]:
        time_embed = advance(time_embed, *fetches)
    my_time = lax.dynamic_index_in_dim(time_embed, place, 0, keepdims=True)
    hidden = my_tokens.astype(single) + my_time
    saved = []
    for layer in range(layers):
        whole = joined[layer]
        gains, offsets = all_gains[layer], all_offsets[layer]
        before = hidden
        normed, packed = project(hidden, gains, offsets, whole)
        if layer == layers - 1:
            packed, out_grad = lax.optimization_barrier((packed, out_grad))
            my_upstream = whole_sequence(out_grad)
        packed = advance(packed, *fetches)
        attended, totals = attend_forward(packed, bias)
        attended = advance(attended, *fetches)
        while running:
            attended = advance(attended, *fetches)
        up = (whole, 4 * features // up_bias.shape[1] // groups) if layer else (ups[0], 0)
        matrices[layer] = (whole, up, downs[layer])
        fetches = []
        middle, second, activated, slope, hidden = feed(
            attended,
            hidden,
            gains,
            offsets,
            all_up_bias[layer][None],
            whole,
            up,
            downs[layer],
            single if layer < layers - 1 else half,
        )
        saved.append((before, normed, packed, totals, attended, middle, second, activated, slope))

    def split_back(result):
        parts = result.reshape(2, -1, features).astype(half)
        return lax.all_to_all(parts, "seq", split_axis=0, concat_axis=0, tiled=True)

    output = split_back(hidden)

    def total_of(addends):
        return functools.reduce(jnp.add, [addend.astype(single) for addend in addends])

    def shares_of(terms, low, high):
        shares, start = [], 0
        for left, right in terms:
            rows, each = [], right.shape[1] // 2
            if high is None:
                each *= 2
            for _ in range(left.shape[1] // (groups * row_unit)):
                window = slice(start, start + each)
                if high is None:
                    rows.append(low[:, window])
                else:
                    rows.append(jnp.concatenate([low[:, window], high[:, window]], axis=1))
                start += each
            shares.append(jnp.concatenate(rows, axis=0))
        return shares

    def scatter_group(terms):
        (whole,) = term_blocks(terms, core, groups, row_unit, False)
        whole = whole.reshape(groups * row_unit, -1)
        (share,) = yield [(whole, to_owners)]
        (received,) = yield [(share, beside_seq)]
        return shares_of(terms, share.astype(single) + received.astype(single), None)

    def reduce_group(terms):
        other, own = term_blocks(terms, core, groups, row_unit, True)
        (received,) = yield [(other, across(1))]
        shape = (2,) * len(chip_bits) + (2, row_unit, own.shape[-1])
        addends = [part.reshape(shape) for part in (own, received)]
        axis = len(chip_bits)
        for bit in [0] + chip_bits[::-1]:
            mine, pass_on = (bit_of(bit), across(bit)) if bit else (place, beside_seq)
            sent = total_of([side_of(part, 1 - mine, axis) for part in addends]).astype(half)
            (received,) = yield [(sent, pass_on)]
            addends = [side_of(part, mine, axis) for part in addends] + [received]
            axis -= 1
        current = total_of(addends).astype(half)
        (received,) = yield [(current, beside_seq)]
        low = jnp.where(place == 0, current, received).astype(single)
        high = jnp.where(place == 0, received, current).astype(single)
        return shares_of(terms, low, high)

    def reduce_small(array):
        bit = 1
        while bit < groups:
            view = array.reshape(-1, 2, array.shape[-1])
            mine = bit_of(bit)
            sent = side_of(view, 1 - mine, 1)
            (received,) = yield [(sent, across(bit))]
            array = side_of(view, mine, 1) + received
            bit *= 2
        (received,) = yield [(array, beside_seq)]
        return (array + received)[0]

    weight_grads = [[None] * 4 for _ in range(layers)]

    def begin_group(steps, layer, named):
        def finish(shares):
            for (part, _), share in zip(named, shares):
                weight_grads[layer][part] = share

        return begin(steps([term for _, term in named]), finish)

    gradient = my_upstream
    small_grads = [None] * layers
    held = []
    for layer in range(layers - 1, -1, -1):
        whole, up, down = matrices[layer]
        gains = all_gains[layer]
        hidden, normed, packed, totals, attended, middle, second, activated, slope = saved[layer]
        steps = scatter_group if layer else reduce_group
        branch, upper, middle_grad, attention_grad, upstream, sums, unit_sums = feed_grad(
            gradient, slope, middle, gains, whole, up, down
        )
        named = [(2, (second, upper)), (1, (attended, attention_grad))]
        if layer:
            held.append(begin_group(steps, layer, [(3, (activated, branch))] + named))
            upstream = launch(upstream, held[-1:])
        else:
            upstream = advance(upstream, first_group)
            upper, attention_grad, upstream = lax.optimization_barrier(
                (upper, attention_grad, upstream)
            )
            named = [(2, (second, upper)), (1, (attended, attention_grad))]
            second_group = begin_group(steps, layer, named)
            upstream = launch(upstream, [second_group])
            upstream = advance(upstream, second_group)
        packed_grad = attend_backward(packed, bias, upstream, totals, attended)
        if layer == layers - 1:
            packed_grad, output = lax.optimization_barrier((packed_grad, output))
            output = output.astype(single)
        named = [(0, (normed, packed_grad))]
        if not layer:
            packed_grad = advance(packed_grad, first_group, second_group, *held[:1])
            last_group = begin_group(steps, layer, named)
            packed_grad = launch(packed_grad, [last_group])
            packed_grad = advance(packed_grad, first_group)
            packed_grad = advance(packed_grad, last_group)
        gradient, *rounded, more_sums = project_grad(
            packed_grad, hidden, middle_grad, gains, whole, (single, half) if layer else (half,)
        )
        if layer == 1:
            below = (saved[0][7], rounded[0])
            first_group = begin_group(reduce_group, 0, [(3, below)])
            gradient = launch(gradient, [first_group])
        if layer:
            held.append(begin_group(steps, layer, named))
            gradient = launch(gradient, held[-1:])
        if layer == 1:
            gradient = advance(gradient, first_group)
        if not layer:
            gradient = advance(gradient, last_group)
            gradient = advance(gradient, first_group, second_group, *held)
        small_grads[layer] = (
            jnp.stack([more_sums[0], sums[1]]),
            jnp.stack([more_sums[1], more_sums[2], more_sums[3], sums[3], sums[2], sums[0]]),
            unit_sums[0],
        )

    def by_owner(parts):
        stacked = jnp.stack(parts)
        stacked = stacked.reshape(layers, -1, groups, stacked.shape[-1] // groups)
        return stacked.transpose(2, 0, 1, 3).reshape(groups, -1)

    owned = jnp.concatenate(
        [by_owner([small_grads[layer][part] for layer in range(layers)]) for part in range(3)],
        axis=1,
    )
    small_result = []
    rest = begin(reduce_small(owned), small_result.append)
    gradient = launch(gradient, [rest])
    input_grad = split_back(gradient)
    while running:
        input_grad = advance(input_grad, last_group)
        input_grad = advance(input_grad, *[entry for entry in running if entry is not last_group])
    input_grad = input_grad.astype(single)
    owned = small_result[0]
    stacked = [
        jnp.stack([weight_grads[layer][part] for layer in range(layers)]) for part in range(4)
    ]
    return (
        output,
        input_grad,
        *stacked,
        owned[:cut_gains].reshape(norm_gains.shape),
        owned[cut_gains:cut_rows].reshape(bias_rows.shape),
        owned[cut_rows:].reshape(up_bias.shape),
    )


def solution(mesh):
    tokens_spec = P("wide", "seq", None)
    matrix_spec = P(None, "wide", None)
    rows_spec = P(None, None, "wide")
    return jax.shard_map(
        per_device,
        mesh=mesh,
        in_specs=(
            tokens_spec,
            P("wide", None),
            P("wide", "seq"),
            P("wide", "seq"),
            tokens_spec,
            matrix_spec,
            matrix_spec,
            matrix_spec,
            matrix_spec,
            rows_spec,
            rows_spec,
            P(None, "wide"),
        ),
        out_specs=(
            tokens_spec,
            tokens_spec,
            matrix_spec,
            matrix_spec,
            matrix_spec,
            matrix_spec,
            rows_spec,
            rows_spec,
            P(None, "wide"),
        ),
        check_vma=False,
    )
```

```python
import functools

import jax
import jax.numpy as jnp
from jax import lax
from jax.experimental import pallas as pl
from jax.experimental.pallas import tpu as pltpu
from jax.sharding import PartitionSpec as P

HEAD_SIZE = 64
PAIR = 2 * HEAD_SIZE
FORWARD_ROWS = 512
BACKWARD_ROWS = 256
ROW_TILE = 256
FF_CHUNK = 1024

epsilon = 1e-05
masked_bias = -1e30
half = jnp.bfloat16
single = jnp.float32


def estimate(flops, size):
    return pl.CostEstimate(flops=flops // 16, bytes_accessed=size // 16, transcendentals=0)


def contract(left, right, left_dim, right_dim):
    return lax.dot_general(
        left, right, (((left_dim,), (right_dim,)), ((), ())), preferred_element_type=jnp.float32
    )


def first_head_lanes():
    return lax.broadcasted_iota(jnp.int32, (1, PAIR), 1) < HEAD_SIZE


def one_head_of(pair, head):
    lanes = first_head_lanes()
    keep = lanes if head == 0 else jnp.logical_not(lanes)
    return jnp.where(keep, pair, jnp.zeros_like(pair))


def attend_kernel(query_ref, key_ref, value_ref, bias_ref, out_ref, total_ref, *, rows):
    keys = key_ref[...]
    values = value_ref[...]
    scale = jnp.asarray(HEAD_SIZE ** (-0.5), half)
    for start in range(0, keys.shape[0], rows):
        window = pl.ds(start, rows)
        queries = query_ref[window, :] * scale
        bias = bias_ref[:, window]
        attended = []
        for head in range(2):
            scores = contract(keys, one_head_of(queries, head), 1, 1) + bias
            top = jnp.max(scores, axis=0, keepdims=True)
            weights = jnp.exp(scores - top)
            total = jnp.sum(weights, axis=0, keepdims=True)
            mixed = contract(values, weights.astype(half), 0, 0) * (1.0 / total)
            attended.append(mixed[HEAD_SIZE * head : HEAD_SIZE * (head + 1)])
            total_ref[head : head + 1, window] = top + jnp.log(total)
        out_ref[window, :] = jnp.concatenate(attended, 0).T.astype(half)


def attend_forward(packed, bias):
    length = packed.shape[0]
    features = packed.shape[1] // 3
    pairs = features // PAIR
    columns = lambda part: pl.BlockSpec((length, PAIR), lambda i: (0, part * pairs + i))
    return pl.pallas_call(
        functools.partial(attend_kernel, rows=FORWARD_ROWS),
        grid=(pairs,),
        in_specs=[
            columns(0),
            columns(1),
            columns(2),
            pl.BlockSpec((length, length), lambda i: (0, 0)),
        ],
        out_specs=[columns(0), pl.BlockSpec((None, 2, length), lambda i: (i, 0, 0))],
        out_shape=[
            jax.ShapeDtypeStruct((length, features), half),
            jax.ShapeDtypeStruct((pairs, 2, length), single),
        ],
        compiler_params=pltpu.CompilerParams(vmem_limit_bytes=56 << 20),
        cost_estimate=estimate(16 * length * length * features, 8 * length * features),
        name="attend_forward",
    )(packed, packed, packed, bias)


def attend_grad_kernel(
    query_ref,
    key_ref,
    value_ref,
    bias_ref,
    upstream_ref,
    total_ref,
    attended_ref,
    out_ref,
    key_sum,
    value_sum,
    *,
    rows,
):
    pair = pl.program_id(0)
    features = out_ref.shape[1] // 3
    keys = key_ref[...]
    values = value_ref[...]
    scale = HEAD_SIZE ** (-0.5)
    for start in range(0, keys.shape[0], rows):
        window = pl.ds(start, rows)
        queries = query_ref[window, :] * jnp.asarray(scale, half)
        upstream = upstream_ref[window, :]
        product = (upstream.astype(single) * attended_ref[window, :].astype(single)).T
        bias = bias_ref[:, window]
        query_grads, key_grad, value_grad = [], 0.0, 0.0
        for head in range(2):
            head_queries = one_head_of(queries, head)
            head_upstream = one_head_of(upstream, head)
            inner = jnp.sum(
                product[HEAD_SIZE * head : HEAD_SIZE * (head + 1)], axis=0, keepdims=True
            )
            scores = contract(keys, head_queries, 1, 1) + bias
            weights = jnp.exp(scores - total_ref[head : head + 1, window])
            weight_grads = contract(values, head_upstream, 1, 1)
            score_grads = (weights * (weight_grads - inner)).astype(half)
            value_grad = value_grad + contract(weights.astype(half), head_upstream, 1, 0)
            key_grad = key_grad + contract(score_grads, head_queries, 1, 0)
            query_grads.append(
                contract(keys, score_grads, 0, 0)[HEAD_SIZE * head : HEAD_SIZE * (head + 1)]
            )
        out_ref[window, pl.ds(pl.multiple_of(pair * PAIR, PAIR), PAIR)] = (
            jnp.concatenate(query_grads, 0).T * scale
        ).astype(half)
        if start == 0:
            key_sum[...] = key_grad
            value_sum[...] = value_grad
        else:
            key_sum[...] += key_grad
            value_sum[...] += value_grad
    out_ref[:, pl.ds(pl.multiple_of(features + pair * PAIR, PAIR), PAIR)] = key_sum[...].astype(
        half
    )
    out_ref[:, pl.ds(pl.multiple_of(2 * features + pair * PAIR, PAIR), PAIR)] = value_sum[
        ...
    ].astype(half)


def attend_backward(packed, bias, upstream, totals, attended):
    length = packed.shape[0]
    features = packed.shape[1] // 3
    pairs = features // PAIR
    columns = lambda part: pl.BlockSpec((length, PAIR), lambda i: (0, part * pairs + i))
    return pl.pallas_call(
        functools.partial(attend_grad_kernel, rows=BACKWARD_ROWS),
        grid=(pairs,),
        in_specs=[
            columns(0),
            columns(1),
            columns(2),
            pl.BlockSpec((length, length), lambda i: (0, 0)),
            columns(0),
            pl.BlockSpec((None, 2, length), lambda i: (i, 0, 0)),
            columns(0),
        ],
        out_specs=pl.BlockSpec((length, 3 * features), lambda i: (0, 0)),
        out_shape=jax.ShapeDtypeStruct((length, 3 * features), half),
        scratch_shapes=[pltpu.VMEM((length, PAIR), single)] * 2,
        compiler_params=pltpu.CompilerParams(vmem_limit_bytes=56 << 20),
        cost_estimate=estimate(40 * length * length * features, 16 * length * features),
        name="attend_backward",
    )(packed, packed, packed, bias, upstream, totals, attended)


def place_pieces(pieces, out_shape, targets, indices):
    def kernel(index_ref, *refs):
        sources, out_ref, semaphores = refs[: len(pieces)], refs[-2], refs[-1]
        copies = [
            pltpu.make_async_copy(
                source, out_ref.at[target(index_ref)], semaphores.at[number]
            )
            for number, (source, target) in enumerate(zip(sources, targets))
        ]
        for copy in copies:
            copy.start()
        for copy in copies:
            copy.wait()

    size = 2 * 2
    for extent in out_shape:
        size *= extent
    anywhere = pl.BlockSpec(memory_space=pl.ANY)
    return pl.pallas_call(
        kernel,
        in_specs=[pl.BlockSpec(memory_space=pltpu.SMEM)] + [anywhere] * len(pieces),
        out_specs=pl.BlockSpec(memory_space=pltpu.VMEM),
        out_shape=jax.ShapeDtypeStruct(out_shape, pieces[0].dtype),
        scratch_shapes=[pltpu.SemaphoreType.DMA((len(pieces),))],
        compiler_params=pltpu.CompilerParams(vmem_limit_bytes=32 << 20),
        cost_estimate=estimate(0, size),
        name="place_pieces",
    )(indices, *pieces)


def normal_of(hidden):
    center = hidden - jnp.mean(hidden, axis=-1, keepdims=True)
    inverse = lax.rsqrt(jnp.mean(center * center, axis=-1, keepdims=True) + epsilon)
    return center * inverse, inverse


def norm_pull(normal, inverse, gain, upstream):
    scaled = upstream * gain
    slope = jnp.mean(scaled, axis=-1, keepdims=True)
    tilt = jnp.mean(scaled * normal, axis=-1, keepdims=True)
    return inverse * (scaled - slope - normal * tilt)


def column_sum(array):
    return jnp.sum(array, axis=0, keepdims=True)


def tile_of(columns):
    return pl.BlockSpec((ROW_TILE, columns), lambda i: (i, 0))


def resident(shape, *index):
    place = index or (0,) * len(shape)
    return pl.BlockSpec(shape, lambda i: place, pipeline_mode=pl.Buffered(1))


def row_tiled(kernel, name, length, in_specs, out_specs, out_shape, operands, flops):
    size = sum(operand.size * operand.dtype.itemsize for operand in operands)
    size += sum(shape.size * jnp.dtype(shape.dtype).itemsize for shape in out_shape)
    return pl.pallas_call(
        kernel,
        grid=(length // ROW_TILE,),
        in_specs=in_specs,
        out_specs=out_specs,
        out_shape=out_shape,
        compiler_params=pltpu.CompilerParams(vmem_limit_bytes=56 << 20),
        cost_estimate=estimate(flops, size),
        name=name,
    )(*operands)


def project_kernel(hidden_ref, gains_ref, offsets_ref, weight_ref, normed_ref, packed_ref):
    features = hidden_ref.shape[1]
    normal, _ = normal_of(hidden_ref[...])
    normed = (normal * gains_ref[0:1] + offsets_ref[0:1]).astype(half)
    normed_ref[...] = normed
    for part in range(3):
        window = slice(part * features, (part + 1) * features)
        product = contract(normed, weight_ref[:, window], 1, 0)
        if part != 1:
            row = 1 if part == 0 else 2
            product = product + offsets_ref[row : row + 1]
        packed_ref[:, window] = product.astype(half)


def project(hidden, gains, offsets, joined):
    length, features = hidden.shape
    return row_tiled(
        project_kernel,
        "project",
        length,
        [
            tile_of(features),
            resident(gains.shape),
            resident(offsets.shape),
            resident((features, 3 * features)),
        ],
        [tile_of(features), tile_of(3 * features)],
        [
            jax.ShapeDtypeStruct((length, features), half),
            jax.ShapeDtypeStruct((length, 3 * features), half),
        ],
        (hidden, gains, offsets, joined),
        6 * length * features * features,
    )


def feed_kernel(
    attended_ref,
    hidden_ref,
    gains_ref,
    offsets_ref,
    up_bias_ref,
    out_weight_ref,
    up_ref,
    down_ref,
    middle_ref,
    second_ref,
    activated_ref,
    slope_ref,
    result_ref,
):
    hidden_units = up_ref.shape[1]
    middle = hidden_ref[...] + (
        contract(attended_ref[...], out_weight_ref[...], 1, 0) + offsets_ref[3:4]
    )
    middle_ref[...] = middle
    normal, _ = normal_of(middle)
    second = (normal * gains_ref[1:2] + offsets_ref[4:5]).astype(half)
    second_ref[...] = second
    result = middle + offsets_ref[5:6]
    rate = 0.7978845608028654
    for start in range(0, hidden_units, FF_CHUNK):
        window = slice(start, start + FF_CHUNK)
        value = contract(second, up_ref[:, window], 1, 0) + up_bias_ref[:, window]
        square = value * value
        bent = jnp.tanh(value * (rate + (rate * 0.044715) * square))
        opened = 0.5 + 0.5 * bent
        activated = (value * opened).astype(half)
        activated_ref[:, window] = activated
        curve = (value * (0.5 * rate + (1.5 * rate * 0.044715) * square)) * (1.0 - bent * bent)
        slope_ref[:, window] = (opened + curve).astype(half)
        result = result + contract(activated, down_ref[window, :], 1, 0)
    result_ref[...] = result.astype(result_ref.dtype)


def feed(attended, hidden, gains, offsets, up_bias, joined, up, down, result_type):
    length, features = hidden.shape
    units = down.shape[0]
    up_array, up_place = up
    shape = jax.ShapeDtypeStruct
    return row_tiled(
        feed_kernel,
        "feed",
        length,
        [
            tile_of(features),
            tile_of(features),
            resident(gains.shape),
            resident(offsets.shape),
            resident(up_bias.shape),
            resident((features, features), 0, 3),
            resident((features, units), 0, up_place),
            resident(down.shape),
        ],
        [tile_of(features), tile_of(features), tile_of(units), tile_of(units), tile_of(features)],
        [
            shape((length, features), single),
            shape((length, features), half),
            shape((length, units), half),
            shape((length, units), half),
            shape((length, features), result_type),
        ],
        (attended, hidden, gains, offsets, up_bias, joined, up_array, down),
        2 * length * features * (features + 2 * units),
    )


def feed_grad_kernel(
    gradient_ref,
    slope_ref,
    middle_ref,
    gains_ref,
    out_weight_ref,
    up_ref,
    down_ref,
    branch_ref,
    upper_ref,
    middle_grad_ref,
    attention_grad_ref,
    upstream_ref,
    sums_ref,
    unit_sums_ref,
):
    units = up_ref.shape[1]

    @pl.when(pl.program_id(0) == 0)
    def _():
        sums_ref[...] = jnp.zeros_like(sums_ref)
        unit_sums_ref[...] = jnp.zeros_like(unit_sums_ref)

    gradient = gradient_ref[...].astype(single)
    branch = gradient.astype(half)
    branch_ref[...] = branch
    sums_ref[0:1] += column_sum(branch.astype(single))
    second_grad = jnp.zeros(gradient.shape, single)
    for start in range(0, units, FF_CHUNK):
        window = slice(start, start + FF_CHUNK)
        pulled = contract(branch, down_ref[window, :], 1, 1) * slope_ref[:, window].astype(single)
        upper = pulled.astype(half)
        upper_ref[:, window] = upper
        unit_sums_ref[:, window] += column_sum(upper.astype(single))
        second_grad = second_grad + contract(upper, up_ref[:, window], 1, 1)
    normal, inverse = normal_of(middle_ref[...])
    middle_grad = gradient + norm_pull(normal, inverse, gains_ref[1:2], second_grad)
    sums_ref[1:2] += column_sum(second_grad * normal)
    sums_ref[2:3] += column_sum(second_grad)
    middle_grad_ref[...] = middle_grad
    attention_grad = middle_grad.astype(half)
    attention_grad_ref[...] = attention_grad
    sums_ref[3:4] += column_sum(attention_grad.astype(single))
    upstream_ref[...] = contract(attention_grad, out_weight_ref[...], 1, 1).astype(half)


def feed_grad(gradient, slope, middle, gains, joined, up, down):
    up_array, up_place = up
    length, features = middle.shape
    units = down.shape[0]
    shape = jax.ShapeDtypeStruct
    return row_tiled(
        feed_grad_kernel,
        "feed_grad",
        length,
        [
            tile_of(features),
            tile_of(units),
            tile_of(features),
            resident(gains.shape),
            resident((features, features), 0, 3),
            resident((features, units), 0, up_place),
            resident(down.shape),
        ],
        [
            tile_of(features),
            tile_of(units),
            tile_of(features),
            tile_of(features),
            tile_of(features),
            resident((8, features)),
            resident((1, units)),
        ],
        [
            shape((length, features), half),
            shape((length, units), half),
            shape((length, features), single),
            shape((length, features), half),
            shape((length, features), half),
            shape((8, features), single),
            shape((1, units), single),
        ],
        (gradient, slope, middle, gains, joined, up_array, down),
        2 * length * features * (features + 2 * units),
    )


def project_grad_kernel(
    packed_grad_ref, hidden_ref, middle_grad_ref, gains_ref, weight_ref, *out_refs
):
    sums_ref = out_refs[-1]
    features = hidden_ref.shape[1]

    @pl.when(pl.program_id(0) == 0)
    def _():
        sums_ref[...] = jnp.zeros_like(sums_ref)

    packed_grad = packed_grad_ref[...]
    normed_grad = contract(packed_grad, weight_ref[...], 1, 1)
    normal, inverse = normal_of(hidden_ref[...])
    result = middle_grad_ref[...] + norm_pull(normal, inverse, gains_ref[0:1], normed_grad)
    for result_ref in out_refs[:-1]:
        result_ref[...] = result.astype(result_ref.dtype)
    sums_ref[0:1] += column_sum(normed_grad * normal)
    sums_ref[1:2] += column_sum(normed_grad)
    sums_ref[2:3] += column_sum(packed_grad[:, :features].astype(single))
    sums_ref[3:4] += column_sum(packed_grad[:, 2 * features :].astype(single))


def project_grad(packed_grad, hidden, middle_grad, gains, joined, result_types):
    length, features = hidden.shape
    shape = jax.ShapeDtypeStruct
    return row_tiled(
        project_grad_kernel,
        "project_grad",
        length,
        [
            tile_of(3 * features),
            tile_of(features),
            tile_of(features),
            resident(gains.shape),
            resident((features, 3 * features)),
        ],
        [tile_of(features) for _ in result_types] + [resident((8, features))],
        [shape((length, features), result_type) for result_type in result_types]
        + [shape((8, features), single)],
        (packed_grad, hidden, middle_grad, gains, joined),
        6 * length * features * features,
    )


def term_blocks(terms, core, groups, row_unit, by_core):
    pieces = [left.shape[1] // (groups * row_unit) for left, _ in terms]
    widths = [right.shape[1] // (2 if by_core else 1) for _, right in terms]
    total = sum(count * width for count, width in zip(pieces, widths))
    chips = groups // 2
    out_shape = (chips, 2, row_unit, total) if by_core else (groups, row_unit, total)
    outputs = 2 if by_core else 1
    if row_unit % 16:
        columns = []
        for (left, right), count, width in zip(terms, pieces, widths):
            part = contract(left, right, 0, 0).astype(half)
            part = part.reshape(chips, 2, count, row_unit, -1, width).transpose(2, 1, 0, 4, 3, 5)
            columns += [part[piece] for piece in range(count)]
        whole = jnp.concatenate(columns, axis=-1)
        if not by_core:
            return [whole[:, :, 0].swapaxes(0, 1).reshape(out_shape)]
        return [
            lax.dynamic_index_in_dim(whole, which, 0, keepdims=False) for which in (1 - core, core)
        ]
    number = len(terms)

    def kernel(core_ref, *refs):
        sources = refs[: 2 * number]
        outs = refs[2 * number : 2 * number + outputs]
        buffers = refs[2 * number + outputs : 4 * number + outputs]
        semaphores = refs[4 * number + outputs]
        first_core = core_ref[0] == 0
        copies = [
            pltpu.make_async_copy(source, buffer, semaphores.at[index])
            for index, (source, buffer) in enumerate(zip(sources, buffers))
        ]
        for copy in copies:
            copy.start()
        start = 0
        for index, (count, width) in enumerate(zip(pieces, widths)):
            copies[2 * index].wait()
            copies[2 * index + 1].wait()
            left, right = buffers[2 * index], buffers[2 * index + 1]
            rows = groups * row_unit
            step = max(size for size in (768, 640, 512, 384, 256, 128) if width % size == 0)
            held = chips // count
            for turn in range(count):
                turned = left[:, turn * rows : (turn + 1) * rows].T
                some = slice(turn * held, (turn + 1) * held)
                for low in range(0, right.shape[1], step):
                    product = contract(turned, right[:, low : low + step], 1, 0).astype(half)
                    product = product.reshape(held, 2, count, row_unit, step)
                    side, inside = divmod(low, width)
                    for piece in range(count):
                        lanes = start + piece * width + inside
                        lanes = slice(lanes, lanes + step)
                        even, odd = product[:, 0, piece], product[:, 1, piece]
                        if by_core:
                            outs[0][some, side, :, lanes] = jnp.where(first_core, odd, even)
                            outs[1][some, side, :, lanes] = jnp.where(first_core, even, odd)
                        else:
                            for chip in range(held):
                                owner = 2 * (turn * held + chip)
                                outs[0][owner, :, lanes] = even[chip]
                                outs[0][owner + 1, :, lanes] = odd[chip]
            start += count * width

    anywhere = pl.BlockSpec(memory_space=pl.ANY)
    operands = [operand for term in terms for operand in term]
    size = sum(operand.size for operand in operands) * 2
    flops = sum(2 * left.size * right.shape[1] for left, right in terms)
    shape = jax.ShapeDtypeStruct(out_shape, half)
    return pl.pallas_call(
        kernel,
        in_specs=[pl.BlockSpec(memory_space=pltpu.SMEM)] + [anywhere] * len(operands),
        out_specs=[pl.BlockSpec(memory_space=pltpu.VMEM)] * outputs,
        out_shape=[shape] * outputs,
        scratch_shapes=[pltpu.VMEM(operand.shape, half) for operand in operands]
        + [pltpu.SemaphoreType.DMA((len(operands),))],
        compiler_params=pltpu.CompilerParams(vmem_limit_bytes=60 << 20),
        cost_estimate=estimate(flops, size + 2 * outputs * shape.size),
        name="term_blocks",
    )(core.reshape(1).astype(jnp.int32), *operands)


def per_device(
    tokens,
    time_embed,
    segment_ids,
    pad_mask,
    out_grad,
    qkv_weight,
    out_weight,
    up_weight,
    down_weight,
    norm_gains,
    bias_rows,
    up_bias,
):
    layers = qkv_weight.shape[0]
    features = tokens.shape[2]
    groups = lax.axis_size("wide")
    swap = [(0, 1), (1, 0)]

    def whole_sequence(part):
        return lax.all_to_all(part, "seq", split_axis=0, concat_axis=1, tiled=True)[0]

    core = lax.axis_index("wide") & 1
    place = lax.axis_index("seq")
    indices = jnp.stack([core, place]).astype(jnp.int32)
    row_unit = qkv_weight.shape[1]

    def across(bit):
        pairs = [(index, index ^ bit) for index in range(groups)]
        return lambda part: lax.ppermute(part, "wide", pairs)

    def beside_seq(part):
        return lax.ppermute(part, "seq", swap)

    def to_owners(part):
        return lax.psum_scatter(part, "wide", scatter_dimension=0, tiled=True)

    bit_of = lambda bit: (lax.axis_index("wide") >> (bit.bit_length() - 1)) & 1
    running = []

    def begin(steps, finish):
        entry = [steps, finish, next(steps), None]
        running.append(entry)
        return entry

    def launch(main, entries):
        fresh = [entry for entry in entries if entry in running and entry[3] is None]
        if fresh:
            sends = [[sent for sent, _ in entry[2]] for entry in fresh]
            main, sends = lax.optimization_barrier((main, sends))
            for entry, sent in zip(fresh, sends):
                entry[3] = [pass_on(part) for part, (_, pass_on) in zip(sent, entry[2])]
        return main

    def advance(main, *only):
        chosen = [entry for entry in only or list(running) if entry in running]
        main = launch(main, chosen)
        if not chosen:
            return main
        main, flying = lax.optimization_barrier((main, [entry[3] for entry in chosen]))
        for entry, arrived in zip(chosen, flying):
            entry[3] = None
            try:
                entry[2] = entry[0].send(arrived)
            except StopIteration as stop:
                entry[1](stop.value)
                running.remove(entry)
        return launch(main, chosen)

    def side_of(array, which, axis):
        return lax.dynamic_index_in_dim(array, which, axis, keepdims=False)

    chip_bits = [1 << number for number in range(groups.bit_length() - 2, 0, -1)]

    def join(current, received, which):
        lead = current.shape[0]
        joined = place_pieces(
            [current, received],
            (lead, 2) + current.shape[1:],
            [lambda ref: (slice(None), ref[0]), lambda ref: (slice(None), 1 - ref[0])],
            which.reshape(1).astype(jnp.int32),
        )
        return joined.reshape((2 * lead,) + current.shape[1:])

    def gather_columns(shard):
        rows, columns = shard.shape[0], shard.shape[1] // 2
        current = lax.dynamic_slice_in_dim(shard, place * columns, columns, axis=1)[None]
        for bit in chip_bits:
            (received,) = yield [(current, across(bit))]
            current = join(current, received, bit_of(bit))
        (aside,) = yield [(current, beside_seq)]
        passed = yield [(part, across(1)) for part in (current, aside)]

        def target(own_core, own_place):
            def where(ref):
                which_core = ref[0] if own_core else 1 - ref[0]
                which_place = ref[1] if own_place else 1 - ref[1]
                start = pl.multiple_of(which_place * columns, columns)
                return (slice(None), which_core, slice(None), pl.ds(start, columns))

            return where

        return place_pieces(
            [current, aside, *passed],
            (current.shape[0], 2, rows, 2 * columns),
            [target(True, True), target(True, False), target(False, True), target(False, False)],
            indices,
        ).reshape(-1, 2 * columns)

    def gather_rows(shard):
        rows, columns = shard.shape[0] // 2, shard.shape[1]
        current = side_of(shard.reshape(2, rows, columns), place, 0)[None]
        for bit in chip_bits[:-1]:
            (received,) = yield [(current, across(bit))]
            current = join(current, received, bit_of(bit))
        (received,) = yield [(current, beside_seq)]
        current = join(current, received, place).reshape(-1, 2 * rows, columns)
        for bit in chip_bits[-1:] + [1]:
            (received,) = yield [(current, across(bit))]
            current = join(current, received, bit_of(bit))
        return current.reshape(-1, columns)

    marks = whole_sequence(jnp.stack([segment_ids, pad_mask], axis=2))
    tokens, marks = lax.optimization_barrier((tokens, marks))
    my_tokens = whole_sequence(tokens)

    small = jnp.concatenate(
        [norm_gains.reshape(-1), bias_rows.reshape(-1), up_bias.reshape(-1)]
    )
    side = small.reshape(row_unit, -1)
    side_width = side.shape[1]
    side = jnp.pad(side, ((0, 0), (0, -side_width % PAIR)))
    joined_parts = [jnp.concatenate([qkv_weight[0], out_weight[0], side], axis=1)]
    for layer in range(1, layers):
        parts = [qkv_weight[layer], out_weight[layer], up_weight[layer]]
        joined_parts.append(jnp.concatenate(parts, axis=1))
    joined = [lax.all_gather(part, "wide", axis=0, tiled=True) for part in joined_parts]
    downs = {
        layer: lax.all_gather(down_weight[layer], "wide", axis=0, tiled=True)
        for layer in range(1, layers)
    }
    small_whole = joined[0][:, -side.shape[1] :][:, :side_width].reshape(groups, -1)
    cut_gains = norm_gains.size
    cut_rows = cut_gains + bias_rows.size

    def whole_rows(part, count):
        parts = part.reshape(groups, layers, count, -1)
        return parts.transpose(1, 2, 0, 3).reshape(layers, count, -1).astype(single)

    all_gains = whole_rows(small_whole[:, :cut_gains], norm_gains.shape[1])
    all_offsets = whole_rows(small_whole[:, cut_gains:cut_rows], bias_rows.shape[1])
    all_up_bias = whole_rows(small_whole[:, cut_rows:], 1)[:, 0]

    doc, pad = marks[:, 0], marks[:, 1]
    positions = jnp.arange(doc.shape[0])
    allowed = (doc[:, None] == doc[None, :]) & (
        (pad[:, None] == 1) | (positions[:, None] == positions[None, :])
    )
    bias = jnp.where(allowed, 0.0, masked_bias)

    matrices = [None] * layers
    ups = {}
    fetches = [
        begin(gather_columns(up_weight[0]), functools.partial(ups.__setitem__, 0)),
        begin(gather_rows(down_weight[0]), functools.partial(downs.__setitem__, 0)),
    ]
    for _ in chip_bits[1:]:
        time_embed = advance(time_embed, *fetches)
    my_time = lax.dynamic_index_in_dim(time_embed, place, 0, keepdims=True)
    hidden = my_tokens.astype(single) + my_time
    saved = []
    for layer in range(layers):
        whole = joined[layer]
        gains, offsets = all_gains[layer], all_offsets[layer]
        before = hidden
        normed, packed = project(hidden, gains, offsets, whole)
        if layer == layers - 1:
            packed, out_grad = lax.optimization_barrier((packed, out_grad))
            my_upstream = whole_sequence(out_grad)
        packed = advance(packed, *fetches)
        attended, totals = attend_forward(packed, bias)
        attended = advance(attended, *fetches)
        while running:
            attended = advance(attended, *fetches)
        up = (whole, 4 * features // up_bias.shape[1] // groups) if layer else (ups[0], 0)
        matrices[layer] = (whole, up, downs[layer])
        fetches = []
        middle, second, activated, slope, hidden = feed(
            attended,
            hidden,
            gains,
            offsets,
            all_up_bias[layer][None],
            whole,
            up,
            downs[layer],
            single if layer < layers - 1 else half,
        )
        saved.append((before, normed, packed, totals, attended, middle, second, activated, slope))

    def split_back(result):
        parts = result.reshape(2, -1, features).astype(half)
        return lax.all_to_all(parts, "seq", split_axis=0, concat_axis=0, tiled=True)

    output = split_back(hidden)

    def total_of(addends):
        return functools.reduce(jnp.add, [addend.astype(single) for addend in addends])

    def shares_of(terms, low, high):
        shares, start = [], 0
        for left, right in terms:
            rows, each = [], right.shape[1] // 2
            if high is None:
                each *= 2
            for _ in range(left.shape[1] // (groups * row_unit)):
                window = slice(start, start + each)
                if high is None:
                    rows.append(low[:, window])
                else:
                    rows.append(jnp.concatenate([low[:, window], high[:, window]], axis=1))
                start += each
            shares.append(jnp.concatenate(rows, axis=0))
        return shares

    def scatter_group(terms):
        (whole,) = term_blocks(terms, core, groups, row_unit, False)
        whole = whole.reshape(groups * row_unit, -1)
        (share,) = yield [(whole, to_owners)]
        (received,) = yield [(share, beside_seq)]
        return shares_of(terms, share.astype(single) + received.astype(single), None)

    def reduce_group(terms):
        other, own = term_blocks(terms, core, groups, row_unit, True)
        (received,) = yield [(other, across(1))]
        shape = (2,) * len(chip_bits) + (2, row_unit, own.shape[-1])
        addends = [part.reshape(shape) for part in (own, received)]
        axis = len(chip_bits)
        for bit in [0] + chip_bits[:1:-1]:
            mine, pass_on = (bit_of(bit), across(bit)) if bit else (place, beside_seq)
            sent = total_of([side_of(part, 1 - mine, axis) for part in addends]).astype(half)
            (received,) = yield [(sent, pass_on)]
            addends = [side_of(part, mine, axis) for part in addends] + [received]
            axis -= 1
        far, near = chip_bits[:2]

        def corner(part, bits):
            part = side_of(part, bit_of(far) ^ (1 if bits & far else 0), 0)
            return side_of(part, bit_of(near) ^ (1 if bits & near else 0), 0)

        received = yield [
            (total_of([corner(part, bits) for part in addends]).astype(half), across(bits))
            for bits in (near, far, near | far)
        ]
        addends = [corner(part, 0) for part in addends] + received
        current = total_of(addends).astype(half)
        (received,) = yield [(current, beside_seq)]
        low = jnp.where(place == 0, current, received).astype(single)
        high = jnp.where(place == 0, received, current).astype(single)
        return shares_of(terms, low, high)

    weight_grads = [[None] * 4 for _ in range(layers)]

    def begin_group(steps, layer, named):
        def finish(shares):
            for (part, _), share in zip(named, shares):
                weight_grads[layer][part] = share

        return begin(steps([term for _, term in named]), finish)

    gradient = my_upstream
    small_grads = [None] * layers
    held = []
    for layer in range(layers - 1, -1, -1):
        whole, up, down = matrices[layer]
        gains = all_gains[layer]
        hidden, normed, packed, totals, attended, middle, second, activated, slope = saved[layer]
        steps = scatter_group if layer else reduce_group
        branch, upper, middle_grad, attention_grad, upstream, sums, unit_sums = feed_grad(
            gradient, slope, middle, gains, whole, up, down
        )
        named = [(2, (second, upper)), (1, (attended, attention_grad))]
        if layer:
            held.append(begin_group(steps, layer, [(3, (activated, branch))] + named))
            upstream = launch(upstream, held[-1:])
        else:
            upstream = advance(upstream, first_group)
            upper, attention_grad, upstream = lax.optimization_barrier(
                (upper, attention_grad, upstream)
            )
            named = [(2, (second, upper)), (1, (attended, attention_grad))]
            second_group = begin_group(steps, layer, named)
            upstream = launch(upstream, [second_group])
            upstream = advance(upstream, second_group)
            upstream = advance(upstream, *held[:1])
        packed_grad = attend_backward(packed, bias, upstream, totals, attended)
        if layer == layers - 1:
            packed_grad, output = lax.optimization_barrier((packed_grad, output))
            output = output.astype(single)
        named = [(0, (normed, packed_grad))]
        if not layer:
            packed_grad = advance(packed_grad, first_group, second_group, *held[:1])
            last_group = begin_group(steps, layer, named)
            packed_grad = launch(packed_grad, [last_group])
            packed_grad = advance(packed_grad, last_group)
        gradient, *rounded, more_sums = project_grad(
            packed_grad, hidden, middle_grad, gains, whole, (single, half) if layer else (half,)
        )
        if layer == 1:
            below = (saved[0][7], rounded[0])
            first_group = begin_group(reduce_group, 0, [(3, below)])
            gradient = launch(gradient, [first_group])
        if layer:
            held.append(begin_group(steps, layer, named))
            gradient = launch(gradient, held[-1:])
        if layer == 1:
            gradient = advance(gradient, first_group)
        if not layer:
            gradient = advance(gradient, last_group)
            gradient = advance(gradient, first_group, second_group, *held)
        small_grads[layer] = (
            jnp.stack([more_sums[0], sums[1]]),
            jnp.stack([more_sums[1], more_sums[2], more_sums[3], sums[3], sums[2], sums[0]]),
            unit_sums[0],
        )

    def by_owner(parts):
        stacked = jnp.stack(parts)
        stacked = stacked.reshape(layers, -1, groups, stacked.shape[-1] // groups)
        return stacked.transpose(2, 0, 1, 3).reshape(groups, -1)

    owned = jnp.concatenate(
        [by_owner([small_grads[layer][part] for layer in range(layers)]) for part in range(3)],
        axis=1,
    )
    owned, result = lax.optimization_barrier((owned, gradient))
    totals = lax.psum(owned, ("wide", "seq"))
    input_grad = split_back(result)
    while running:
        output = advance(output, last_group)
        output = advance(output, *[entry for entry in running if entry is not last_group])
    output, totals = lax.optimization_barrier((output, totals))
    owned = lax.dynamic_index_in_dim(totals, lax.axis_index("wide"), 0, keepdims=False)
    input_grad = input_grad.astype(single)
    stacked = [
        jnp.stack([weight_grads[layer][part] for layer in range(layers)]) for part in range(4)
    ]
    return (
        output,
        input_grad,
        *stacked,
        owned[:cut_gains].reshape(norm_gains.shape),
        owned[cut_gains:cut_rows].reshape(bias_rows.shape),
        owned[cut_rows:].reshape(up_bias.shape),
    )


def solution(mesh):
    tokens_spec = P("wide", "seq", None)
    matrix_spec = P(None, "wide", None)
    rows_spec = P(None, None, "wide")
    return jax.shard_map(
        per_device,
        mesh=mesh,
        in_specs=(
            tokens_spec,
            P("wide", None),
            P("wide", "seq"),
            P("wide", "seq"),
            tokens_spec,
            matrix_spec,
            matrix_spec,
            matrix_spec,
            matrix_spec,
            rows_spec,
            rows_spec,
            P(None, "wide"),
        ),
        out_specs=(
            tokens_spec,
            tokens_spec,
            matrix_spec,
            matrix_spec,
            matrix_spec,
            matrix_spec,
            rows_spec,
            rows_spec,
            P(None, "wide"),
        ),
        check_vma=False,
    )
```

```python
import functools

import jax
import jax.numpy as jnp
from jax import lax
from jax.experimental import pallas as pl
from jax.experimental.pallas import tpu as pltpu
from jax.sharding import PartitionSpec as P

HEAD_SIZE = 64
PAIR = 2 * HEAD_SIZE
FORWARD_ROWS = 512
BACKWARD_ROWS = 256
ROW_TILE = 256
FF_CHUNK = 1024

epsilon = 1e-05
masked_bias = -1e30
half = jnp.bfloat16
single = jnp.float32


def estimate(flops, size):
    return pl.CostEstimate(flops=flops // 16, bytes_accessed=size // 16, transcendentals=0)


def contract(left, right, left_dim, right_dim):
    return lax.dot_general(
        left, right, (((left_dim,), (right_dim,)), ((), ())), preferred_element_type=jnp.float32
    )


def first_head_lanes():
    return lax.broadcasted_iota(jnp.int32, (1, PAIR), 1) < HEAD_SIZE


def one_head_of(pair, head):
    lanes = first_head_lanes()
    keep = lanes if head == 0 else jnp.logical_not(lanes)
    return jnp.where(keep, pair, jnp.zeros_like(pair))


def attend_kernel(query_ref, key_ref, value_ref, bias_ref, out_ref, total_ref, *, rows):
    keys = key_ref[...]
    values = value_ref[...]
    scale = jnp.asarray(HEAD_SIZE ** (-0.5), half)
    for start in range(0, keys.shape[0], rows):
        window = pl.ds(start, rows)
        queries = query_ref[window, :] * scale
        bias = bias_ref[:, window]
        attended = []
        for head in range(2):
            scores = contract(keys, one_head_of(queries, head), 1, 1) + bias
            top = jnp.max(scores, axis=0, keepdims=True)
            weights = jnp.exp(scores - top)
            total = jnp.sum(weights, axis=0, keepdims=True)
            mixed = contract(values, weights.astype(half), 0, 0) * (1.0 / total)
            attended.append(mixed[HEAD_SIZE * head : HEAD_SIZE * (head + 1)])
            total_ref[head : head + 1, window] = top + jnp.log(total)
        out_ref[window, :] = jnp.concatenate(attended, 0).T.astype(half)


def attend_forward(packed, bias):
    length = packed.shape[0]
    features = packed.shape[1] // 3
    pairs = features // PAIR
    columns = lambda part: pl.BlockSpec((length, PAIR), lambda i: (0, part * pairs + i))
    return pl.pallas_call(
        functools.partial(attend_kernel, rows=FORWARD_ROWS),
        grid=(pairs,),
        in_specs=[
            columns(0),
            columns(1),
            columns(2),
            pl.BlockSpec((length, length), lambda i: (0, 0)),
        ],
        out_specs=[columns(0), pl.BlockSpec((None, 2, length), lambda i: (i, 0, 0))],
        out_shape=[
            jax.ShapeDtypeStruct((length, features), half),
            jax.ShapeDtypeStruct((pairs, 2, length), single),
        ],
        compiler_params=pltpu.CompilerParams(vmem_limit_bytes=56 << 20),
        cost_estimate=estimate(16 * length * length * features, 8 * length * features),
        name="attend_forward",
    )(packed, packed, packed, bias)


def attend_grad_kernel(
    query_ref,
    key_ref,
    value_ref,
    bias_ref,
    upstream_ref,
    total_ref,
    attended_ref,
    out_ref,
    key_sum,
    value_sum,
    *,
    rows,
):
    pair = pl.program_id(0)
    features = out_ref.shape[1] // 3
    keys = key_ref[...]
    values = value_ref[...]
    scale = HEAD_SIZE ** (-0.5)
    for start in range(0, keys.shape[0], rows):
        window = pl.ds(start, rows)
        queries = query_ref[window, :] * jnp.asarray(scale, half)
        upstream = upstream_ref[window, :]
        product = (upstream.astype(single) * attended_ref[window, :].astype(single)).T
        bias = bias_ref[:, window]
        query_grads, key_grad, value_grad = [], 0.0, 0.0
        for head in range(2):
            head_queries = one_head_of(queries, head)
            head_upstream = one_head_of(upstream, head)
            inner = jnp.sum(
                product[HEAD_SIZE * head : HEAD_SIZE * (head + 1)], axis=0, keepdims=True
            )
            scores = contract(keys, head_queries, 1, 1) + bias
            weights = jnp.exp(scores - total_ref[head : head + 1, window])
            weight_grads = contract(values, head_upstream, 1, 1)
            score_grads = (weights * (weight_grads - inner)).astype(half)
            value_grad = value_grad + contract(weights.astype(half), head_upstream, 1, 0)
            key_grad = key_grad + contract(score_grads, head_queries, 1, 0)
            query_grads.append(
                contract(keys, score_grads, 0, 0)[HEAD_SIZE * head : HEAD_SIZE * (head + 1)]
            )
        out_ref[window, pl.ds(pl.multiple_of(pair * PAIR, PAIR), PAIR)] = (
            jnp.concatenate(query_grads, 0).T * scale
        ).astype(half)
        if start == 0:
            key_sum[...] = key_grad
            value_sum[...] = value_grad
        else:
            key_sum[...] += key_grad
            value_sum[...] += value_grad
    out_ref[:, pl.ds(pl.multiple_of(features + pair * PAIR, PAIR), PAIR)] = key_sum[...].astype(
        half
    )
    out_ref[:, pl.ds(pl.multiple_of(2 * features + pair * PAIR, PAIR), PAIR)] = value_sum[
        ...
    ].astype(half)


def attend_backward(packed, bias, upstream, totals, attended):
    length = packed.shape[0]
    features = packed.shape[1] // 3
    pairs = features // PAIR
    columns = lambda part: pl.BlockSpec((length, PAIR), lambda i: (0, part * pairs + i))
    return pl.pallas_call(
        functools.partial(attend_grad_kernel, rows=BACKWARD_ROWS),
        grid=(pairs,),
        in_specs=[
            columns(0),
            columns(1),
            columns(2),
            pl.BlockSpec((length, length), lambda i: (0, 0)),
            columns(0),
            pl.BlockSpec((None, 2, length), lambda i: (i, 0, 0)),
            columns(0),
        ],
        out_specs=pl.BlockSpec((length, 3 * features), lambda i: (0, 0)),
        out_shape=jax.ShapeDtypeStruct((length, 3 * features), half),
        scratch_shapes=[pltpu.VMEM((length, PAIR), single)] * 2,
        compiler_params=pltpu.CompilerParams(vmem_limit_bytes=56 << 20),
        cost_estimate=estimate(40 * length * length * features, 16 * length * features),
        name="attend_backward",
    )(packed, packed, packed, bias, upstream, totals, attended)


def place_pieces(pieces, out_shape, targets, indices):
    def kernel(index_ref, *refs):
        sources, out_ref, semaphores = refs[: len(pieces)], refs[-2], refs[-1]
        copies = [
            pltpu.make_async_copy(
                source, out_ref.at[target(index_ref)], semaphores.at[number]
            )
            for number, (source, target) in enumerate(zip(sources, targets))
        ]
        for copy in copies:
            copy.start()
        for copy in copies:
            copy.wait()

    size = 2 * 2
    for extent in out_shape:
        size *= extent
    anywhere = pl.BlockSpec(memory_space=pl.ANY)
    return pl.pallas_call(
        kernel,
        in_specs=[pl.BlockSpec(memory_space=pltpu.SMEM)] + [anywhere] * len(pieces),
        out_specs=pl.BlockSpec(memory_space=pltpu.VMEM),
        out_shape=jax.ShapeDtypeStruct(out_shape, pieces[0].dtype),
        scratch_shapes=[pltpu.SemaphoreType.DMA((len(pieces),))],
        compiler_params=pltpu.CompilerParams(vmem_limit_bytes=32 << 20),
        cost_estimate=estimate(0, size),
        name="place_pieces",
    )(indices, *pieces)


def normal_of(hidden):
    center = hidden - jnp.mean(hidden, axis=-1, keepdims=True)
    inverse = lax.rsqrt(jnp.mean(center * center, axis=-1, keepdims=True) + epsilon)
    return center * inverse, inverse


def norm_pull(normal, inverse, gain, upstream):
    scaled = upstream * gain
    slope = jnp.mean(scaled, axis=-1, keepdims=True)
    tilt = jnp.mean(scaled * normal, axis=-1, keepdims=True)
    return inverse * (scaled - slope - normal * tilt)


def column_sum(array):
    return jnp.sum(array, axis=0, keepdims=True)


def tile_of(columns):
    return pl.BlockSpec((ROW_TILE, columns), lambda i: (i, 0))


def resident(shape, *index):
    place = index or (0,) * len(shape)
    return pl.BlockSpec(shape, lambda i: place, pipeline_mode=pl.Buffered(1))


def row_tiled(kernel, name, length, in_specs, out_specs, out_shape, operands, flops):
    size = sum(operand.size * operand.dtype.itemsize for operand in operands)
    size += sum(shape.size * jnp.dtype(shape.dtype).itemsize for shape in out_shape)
    return pl.pallas_call(
        kernel,
        grid=(length // ROW_TILE,),
        in_specs=in_specs,
        out_specs=out_specs,
        out_shape=out_shape,
        compiler_params=pltpu.CompilerParams(vmem_limit_bytes=56 << 20),
        cost_estimate=estimate(flops, size),
        name=name,
    )(*operands)


def project_kernel(hidden_ref, gains_ref, offsets_ref, weight_ref, normed_ref, packed_ref):
    features = hidden_ref.shape[1]
    normal, _ = normal_of(hidden_ref[...])
    normed = (normal * gains_ref[0:1] + offsets_ref[0:1]).astype(half)
    normed_ref[...] = normed
    for part in range(3):
        window = slice(part * features, (part + 1) * features)
        product = contract(normed, weight_ref[:, window], 1, 0)
        if part != 1:
            row = 1 if part == 0 else 2
            product = product + offsets_ref[row : row + 1]
        packed_ref[:, window] = product.astype(half)


def project(hidden, gains, offsets, joined):
    length, features = hidden.shape
    return row_tiled(
        project_kernel,
        "project",
        length,
        [
            tile_of(features),
            resident(gains.shape),
            resident(offsets.shape),
            resident((features, 3 * features)),
        ],
        [tile_of(features), tile_of(3 * features)],
        [
            jax.ShapeDtypeStruct((length, features), half),
            jax.ShapeDtypeStruct((length, 3 * features), half),
        ],
        (hidden, gains, offsets, joined),
        6 * length * features * features,
    )


def feed_kernel(
    attended_ref,
    hidden_ref,
    gains_ref,
    offsets_ref,
    up_bias_ref,
    out_weight_ref,
    up_ref,
    down_ref,
    middle_ref,
    second_ref,
    activated_ref,
    slope_ref,
    result_ref,
):
    hidden_units = up_ref.shape[1]
    middle = hidden_ref[...] + (
        contract(attended_ref[...], out_weight_ref[...], 1, 0) + offsets_ref[3:4]
    )
    middle_ref[...] = middle
    normal, _ = normal_of(middle)
    second = (normal * gains_ref[1:2] + offsets_ref[4:5]).astype(half)
    second_ref[...] = second
    result = middle + offsets_ref[5:6]
    rate = 0.7978845608028654
    for start in range(0, hidden_units, FF_CHUNK):
        window = slice(start, start + FF_CHUNK)
        value = contract(second, up_ref[:, window], 1, 0) + up_bias_ref[:, window]
        square = value * value
        bent = jnp.tanh(value * (rate + (rate * 0.044715) * square))
        opened = 0.5 + 0.5 * bent
        activated = (value * opened).astype(half)
        activated_ref[:, window] = activated
        curve = (value * (0.5 * rate + (1.5 * rate * 0.044715) * square)) * (1.0 - bent * bent)
        slope_ref[:, window] = (opened + curve).astype(half)
        result = result + contract(activated, down_ref[window, :], 1, 0)
    result_ref[...] = result.astype(result_ref.dtype)


def feed(attended, hidden, gains, offsets, up_bias, joined, up, down, result_type):
    length, features = hidden.shape
    units = down.shape[0]
    up_array, up_place = up
    shape = jax.ShapeDtypeStruct
    return row_tiled(
        feed_kernel,
        "feed",
        length,
        [
            tile_of(features),
            tile_of(features),
            resident(gains.shape),
            resident(offsets.shape),
            resident(up_bias.shape),
            resident((features, features), 0, 3),
            resident((features, units), 0, up_place),
            resident(down.shape),
        ],
        [tile_of(features), tile_of(features), tile_of(units), tile_of(units), tile_of(features)],
        [
            shape((length, features), single),
            shape((length, features), half),
            shape((length, units), half),
            shape((length, units), half),
            shape((length, features), result_type),
        ],
        (attended, hidden, gains, offsets, up_bias, joined, up_array, down),
        2 * length * features * (features + 2 * units),
    )


def feed_grad_kernel(
    gradient_ref,
    slope_ref,
    middle_ref,
    gains_ref,
    out_weight_ref,
    up_ref,
    down_ref,
    branch_ref,
    upper_ref,
    middle_grad_ref,
    attention_grad_ref,
    upstream_ref,
    sums_ref,
    unit_sums_ref,
):
    units = up_ref.shape[1]

    @pl.when(pl.program_id(0) == 0)
    def _():
        sums_ref[...] = jnp.zeros_like(sums_ref)
        unit_sums_ref[...] = jnp.zeros_like(unit_sums_ref)

    gradient = gradient_ref[...].astype(single)
    branch = gradient.astype(half)
    branch_ref[...] = branch
    sums_ref[0:1] += column_sum(branch.astype(single))
    second_grad = jnp.zeros(gradient.shape, single)
    for start in range(0, units, FF_CHUNK):
        window = slice(start, start + FF_CHUNK)
        pulled = contract(branch, down_ref[window, :], 1, 1) * slope_ref[:, window].astype(single)
        upper = pulled.astype(half)
        upper_ref[:, window] = upper
        unit_sums_ref[:, window] += column_sum(upper.astype(single))
        second_grad = second_grad + contract(upper, up_ref[:, window], 1, 1)
    normal, inverse = normal_of(middle_ref[...])
    middle_grad = gradient + norm_pull(normal, inverse, gains_ref[1:2], second_grad)
    sums_ref[1:2] += column_sum(second_grad * normal)
    sums_ref[2:3] += column_sum(second_grad)
    middle_grad_ref[...] = middle_grad
    attention_grad = middle_grad.astype(half)
    attention_grad_ref[...] = attention_grad
    sums_ref[3:4] += column_sum(attention_grad.astype(single))
    upstream_ref[...] = contract(attention_grad, out_weight_ref[...], 1, 1).astype(half)


def feed_grad(gradient, slope, middle, gains, joined, up, down):
    up_array, up_place = up
    length, features = middle.shape
    units = down.shape[0]
    shape = jax.ShapeDtypeStruct
    return row_tiled(
        feed_grad_kernel,
        "feed_grad",
        length,
        [
            tile_of(features),
            tile_of(units),
            tile_of(features),
            resident(gains.shape),
            resident((features, features), 0, 3),
            resident((features, units), 0, up_place),
            resident(down.shape),
        ],
        [
            tile_of(features),
            tile_of(units),
            tile_of(features),
            tile_of(features),
            tile_of(features),
            resident((8, features)),
            resident((1, units)),
        ],
        [
            shape((length, features), half),
            shape((length, units), half),
            shape((length, features), single),
            shape((length, features), half),
            shape((length, features), half),
            shape((8, features), single),
            shape((1, units), single),
        ],
        (gradient, slope, middle, gains, joined, up_array, down),
        2 * length * features * (features + 2 * units),
    )


def project_grad_kernel(
    packed_grad_ref, hidden_ref, middle_grad_ref, gains_ref, weight_ref, *out_refs
):
    sums_ref = out_refs[-1]
    features = hidden_ref.shape[1]

    @pl.when(pl.program_id(0) == 0)
    def _():
        sums_ref[...] = jnp.zeros_like(sums_ref)

    packed_grad = packed_grad_ref[...]
    normed_grad = contract(packed_grad, weight_ref[...], 1, 1)
    normal, inverse = normal_of(hidden_ref[...])
    result = middle_grad_ref[...] + norm_pull(normal, inverse, gains_ref[0:1], normed_grad)
    for result_ref in out_refs[:-1]:
        result_ref[...] = result.astype(result_ref.dtype)
    sums_ref[0:1] += column_sum(normed_grad * normal)
    sums_ref[1:2] += column_sum(normed_grad)
    sums_ref[2:3] += column_sum(packed_grad[:, :features].astype(single))
    sums_ref[3:4] += column_sum(packed_grad[:, 2 * features :].astype(single))


def project_grad(packed_grad, hidden, middle_grad, gains, joined, result_types):
    length, features = hidden.shape
    shape = jax.ShapeDtypeStruct
    return row_tiled(
        project_grad_kernel,
        "project_grad",
        length,
        [
            tile_of(3 * features),
            tile_of(features),
            tile_of(features),
            resident(gains.shape),
            resident((features, 3 * features)),
        ],
        [tile_of(features) for _ in result_types] + [resident((8, features))],
        [shape((length, features), result_type) for result_type in result_types]
        + [shape((8, features), single)],
        (packed_grad, hidden, middle_grad, gains, joined),
        6 * length * features * features,
    )


def term_blocks(terms, core, groups, row_unit, by_core):
    pieces = [left.shape[1] // (groups * row_unit) for left, _ in terms]
    widths = [right.shape[1] // (2 if by_core else 1) for _, right in terms]
    total = sum(count * width for count, width in zip(pieces, widths))
    chips = groups // 2
    out_shape = (chips, 2, row_unit, total) if by_core else (groups, row_unit, total)
    outputs = 2 if by_core else 1
    if row_unit % 16:
        columns = []
        for (left, right), count, width in zip(terms, pieces, widths):
            part = contract(left, right, 0, 0).astype(half)
            part = part.reshape(chips, 2, count, row_unit, -1, width).transpose(2, 1, 0, 4, 3, 5)
            columns += [part[piece] for piece in range(count)]
        whole = jnp.concatenate(columns, axis=-1)
        if not by_core:
            return [whole[:, :, 0].swapaxes(0, 1).reshape(out_shape)]
        return [
            lax.dynamic_index_in_dim(whole, which, 0, keepdims=False) for which in (1 - core, core)
        ]
    number = len(terms)

    def kernel(core_ref, *refs):
        sources = refs[: 2 * number]
        outs = refs[2 * number : 2 * number + outputs]
        buffers = refs[2 * number + outputs : 4 * number + outputs]
        semaphores = refs[4 * number + outputs]
        first_core = core_ref[0] == 0
        copies = [
            pltpu.make_async_copy(source, buffer, semaphores.at[index])
            for index, (source, buffer) in enumerate(zip(sources, buffers))
        ]
        for copy in copies:
            copy.start()
        start = 0
        for index, (count, width) in enumerate(zip(pieces, widths)):
            copies[2 * index].wait()
            copies[2 * index + 1].wait()
            left, right = buffers[2 * index], buffers[2 * index + 1]
            rows = groups * row_unit
            step = max(size for size in (768, 640, 512, 384, 256, 128) if width % size == 0)
            held = chips // count
            for turn in range(count):
                turned = left[:, turn * rows : (turn + 1) * rows].T
                some = slice(turn * held, (turn + 1) * held)
                for low in range(0, right.shape[1], step):
                    product = contract(turned, right[:, low : low + step], 1, 0).astype(half)
                    product = product.reshape(held, 2, count, row_unit, step)
                    side, inside = divmod(low, width)
                    for piece in range(count):
                        lanes = start + piece * width + inside
                        lanes = slice(lanes, lanes + step)
                        even, odd = product[:, 0, piece], product[:, 1, piece]
                        if by_core:
                            outs[0][some, side, :, lanes] = jnp.where(first_core, odd, even)
                            outs[1][some, side, :, lanes] = jnp.where(first_core, even, odd)
                        else:
                            for chip in range(held):
                                owner = 2 * (turn * held + chip)
                                outs[0][owner, :, lanes] = even[chip]
                                outs[0][owner + 1, :, lanes] = odd[chip]
            start += count * width

    anywhere = pl.BlockSpec(memory_space=pl.ANY)
    operands = [operand for term in terms for operand in term]
    size = sum(operand.size for operand in operands) * 2
    flops = sum(2 * left.size * right.shape[1] for left, right in terms)
    shape = jax.ShapeDtypeStruct(out_shape, half)
    return pl.pallas_call(
        kernel,
        in_specs=[pl.BlockSpec(memory_space=pltpu.SMEM)] + [anywhere] * len(operands),
        out_specs=[pl.BlockSpec(memory_space=pltpu.VMEM)] * outputs,
        out_shape=[shape] * outputs,
        scratch_shapes=[pltpu.VMEM(operand.shape, half) for operand in operands]
        + [pltpu.SemaphoreType.DMA((len(operands),))],
        compiler_params=pltpu.CompilerParams(vmem_limit_bytes=60 << 20),
        cost_estimate=estimate(flops, size + 2 * outputs * shape.size),
        name="term_blocks",
    )(core.reshape(1).astype(jnp.int32), *operands)


def per_device(
    tokens,
    time_embed,
    segment_ids,
    pad_mask,
    out_grad,
    qkv_weight,
    out_weight,
    up_weight,
    down_weight,
    norm_gains,
    bias_rows,
    up_bias,
):
    layers = qkv_weight.shape[0]
    features = tokens.shape[2]
    groups = lax.axis_size("wide")
    swap = [(0, 1), (1, 0)]

    def whole_sequence(part):
        return lax.all_to_all(part, "seq", split_axis=0, concat_axis=1, tiled=True)[0]

    core = lax.axis_index("wide") & 1
    place = lax.axis_index("seq")
    indices = jnp.stack([core, place]).astype(jnp.int32)
    row_unit = qkv_weight.shape[1]

    def across(bit):
        pairs = [(index, index ^ bit) for index in range(groups)]
        return lambda part: lax.ppermute(part, "wide", pairs)

    def beside_seq(part):
        return lax.ppermute(part, "seq", swap)

    def to_owners(part):
        return lax.psum_scatter(part, "wide", scatter_dimension=0, tiled=True)

    bit_of = lambda bit: (lax.axis_index("wide") >> (bit.bit_length() - 1)) & 1
    running = []

    def begin(steps, finish):
        entry = [steps, finish, next(steps), None]
        running.append(entry)
        return entry

    def launch(main, entries):
        fresh = [entry for entry in entries if entry in running and entry[3] is None]
        if fresh:
            sends = [[sent for sent, _ in entry[2]] for entry in fresh]
            main, sends = lax.optimization_barrier((main, sends))
            for entry, sent in zip(fresh, sends):
                entry[3] = [pass_on(part) for part, (_, pass_on) in zip(sent, entry[2])]
        return main

    def advance(main, *only):
        chosen = [entry for entry in only or list(running) if entry in running]
        main = launch(main, chosen)
        if not chosen:
            return main
        main, flying = lax.optimization_barrier((main, [entry[3] for entry in chosen]))
        for entry, arrived in zip(chosen, flying):
            entry[3] = None
            try:
                entry[2] = entry[0].send(arrived)
            except StopIteration as stop:
                entry[1](stop.value)
                running.remove(entry)
        return launch(main, chosen)

    def side_of(array, which, axis):
        return lax.dynamic_index_in_dim(array, which, axis, keepdims=False)

    chip_bits = [1 << number for number in range(groups.bit_length() - 2, 0, -1)]

    def join(current, received, which):
        lead = current.shape[0]
        joined = place_pieces(
            [current, received],
            (lead, 2) + current.shape[1:],
            [lambda ref: (slice(None), ref[0]), lambda ref: (slice(None), 1 - ref[0])],
            which.reshape(1).astype(jnp.int32),
        )
        return joined.reshape((2 * lead,) + current.shape[1:])

    def gather_columns(shard):
        rows, columns = shard.shape[0], shard.shape[1] // 2
        current = lax.dynamic_slice_in_dim(shard, place * columns, columns, axis=1)[None]
        for bit in chip_bits:
            (received,) = yield [(current, across(bit))]
            current = join(current, received, bit_of(bit))
        (aside,) = yield [(current, beside_seq)]
        passed = yield [(part, across(1)) for part in (current, aside)]

        def target(own_core, own_place):
            def where(ref):
                which_core = ref[0] if own_core else 1 - ref[0]
                which_place = ref[1] if own_place else 1 - ref[1]
                start = pl.multiple_of(which_place * columns, columns)
                return (slice(None), which_core, slice(None), pl.ds(start, columns))

            return where

        return place_pieces(
            [current, aside, *passed],
            (current.shape[0], 2, rows, 2 * columns),
            [target(True, True), target(True, False), target(False, True), target(False, False)],
            indices,
        ).reshape(-1, 2 * columns)

    def gather_rows(shard):
        rows, columns = shard.shape[0] // 2, shard.shape[1]
        current = side_of(shard.reshape(2, rows, columns), place, 0)[None]
        for bit in chip_bits[:-1]:
            (received,) = yield [(current, across(bit))]
            current = join(current, received, bit_of(bit))
        (received,) = yield [(current, beside_seq)]
        current = join(current, received, place).reshape(-1, 2 * rows, columns)
        for bit in chip_bits[-1:] + [1]:
            (received,) = yield [(current, across(bit))]
            current = join(current, received, bit_of(bit))
        return current.reshape(-1, columns)

    my_tokens = whole_sequence(tokens)

    small = jnp.concatenate(
        [norm_gains.reshape(-1), bias_rows.reshape(-1), up_bias.reshape(-1)]
    )
    side = small.reshape(row_unit, -1)
    side_width = side.shape[1]
    side = jnp.pad(side, ((0, 0), (0, -side_width % PAIR)))
    joined_parts = [jnp.concatenate([qkv_weight[0], out_weight[0], side], axis=1)]
    for layer in range(1, layers):
        parts = [qkv_weight[layer], out_weight[layer], up_weight[layer]]
        joined_parts.append(jnp.concatenate(parts, axis=1))
    joined = [lax.all_gather(part, "wide", axis=0, tiled=True) for part in joined_parts]
    downs = {
        layer: lax.all_gather(down_weight[layer], "wide", axis=0, tiled=True)
        for layer in range(1, layers)
    }
    small_whole = joined[0][:, -side.shape[1] :][:, :side_width].reshape(groups, -1)
    cut_gains = norm_gains.size
    cut_rows = cut_gains + bias_rows.size

    def whole_rows(part, count):
        parts = part.reshape(groups, layers, count, -1)
        return parts.transpose(1, 2, 0, 3).reshape(layers, count, -1).astype(single)

    all_gains = whole_rows(small_whole[:, :cut_gains], norm_gains.shape[1])
    all_offsets = whole_rows(small_whole[:, cut_gains:cut_rows], bias_rows.shape[1])
    all_up_bias = whole_rows(small_whole[:, cut_rows:], 1)[:, 0]

    matrices = [None] * layers
    ups = {}
    fetches = [
        begin(gather_columns(up_weight[0]), functools.partial(ups.__setitem__, 0)),
        begin(gather_rows(down_weight[0]), functools.partial(downs.__setitem__, 0)),
    ]
    marks = jnp.stack([segment_ids, pad_mask], axis=2)
    for _ in chip_bits[1:]:
        time_embed, marks = advance((time_embed, marks), *fetches)
    marks = whole_sequence(marks)
    doc, pad = marks[:, 0], marks[:, 1]
    positions = jnp.arange(doc.shape[0])
    allowed = (doc[:, None] == doc[None, :]) & (
        (pad[:, None] == 1) | (positions[:, None] == positions[None, :])
    )
    bias = jnp.where(allowed, 0.0, masked_bias)

    my_time = lax.dynamic_index_in_dim(time_embed, place, 0, keepdims=True)
    hidden = my_tokens.astype(single) + my_time
    saved = []
    for layer in range(layers):
        whole = joined[layer]
        gains, offsets = all_gains[layer], all_offsets[layer]
        before = hidden
        normed, packed = project(hidden, gains, offsets, whole)
        if layer == layers - 1:
            packed, out_grad = lax.optimization_barrier((packed, out_grad))
            my_upstream = whole_sequence(out_grad)
        packed = advance(packed, *fetches)
        attended, totals = attend_forward(packed, bias)
        attended = advance(attended, *fetches)
        while running:
            attended = advance(attended, *fetches)
        up = (whole, 4 * features // up_bias.shape[1] // groups) if layer else (ups[0], 0)
        matrices[layer] = (whole, up, downs[layer])
        fetches = []
        middle, second, activated, slope, hidden = feed(
            attended,
            hidden,
            gains,
            offsets,
            all_up_bias[layer][None],
            whole,
            up,
            downs[layer],
            single if layer < layers - 1 else half,
        )
        saved.append((before, normed, packed, totals, attended, middle, second, activated, slope))

    def split_back(result):
        parts = result.reshape(2, -1, features).astype(half)
        return lax.all_to_all(parts, "seq", split_axis=0, concat_axis=0, tiled=True)

    output = split_back(hidden)

    def total_of(addends):
        return functools.reduce(jnp.add, [addend.astype(single) for addend in addends])

    def shares_of(terms, low, high):
        shares, start = [], 0
        for left, right in terms:
            rows, each = [], right.shape[1] // 2
            if high is None:
                each *= 2
            for _ in range(left.shape[1] // (groups * row_unit)):
                window = slice(start, start + each)
                if high is None:
                    rows.append(low[:, window])
                else:
                    rows.append(jnp.concatenate([low[:, window], high[:, window]], axis=1))
                start += each
            shares.append(jnp.concatenate(rows, axis=0))
        return shares

    def scatter_group(terms):
        (whole,) = term_blocks(terms, core, groups, row_unit, False)
        whole = whole.reshape(groups * row_unit, -1)
        (share,) = yield [(whole, to_owners)]
        (received,) = yield [(share, beside_seq)]
        return shares_of(terms, share.astype(single) + received.astype(single), None)

    def reduce_group(terms):
        other, own = term_blocks(terms, core, groups, row_unit, True)
        (received,) = yield [(other, across(1))]
        shape = (2,) * len(chip_bits) + (2, row_unit, own.shape[-1])
        addends = [part.reshape(shape) for part in (own, received)]
        axis = len(chip_bits)
        for bit in [0] + chip_bits[:1:-1]:
            mine, pass_on = (bit_of(bit), across(bit)) if bit else (place, beside_seq)
            sent = total_of([side_of(part, 1 - mine, axis) for part in addends]).astype(half)
            (received,) = yield [(sent, pass_on)]
            addends = [side_of(part, mine, axis) for part in addends] + [received]
            axis -= 1
        far, near = chip_bits[:2]

        def corner(part, bits):
            part = side_of(part, bit_of(far) ^ (1 if bits & far else 0), 0)
            return side_of(part, bit_of(near) ^ (1 if bits & near else 0), 0)

        received = yield [
            (total_of([corner(part, bits) for part in addends]).astype(half), across(bits))
            for bits in (near, far, near | far)
        ]
        addends = [corner(part, 0) for part in addends] + received
        current = total_of(addends).astype(half)
        (received,) = yield [(current, beside_seq)]
        low = jnp.where(place == 0, current, received).astype(single)
        high = jnp.where(place == 0, received, current).astype(single)
        return shares_of(terms, low, high)

    def reduce_small(array):
        parts = [array.reshape((2,) * (len(chip_bits) + 1) + array.shape[1:])]
        pairs = [(2, 1, len(chip_bits) - 1)]
        pairs += [(bit, None, chip_bits.index(bit)) for bit in chip_bits[-2:1:-1]]
        pairs += [(chip_bits[0], chip_bits[1], 0)]
        for high, low, axis in pairs:

            def chosen(bits):
                def pick(part):
                    if low is not None:
                        part = side_of(part, bit_of(low) ^ (1 if bits & low else 0), axis + 1)
                    return side_of(part, bit_of(high) ^ (1 if bits & high else 0), axis)

                return total_of([pick(part) for part in parts])

            masks = [high] if low is None else [low, high, low | high]
            received = yield [(chosen(bits), across(bits)) for bits in masks]
            parts = [chosen(0)] + received
        current = total_of(parts)
        (received,) = yield [(current, beside_seq)]
        return current + received

    weight_grads = [[None] * 4 for _ in range(layers)]

    def begin_group(steps, layer, named):
        def finish(shares):
            for (part, _), share in zip(named, shares):
                weight_grads[layer][part] = share

        return begin(steps([term for _, term in named]), finish)

    gradient = my_upstream
    small_grads = [None] * layers
    held = []
    for layer in range(layers - 1, -1, -1):
        whole, up, down = matrices[layer]
        gains = all_gains[layer]
        hidden, normed, packed, totals, attended, middle, second, activated, slope = saved[layer]
        steps = scatter_group if layer else reduce_group
        branch, upper, middle_grad, attention_grad, upstream, sums, unit_sums = feed_grad(
            gradient, slope, middle, gains, whole, up, down
        )
        named = [(2, (second, upper)), (1, (attended, attention_grad))]
        if layer:
            held.append(begin_group(steps, layer, [(3, (activated, branch))] + named))
            upstream = launch(upstream, held[-1:])
        else:
            upstream = advance(upstream, first_group)
            upper, attention_grad, upstream = lax.optimization_barrier(
                (upper, attention_grad, upstream)
            )
            named = [(2, (second, upper)), (1, (attended, attention_grad))]
            second_group = begin_group(steps, layer, named)
            upstream = launch(upstream, [second_group])
            upstream = advance(upstream, second_group)
            upstream = advance(upstream, *held[:1])
        packed_grad = attend_backward(packed, bias, upstream, totals, attended)
        if layer == layers - 1:
            packed_grad, output = lax.optimization_barrier((packed_grad, output))
            output = output.astype(single)
        named = [(0, (normed, packed_grad))]
        if not layer:
            packed_grad = advance(packed_grad, first_group, second_group, *held[:1])
            last_group = begin_group(steps, layer, named)
            packed_grad = launch(packed_grad, [last_group])
            packed_grad = advance(packed_grad, last_group)
        gradient, *rounded, more_sums = project_grad(
            packed_grad, hidden, middle_grad, gains, whole, (single, half) if layer else (half,)
        )
        if layer == 1:
            below = (saved[0][7], rounded[0])
            first_group = begin_group(reduce_group, 0, [(3, below)])
            gradient = launch(gradient, [first_group])
        if layer:
            held.append(begin_group(steps, layer, named))
            gradient = launch(gradient, held[-1:])
        if layer == 1:
            gradient = advance(gradient, first_group)
        if not layer:
            gradient = advance(gradient, last_group)
        small_grads[layer] = (
            jnp.stack([more_sums[0], sums[1]]),
            jnp.stack([more_sums[1], more_sums[2], more_sums[3], sums[3], sums[2], sums[0]]),
            unit_sums[0],
        )

    def by_owner(parts):
        stacked = jnp.stack(parts)
        stacked = stacked.reshape(layers, -1, groups, stacked.shape[-1] // groups)
        return stacked.transpose(2, 0, 1, 3).reshape(groups, -1)

    owned = jnp.concatenate(
        [by_owner([small_grads[layer][part] for layer in range(layers)]) for part in range(3)],
        axis=1,
    )
    small_result = []
    begin(reduce_small(owned), small_result.append)
    output = launch(output, running[-1:])
    output = advance(output, first_group, second_group, *held)
    input_grad = split_back(gradient)
    while running:
        output = advance(output, last_group)
        output = advance(output, *[entry for entry in running if entry is not last_group])
    owned = small_result[0]
    input_grad = input_grad.astype(single)
    stacked = [
        jnp.stack([weight_grads[layer][part] for layer in range(layers)]) for part in range(4)
    ]
    return (
        output,
        input_grad,
        *stacked,
        owned[:cut_gains].reshape(norm_gains.shape),
        owned[cut_gains:cut_rows].reshape(bias_rows.shape),
        owned[cut_rows:].reshape(up_bias.shape),
    )


def solution(mesh):
    tokens_spec = P("wide", "seq", None)
    matrix_spec = P(None, "wide", None)
    rows_spec = P(None, None, "wide")
    return jax.shard_map(
        per_device,
        mesh=mesh,
        in_specs=(
            tokens_spec,
            P("wide", None),
            P("wide", "seq"),
            P("wide", "seq"),
            tokens_spec,
            matrix_spec,
            matrix_spec,
            matrix_spec,
            matrix_spec,
            rows_spec,
            rows_spec,
            P(None, "wide"),
        ),
        out_specs=(
            tokens_spec,
            tokens_spec,
            matrix_spec,
            matrix_spec,
            matrix_spec,
            matrix_spec,
            rows_spec,
            rows_spec,
            P(None, "wide"),
        ),
        check_vma=False,
    )
```

```python
import functools

import jax
import jax.numpy as jnp
from jax import lax
from jax.experimental import pallas as pl
from jax.experimental.pallas import tpu as pltpu
from jax.sharding import PartitionSpec as P

HEAD_SIZE = 64
PAIR = 2 * HEAD_SIZE
FORWARD_ROWS = 512
BACKWARD_ROWS = 256
ROW_TILE = 256
FF_CHUNK = 1024

epsilon = 1e-05
masked_bias = -1e30
half = jnp.bfloat16
single = jnp.float32


def estimate(flops, size):
    return pl.CostEstimate(flops=flops // 16, bytes_accessed=size // 16, transcendentals=0)


def contract(left, right, left_dim, right_dim):
    return lax.dot_general(
        left, right, (((left_dim,), (right_dim,)), ((), ())), preferred_element_type=jnp.float32
    )


def first_head_lanes():
    return lax.broadcasted_iota(jnp.int32, (1, PAIR), 1) < HEAD_SIZE


def one_head_of(pair, head):
    lanes = first_head_lanes()
    keep = lanes if head == 0 else jnp.logical_not(lanes)
    return jnp.where(keep, pair, jnp.zeros_like(pair))


def attend_kernel(query_ref, key_ref, value_ref, bias_ref, out_ref, total_ref, *, rows):
    keys = key_ref[...]
    values = value_ref[...]
    scale = jnp.asarray(HEAD_SIZE ** (-0.5), half)
    for start in range(0, keys.shape[0], rows):
        window = pl.ds(start, rows)
        queries = query_ref[window, :] * scale
        bias = bias_ref[:, window]
        attended = []
        for head in range(2):
            scores = contract(keys, one_head_of(queries, head), 1, 1) + bias
            top = jnp.max(scores, axis=0, keepdims=True)
            weights = jnp.exp(scores - top)
            total = jnp.sum(weights, axis=0, keepdims=True)
            mixed = contract(values, weights.astype(half), 0, 0) * (1.0 / total)
            attended.append(mixed[HEAD_SIZE * head : HEAD_SIZE * (head + 1)])
            total_ref[head : head + 1, window] = top + jnp.log(total)
        out_ref[window, :] = jnp.concatenate(attended, 0).T.astype(half)


def attend_forward(packed, bias):
    length = packed.shape[0]
    features = packed.shape[1] // 3
    pairs = features // PAIR
    columns = lambda part: pl.BlockSpec((length, PAIR), lambda i: (0, part * pairs + i))
    return pl.pallas_call(
        functools.partial(attend_kernel, rows=FORWARD_ROWS),
        grid=(pairs,),
        in_specs=[
            columns(0),
            columns(1),
            columns(2),
            pl.BlockSpec((length, length), lambda i: (0, 0)),
        ],
        out_specs=[columns(0), pl.BlockSpec((None, 2, length), lambda i: (i, 0, 0))],
        out_shape=[
            jax.ShapeDtypeStruct((length, features), half),
            jax.ShapeDtypeStruct((pairs, 2, length), single),
        ],
        compiler_params=pltpu.CompilerParams(vmem_limit_bytes=56 << 20),
        cost_estimate=estimate(16 * length * length * features, 8 * length * features),
        name="attend_forward",
    )(packed, packed, packed, bias)


def attend_grad_kernel(
    query_ref,
    key_ref,
    value_ref,
    bias_ref,
    upstream_ref,
    total_ref,
    attended_ref,
    out_ref,
    key_sum,
    value_sum,
    *,
    rows,
):
    pair = pl.program_id(0)
    features = out_ref.shape[1] // 3
    keys = key_ref[...]
    values = value_ref[...]
    scale = HEAD_SIZE ** (-0.5)
    for start in range(0, keys.shape[0], rows):
        window = pl.ds(start, rows)
        queries = query_ref[window, :] * jnp.asarray(scale, half)
        upstream = upstream_ref[window, :]
        product = (upstream.astype(single) * attended_ref[window, :].astype(single)).T
        bias = bias_ref[:, window]
        query_grads, key_grad, value_grad = [], 0.0, 0.0
        for head in range(2):
            head_queries = one_head_of(queries, head)
            head_upstream = one_head_of(upstream, head)
            inner = jnp.sum(
                product[HEAD_SIZE * head : HEAD_SIZE * (head + 1)], axis=0, keepdims=True
            )
            scores = contract(keys, head_queries, 1, 1) + bias
            weights = jnp.exp(scores - total_ref[head : head + 1, window])
            weight_grads = contract(values, head_upstream, 1, 1)
            score_grads = (weights * (weight_grads - inner)).astype(half)
            value_grad = value_grad + contract(weights.astype(half), head_upstream, 1, 0)
            key_grad = key_grad + contract(score_grads, head_queries, 1, 0)
            query_grads.append(
                contract(keys, score_grads, 0, 0)[HEAD_SIZE * head : HEAD_SIZE * (head + 1)]
            )
        out_ref[window, pl.ds(pl.multiple_of(pair * PAIR, PAIR), PAIR)] = (
            jnp.concatenate(query_grads, 0).T * scale
        ).astype(half)
        if start == 0:
            key_sum[...] = key_grad
            value_sum[...] = value_grad
        else:
            key_sum[...] += key_grad
            value_sum[...] += value_grad
    out_ref[:, pl.ds(pl.multiple_of(features + pair * PAIR, PAIR), PAIR)] = key_sum[...].astype(
        half
    )
    out_ref[:, pl.ds(pl.multiple_of(2 * features + pair * PAIR, PAIR), PAIR)] = value_sum[
        ...
    ].astype(half)


def attend_backward(packed, bias, upstream, totals, attended):
    length = packed.shape[0]
    features = packed.shape[1] // 3
    pairs = features // PAIR
    columns = lambda part: pl.BlockSpec((length, PAIR), lambda i: (0, part * pairs + i))
    return pl.pallas_call(
        functools.partial(attend_grad_kernel, rows=BACKWARD_ROWS),
        grid=(pairs,),
        in_specs=[
            columns(0),
            columns(1),
            columns(2),
            pl.BlockSpec((length, length), lambda i: (0, 0)),
            columns(0),
            pl.BlockSpec((None, 2, length), lambda i: (i, 0, 0)),
            columns(0),
        ],
        out_specs=pl.BlockSpec((length, 3 * features), lambda i: (0, 0)),
        out_shape=jax.ShapeDtypeStruct((length, 3 * features), half),
        scratch_shapes=[pltpu.VMEM((length, PAIR), single)] * 2,
        compiler_params=pltpu.CompilerParams(vmem_limit_bytes=56 << 20),
        cost_estimate=estimate(40 * length * length * features, 16 * length * features),
        name="attend_backward",
    )(packed, packed, packed, bias, upstream, totals, attended)


def place_pieces(pieces, out_shape, targets, indices):
    def kernel(index_ref, *refs):
        sources, out_ref, semaphores = refs[: len(pieces)], refs[-2], refs[-1]
        copies = [
            pltpu.make_async_copy(
                source, out_ref.at[target(index_ref)], semaphores.at[number]
            )
            for number, (source, target) in enumerate(zip(sources, targets))
        ]
        for copy in copies:
            copy.start()
        for copy in copies:
            copy.wait()

    size = 2 * 2
    for extent in out_shape:
        size *= extent
    anywhere = pl.BlockSpec(memory_space=pl.ANY)
    return pl.pallas_call(
        kernel,
        in_specs=[pl.BlockSpec(memory_space=pltpu.SMEM)] + [anywhere] * len(pieces),
        out_specs=pl.BlockSpec(memory_space=pltpu.VMEM),
        out_shape=jax.ShapeDtypeStruct(out_shape, pieces[0].dtype),
        scratch_shapes=[pltpu.SemaphoreType.DMA((len(pieces),))],
        compiler_params=pltpu.CompilerParams(vmem_limit_bytes=32 << 20),
        cost_estimate=estimate(0, size),
        name="place_pieces",
    )(indices, *pieces)


def normal_of(hidden):
    center = hidden - jnp.mean(hidden, axis=-1, keepdims=True)
    inverse = lax.rsqrt(jnp.mean(center * center, axis=-1, keepdims=True) + epsilon)
    return center * inverse, inverse


def norm_pull(normal, inverse, gain, upstream):
    scaled = upstream * gain
    slope = jnp.mean(scaled, axis=-1, keepdims=True)
    tilt = jnp.mean(scaled * normal, axis=-1, keepdims=True)
    return inverse * (scaled - slope - normal * tilt)


def column_sum(array):
    return jnp.sum(array, axis=0, keepdims=True)


def tile_of(columns):
    return pl.BlockSpec((ROW_TILE, columns), lambda i: (i, 0))


def resident(shape, *index):
    place = index or (0,) * len(shape)
    return pl.BlockSpec(shape, lambda i: place, pipeline_mode=pl.Buffered(1))


def row_tiled(kernel, name, length, in_specs, out_specs, out_shape, operands, flops):
    size = sum(operand.size * operand.dtype.itemsize for operand in operands)
    size += sum(shape.size * jnp.dtype(shape.dtype).itemsize for shape in out_shape)
    return pl.pallas_call(
        kernel,
        grid=(length // ROW_TILE,),
        in_specs=in_specs,
        out_specs=out_specs,
        out_shape=out_shape,
        compiler_params=pltpu.CompilerParams(vmem_limit_bytes=56 << 20),
        cost_estimate=estimate(flops, size),
        name=name,
    )(*operands)


def project_kernel(hidden_ref, rows_ref, weight_ref, normed_ref, packed_ref, *, gain, shift):
    features = hidden_ref.shape[1]
    normal, _ = normal_of(hidden_ref[...])
    normed = (normal * rows_ref[gain : gain + 1] + rows_ref[shift : shift + 1]).astype(half)
    normed_ref[...] = normed
    for part in range(3):
        window = slice(part * features, (part + 1) * features)
        product = contract(normed, weight_ref[:, window], 1, 0)
        if part != 1:
            row = shift + (1 if part == 0 else 2)
            product = product + rows_ref[row : row + 1]
        packed_ref[:, window] = product.astype(half)


def project(hidden, rows, gain, shift, joined):
    length, features = hidden.shape
    return row_tiled(
        functools.partial(project_kernel, gain=gain, shift=shift),
        "project",
        length,
        [
            tile_of(features),
            resident(rows.shape),
            resident((features, 3 * features)),
        ],
        [tile_of(features), tile_of(3 * features)],
        [
            jax.ShapeDtypeStruct((length, features), half),
            jax.ShapeDtypeStruct((length, 3 * features), half),
        ],
        (hidden, rows, joined),
        6 * length * features * features,
    )


def feed_kernel(
    attended_ref,
    hidden_ref,
    rows_ref,
    up_bias_ref,
    out_weight_ref,
    up_ref,
    down_ref,
    middle_ref,
    second_ref,
    activated_ref,
    slope_ref,
    result_ref,
    *,
    gain,
    shift,
):
    hidden_units = up_ref.shape[1]
    middle = hidden_ref[...] + (
        contract(attended_ref[...], out_weight_ref[...], 1, 0) + rows_ref[shift + 3 : shift + 4]
    )
    middle_ref[...] = middle
    normal, _ = normal_of(middle)
    second = normal * rows_ref[gain + 1 : gain + 2] + rows_ref[shift + 4 : shift + 5]
    second = second.astype(half)
    second_ref[...] = second
    result = middle + rows_ref[shift + 5 : shift + 6]
    rate = 0.7978845608028654
    for start in range(0, hidden_units, FF_CHUNK):
        window = slice(start, start + FF_CHUNK)
        value = contract(second, up_ref[:, window], 1, 0) + up_bias_ref[:, window]
        square = value * value
        bent = jnp.tanh(value * (rate + (rate * 0.044715) * square))
        opened = 0.5 + 0.5 * bent
        activated = (value * opened).astype(half)
        activated_ref[:, window] = activated
        curve = (value * (0.5 * rate + (1.5 * rate * 0.044715) * square)) * (1.0 - bent * bent)
        slope_ref[:, window] = (opened + curve).astype(half)
        result = result + contract(activated, down_ref[window, :], 1, 0)
    result_ref[...] = result.astype(result_ref.dtype)


def feed(attended, hidden, rows, gain, shift, up_bias, joined, up, down, result_type):
    length, features = hidden.shape
    units = down.shape[0]
    up_array, up_place = up
    shape = jax.ShapeDtypeStruct
    return row_tiled(
        functools.partial(feed_kernel, gain=gain, shift=shift),
        "feed",
        length,
        [
            tile_of(features),
            tile_of(features),
            resident(rows.shape),
            resident(up_bias.shape),
            resident((features, features), 0, 3),
            resident((features, units), 0, up_place),
            resident(down.shape),
        ],
        [tile_of(features), tile_of(features), tile_of(units), tile_of(units), tile_of(features)],
        [
            shape((length, features), single),
            shape((length, features), half),
            shape((length, units), half),
            shape((length, units), half),
            shape((length, features), result_type),
        ],
        (attended, hidden, rows, up_bias, joined, up_array, down),
        2 * length * features * (features + 2 * units),
    )


def feed_grad_kernel(
    gradient_ref,
    slope_ref,
    middle_ref,
    rows_ref,
    out_weight_ref,
    up_ref,
    down_ref,
    branch_ref,
    upper_ref,
    middle_grad_ref,
    attention_grad_ref,
    upstream_ref,
    sums_ref,
    unit_sums_ref,
    *,
    gain,
):
    units = up_ref.shape[1]

    @pl.when(pl.program_id(0) == 0)
    def _():
        sums_ref[...] = jnp.zeros_like(sums_ref)
        unit_sums_ref[...] = jnp.zeros_like(unit_sums_ref)

    gradient = gradient_ref[...].astype(single)
    branch = gradient.astype(half)
    branch_ref[...] = branch
    sums_ref[0:1] += column_sum(branch.astype(single))
    second_grad = jnp.zeros(gradient.shape, single)
    for start in range(0, units, FF_CHUNK):
        window = slice(start, start + FF_CHUNK)
        pulled = contract(branch, down_ref[window, :], 1, 1) * slope_ref[:, window].astype(single)
        upper = pulled.astype(half)
        upper_ref[:, window] = upper
        unit_sums_ref[:, window] += column_sum(upper.astype(single))
        second_grad = second_grad + contract(upper, up_ref[:, window], 1, 1)
    normal, inverse = normal_of(middle_ref[...])
    middle_grad = gradient + norm_pull(
        normal, inverse, rows_ref[gain + 1 : gain + 2], second_grad
    )
    sums_ref[1:2] += column_sum(second_grad * normal)
    sums_ref[2:3] += column_sum(second_grad)
    middle_grad_ref[...] = middle_grad
    attention_grad = middle_grad.astype(half)
    attention_grad_ref[...] = attention_grad
    sums_ref[3:4] += column_sum(attention_grad.astype(single))
    upstream_ref[...] = contract(attention_grad, out_weight_ref[...], 1, 1).astype(half)


def feed_grad(gradient, slope, middle, rows, gain, joined, up, down):
    up_array, up_place = up
    length, features = middle.shape
    units = down.shape[0]
    shape = jax.ShapeDtypeStruct
    return row_tiled(
        functools.partial(feed_grad_kernel, gain=gain),
        "feed_grad",
        length,
        [
            tile_of(features),
            tile_of(units),
            tile_of(features),
            resident(rows.shape),
            resident((features, features), 0, 3),
            resident((features, units), 0, up_place),
            resident(down.shape),
        ],
        [
            tile_of(features),
            tile_of(units),
            tile_of(features),
            tile_of(features),
            tile_of(features),
            resident((8, features)),
            resident((1, units)),
        ],
        [
            shape((length, features), half),
            shape((length, units), half),
            shape((length, features), single),
            shape((length, features), half),
            shape((length, features), half),
            shape((8, features), single),
            shape((1, units), single),
        ],
        (gradient, slope, middle, rows, joined, up_array, down),
        2 * length * features * (features + 2 * units),
    )


def project_grad_kernel(
    packed_grad_ref, hidden_ref, middle_grad_ref, rows_ref, weight_ref, *out_refs, gain
):
    sums_ref = out_refs[-1]
    features = hidden_ref.shape[1]

    @pl.when(pl.program_id(0) == 0)
    def _():
        sums_ref[...] = jnp.zeros_like(sums_ref)

    packed_grad = packed_grad_ref[...]
    normed_grad = contract(packed_grad, weight_ref[...], 1, 1)
    normal, inverse = normal_of(hidden_ref[...])
    result = middle_grad_ref[...] + norm_pull(
        normal, inverse, rows_ref[gain : gain + 1], normed_grad
    )
    for result_ref in out_refs[:-1]:
        result_ref[...] = result.astype(result_ref.dtype)
    sums_ref[0:1] += column_sum(normed_grad * normal)
    sums_ref[1:2] += column_sum(normed_grad)
    sums_ref[2:3] += column_sum(packed_grad[:, :features].astype(single))
    sums_ref[3:4] += column_sum(packed_grad[:, 2 * features :].astype(single))


def project_grad(packed_grad, hidden, middle_grad, rows, gain, joined, result_types):
    length, features = hidden.shape
    shape = jax.ShapeDtypeStruct
    return row_tiled(
        functools.partial(project_grad_kernel, gain=gain),
        "project_grad",
        length,
        [
            tile_of(3 * features),
            tile_of(features),
            tile_of(features),
            resident(rows.shape),
            resident((features, 3 * features)),
        ],
        [tile_of(features) for _ in result_types] + [resident((8, features))],
        [shape((length, features), result_type) for result_type in result_types]
        + [shape((8, features), single)],
        (packed_grad, hidden, middle_grad, rows, joined),
        6 * length * features * features,
    )


def term_blocks(terms, core, groups, row_unit, by_core):
    pieces = [left.shape[1] // (groups * row_unit) for left, _ in terms]
    widths = [right.shape[1] // (2 if by_core else 1) for _, right in terms]
    total = sum(count * width for count, width in zip(pieces, widths))
    chips = groups // 2
    out_shape = (chips, 2, row_unit, total) if by_core else (groups, row_unit, total)
    outputs = 2 if by_core else 1
    if row_unit % 16:
        columns = []
        for (left, right), count, width in zip(terms, pieces, widths):
            part = contract(left, right, 0, 0).astype(half)
            part = part.reshape(chips, 2, count, row_unit, -1, width).transpose(2, 1, 0, 4, 3, 5)
            columns += [part[piece] for piece in range(count)]
        whole = jnp.concatenate(columns, axis=-1)
        if not by_core:
            return [whole[:, :, 0].swapaxes(0, 1).reshape(out_shape)]
        return [
            lax.dynamic_index_in_dim(whole, which, 0, keepdims=False) for which in (1 - core, core)
        ]
    number = len(terms)

    def kernel(core_ref, *refs):
        sources = refs[: 2 * number]
        outs = refs[2 * number : 2 * number + outputs]
        buffers = refs[2 * number + outputs : 4 * number + outputs]
        semaphores = refs[4 * number + outputs]
        first_core = core_ref[0] == 0
        copies = [
            pltpu.make_async_copy(source, buffer, semaphores.at[index])
            for index, (source, buffer) in enumerate(zip(sources, buffers))
        ]
        for copy in copies:
            copy.start()
        start = 0
        for index, (count, width) in enumerate(zip(pieces, widths)):
            copies[2 * index].wait()
            copies[2 * index + 1].wait()
            left, right = buffers[2 * index], buffers[2 * index + 1]
            rows = groups * row_unit
            step = max(size for size in (768, 640, 512, 384, 256, 128) if width % size == 0)
            held = chips // count
            for turn in range(count):
                turned = left[:, turn * rows : (turn + 1) * rows].T
                some = slice(turn * held, (turn + 1) * held)
                for low in range(0, right.shape[1], step):
                    product = contract(turned, right[:, low : low + step], 1, 0).astype(half)
                    product = product.reshape(held, 2, count, row_unit, step)
                    side, inside = divmod(low, width)
                    for piece in range(count):
                        lanes = start + piece * width + inside
                        lanes = slice(lanes, lanes + step)
                        even, odd = product[:, 0, piece], product[:, 1, piece]
                        if by_core:
                            outs[0][some, side, :, lanes] = jnp.where(first_core, odd, even)
                            outs[1][some, side, :, lanes] = jnp.where(first_core, even, odd)
                        else:
                            for chip in range(held):
                                owner = 2 * (turn * held + chip)
                                outs[0][owner, :, lanes] = even[chip]
                                outs[0][owner + 1, :, lanes] = odd[chip]
            start += count * width

    anywhere = pl.BlockSpec(memory_space=pl.ANY)
    operands = [operand for term in terms for operand in term]
    size = sum(operand.size for operand in operands) * 2
    flops = sum(2 * left.size * right.shape[1] for left, right in terms)
    shape = jax.ShapeDtypeStruct(out_shape, half)
    return pl.pallas_call(
        kernel,
        in_specs=[pl.BlockSpec(memory_space=pltpu.SMEM)] + [anywhere] * len(operands),
        out_specs=[pl.BlockSpec(memory_space=pltpu.VMEM)] * outputs,
        out_shape=[shape] * outputs,
        scratch_shapes=[pltpu.VMEM(operand.shape, half) for operand in operands]
        + [pltpu.SemaphoreType.DMA((len(operands),))],
        compiler_params=pltpu.CompilerParams(vmem_limit_bytes=60 << 20),
        cost_estimate=estimate(flops, size + 2 * outputs * shape.size),
        name="term_blocks",
    )(core.reshape(1).astype(jnp.int32), *operands)


def per_device(
    tokens,
    time_embed,
    segment_ids,
    pad_mask,
    out_grad,
    qkv_weight,
    out_weight,
    up_weight,
    down_weight,
    norm_gains,
    bias_rows,
    up_bias,
):
    layers = qkv_weight.shape[0]
    features = tokens.shape[2]
    groups = lax.axis_size("wide")
    swap = [(0, 1), (1, 0)]

    def whole_sequence(part):
        return lax.all_to_all(part, "seq", split_axis=0, concat_axis=1, tiled=True)[0]

    core = lax.axis_index("wide") & 1
    place = lax.axis_index("seq")
    indices = jnp.stack([core, place]).astype(jnp.int32)
    row_unit = qkv_weight.shape[1]

    def across(bit):
        pairs = [(index, index ^ bit) for index in range(groups)]
        return lambda part: lax.ppermute(part, "wide", pairs)

    def beside_seq(part):
        return lax.ppermute(part, "seq", swap)

    def to_owners(part):
        return lax.psum_scatter(part, "wide", scatter_dimension=0, tiled=True)

    bit_of = lambda bit: (lax.axis_index("wide") >> (bit.bit_length() - 1)) & 1
    running = []

    def begin(steps, finish):
        entry = [steps, finish, next(steps), None]
        running.append(entry)
        return entry

    def launch(main, entries):
        fresh = [entry for entry in entries if entry in running and entry[3] is None]
        if fresh:
            sends = [[sent for sent, _ in entry[2]] for entry in fresh]
            main, sends = lax.optimization_barrier((main, sends))
            for entry, sent in zip(fresh, sends):
                entry[3] = [pass_on(part) for part, (_, pass_on) in zip(sent, entry[2])]
        return main

    def advance(main, *only):
        chosen = [entry for entry in only or list(running) if entry in running]
        main = launch(main, chosen)
        if not chosen:
            return main
        main, flying = lax.optimization_barrier((main, [entry[3] for entry in chosen]))
        for entry, arrived in zip(chosen, flying):
            entry[3] = None
            try:
                entry[2] = entry[0].send(arrived)
            except StopIteration as stop:
                entry[1](stop.value)
                running.remove(entry)
        return launch(main, chosen)

    def side_of(array, which, axis):
        return lax.dynamic_index_in_dim(array, which, axis, keepdims=False)

    chip_bits = [1 << number for number in range(groups.bit_length() - 2, 0, -1)]

    def join(current, received, which):
        lead = current.shape[0]
        joined = place_pieces(
            [current, received],
            (lead, 2) + current.shape[1:],
            [lambda ref: (slice(None), ref[0]), lambda ref: (slice(None), 1 - ref[0])],
            which.reshape(1).astype(jnp.int32),
        )
        return joined.reshape((2 * lead,) + current.shape[1:])

    def gather_columns(shard):
        rows, columns = shard.shape[0], shard.shape[1] // 2
        current = lax.dynamic_slice_in_dim(shard, place * columns, columns, axis=1)[None]
        for bit in chip_bits:
            (received,) = yield [(current, across(bit))]
            current = join(current, received, bit_of(bit))
        (aside,) = yield [(current, beside_seq)]
        passed = yield [(part, across(1)) for part in (current, aside)]

        def target(own_core, own_place):
            def where(ref):
                which_core = ref[0] if own_core else 1 - ref[0]
                which_place = ref[1] if own_place else 1 - ref[1]
                start = pl.multiple_of(which_place * columns, columns)
                return (slice(None), which_core, slice(None), pl.ds(start, columns))

            return where

        return place_pieces(
            [current, aside, *passed],
            (current.shape[0], 2, rows, 2 * columns),
            [target(True, True), target(True, False), target(False, True), target(False, False)],
            indices,
        ).reshape(-1, 2 * columns)

    def gather_rows(shard):
        rows, columns = shard.shape[0] // 2, shard.shape[1]
        current = side_of(shard.reshape(2, rows, columns), place, 0)[None]
        for bit in chip_bits[:-1]:
            (received,) = yield [(current, across(bit))]
            current = join(current, received, bit_of(bit))
        (received,) = yield [(current, beside_seq)]
        current = join(current, received, place).reshape(-1, 2 * rows, columns)
        for bit in chip_bits[-1:] + [1]:
            (received,) = yield [(current, across(bit))]
            current = join(current, received, bit_of(bit))
        return current.reshape(-1, columns)

    my_tokens = whole_sequence(tokens)

    gain_count = layers * norm_gains.shape[1]
    row_count = gain_count + layers * bias_rows.shape[1]
    up_pieces = up_bias.shape[1] // row_unit
    small = jnp.concatenate(
        [
            norm_gains.reshape(gain_count, row_unit),
            bias_rows.reshape(row_count - gain_count, row_unit),
            up_bias.reshape(layers * up_pieces, row_unit),
        ]
    )
    side = jnp.pad(small.T, ((0, 0), (0, -small.shape[0] % PAIR)))
    joined_parts = [jnp.concatenate([qkv_weight[0], out_weight[0], side], axis=1)]
    for layer in range(1, layers):
        parts = [qkv_weight[layer], out_weight[layer], up_weight[layer]]
        joined_parts.append(jnp.concatenate(parts, axis=1))
    joined = [lax.all_gather(part, "wide", axis=0, tiled=True) for part in joined_parts]
    downs = {
        layer: lax.all_gather(down_weight[layer], "wide", axis=0, tiled=True)
        for layer in range(1, layers)
    }
    rows = joined[0][:, -side.shape[1] :].T.astype(single)
    spread_bias = rows[row_count : row_count + layers * up_pieces]
    spread_bias = spread_bias.reshape(layers, up_pieces, groups, row_unit).swapaxes(1, 2)
    all_up_bias = spread_bias.reshape(layers, 1, -1)
    cut_gains = norm_gains.size
    cut_rows = cut_gains + bias_rows.size
    gain_row = lambda layer: layer * norm_gains.shape[1]
    shift_row = lambda layer: gain_count + layer * bias_rows.shape[1]
    matrices = [None] * layers
    ups = {}
    fetches = [
        begin(gather_columns(up_weight[0]), functools.partial(ups.__setitem__, 0)),
        begin(gather_rows(down_weight[0]), functools.partial(downs.__setitem__, 0)),
    ]
    marks = jnp.stack([segment_ids, pad_mask], axis=2)
    time_embed, marks = advance((time_embed, marks), *fetches)
    marks = whole_sequence(marks)
    for _ in chip_bits[2:]:
        time_embed, marks = advance((time_embed, marks), *fetches)
    doc, pad = marks[:, 0], marks[:, 1]
    positions = jnp.arange(doc.shape[0])
    allowed = (doc[:, None] == doc[None, :]) & (
        (pad[:, None] == 1) | (positions[:, None] == positions[None, :])
    )
    bias = jnp.where(allowed, 0.0, masked_bias)

    my_time = lax.dynamic_index_in_dim(time_embed, place, 0, keepdims=True)
    hidden = my_tokens.astype(single) + my_time
    saved = []
    for layer in range(layers):
        whole = joined[layer]
        before = hidden
        normed, packed = project(hidden, rows, gain_row(layer), shift_row(layer), whole)
        if layer == layers - 1:
            packed, out_grad = lax.optimization_barrier((packed, out_grad))
            my_upstream = whole_sequence(out_grad)
        packed = advance(packed, *fetches)
        attended, totals = attend_forward(packed, bias)
        attended = advance(attended, *fetches)
        while running:
            attended = advance(attended, *fetches)
        up = (whole, 4 * features // up_bias.shape[1] // groups) if layer else (ups[0], 0)
        matrices[layer] = (whole, up, downs[layer])
        fetches = []
        middle, second, activated, slope, hidden = feed(
            attended,
            hidden,
            rows,
            gain_row(layer),
            shift_row(layer),
            all_up_bias[layer],
            whole,
            up,
            downs[layer],
            single if layer < layers - 1 else half,
        )
        saved.append((before, normed, packed, totals, attended, middle, second, activated, slope))

    def split_back(result):
        parts = result.reshape(2, -1, features).astype(half)
        return lax.all_to_all(parts, "seq", split_axis=0, concat_axis=0, tiled=True)

    output = split_back(hidden)

    def total_of(addends):
        return functools.reduce(jnp.add, [addend.astype(single) for addend in addends])

    def shares_of(terms, low, high):
        shares, start = [], 0
        for left, right in terms:
            rows, each = [], right.shape[1] // 2
            if high is None:
                each *= 2
            for _ in range(left.shape[1] // (groups * row_unit)):
                window = slice(start, start + each)
                if high is None:
                    rows.append(low[:, window])
                else:
                    rows.append(jnp.concatenate([low[:, window], high[:, window]], axis=1))
                start += each
            shares.append(jnp.concatenate(rows, axis=0))
        return shares

    def scatter_group(terms):
        (whole,) = term_blocks(terms, core, groups, row_unit, False)
        whole = whole.reshape(groups * row_unit, -1)
        (share,) = yield [(whole, to_owners)]
        (received,) = yield [(share, beside_seq)]
        return shares_of(terms, share.astype(single) + received.astype(single), None)

    def reduce_group(terms):
        other, own = term_blocks(terms, core, groups, row_unit, True)
        (received,) = yield [(other, across(1))]
        shape = (2,) * len(chip_bits) + (2, row_unit, own.shape[-1])
        addends = [part.reshape(shape) for part in (own, received)]
        axis = len(chip_bits)
        for bit in [0] + chip_bits[:1:-1]:
            mine, pass_on = (bit_of(bit), across(bit)) if bit else (place, beside_seq)
            sent = total_of([side_of(part, 1 - mine, axis) for part in addends]).astype(half)
            (received,) = yield [(sent, pass_on)]
            addends = [side_of(part, mine, axis) for part in addends] + [received]
            axis -= 1
        far, near = chip_bits[:2]

        def corner(part, bits):
            part = side_of(part, bit_of(far) ^ (1 if bits & far else 0), 0)
            return side_of(part, bit_of(near) ^ (1 if bits & near else 0), 0)

        received = yield [
            (total_of([corner(part, bits) for part in addends]).astype(half), across(bits))
            for bits in (near, far, near | far)
        ]
        addends = [corner(part, 0) for part in addends] + received
        current = total_of(addends).astype(half)
        (received,) = yield [(current, beside_seq)]
        low = jnp.where(place == 0, current, received).astype(single)
        high = jnp.where(place == 0, received, current).astype(single)
        return shares_of(terms, low, high)

    def reduce_small(array):
        parts = [array.reshape((2,) * (len(chip_bits) + 1) + array.shape[1:])]
        pairs = [(2, 1, len(chip_bits) - 1)]
        pairs += [(bit, None, chip_bits.index(bit)) for bit in chip_bits[-2:1:-1]]
        pairs += [(chip_bits[0], chip_bits[1], 0)]
        for high, low, axis in pairs:

            def chosen(bits):
                def pick(part):
                    if low is not None:
                        part = side_of(part, bit_of(low) ^ (1 if bits & low else 0), axis + 1)
                    return side_of(part, bit_of(high) ^ (1 if bits & high else 0), axis)

                return total_of([pick(part) for part in parts])

            masks = [high] if low is None else [low, high, low | high]
            received = yield [(chosen(bits), across(bits)) for bits in masks]
            parts = [chosen(0)] + received
        current = total_of(parts)
        (received,) = yield [(current, beside_seq)]
        return current + received

    weight_grads = [[None] * 4 for _ in range(layers)]

    def begin_group(steps, layer, named):
        def finish(shares):
            for (part, _), share in zip(named, shares):
                weight_grads[layer][part] = share

        return begin(steps([term for _, term in named]), finish)

    gradient = my_upstream
    small_grads = [None] * layers
    held = []
    for layer in range(layers - 1, -1, -1):
        whole, up, down = matrices[layer]
        hidden, normed, packed, totals, attended, middle, second, activated, slope = saved[layer]
        steps = scatter_group if layer else reduce_group
        branch, upper, middle_grad, attention_grad, upstream, sums, unit_sums = feed_grad(
            gradient, slope, middle, rows, gain_row(layer), whole, up, down
        )
        named = [(2, (second, upper)), (1, (attended, attention_grad))]
        if layer:
            held.append(begin_group(steps, layer, [(3, (activated, branch))] + named))
            upstream = launch(upstream, held[-1:])
        else:
            upstream = advance(upstream, first_group)
            upper, attention_grad, upstream = lax.optimization_barrier(
                (upper, attention_grad, upstream)
            )
            named = [(2, (second, upper)), (1, (attended, attention_grad))]
            second_group = begin_group(steps, layer, named)
            upstream = launch(upstream, [second_group])
            upstream = advance(upstream, second_group)
            upstream = advance(upstream, *held[:1])
        packed_grad = attend_backward(packed, bias, upstream, totals, attended)
        if layer == layers - 1:
            packed_grad, output = lax.optimization_barrier((packed_grad, output))
            output = output.astype(single)
        named = [(0, (normed, packed_grad))]
        if not layer:
            packed_grad = advance(packed_grad, first_group, second_group, *held[:1])
            last_group = begin_group(steps, layer, named)
            packed_grad = launch(packed_grad, [last_group])
            packed_grad = advance(packed_grad, last_group)
        gradient, *rounded, more_sums = project_grad(
            packed_grad,
            hidden,
            middle_grad,
            rows,
            gain_row(layer),
            whole,
            (single, half) if layer else (half,),
        )
        if layer == 1:
            below = (saved[0][7], rounded[0])
            first_group = begin_group(reduce_group, 0, [(3, below)])
            gradient = launch(gradient, [first_group])
        if layer:
            held.append(begin_group(steps, layer, named))
            gradient = launch(gradient, held[-1:])
        if layer == 1:
            gradient = advance(gradient, first_group)
        if not layer:
            gradient = advance(gradient, last_group)
        small_grads[layer] = (
            jnp.stack([more_sums[0], sums[1]]),
            jnp.stack([more_sums[1], more_sums[2], more_sums[3], sums[3], sums[2], sums[0]]),
            unit_sums[0],
        )

    def by_owner(parts):
        stacked = jnp.stack(parts)
        stacked = stacked.reshape(layers, -1, groups, stacked.shape[-1] // groups)
        return stacked.transpose(2, 0, 1, 3).reshape(groups, -1)

    owned = jnp.concatenate(
        [by_owner([small_grads[layer][part] for layer in range(layers)]) for part in range(3)],
        axis=1,
    )
    small_result = []
    begin(reduce_small(owned), small_result.append)
    output = launch(output, running[-1:])
    output = advance(output, first_group, second_group, *held)
    input_grad = split_back(gradient)
    while running:
        output = advance(output, last_group)
        output = advance(output, *[entry for entry in running if entry is not last_group])
    owned = small_result[0]
    input_grad = input_grad.astype(single)
    stacked = [
        jnp.stack([weight_grads[layer][part] for layer in range(layers)]) for part in range(4)
    ]
    return (
        output,
        input_grad,
        *stacked,
        owned[:cut_gains].reshape(norm_gains.shape),
        owned[cut_gains:cut_rows].reshape(bias_rows.shape),
        owned[cut_rows:].reshape(up_bias.shape),
    )


def solution(mesh):
    tokens_spec = P("wide", "seq", None)
    matrix_spec = P(None, "wide", None)
    rows_spec = P(None, None, "wide")
    return jax.shard_map(
        per_device,
        mesh=mesh,
        in_specs=(
            tokens_spec,
            P("wide", None),
            P("wide", "seq"),
            P("wide", "seq"),
            tokens_spec,
            matrix_spec,
            matrix_spec,
            matrix_spec,
            matrix_spec,
            rows_spec,
            rows_spec,
            P(None, "wide"),
        ),
        out_specs=(
            tokens_spec,
            tokens_spec,
            matrix_spec,
            matrix_spec,
            matrix_spec,
            matrix_spec,
            rows_spec,
            rows_spec,
            P(None, "wide"),
        ),
        check_vma=False,
    )
```

```python
import functools

import jax
import jax.numpy as jnp
from jax import lax
from jax.experimental import pallas as pl
from jax.experimental.pallas import tpu as pltpu
from jax.sharding import PartitionSpec as P

HEAD_SIZE = 64
PAIR = 2 * HEAD_SIZE
FORWARD_ROWS = 1024
BACKWARD_ROWS = 256
ROW_TILE = 256
FF_CHUNK = 1024

epsilon = 1e-05
masked_bias = -1e30
half = jnp.bfloat16
single = jnp.float32


def estimate(flops, size):
    return pl.CostEstimate(flops=flops // 16, bytes_accessed=size // 16, transcendentals=0)


def contract(left, right, left_dim, right_dim):
    return lax.dot_general(
        left, right, (((left_dim,), (right_dim,)), ((), ())), preferred_element_type=jnp.float32
    )


def first_head_lanes():
    return lax.broadcasted_iota(jnp.int32, (1, PAIR), 1) < HEAD_SIZE


def one_head_of(pair, head):
    lanes = first_head_lanes()
    keep = lanes if head == 0 else jnp.logical_not(lanes)
    return jnp.where(keep, pair, jnp.zeros_like(pair))


def attend_kernel(query_ref, key_ref, value_ref, bias_ref, out_ref, total_ref, *, rows):
    keys = key_ref[...]
    values = value_ref[...]
    scale = jnp.asarray(HEAD_SIZE ** (-0.5), half)
    for start in range(0, keys.shape[0], rows):
        window = pl.ds(start, rows)
        queries = query_ref[window, :] * scale
        bias = bias_ref[:, window]
        attended = []
        for head in range(2):
            scores = contract(keys, one_head_of(queries, head), 1, 1) + bias
            top = jnp.max(scores, axis=0, keepdims=True)
            weights = jnp.exp(scores - top)
            total = jnp.sum(weights, axis=0, keepdims=True)
            mixed = contract(values, weights.astype(half), 0, 0) * (1.0 / total)
            attended.append(mixed[HEAD_SIZE * head : HEAD_SIZE * (head + 1)])
            total_ref[head : head + 1, window] = top + jnp.log(total)
        out_ref[window, :] = jnp.concatenate(attended, 0).T.astype(half)


def attend_forward(packed, bias):
    length = packed.shape[0]
    features = packed.shape[1] // 3
    pairs = features // PAIR
    columns = lambda part: pl.BlockSpec((length, PAIR), lambda i: (0, part * pairs + i))
    return pl.pallas_call(
        functools.partial(attend_kernel, rows=FORWARD_ROWS),
        grid=(pairs,),
        in_specs=[
            columns(0),
            columns(1),
            columns(2),
            pl.BlockSpec((length, length), lambda i: (0, 0)),
        ],
        out_specs=[columns(0), pl.BlockSpec((None, 2, length), lambda i: (i, 0, 0))],
        out_shape=[
            jax.ShapeDtypeStruct((length, features), half),
            jax.ShapeDtypeStruct((pairs, 2, length), single),
        ],
        compiler_params=pltpu.CompilerParams(vmem_limit_bytes=56 << 20),
        cost_estimate=estimate(16 * length * length * features, 8 * length * features),
        name="attend_forward",
    )(packed, packed, packed, bias)


def attend_grad_kernel(
    query_ref,
    key_ref,
    value_ref,
    bias_ref,
    upstream_ref,
    total_ref,
    attended_ref,
    out_ref,
    key_sum,
    value_sum,
    *,
    rows,
):
    pair = pl.program_id(0)
    features = out_ref.shape[1] // 3
    keys = key_ref[...]
    values = value_ref[...]
    scale = HEAD_SIZE ** (-0.5)
    for start in range(0, keys.shape[0], rows):
        window = pl.ds(start, rows)
        queries = query_ref[window, :] * jnp.asarray(scale, half)
        upstream = upstream_ref[window, :]
        product = (upstream.astype(single) * attended_ref[window, :].astype(single)).T
        bias = bias_ref[:, window]
        query_grads, key_grad, value_grad = [], 0.0, 0.0
        for head in range(2):
            head_queries = one_head_of(queries, head)
            head_upstream = one_head_of(upstream, head)
            inner = jnp.sum(
                product[HEAD_SIZE * head : HEAD_SIZE * (head + 1)], axis=0, keepdims=True
            )
            scores = contract(keys, head_queries, 1, 1) + bias
            weights = jnp.exp(scores - total_ref[head : head + 1, window])
            weight_grads = contract(values, head_upstream, 1, 1)
            score_grads = (weights * (weight_grads - inner)).astype(half)
            value_grad = value_grad + contract(weights.astype(half), head_upstream, 1, 0)
            key_grad = key_grad + contract(score_grads, head_queries, 1, 0)
            query_grads.append(
                contract(keys, score_grads, 0, 0)[HEAD_SIZE * head : HEAD_SIZE * (head + 1)]
            )
        out_ref[window, pl.ds(pl.multiple_of(pair * PAIR, PAIR), PAIR)] = (
            jnp.concatenate(query_grads, 0).T * scale
        ).astype(half)
        if start == 0:
            key_sum[...] = key_grad
            value_sum[...] = value_grad
        else:
            key_sum[...] += key_grad
            value_sum[...] += value_grad
    out_ref[:, pl.ds(pl.multiple_of(features + pair * PAIR, PAIR), PAIR)] = key_sum[...].astype(
        half
    )
    out_ref[:, pl.ds(pl.multiple_of(2 * features + pair * PAIR, PAIR), PAIR)] = value_sum[
        ...
    ].astype(half)


def attend_backward(packed, bias, upstream, totals, attended):
    length = packed.shape[0]
    features = packed.shape[1] // 3
    pairs = features // PAIR
    columns = lambda part: pl.BlockSpec((length, PAIR), lambda i: (0, part * pairs + i))
    return pl.pallas_call(
        functools.partial(attend_grad_kernel, rows=BACKWARD_ROWS),
        grid=(pairs,),
        in_specs=[
            columns(0),
            columns(1),
            columns(2),
            pl.BlockSpec((length, length), lambda i: (0, 0)),
            columns(0),
            pl.BlockSpec((None, 2, length), lambda i: (i, 0, 0)),
            columns(0),
        ],
        out_specs=pl.BlockSpec((length, 3 * features), lambda i: (0, 0)),
        out_shape=jax.ShapeDtypeStruct((length, 3 * features), half),
        scratch_shapes=[pltpu.VMEM((length, PAIR), single)] * 2,
        compiler_params=pltpu.CompilerParams(vmem_limit_bytes=56 << 20),
        cost_estimate=estimate(40 * length * length * features, 16 * length * features),
        name="attend_backward",
    )(packed, packed, packed, bias, upstream, totals, attended)


def place_pieces(pieces, out_shape, targets, indices):
    def kernel(index_ref, *refs):
        sources, out_ref, semaphores = refs[: len(pieces)], refs[-2], refs[-1]
        copies = [
            pltpu.make_async_copy(
                source, out_ref.at[target(index_ref)], semaphores.at[number]
            )
            for number, (source, target) in enumerate(zip(sources, targets))
        ]
        for copy in copies:
            copy.start()
        for copy in copies:
            copy.wait()

    size = 2 * 2
    for extent in out_shape:
        size *= extent
    anywhere = pl.BlockSpec(memory_space=pl.ANY)
    return pl.pallas_call(
        kernel,
        in_specs=[pl.BlockSpec(memory_space=pltpu.SMEM)] + [anywhere] * len(pieces),
        out_specs=pl.BlockSpec(memory_space=pltpu.VMEM),
        out_shape=jax.ShapeDtypeStruct(out_shape, pieces[0].dtype),
        scratch_shapes=[pltpu.SemaphoreType.DMA((len(pieces),))],
        compiler_params=pltpu.CompilerParams(vmem_limit_bytes=32 << 20),
        cost_estimate=estimate(0, size),
        name="place_pieces",
    )(indices, *pieces)


def normal_of(hidden):
    center = hidden - jnp.mean(hidden, axis=-1, keepdims=True)
    inverse = lax.rsqrt(jnp.mean(center * center, axis=-1, keepdims=True) + epsilon)
    return center * inverse, inverse


def norm_pull(normal, inverse, gain, upstream):
    scaled = upstream * gain
    slope = jnp.mean(scaled, axis=-1, keepdims=True)
    tilt = jnp.mean(scaled * normal, axis=-1, keepdims=True)
    return inverse * (scaled - slope - normal * tilt)


def column_sum(array):
    return jnp.sum(array, axis=0, keepdims=True)


def tile_of(columns):
    return pl.BlockSpec((ROW_TILE, columns), lambda i: (i, 0))


def resident(shape, *index):
    place = index or (0,) * len(shape)
    return pl.BlockSpec(shape, lambda i: place, pipeline_mode=pl.Buffered(1))


def row_tiled(kernel, name, length, in_specs, out_specs, out_shape, operands, flops):
    size = sum(operand.size * operand.dtype.itemsize for operand in operands)
    size += sum(shape.size * jnp.dtype(shape.dtype).itemsize for shape in out_shape)
    return pl.pallas_call(
        kernel,
        grid=(length // ROW_TILE,),
        in_specs=in_specs,
        out_specs=out_specs,
        out_shape=out_shape,
        compiler_params=pltpu.CompilerParams(vmem_limit_bytes=56 << 20),
        cost_estimate=estimate(flops, size),
        name=name,
    )(*operands)


def project_kernel(hidden_ref, rows_ref, weight_ref, normed_ref, packed_ref, *, gain, shift):
    features = hidden_ref.shape[1]
    normal, _ = normal_of(hidden_ref[...])
    normed = (normal * rows_ref[gain : gain + 1] + rows_ref[shift : shift + 1]).astype(half)
    normed_ref[...] = normed
    for part in range(3):
        window = slice(part * features, (part + 1) * features)
        product = contract(normed, weight_ref[:, window], 1, 0)
        if part != 1:
            row = shift + (1 if part == 0 else 2)
            product = product + rows_ref[row : row + 1]
        packed_ref[:, window] = product.astype(half)


def project(hidden, rows, gain, shift, joined):
    length, features = hidden.shape
    return row_tiled(
        functools.partial(project_kernel, gain=gain, shift=shift),
        "project",
        length,
        [
            tile_of(features),
            resident(rows.shape),
            resident((features, 3 * features)),
        ],
        [tile_of(features), tile_of(3 * features)],
        [
            jax.ShapeDtypeStruct((length, features), half),
            jax.ShapeDtypeStruct((length, 3 * features), half),
        ],
        (hidden, rows, joined),
        6 * length * features * features,
    )


def feed_kernel(
    attended_ref,
    hidden_ref,
    rows_ref,
    up_bias_ref,
    out_weight_ref,
    up_ref,
    down_ref,
    middle_ref,
    second_ref,
    activated_ref,
    slope_ref,
    result_ref,
    *,
    gain,
    shift,
):
    hidden_units = up_ref.shape[1]
    middle = hidden_ref[...] + (
        contract(attended_ref[...], out_weight_ref[...], 1, 0) + rows_ref[shift + 3 : shift + 4]
    )
    middle_ref[...] = middle
    normal, _ = normal_of(middle)
    second = normal * rows_ref[gain + 1 : gain + 2] + rows_ref[shift + 4 : shift + 5]
    second = second.astype(half)
    second_ref[...] = second
    result = middle + rows_ref[shift + 5 : shift + 6]
    rate = 0.7978845608028654
    for start in range(0, hidden_units, FF_CHUNK):
        window = slice(start, start + FF_CHUNK)
        value = contract(second, up_ref[:, window], 1, 0) + up_bias_ref[:, window]
        square = value * value
        bent = jnp.tanh(value * (rate + (rate * 0.044715) * square))
        opened = 0.5 + 0.5 * bent
        activated = (value * opened).astype(half)
        activated_ref[:, window] = activated
        curve = (value * (0.5 * rate + (1.5 * rate * 0.044715) * square)) * (1.0 - bent * bent)
        slope_ref[:, window] = (opened + curve).astype(half)
        result = result + contract(activated, down_ref[window, :], 1, 0)
    result_ref[...] = result.astype(result_ref.dtype)


def feed(attended, hidden, rows, gain, shift, up_bias, joined, up, down, result_type):
    length, features = hidden.shape
    units = down.shape[0]
    up_array, up_place = up
    shape = jax.ShapeDtypeStruct
    return row_tiled(
        functools.partial(feed_kernel, gain=gain, shift=shift),
        "feed",
        length,
        [
            tile_of(features),
            tile_of(features),
            resident(rows.shape),
            resident(up_bias.shape),
            resident((features, features), 0, 3),
            resident((features, units), 0, up_place),
            resident(down.shape),
        ],
        [tile_of(features), tile_of(features), tile_of(units), tile_of(units), tile_of(features)],
        [
            shape((length, features), single),
            shape((length, features), half),
            shape((length, units), half),
            shape((length, units), half),
            shape((length, features), result_type),
        ],
        (attended, hidden, rows, up_bias, joined, up_array, down),
        2 * length * features * (features + 2 * units),
    )


def feed_grad_kernel(
    gradient_ref,
    slope_ref,
    middle_ref,
    rows_ref,
    out_weight_ref,
    up_ref,
    down_ref,
    branch_ref,
    upper_ref,
    middle_grad_ref,
    attention_grad_ref,
    upstream_ref,
    sums_ref,
    unit_sums_ref,
    *,
    gain,
):
    units = up_ref.shape[1]

    @pl.when(pl.program_id(0) == 0)
    def _():
        sums_ref[...] = jnp.zeros_like(sums_ref)
        unit_sums_ref[...] = jnp.zeros_like(unit_sums_ref)

    gradient = gradient_ref[...].astype(single)
    branch = gradient.astype(half)
    branch_ref[...] = branch
    sums_ref[0:1] += column_sum(branch.astype(single))
    second_grad = jnp.zeros(gradient.shape, single)
    for start in range(0, units, FF_CHUNK):
        window = slice(start, start + FF_CHUNK)
        pulled = contract(branch, down_ref[window, :], 1, 1) * slope_ref[:, window].astype(single)
        upper = pulled.astype(half)
        upper_ref[:, window] = upper
        unit_sums_ref[:, window] += column_sum(upper.astype(single))
        second_grad = second_grad + contract(upper, up_ref[:, window], 1, 1)
    normal, inverse = normal_of(middle_ref[...])
    middle_grad = gradient + norm_pull(
        normal, inverse, rows_ref[gain + 1 : gain + 2], second_grad
    )
    sums_ref[1:2] += column_sum(second_grad * normal)
    sums_ref[2:3] += column_sum(second_grad)
    middle_grad_ref[...] = middle_grad
    attention_grad = middle_grad.astype(half)
    attention_grad_ref[...] = attention_grad
    sums_ref[3:4] += column_sum(attention_grad.astype(single))
    upstream_ref[...] = contract(attention_grad, out_weight_ref[...], 1, 1).astype(half)


def feed_grad(gradient, slope, middle, rows, gain, joined, up, down):
    up_array, up_place = up
    length, features = middle.shape
    units = down.shape[0]
    shape = jax.ShapeDtypeStruct
    return row_tiled(
        functools.partial(feed_grad_kernel, gain=gain),
        "feed_grad",
        length,
        [
            tile_of(features),
            tile_of(units),
            tile_of(features),
            resident(rows.shape),
            resident((features, features), 0, 3),
            resident((features, units), 0, up_place),
            resident(down.shape),
        ],
        [
            tile_of(features),
            tile_of(units),
            tile_of(features),
            tile_of(features),
            tile_of(features),
            resident((8, features)),
            resident((1, units)),
        ],
        [
            shape((length, features), half),
            shape((length, units), half),
            shape((length, features), single),
            shape((length, features), half),
            shape((length, features), half),
            shape((8, features), single),
            shape((1, units), single),
        ],
        (gradient, slope, middle, rows, joined, up_array, down),
        2 * length * features * (features + 2 * units),
    )


def project_grad_kernel(
    packed_grad_ref, hidden_ref, middle_grad_ref, rows_ref, weight_ref, *out_refs, gain
):
    sums_ref = out_refs[-1]
    features = hidden_ref.shape[1]

    @pl.when(pl.program_id(0) == 0)
    def _():
        sums_ref[...] = jnp.zeros_like(sums_ref)

    packed_grad = packed_grad_ref[...]
    normed_grad = contract(packed_grad, weight_ref[...], 1, 1)
    normal, inverse = normal_of(hidden_ref[...])
    result = middle_grad_ref[...] + norm_pull(
        normal, inverse, rows_ref[gain : gain + 1], normed_grad
    )
    for result_ref in out_refs[:-1]:
        result_ref[...] = result.astype(result_ref.dtype)
    sums_ref[0:1] += column_sum(normed_grad * normal)
    sums_ref[1:2] += column_sum(normed_grad)
    sums_ref[2:3] += column_sum(packed_grad[:, :features].astype(single))
    sums_ref[3:4] += column_sum(packed_grad[:, 2 * features :].astype(single))


def project_grad(packed_grad, hidden, middle_grad, rows, gain, joined, result_types):
    length, features = hidden.shape
    shape = jax.ShapeDtypeStruct
    return row_tiled(
        functools.partial(project_grad_kernel, gain=gain),
        "project_grad",
        length,
        [
            tile_of(3 * features),
            tile_of(features),
            tile_of(features),
            resident(rows.shape),
            resident((features, 3 * features)),
        ],
        [tile_of(features) for _ in result_types] + [resident((8, features))],
        [shape((length, features), result_type) for result_type in result_types]
        + [shape((8, features), single)],
        (packed_grad, hidden, middle_grad, rows, joined),
        6 * length * features * features,
    )


def term_blocks(terms, core, groups, row_unit, by_core):
    pieces = [left.shape[1] // (groups * row_unit) for left, _ in terms]
    widths = [right.shape[1] // (2 if by_core else 1) for _, right in terms]
    total = sum(count * width for count, width in zip(pieces, widths))
    chips = groups // 2
    out_shape = (chips, 2, row_unit, total) if by_core else (groups, row_unit, total)
    outputs = 2 if by_core else 1
    if row_unit % 16:
        columns = []
        for (left, right), count, width in zip(terms, pieces, widths):
            part = contract(left, right, 0, 0).astype(half)
            part = part.reshape(chips, 2, count, row_unit, -1, width).transpose(2, 1, 0, 4, 3, 5)
            columns += [part[piece] for piece in range(count)]
        whole = jnp.concatenate(columns, axis=-1)
        if not by_core:
            return [whole[:, :, 0].swapaxes(0, 1).reshape(out_shape)]
        return [
            lax.dynamic_index_in_dim(whole, which, 0, keepdims=False) for which in (1 - core, core)
        ]
    number = len(terms)

    def kernel(core_ref, *refs):
        sources = refs[: 2 * number]
        outs = refs[2 * number : 2 * number + outputs]
        buffers = refs[2 * number + outputs : 4 * number + outputs]
        semaphores = refs[4 * number + outputs]
        first_core = core_ref[0] == 0
        copies = [
            pltpu.make_async_copy(source, buffer, semaphores.at[index])
            for index, (source, buffer) in enumerate(zip(sources, buffers))
        ]
        for copy in copies:
            copy.start()
        start = 0
        for index, (count, width) in enumerate(zip(pieces, widths)):
            copies[2 * index].wait()
            copies[2 * index + 1].wait()
            left, right = buffers[2 * index], buffers[2 * index + 1]
            rows = groups * row_unit
            step = max(size for size in (768, 640, 512, 384, 256, 128) if width % size == 0)
            held = chips // count
            for turn in range(count):
                turned = left[:, turn * rows : (turn + 1) * rows].T
                some = slice(turn * held, (turn + 1) * held)
                for low in range(0, right.shape[1], step):
                    product = contract(turned, right[:, low : low + step], 1, 0).astype(half)
                    product = product.reshape(held, 2, count, row_unit, step)
                    side, inside = divmod(low, width)
                    for piece in range(count):
                        lanes = start + piece * width + inside
                        lanes = slice(lanes, lanes + step)
                        even, odd = product[:, 0, piece], product[:, 1, piece]
                        if by_core:
                            outs[0][some, side, :, lanes] = jnp.where(first_core, odd, even)
                            outs[1][some, side, :, lanes] = jnp.where(first_core, even, odd)
                        else:
                            for chip in range(held):
                                owner = 2 * (turn * held + chip)
                                outs[0][owner, :, lanes] = even[chip]
                                outs[0][owner + 1, :, lanes] = odd[chip]
            start += count * width

    anywhere = pl.BlockSpec(memory_space=pl.ANY)
    operands = [operand for term in terms for operand in term]
    size = sum(operand.size for operand in operands) * 2
    flops = sum(2 * left.size * right.shape[1] for left, right in terms)
    shape = jax.ShapeDtypeStruct(out_shape, half)
    return pl.pallas_call(
        kernel,
        in_specs=[pl.BlockSpec(memory_space=pltpu.SMEM)] + [anywhere] * len(operands),
        out_specs=[pl.BlockSpec(memory_space=pltpu.VMEM)] * outputs,
        out_shape=[shape] * outputs,
        scratch_shapes=[pltpu.VMEM(operand.shape, half) for operand in operands]
        + [pltpu.SemaphoreType.DMA((len(operands),))],
        compiler_params=pltpu.CompilerParams(vmem_limit_bytes=60 << 20),
        cost_estimate=estimate(flops, size + 2 * outputs * shape.size),
        name="term_blocks",
    )(core.reshape(1).astype(jnp.int32), *operands)


def per_device(
    tokens,
    time_embed,
    segment_ids,
    pad_mask,
    out_grad,
    qkv_weight,
    out_weight,
    up_weight,
    down_weight,
    norm_gains,
    bias_rows,
    up_bias,
):
    layers = qkv_weight.shape[0]
    features = tokens.shape[2]
    groups = lax.axis_size("wide")
    swap = [(0, 1), (1, 0)]

    def whole_sequence(part):
        return lax.all_to_all(part, "seq", split_axis=0, concat_axis=1, tiled=True)[0]

    core = lax.axis_index("wide") & 1
    place = lax.axis_index("seq")
    row_unit = qkv_weight.shape[1]

    def across(bit):
        pairs = [(index, index ^ bit) for index in range(groups)]
        return lambda part: lax.ppermute(part, "wide", pairs)

    def beside_seq(part):
        return lax.ppermute(part, "seq", swap)

    def to_owners(part):
        return lax.psum_scatter(part, "wide", scatter_dimension=0, tiled=True)

    bit_of = lambda bit: (lax.axis_index("wide") >> (bit.bit_length() - 1)) & 1
    running = []

    def begin(steps, finish):
        entry = [steps, finish, next(steps), None]
        running.append(entry)
        return entry

    def launch(main, entries):
        fresh = [entry for entry in entries if entry in running and entry[3] is None]
        if fresh:
            sends = [[sent for sent, _ in entry[2]] for entry in fresh]
            main, sends = lax.optimization_barrier((main, sends))
            for entry, sent in zip(fresh, sends):
                entry[3] = [pass_on(part) for part, (_, pass_on) in zip(sent, entry[2])]
        return main

    def advance(main, *only):
        chosen = [entry for entry in only or list(running) if entry in running]
        main = launch(main, chosen)
        if not chosen:
            return main
        main, flying = lax.optimization_barrier((main, [entry[3] for entry in chosen]))
        for entry, arrived in zip(chosen, flying):
            entry[3] = None
            try:
                entry[2] = entry[0].send(arrived)
            except StopIteration as stop:
                entry[1](stop.value)
                running.remove(entry)
        return launch(main, chosen)

    def side_of(array, which, axis):
        return lax.dynamic_index_in_dim(array, which, axis, keepdims=False)

    chip_bits = [1 << number for number in range(groups.bit_length() - 2, 0, -1)]

    def join(current, received, which):
        lead = current.shape[0]
        joined = place_pieces(
            [current, received],
            (lead, 2) + current.shape[1:],
            [lambda ref: (slice(None), ref[0]), lambda ref: (slice(None), 1 - ref[0])],
            which.reshape(1).astype(jnp.int32),
        )
        return joined.reshape((2 * lead,) + current.shape[1:])

    def gather_rows(shard):
        rows, columns = shard.shape[0] // 2, shard.shape[1]
        current = side_of(shard.reshape(2, rows, columns), place, 0)[None]
        for bit in chip_bits[:-1]:
            (received,) = yield [(current, across(bit))]
            current = join(current, received, bit_of(bit))
        (received,) = yield [(current, beside_seq)]
        current = join(current, received, place).reshape(-1, 2 * rows, columns)
        for bit in chip_bits[-1:] + [1]:
            (received,) = yield [(current, across(bit))]
            current = join(current, received, bit_of(bit))
        return current.reshape(-1, columns)

    my_tokens = whole_sequence(tokens)

    gain_count = layers * norm_gains.shape[1]
    row_count = gain_count + layers * bias_rows.shape[1]
    up_pieces = up_bias.shape[1] // row_unit
    small = jnp.concatenate(
        [
            norm_gains.reshape(gain_count, row_unit),
            bias_rows.reshape(row_count - gain_count, row_unit),
            up_bias.reshape(layers * up_pieces, row_unit),
        ]
    )
    side = jnp.pad(small.T, ((0, 0), (0, -small.shape[0] % PAIR)))
    joined_parts = [
        jnp.concatenate([qkv_weight[0], out_weight[0], up_weight[0], side], axis=1)
    ]
    for layer in range(1, layers):
        joined_parts.append(jnp.concatenate([qkv_weight[layer], out_weight[layer]], axis=1))

    def whole_matrix(part):
        return lax.all_gather(part, "wide", axis=0, tiled=True)

    joined = [whole_matrix(part) for part in joined_parts]
    ups = [(joined[0], 4 * features // (up_bias.shape[1] * groups))]
    ups += [(whole_matrix(up_weight[layer]), 0) for layer in range(1, layers)]
    downs = {}

    def fetch_down(layer):
        return begin(
            gather_rows(down_weight[layer]), functools.partial(downs.__setitem__, layer)
        )

    rows = joined[0][:, -side.shape[1] :].T.astype(single)
    spread_bias = rows[row_count : row_count + layers * up_pieces]
    spread_bias = spread_bias.reshape(layers, up_pieces, groups, row_unit).swapaxes(1, 2)
    all_up_bias = spread_bias.reshape(layers, 1, -1)
    cut_gains = norm_gains.size
    cut_rows = cut_gains + bias_rows.size
    gain_row = lambda layer: layer * norm_gains.shape[1]
    shift_row = lambda layer: gain_count + layer * bias_rows.shape[1]
    matrices = [None] * layers
    fetch = fetch_down(0)
    marks = jnp.stack([segment_ids, pad_mask], axis=2)
    time_embed, marks = advance((time_embed, marks), fetch)
    marks = whole_sequence(marks)
    for _ in chip_bits[1:]:
        time_embed, marks = advance((time_embed, marks), fetch)
    doc, pad = marks[:, 0], marks[:, 1]
    positions = jnp.arange(doc.shape[0])
    allowed = (doc[:, None] == doc[None, :]) & (
        (pad[:, None] == 1) | (positions[:, None] == positions[None, :])
    )
    bias = jnp.where(allowed, 0.0, masked_bias)

    my_time = lax.dynamic_index_in_dim(time_embed, place, 0, keepdims=True)
    hidden = my_tokens.astype(single) + my_time
    saved = []
    for layer in range(layers):
        whole = joined[layer]
        before = hidden
        normed, packed = project(hidden, rows, gain_row(layer), shift_row(layer), whole)
        if layer == layers - 1:
            packed, out_grad = lax.optimization_barrier((packed, out_grad))
            my_upstream = whole_sequence(out_grad)
        packed = advance(packed, fetch)
        later = None
        if layer < layers - 1:
            later = fetch_down(layer + 1)
            packed = launch(packed, [later])
        attended, totals = attend_forward(packed, bias)
        while layer not in downs:
            attended = advance(attended, fetch)
        if later is not None:
            attended = advance(attended, later)
            fetch = later
        up = ups[layer]
        matrices[layer] = (whole, up, downs[layer])
        middle, second, activated, slope, hidden = feed(
            attended,
            hidden,
            rows,
            gain_row(layer),
            shift_row(layer),
            all_up_bias[layer],
            whole,
            up,
            downs[layer],
            single if layer < layers - 1 else half,
        )
        if later is not None:
            hidden = advance(hidden, later)
        saved.append((before, normed, packed, totals, attended, middle, second, activated, slope))

    def split_back(result):
        parts = result.reshape(2, -1, features).astype(half)
        return lax.all_to_all(parts, "seq", split_axis=0, concat_axis=0, tiled=True)

    output = split_back(hidden)

    def total_of(addends):
        return functools.reduce(jnp.add, [addend.astype(single) for addend in addends])

    def shares_of(terms, low, high):
        shares, start = [], 0
        for left, right in terms:
            rows, each = [], right.shape[1] // 2
            if high is None:
                each *= 2
            for _ in range(left.shape[1] // (groups * row_unit)):
                window = slice(start, start + each)
                if high is None:
                    rows.append(low[:, window])
                else:
                    rows.append(jnp.concatenate([low[:, window], high[:, window]], axis=1))
                start += each
            shares.append(jnp.concatenate(rows, axis=0))
        return shares

    def scatter_group(terms):
        (whole,) = term_blocks(terms, core, groups, row_unit, False)
        whole = whole.reshape(groups * row_unit, -1)
        (share,) = yield [(whole, to_owners)]
        (received,) = yield [(share, beside_seq)]
        return shares_of(terms, share.astype(single) + received.astype(single), None)

    def reduce_group(terms):
        other, own = term_blocks(terms, core, groups, row_unit, True)
        (received,) = yield [(other, across(1))]
        shape = (2,) * len(chip_bits) + (2, row_unit, own.shape[-1])
        addends = [part.reshape(shape) for part in (own, received)]
        axis = len(chip_bits)
        for bit in [0] + chip_bits[:1:-1]:
            mine, pass_on = (bit_of(bit), across(bit)) if bit else (place, beside_seq)
            sent = total_of([side_of(part, 1 - mine, axis) for part in addends]).astype(half)
            (received,) = yield [(sent, pass_on)]
            addends = [side_of(part, mine, axis) for part in addends] + [received]
            axis -= 1
        far, near = chip_bits[:2]

        def corner(part, bits):
            part = side_of(part, bit_of(far) ^ (1 if bits & far else 0), 0)
            return side_of(part, bit_of(near) ^ (1 if bits & near else 0), 0)

        received = yield [
            (total_of([corner(part, bits) for part in addends]).astype(half), across(bits))
            for bits in (near, far, near | far)
        ]
        addends = [corner(part, 0) for part in addends] + received
        current = total_of(addends).astype(half)
        (received,) = yield [(current, beside_seq)]
        low = jnp.where(place == 0, current, received).astype(single)
        high = jnp.where(place == 0, received, current).astype(single)
        return shares_of(terms, low, high)

    def reduce_small(array):
        parts = [array.reshape((2,) * (len(chip_bits) + 1) + array.shape[1:])]
        pairs = [(2, 1, len(chip_bits) - 1)]
        pairs += [(bit, None, chip_bits.index(bit)) for bit in chip_bits[-2:1:-1]]
        pairs += [(chip_bits[0], chip_bits[1], 0)]
        for high, low, axis in pairs:

            def chosen(bits):
                def pick(part):
                    if low is not None:
                        part = side_of(part, bit_of(low) ^ (1 if bits & low else 0), axis + 1)
                    return side_of(part, bit_of(high) ^ (1 if bits & high else 0), axis)

                return total_of([pick(part) for part in parts])

            masks = [high] if low is None else [low, high, low | high]
            received = yield [(chosen(bits), across(bits)) for bits in masks]
            parts = [chosen(0)] + received
        current = total_of(parts)
        (received,) = yield [(current, beside_seq)]
        return current + received

    weight_grads = [[None] * 4 for _ in range(layers)]

    def begin_group(steps, layer, named):
        def finish(shares):
            for (part, _), share in zip(named, shares):
                weight_grads[layer][part] = share

        return begin(steps([term for _, term in named]), finish)

    gradient = my_upstream
    small_grads = [None] * layers
    held = []
    for layer in range(layers - 1, -1, -1):
        whole, up, down = matrices[layer]
        hidden, normed, packed, totals, attended, middle, second, activated, slope = saved[layer]
        steps = scatter_group if layer else reduce_group
        branch, upper, middle_grad, attention_grad, upstream, sums, unit_sums = feed_grad(
            gradient, slope, middle, rows, gain_row(layer), whole, up, down
        )
        named = [(2, (second, upper)), (1, (attended, attention_grad))]
        if layer:
            held.append(begin_group(steps, layer, [(3, (activated, branch))] + named))
            upstream = launch(upstream, held[-1:])
        else:
            upstream = advance(upstream, first_group)
            upper, attention_grad, upstream = lax.optimization_barrier(
                (upper, attention_grad, upstream)
            )
            named = [(2, (second, upper)), (1, (attended, attention_grad))]
            second_group = begin_group(steps, layer, named)
            upstream = launch(upstream, [second_group])
            upstream = advance(upstream, second_group)
            upstream = advance(upstream, *held[:1])
        packed_grad = attend_backward(packed, bias, upstream, totals, attended)
        if layer == layers - 1:
            packed_grad, output = lax.optimization_barrier((packed_grad, output))
            output = output.astype(single)
        named = [(0, (normed, packed_grad))]
        if not layer:
            packed_grad = advance(packed_grad, first_group, second_group, *held[:1])
            last_group = begin_group(steps, layer, named)
            packed_grad = launch(packed_grad, [last_group])
            packed_grad = advance(packed_grad, last_group)
        gradient, *rounded, more_sums = project_grad(
            packed_grad,
            hidden,
            middle_grad,
            rows,
            gain_row(layer),
            whole,
            (single, half) if layer else (half,),
        )
        if layer == 1:
            below = (saved[0][7], rounded[0])
            first_group = begin_group(reduce_group, 0, [(3, below)])
            gradient = launch(gradient, [first_group])
        if layer:
            held.append(begin_group(steps, layer, named))
            gradient = launch(gradient, held[-1:])
        if layer == 1:
            gradient = advance(gradient, first_group)
        if not layer:
            gradient = advance(gradient, last_group)
        small_grads[layer] = (
            jnp.stack([more_sums[0], sums[1]]),
            jnp.stack([more_sums[1], more_sums[2], more_sums[3], sums[3], sums[2], sums[0]]),
            unit_sums[0],
        )

    def by_owner(parts):
        stacked = jnp.stack(parts)
        stacked = stacked.reshape(layers, -1, groups, stacked.shape[-1] // groups)
        return stacked.transpose(2, 0, 1, 3).reshape(groups, -1)

    owned = jnp.concatenate(
        [by_owner([small_grads[layer][part] for layer in range(layers)]) for part in range(3)],
        axis=1,
    )
    small_result = []
    begin(reduce_small(owned), small_result.append)
    output = launch(output, running[-1:])
    output = advance(output, first_group, second_group, *held)
    input_grad = split_back(gradient)
    while running:
        output = advance(output, last_group)
        output = advance(output, *[entry for entry in running if entry is not last_group])
    owned = small_result[0]
    input_grad = input_grad.astype(single)
    stacked = [
        jnp.stack([weight_grads[layer][part] for layer in range(layers)]) for part in range(4)
    ]
    return (
        output,
        input_grad,
        *stacked,
        owned[:cut_gains].reshape(norm_gains.shape),
        owned[cut_gains:cut_rows].reshape(bias_rows.shape),
        owned[cut_rows:].reshape(up_bias.shape),
    )


def solution(mesh):
    tokens_spec = P("wide", "seq", None)
    matrix_spec = P(None, "wide", None)
    rows_spec = P(None, None, "wide")
    return jax.shard_map(
        per_device,
        mesh=mesh,
        in_specs=(
            tokens_spec,
            P("wide", None),
            P("wide", "seq"),
            P("wide", "seq"),
            tokens_spec,
            matrix_spec,
            matrix_spec,
            matrix_spec,
            matrix_spec,
            rows_spec,
            rows_spec,
            P(None, "wide"),
        ),
        out_specs=(
            tokens_spec,
            tokens_spec,
            matrix_spec,
            matrix_spec,
            matrix_spec,
            matrix_spec,
            rows_spec,
            rows_spec,
            P(None, "wide"),
        ),
        check_vma=False,
    )
```

```python
import functools

import jax
import jax.numpy as jnp
from jax import lax
from jax.experimental import pallas as pl
from jax.experimental.pallas import tpu as pltpu
from jax.sharding import PartitionSpec as P

HEAD_SIZE = 64
PAIR = 2 * HEAD_SIZE
FORWARD_ROWS = 1024
BACKWARD_ROWS = 256
ROW_TILE = 256
FF_CHUNK = 1024

epsilon = 1e-05
masked_bias = -1e30
half = jnp.bfloat16
single = jnp.float32


def estimate(flops, size):
    return pl.CostEstimate(flops=flops // 16, bytes_accessed=size // 16, transcendentals=0)


def contract(left, right, left_dim, right_dim):
    return lax.dot_general(
        left, right, (((left_dim,), (right_dim,)), ((), ())), preferred_element_type=jnp.float32
    )


def first_head_lanes():
    return lax.broadcasted_iota(jnp.int32, (1, PAIR), 1) < HEAD_SIZE


def one_head_of(pair, head):
    lanes = first_head_lanes()
    keep = lanes if head == 0 else jnp.logical_not(lanes)
    return jnp.where(keep, pair, jnp.zeros_like(pair))


def attend_kernel(query_ref, key_ref, value_ref, bias_ref, out_ref, total_ref, *, rows):
    keys = key_ref[...]
    values = value_ref[...]
    scale = jnp.asarray(HEAD_SIZE ** (-0.5), half)
    for start in range(0, keys.shape[0], rows):
        window = pl.ds(start, rows)
        queries = query_ref[window, :] * scale
        bias = bias_ref[:, window]
        attended = []
        for head in range(2):
            scores = contract(keys, one_head_of(queries, head), 1, 1) + bias
            top = jnp.max(scores, axis=0, keepdims=True)
            weights = jnp.exp(scores - top)
            total = jnp.sum(weights, axis=0, keepdims=True)
            mixed = contract(values, weights.astype(half), 0, 0) * (1.0 / total)
            attended.append(mixed[HEAD_SIZE * head : HEAD_SIZE * (head + 1)])
            total_ref[head : head + 1, window] = top + jnp.log(total)
        out_ref[window, :] = jnp.concatenate(attended, 0).T.astype(half)


def attend_forward(packed, bias):
    length = packed.shape[0]
    features = packed.shape[1] // 3
    pairs = features // PAIR
    columns = lambda part: pl.BlockSpec((length, PAIR), lambda i: (0, part * pairs + i))
    return pl.pallas_call(
        functools.partial(attend_kernel, rows=FORWARD_ROWS),
        grid=(pairs,),
        in_specs=[
            columns(0),
            columns(1),
            columns(2),
            pl.BlockSpec((length, length), lambda i: (0, 0)),
        ],
        out_specs=[columns(0), pl.BlockSpec((None, 2, length), lambda i: (i, 0, 0))],
        out_shape=[
            jax.ShapeDtypeStruct((length, features), half),
            jax.ShapeDtypeStruct((pairs, 2, length), single),
        ],
        compiler_params=pltpu.CompilerParams(vmem_limit_bytes=56 << 20),
        cost_estimate=estimate(16 * length * length * features, 8 * length * features),
        name="attend_forward",
    )(packed, packed, packed, bias)


def attend_grad_kernel(
    query_ref,
    key_ref,
    value_ref,
    bias_ref,
    upstream_ref,
    total_ref,
    attended_ref,
    out_ref,
    key_sum,
    value_sum,
    *,
    rows,
):
    pair = pl.program_id(0)
    features = out_ref.shape[1] // 3
    keys = key_ref[...]
    values = value_ref[...]
    scale = HEAD_SIZE ** (-0.5)
    for start in range(0, keys.shape[0], rows):
        window = pl.ds(start, rows)
        queries = query_ref[window, :] * jnp.asarray(scale, half)
        upstream = upstream_ref[window, :]
        product = (upstream.astype(single) * attended_ref[window, :].astype(single)).T
        bias = bias_ref[:, window]
        query_grads, key_grad, value_grad = [], 0.0, 0.0
        for head in range(2):
            head_queries = one_head_of(queries, head)
            head_upstream = one_head_of(upstream, head)
            inner = jnp.sum(
                product[HEAD_SIZE * head : HEAD_SIZE * (head + 1)], axis=0, keepdims=True
            )
            scores = contract(keys, head_queries, 1, 1) + bias
            weights = jnp.exp(scores - total_ref[head : head + 1, window])
            weight_grads = contract(values, head_upstream, 1, 1)
            score_grads = (weights * (weight_grads - inner)).astype(half)
            value_grad = value_grad + contract(weights.astype(half), head_upstream, 1, 0)
            key_grad = key_grad + contract(score_grads, head_queries, 1, 0)
            query_grads.append(
                contract(keys, score_grads, 0, 0)[HEAD_SIZE * head : HEAD_SIZE * (head + 1)]
            )
        out_ref[window, pl.ds(pl.multiple_of(pair * PAIR, PAIR), PAIR)] = (
            jnp.concatenate(query_grads, 0).T * scale
        ).astype(half)
        if start == 0:
            key_sum[...] = key_grad
            value_sum[...] = value_grad
        else:
            key_sum[...] += key_grad
            value_sum[...] += value_grad
    out_ref[:, pl.ds(pl.multiple_of(features + pair * PAIR, PAIR), PAIR)] = key_sum[...].astype(
        half
    )
    out_ref[:, pl.ds(pl.multiple_of(2 * features + pair * PAIR, PAIR), PAIR)] = value_sum[
        ...
    ].astype(half)


def attend_backward(packed, bias, upstream, totals, attended):
    length = packed.shape[0]
    features = packed.shape[1] // 3
    pairs = features // PAIR
    columns = lambda part: pl.BlockSpec((length, PAIR), lambda i: (0, part * pairs + i))
    return pl.pallas_call(
        functools.partial(attend_grad_kernel, rows=BACKWARD_ROWS),
        grid=(pairs,),
        in_specs=[
            columns(0),
            columns(1),
            columns(2),
            pl.BlockSpec((length, length), lambda i: (0, 0)),
            columns(0),
            pl.BlockSpec((None, 2, length), lambda i: (i, 0, 0)),
            columns(0),
        ],
        out_specs=pl.BlockSpec((length, 3 * features), lambda i: (0, 0)),
        out_shape=jax.ShapeDtypeStruct((length, 3 * features), half),
        scratch_shapes=[pltpu.VMEM((length, PAIR), single)] * 2,
        compiler_params=pltpu.CompilerParams(vmem_limit_bytes=56 << 20),
        cost_estimate=estimate(40 * length * length * features, 16 * length * features),
        name="attend_backward",
    )(packed, packed, packed, bias, upstream, totals, attended)


def place_pieces(pieces, out_shape, targets, indices):
    def kernel(index_ref, *refs):
        sources, out_ref, held, semaphores = refs[: len(pieces)], *refs[-3:]
        copies = [
            pltpu.make_async_copy(source, held.at[target(index_ref)], semaphores.at[number])
            for number, (source, target) in enumerate(zip(sources, targets))
        ]
        for copy in copies:
            copy.start()
        for copy in copies:
            copy.wait()
        last = pltpu.make_async_copy(held, out_ref, semaphores.at[len(pieces)])
        last.start()
        last.wait()

    size = 2 * 2
    for extent in out_shape:
        size *= extent
    anywhere = pl.BlockSpec(memory_space=pl.ANY)
    return pl.pallas_call(
        kernel,
        in_specs=[pl.BlockSpec(memory_space=pltpu.SMEM)] + [anywhere] * len(pieces),
        out_specs=anywhere,
        out_shape=jax.ShapeDtypeStruct(out_shape, pieces[0].dtype),
        scratch_shapes=[
            pltpu.VMEM(out_shape, pieces[0].dtype),
            pltpu.SemaphoreType.DMA((len(pieces) + 1,)),
        ],
        compiler_params=pltpu.CompilerParams(vmem_limit_bytes=60 << 20),
        cost_estimate=estimate(0, size),
        name="place_pieces",
    )(indices, *pieces)


def normal_of(hidden):
    center = hidden - jnp.mean(hidden, axis=-1, keepdims=True)
    inverse = lax.rsqrt(jnp.mean(center * center, axis=-1, keepdims=True) + epsilon)
    return center * inverse, inverse


def norm_pull(normal, inverse, gain, upstream):
    scaled = upstream * gain
    slope = jnp.mean(scaled, axis=-1, keepdims=True)
    tilt = jnp.mean(scaled * normal, axis=-1, keepdims=True)
    return inverse * (scaled - slope - normal * tilt)


def column_sum(array):
    return jnp.sum(array, axis=0, keepdims=True)


def tile_of(columns):
    return pl.BlockSpec((ROW_TILE, columns), lambda i: (i, 0))


def resident(shape, *index):
    place = index or (0,) * len(shape)
    return pl.BlockSpec(shape, lambda i: place, pipeline_mode=pl.Buffered(1))


def row_tiled(kernel, name, length, in_specs, out_specs, out_shape, operands, flops):
    size = sum(operand.size * operand.dtype.itemsize for operand in operands)
    size += sum(shape.size * jnp.dtype(shape.dtype).itemsize for shape in out_shape)
    return pl.pallas_call(
        kernel,
        grid=(length // ROW_TILE,),
        in_specs=in_specs,
        out_specs=out_specs,
        out_shape=out_shape,
        compiler_params=pltpu.CompilerParams(vmem_limit_bytes=56 << 20),
        cost_estimate=estimate(flops, size),
        name=name,
    )(*operands)


def project_kernel(hidden_ref, rows_ref, weight_ref, normed_ref, packed_ref, *, gain, shift):
    features = hidden_ref.shape[1]
    normal, _ = normal_of(hidden_ref[...])
    normed = (normal * rows_ref[gain : gain + 1] + rows_ref[shift : shift + 1]).astype(half)
    normed_ref[...] = normed
    for part in range(3):
        window = slice(part * features, (part + 1) * features)
        product = contract(normed, weight_ref[:, window], 1, 0)
        if part != 1:
            row = shift + (1 if part == 0 else 2)
            product = product + rows_ref[row : row + 1]
        packed_ref[:, window] = product.astype(half)


def project(hidden, rows, gain, shift, joined):
    length, features = hidden.shape
    return row_tiled(
        functools.partial(project_kernel, gain=gain, shift=shift),
        "project",
        length,
        [
            tile_of(features),
            resident(rows.shape),
            resident((features, 3 * features)),
        ],
        [tile_of(features), tile_of(3 * features)],
        [
            jax.ShapeDtypeStruct((length, features), half),
            jax.ShapeDtypeStruct((length, 3 * features), half),
        ],
        (hidden, rows, joined),
        6 * length * features * features,
    )


def feed_kernel(
    attended_ref,
    hidden_ref,
    rows_ref,
    up_bias_ref,
    out_weight_ref,
    up_ref,
    down_ref,
    middle_ref,
    second_ref,
    activated_ref,
    slope_ref,
    result_ref,
    *,
    gain,
    shift,
):
    hidden_units = up_ref.shape[1]
    middle = hidden_ref[...] + (
        contract(attended_ref[...], out_weight_ref[...], 1, 0) + rows_ref[shift + 3 : shift + 4]
    )
    middle_ref[...] = middle
    normal, _ = normal_of(middle)
    second = normal * rows_ref[gain + 1 : gain + 2] + rows_ref[shift + 4 : shift + 5]
    second = second.astype(half)
    second_ref[...] = second
    result = middle + rows_ref[shift + 5 : shift + 6]
    rate = 0.7978845608028654
    for start in range(0, hidden_units, FF_CHUNK):
        window = slice(start, start + FF_CHUNK)
        value = contract(second, up_ref[:, window], 1, 0) + up_bias_ref[:, window]
        square = value * value
        bent = jnp.tanh(value * (rate + (rate * 0.044715) * square))
        opened = 0.5 + 0.5 * bent
        activated = (value * opened).astype(half)
        activated_ref[:, window] = activated
        curve = (value * (0.5 * rate + (1.5 * rate * 0.044715) * square)) * (1.0 - bent * bent)
        slope_ref[:, window] = (opened + curve).astype(half)
        result = result + contract(activated, down_ref[window, :], 1, 0)
    result_ref[...] = result.astype(result_ref.dtype)


def feed(attended, hidden, rows, gain, shift, up_bias, joined, up, down, result_type):
    length, features = hidden.shape
    units = down.shape[0]
    up_array, up_place = up
    shape = jax.ShapeDtypeStruct
    return row_tiled(
        functools.partial(feed_kernel, gain=gain, shift=shift),
        "feed",
        length,
        [
            tile_of(features),
            tile_of(features),
            resident(rows.shape),
            resident(up_bias.shape),
            resident((features, features), 0, 3),
            resident((features, units), 0, up_place),
            resident(down.shape),
        ],
        [tile_of(features), tile_of(features), tile_of(units), tile_of(units), tile_of(features)],
        [
            shape((length, features), single),
            shape((length, features), half),
            shape((length, units), half),
            shape((length, units), half),
            shape((length, features), result_type),
        ],
        (attended, hidden, rows, up_bias, joined, up_array, down),
        2 * length * features * (features + 2 * units),
    )


def feed_grad_kernel(
    gradient_ref,
    slope_ref,
    middle_ref,
    rows_ref,
    out_weight_ref,
    up_ref,
    down_ref,
    branch_ref,
    upper_ref,
    middle_grad_ref,
    attention_grad_ref,
    upstream_ref,
    sums_ref,
    unit_sums_ref,
    *,
    gain,
):
    units = up_ref.shape[1]

    @pl.when(pl.program_id(0) == 0)
    def _():
        sums_ref[...] = jnp.zeros_like(sums_ref)
        unit_sums_ref[...] = jnp.zeros_like(unit_sums_ref)

    gradient = gradient_ref[...].astype(single)
    branch = gradient.astype(half)
    branch_ref[...] = branch
    sums_ref[0:1] += column_sum(branch.astype(single))
    second_grad = jnp.zeros(gradient.shape, single)
    for start in range(0, units, FF_CHUNK):
        window = slice(start, start + FF_CHUNK)
        pulled = contract(branch, down_ref[window, :], 1, 1) * slope_ref[:, window].astype(single)
        upper = pulled.astype(half)
        upper_ref[:, window] = upper
        unit_sums_ref[:, window] += column_sum(upper.astype(single))
        second_grad = second_grad + contract(upper, up_ref[:, window], 1, 1)
    normal, inverse = normal_of(middle_ref[...])
    middle_grad = gradient + norm_pull(
        normal, inverse, rows_ref[gain + 1 : gain + 2], second_grad
    )
    sums_ref[1:2] += column_sum(second_grad * normal)
    sums_ref[2:3] += column_sum(second_grad)
    middle_grad_ref[...] = middle_grad
    attention_grad = middle_grad.astype(half)
    attention_grad_ref[...] = attention_grad
    sums_ref[3:4] += column_sum(attention_grad.astype(single))
    upstream_ref[...] = contract(attention_grad, out_weight_ref[...], 1, 1).astype(half)


def feed_grad(gradient, slope, middle, rows, gain, joined, up, down):
    up_array, up_place = up
    length, features = middle.shape
    units = down.shape[0]
    shape = jax.ShapeDtypeStruct
    return row_tiled(
        functools.partial(feed_grad_kernel, gain=gain),
        "feed_grad",
        length,
        [
            tile_of(features),
            tile_of(units),
            tile_of(features),
            resident(rows.shape),
            resident((features, features), 0, 3),
            resident((features, units), 0, up_place),
            resident(down.shape),
        ],
        [
            tile_of(features),
            tile_of(units),
            tile_of(features),
            tile_of(features),
            tile_of(features),
            resident((8, features)),
            resident((1, units)),
        ],
        [
            shape((length, features), half),
            shape((length, units), half),
            shape((length, features), single),
            shape((length, features), half),
            shape((length, features), half),
            shape((8, features), single),
            shape((1, units), single),
        ],
        (gradient, slope, middle, rows, joined, up_array, down),
        2 * length * features * (features + 2 * units),
    )


def project_grad_kernel(
    packed_grad_ref, hidden_ref, middle_grad_ref, rows_ref, weight_ref, *out_refs, gain
):
    sums_ref = out_refs[-1]
    features = hidden_ref.shape[1]

    @pl.when(pl.program_id(0) == 0)
    def _():
        sums_ref[...] = jnp.zeros_like(sums_ref)

    packed_grad = packed_grad_ref[...]
    normed_grad = contract(packed_grad, weight_ref[...], 1, 1)
    normal, inverse = normal_of(hidden_ref[...])
    result = middle_grad_ref[...] + norm_pull(
        normal, inverse, rows_ref[gain : gain + 1], normed_grad
    )
    for result_ref in out_refs[:-1]:
        result_ref[...] = result.astype(result_ref.dtype)
    sums_ref[0:1] += column_sum(normed_grad * normal)
    sums_ref[1:2] += column_sum(normed_grad)
    sums_ref[2:3] += column_sum(packed_grad[:, :features].astype(single))
    sums_ref[3:4] += column_sum(packed_grad[:, 2 * features :].astype(single))


def project_grad(packed_grad, hidden, middle_grad, rows, gain, joined, result_types):
    length, features = hidden.shape
    shape = jax.ShapeDtypeStruct
    return row_tiled(
        functools.partial(project_grad_kernel, gain=gain),
        "project_grad",
        length,
        [
            tile_of(3 * features),
            tile_of(features),
            tile_of(features),
            resident(rows.shape),
            resident((features, 3 * features)),
        ],
        [tile_of(features) for _ in result_types] + [resident((8, features))],
        [shape((length, features), result_type) for result_type in result_types]
        + [shape((8, features), single)],
        (packed_grad, hidden, middle_grad, rows, joined),
        6 * length * features * features,
    )


def term_blocks(terms, core, groups, row_unit, by_core):
    pieces = [left.shape[1] // (groups * row_unit) for left, _ in terms]
    widths = [right.shape[1] // (2 if by_core else 1) for _, right in terms]
    total = sum(count * width for count, width in zip(pieces, widths))
    chips = groups // 2
    out_shape = (chips, 2, row_unit, total) if by_core else (groups, row_unit, total)
    outputs = 2 if by_core else 1
    if row_unit % 16:
        columns = []
        for (left, right), count, width in zip(terms, pieces, widths):
            part = contract(left, right, 0, 0).astype(half)
            part = part.reshape(chips, 2, count, row_unit, -1, width).transpose(2, 1, 0, 4, 3, 5)
            columns += [part[piece] for piece in range(count)]
        whole = jnp.concatenate(columns, axis=-1)
        if not by_core:
            return [whole[:, :, 0].swapaxes(0, 1).reshape(out_shape)]
        return [
            lax.dynamic_index_in_dim(whole, which, 0, keepdims=False) for which in (1 - core, core)
        ]
    number = len(terms)

    def kernel(core_ref, *refs):
        sources = refs[: 2 * number]
        outs = refs[2 * number : 2 * number + outputs]
        buffers = refs[2 * number + outputs : 4 * number + outputs]
        semaphores = refs[4 * number + outputs]
        first_core = core_ref[0] == 0
        copies = [
            pltpu.make_async_copy(source, buffer, semaphores.at[index])
            for index, (source, buffer) in enumerate(zip(sources, buffers))
        ]
        for copy in copies:
            copy.start()
        start = 0
        for index, (count, width) in enumerate(zip(pieces, widths)):
            copies[2 * index].wait()
            copies[2 * index + 1].wait()
            left, right = buffers[2 * index], buffers[2 * index + 1]
            rows = groups * row_unit
            step = max(size for size in (768, 640, 512, 384, 256, 128) if width % size == 0)
            held = chips // count
            for turn in range(count):
                turned = left[:, turn * rows : (turn + 1) * rows].T
                some = slice(turn * held, (turn + 1) * held)
                for low in range(0, right.shape[1], step):
                    product = contract(turned, right[:, low : low + step], 1, 0).astype(half)
                    product = product.reshape(held, 2, count, row_unit, step)
                    side, inside = divmod(low, width)
                    for piece in range(count):
                        lanes = start + piece * width + inside
                        lanes = slice(lanes, lanes + step)
                        even, odd = product[:, 0, piece], product[:, 1, piece]
                        if by_core:
                            outs[0][some, side, :, lanes] = jnp.where(first_core, odd, even)
                            outs[1][some, side, :, lanes] = jnp.where(first_core, even, odd)
                        else:
                            for chip in range(held):
                                owner = 2 * (turn * held + chip)
                                outs[0][owner, :, lanes] = even[chip]
                                outs[0][owner + 1, :, lanes] = odd[chip]
            start += count * width

    anywhere = pl.BlockSpec(memory_space=pl.ANY)
    operands = [operand for term in terms for operand in term]
    size = sum(operand.size for operand in operands) * 2
    flops = sum(2 * left.size * right.shape[1] for left, right in terms)
    shape = jax.ShapeDtypeStruct(out_shape, half)
    return pl.pallas_call(
        kernel,
        in_specs=[pl.BlockSpec(memory_space=pltpu.SMEM)] + [anywhere] * len(operands),
        out_specs=[pl.BlockSpec(memory_space=pltpu.VMEM)] * outputs,
        out_shape=[shape] * outputs,
        scratch_shapes=[pltpu.VMEM(operand.shape, half) for operand in operands]
        + [pltpu.SemaphoreType.DMA((len(operands),))],
        compiler_params=pltpu.CompilerParams(vmem_limit_bytes=60 << 20),
        cost_estimate=estimate(flops, size + 2 * outputs * shape.size),
        name="term_blocks",
    )(core.reshape(1).astype(jnp.int32), *operands)


def per_device(
    tokens,
    time_embed,
    segment_ids,
    pad_mask,
    out_grad,
    qkv_weight,
    out_weight,
    up_weight,
    down_weight,
    norm_gains,
    bias_rows,
    up_bias,
):
    layers = qkv_weight.shape[0]
    features = tokens.shape[2]
    groups = lax.axis_size("wide")
    swap = [(0, 1), (1, 0)]

    def whole_sequence(part):
        return lax.all_to_all(part, "seq", split_axis=0, concat_axis=1, tiled=True)[0]

    core = lax.axis_index("wide") & 1
    place = lax.axis_index("seq")
    indices = jnp.stack([core, place]).astype(jnp.int32)
    row_unit = qkv_weight.shape[1]

    def across(bit):
        pairs = [(index, index ^ bit) for index in range(groups)]
        return lambda part: lax.ppermute(part, "wide", pairs)

    def beside_seq(part):
        return lax.ppermute(part, "seq", swap)

    def to_owners(part):
        return lax.psum_scatter(part, "wide", scatter_dimension=0, tiled=True)

    bit_of = lambda bit: (lax.axis_index("wide") >> (bit.bit_length() - 1)) & 1
    running = []

    def begin(steps, finish):
        entry = [steps, finish, next(steps), None]
        running.append(entry)
        return entry

    def launch(main, entries):
        fresh = [entry for entry in entries if entry in running and entry[3] is None]
        if fresh:
            sends = [[sent for sent, _ in entry[2]] for entry in fresh]
            main, sends = lax.optimization_barrier((main, sends))
            for entry, sent in zip(fresh, sends):
                entry[3] = [pass_on(part) for part, (_, pass_on) in zip(sent, entry[2])]
        return main

    def advance(main, *only):
        chosen = [entry for entry in only or list(running) if entry in running]
        main = launch(main, chosen)
        if not chosen:
            return main
        main, flying = lax.optimization_barrier((main, [entry[3] for entry in chosen]))
        for entry, arrived in zip(chosen, flying):
            entry[3] = None
            try:
                entry[2] = entry[0].send(arrived)
            except StopIteration as stop:
                entry[1](stop.value)
                running.remove(entry)
        return launch(main, chosen)

    def side_of(array, which, axis):
        return lax.dynamic_index_in_dim(array, which, axis, keepdims=False)

    chip_bits = [1 << number for number in range(groups.bit_length() - 2, 0, -1)]

    def join(current, received, which):
        lead = current.shape[0]
        joined = place_pieces(
            [current, received],
            (lead, 2) + current.shape[1:],
            [lambda ref: (slice(None), ref[0]), lambda ref: (slice(None), 1 - ref[0])],
            which.reshape(1).astype(jnp.int32),
        )
        return joined.reshape((2 * lead,) + current.shape[1:])

    def gather_columns(shard):
        rows, columns = shard.shape[0], shard.shape[1] // 2
        current = lax.dynamic_slice_in_dim(shard, place * columns, columns, axis=1)[None]
        for bit in chip_bits:
            (received,) = yield [(current, across(bit))]
            current = join(current, received, bit_of(bit))
        (aside,) = yield [(current, beside_seq)]
        passed = yield [(part, across(1)) for part in (current, aside)]

        def target(own_core, own_place):
            def where(ref):
                which_core = ref[0] if own_core else 1 - ref[0]
                which_place = ref[1] if own_place else 1 - ref[1]
                start = pl.multiple_of(which_place * columns, columns)
                return (slice(None), which_core, slice(None), pl.ds(start, columns))

            return where

        return place_pieces(
            [current, aside, *passed],
            (current.shape[0], 2, rows, 2 * columns),
            [target(True, True), target(True, False), target(False, True), target(False, False)],
            indices,
        ).reshape(-1, 2 * columns)

    def gather_rows(shard):
        rows, columns = shard.shape[0] // 2, shard.shape[1]
        current = side_of(shard.reshape(2, rows, columns), place, 0)[None]
        for bit in chip_bits[:-1]:
            (received,) = yield [(current, across(bit))]
            current = join(current, received, bit_of(bit))
        (received,) = yield [(current, beside_seq)]
        current = join(current, received, place).reshape(-1, 2 * rows, columns)
        for bit in chip_bits[-1:] + [1]:
            (received,) = yield [(current, across(bit))]
            current = join(current, received, bit_of(bit))
        return current.reshape(-1, columns)

    my_tokens = whole_sequence(tokens)

    gain_count = layers * norm_gains.shape[1]
    row_count = gain_count + layers * bias_rows.shape[1]
    up_pieces = up_bias.shape[1] // row_unit
    small = jnp.concatenate(
        [
            norm_gains.reshape(gain_count, row_unit),
            bias_rows.reshape(row_count - gain_count, row_unit),
            up_bias.reshape(layers * up_pieces, row_unit),
        ]
    )
    side = jnp.pad(small.T, ((0, 0), (0, -small.shape[0] % PAIR)))
    joined_parts = [jnp.concatenate([qkv_weight[0], out_weight[0], side], axis=1)]
    for layer in range(1, layers):
        parts = [qkv_weight[layer], out_weight[layer], up_weight[layer]]
        joined_parts.append(jnp.concatenate(parts, axis=1))
    joined = [lax.all_gather(part, "wide", axis=0, tiled=True) for part in joined_parts]
    downs = {
        layer: lax.all_gather(down_weight[layer], "wide", axis=0, tiled=True)
        for layer in range(1, layers)
    }
    rows = joined[0][:, -side.shape[1] :].T.astype(single)
    spread_bias = rows[row_count : row_count + layers * up_pieces]
    rows = rows[:row_count]
    spread_bias = spread_bias.reshape(layers, up_pieces, groups, row_unit).swapaxes(1, 2)
    all_up_bias = spread_bias.reshape(layers, 1, -1)
    cut_gains = norm_gains.size
    cut_rows = cut_gains + bias_rows.size
    gain_row = lambda layer: layer * norm_gains.shape[1]
    shift_row = lambda layer: gain_count + layer * bias_rows.shape[1]
    matrices = [None] * layers
    ups = {}
    fetches = [
        begin(gather_columns(up_weight[0]), functools.partial(ups.__setitem__, 0)),
        begin(gather_rows(down_weight[0]), functools.partial(downs.__setitem__, 0)),
    ]
    marks = jnp.stack([segment_ids, pad_mask], axis=2)
    time_embed, marks = advance((time_embed, marks), *fetches)
    marks = whole_sequence(marks)
    for _ in chip_bits[2:]:
        time_embed, marks = advance((time_embed, marks), *fetches)
    doc, pad = marks[:, 0], marks[:, 1]
    positions = jnp.arange(doc.shape[0])
    allowed = (doc[:, None] == doc[None, :]) & (
        (pad[:, None] == 1) | (positions[:, None] == positions[None, :])
    )
    bias = jnp.where(allowed, 0.0, masked_bias)

    my_time = lax.dynamic_index_in_dim(time_embed, place, 0, keepdims=True)
    hidden = my_tokens.astype(single) + my_time
    saved = []
    for layer in range(layers):
        whole = joined[layer]
        before = hidden
        normed, packed = project(hidden, rows, gain_row(layer), shift_row(layer), whole)
        if layer == layers - 1:
            packed, out_grad = lax.optimization_barrier((packed, out_grad))
            my_upstream = whole_sequence(out_grad)
        packed = advance(packed, *fetches)
        attended, totals = attend_forward(packed, bias)
        attended = advance(attended, *fetches)
        while running:
            attended = advance(attended, *fetches)
        up = (whole, 4 * features // up_bias.shape[1] // groups) if layer else (ups[0], 0)
        matrices[layer] = (whole, up, downs[layer])
        fetches = []
        middle, second, activated, slope, hidden = feed(
            attended,
            hidden,
            rows,
            gain_row(layer),
            shift_row(layer),
            all_up_bias[layer],
            whole,
            up,
            downs[layer],
            single if layer < layers - 1 else half,
        )
        saved.append((before, normed, packed, totals, attended, middle, second, activated, slope))

    def split_back(result):
        parts = result.reshape(2, -1, features).astype(half)
        return lax.all_to_all(parts, "seq", split_axis=0, concat_axis=0, tiled=True)

    output = split_back(hidden)

    def total_of(addends):
        return functools.reduce(jnp.add, [addend.astype(single) for addend in addends])

    def shares_of(terms, low, high):
        shares, start = [], 0
        for left, right in terms:
            rows, each = [], right.shape[1] // 2
            if high is None:
                each *= 2
            for _ in range(left.shape[1] // (groups * row_unit)):
                window = slice(start, start + each)
                if high is None:
                    rows.append(low[:, window])
                else:
                    rows.append(jnp.concatenate([low[:, window], high[:, window]], axis=1))
                start += each
            shares.append(jnp.concatenate(rows, axis=0))
        return shares

    def scatter_group(terms):
        (whole,) = term_blocks(terms, core, groups, row_unit, False)
        whole = whole.reshape(groups * row_unit, -1)
        (share,) = yield [(whole, to_owners)]
        (received,) = yield [(share, beside_seq)]
        return shares_of(terms, share.astype(single) + received.astype(single), None)

    def reduce_group(terms):
        other, own = term_blocks(terms, core, groups, row_unit, True)
        (received,) = yield [(other, across(1))]
        shape = (2,) * len(chip_bits) + (2, row_unit, own.shape[-1])
        addends = [part.reshape(shape) for part in (own, received)]
        axis = len(chip_bits)
        for bit in [0] + chip_bits[:1:-1]:
            mine, pass_on = (bit_of(bit), across(bit)) if bit else (place, beside_seq)
            sent = total_of([side_of(part, 1 - mine, axis) for part in addends]).astype(half)
            (received,) = yield [(sent, pass_on)]
            addends = [side_of(part, mine, axis) for part in addends] + [received]
            axis -= 1
        far, near = chip_bits[:2]

        def corner(part, bits):
            part = side_of(part, bit_of(far) ^ (1 if bits & far else 0), 0)
            return side_of(part, bit_of(near) ^ (1 if bits & near else 0), 0)

        received = yield [
            (total_of([corner(part, bits) for part in addends]).astype(half), across(bits))
            for bits in (near, far, near | far)
        ]
        addends = [corner(part, 0) for part in addends] + received
        current = total_of(addends).astype(half)
        (received,) = yield [(current, beside_seq)]
        low = jnp.where(place == 0, current, received).astype(single)
        high = jnp.where(place == 0, received, current).astype(single)
        return shares_of(terms, low, high)

    def reduce_small(array):
        parts = [array.reshape((2,) * (len(chip_bits) + 1) + array.shape[1:])]
        pairs = [(2, 1, len(chip_bits) - 1)]
        pairs += [(bit, None, chip_bits.index(bit)) for bit in chip_bits[-2:1:-1]]
        pairs += [(chip_bits[0], chip_bits[1], 0)]
        for high, low, axis in pairs:

            def chosen(bits):
                def pick(part):
                    if low is not None:
                        part = side_of(part, bit_of(low) ^ (1 if bits & low else 0), axis + 1)
                    return side_of(part, bit_of(high) ^ (1 if bits & high else 0), axis)

                return total_of([pick(part) for part in parts])

            masks = [high] if low is None else [low, high, low | high]
            received = yield [(chosen(bits), across(bits)) for bits in masks]
            parts = [chosen(0)] + received
        current = total_of(parts)
        (received,) = yield [(current, beside_seq)]
        return current + received

    weight_grads = [[None] * 4 for _ in range(layers)]

    def begin_group(steps, layer, named):
        def finish(shares):
            for (part, _), share in zip(named, shares):
                weight_grads[layer][part] = share

        return begin(steps([term for _, term in named]), finish)

    gradient = my_upstream
    small_grads = [None] * layers
    held = []
    for layer in range(layers - 1, -1, -1):
        whole, up, down = matrices[layer]
        hidden, normed, packed, totals, attended, middle, second, activated, slope = saved[layer]
        steps = scatter_group if layer else reduce_group
        branch, upper, middle_grad, attention_grad, upstream, sums, unit_sums = feed_grad(
            gradient, slope, middle, rows, gain_row(layer), whole, up, down
        )
        named = [(2, (second, upper)), (1, (attended, attention_grad))]
        if layer:
            held.append(begin_group(steps, layer, [(3, (activated, branch))] + named))
            upstream = launch(upstream, held[-1:])
        else:
            upstream = advance(upstream, first_group)
            upper, attention_grad, upstream = lax.optimization_barrier(
                (upper, attention_grad, upstream)
            )
            named = [(2, (second, upper)), (1, (attended, attention_grad))]
            second_group = begin_group(steps, layer, named)
            upstream = launch(upstream, [second_group])
            upstream = advance(upstream, second_group)
            upstream = advance(upstream, *held[:1])
        packed_grad = attend_backward(packed, bias, upstream, totals, attended)
        if layer == layers - 1:
            packed_grad, output = lax.optimization_barrier((packed_grad, output))
            output = output.astype(single)
        named = [(0, (normed, packed_grad))]
        if not layer:
            packed_grad = advance(packed_grad, first_group, second_group, *held[:1])
            last_group = begin_group(steps, layer, named)
            packed_grad = launch(packed_grad, [last_group])
            packed_grad = advance(packed_grad, last_group)
        gradient, *rounded, more_sums = project_grad(
            packed_grad,
            hidden,
            middle_grad,
            rows,
            gain_row(layer),
            whole,
            (single, half) if layer else (half,),
        )
        if layer == 1:
            below = (saved[0][7], rounded[0])
            first_group = begin_group(reduce_group, 0, [(3, below)])
            gradient = launch(gradient, [first_group])
        if layer:
            held.append(begin_group(steps, layer, named))
            gradient = launch(gradient, held[-1:])
        if layer == 1:
            gradient = advance(gradient, first_group)
        if not layer:
            gradient = advance(gradient, last_group)
        small_grads[layer] = (
            jnp.stack([more_sums[0], sums[1]]),
            jnp.stack([more_sums[1], more_sums[2], more_sums[3], sums[3], sums[2], sums[0]]),
            unit_sums[0],
        )

    def by_owner(parts):
        stacked = jnp.stack(parts)
        stacked = stacked.reshape(layers, -1, groups, stacked.shape[-1] // groups)
        return stacked.transpose(2, 0, 1, 3).reshape(groups, -1)

    owned = jnp.concatenate(
        [by_owner([small_grads[layer][part] for layer in range(layers)]) for part in range(3)],
        axis=1,
    )
    small_result = []
    begin(reduce_small(owned), small_result.append)
    output = launch(output, running[-1:])
    output = advance(output, first_group, second_group, *held)
    input_grad = split_back(gradient)
    while running:
        output = advance(output, last_group)
        output = advance(output, *[entry for entry in running if entry is not last_group])
    owned = small_result[0]
    input_grad = input_grad.astype(single)
    stacked = [
        jnp.stack([weight_grads[layer][part] for layer in range(layers)]) for part in range(4)
    ]
    return (
        output,
        input_grad,
        *stacked,
        owned[:cut_gains].reshape(norm_gains.shape),
        owned[cut_gains:cut_rows].reshape(bias_rows.shape),
        owned[cut_rows:].reshape(up_bias.shape),
    )


def solution(mesh):
    tokens_spec = P("wide", "seq", None)
    matrix_spec = P(None, "wide", None)
    rows_spec = P(None, None, "wide")
    return jax.shard_map(
        per_device,
        mesh=mesh,
        in_specs=(
            tokens_spec,
            P("wide", None),
            P("wide", "seq"),
            P("wide", "seq"),
            tokens_spec,
            matrix_spec,
            matrix_spec,
            matrix_spec,
            matrix_spec,
            rows_spec,
            rows_spec,
            P(None, "wide"),
        ),
        out_specs=(
            tokens_spec,
            tokens_spec,
            matrix_spec,
            matrix_spec,
            matrix_spec,
            matrix_spec,
            rows_spec,
            rows_spec,
            P(None, "wide"),
        ),
        check_vma=False,
    )
```

```python
import functools

import jax
import jax.numpy as jnp
from jax import lax
from jax.experimental import pallas as pl
from jax.experimental.pallas import tpu as pltpu
from jax.sharding import PartitionSpec as P

HEAD_SIZE = 64
PAIR = 2 * HEAD_SIZE
FORWARD_ROWS = 1024
BACKWARD_ROWS = 256
ROW_TILE = 256
FF_CHUNK = 1024

epsilon = 1e-05
masked_bias = -1e30
half = jnp.bfloat16
single = jnp.float32


def estimate(flops, size):
    return pl.CostEstimate(flops=flops // 16, bytes_accessed=size // 16, transcendentals=0)


def contract(left, right, left_dim, right_dim):
    return lax.dot_general(
        left, right, (((left_dim,), (right_dim,)), ((), ())), preferred_element_type=jnp.float32
    )


def first_head_lanes():
    return lax.broadcasted_iota(jnp.int32, (1, PAIR), 1) < HEAD_SIZE


def one_head_of(pair, head):
    lanes = first_head_lanes()
    keep = lanes if head == 0 else jnp.logical_not(lanes)
    return jnp.where(keep, pair, jnp.zeros_like(pair))


def attend_kernel(query_ref, key_ref, value_ref, bias_ref, out_ref, total_ref, *, rows):
    keys = key_ref[...]
    values = value_ref[...]
    scale = jnp.asarray(HEAD_SIZE ** (-0.5), half)
    for start in range(0, keys.shape[0], rows):
        window = pl.ds(start, rows)
        queries = query_ref[window, :] * scale
        bias = bias_ref[:, window]
        attended = []
        for head in range(2):
            scores = contract(keys, one_head_of(queries, head), 1, 1) + bias
            top = jnp.max(scores, axis=0, keepdims=True)
            weights = jnp.exp(scores - top)
            total = jnp.sum(weights, axis=0, keepdims=True)
            mixed = contract(values, weights.astype(half), 0, 0) * (1.0 / total)
            attended.append(mixed[HEAD_SIZE * head : HEAD_SIZE * (head + 1)])
            total_ref[head : head + 1, window] = top + jnp.log(total)
        out_ref[window, :] = jnp.concatenate(attended, 0).T.astype(half)


def attend_forward(packed, bias):
    length = packed.shape[0]
    features = packed.shape[1] // 3
    pairs = features // PAIR
    columns = lambda part: pl.BlockSpec((length, PAIR), lambda i: (0, part * pairs + i))
    return pl.pallas_call(
        functools.partial(attend_kernel, rows=FORWARD_ROWS),
        grid=(pairs,),
        in_specs=[
            columns(0),
            columns(1),
            columns(2),
            pl.BlockSpec((length, length), lambda i: (0, 0)),
        ],
        out_specs=[columns(0), pl.BlockSpec((None, 2, length), lambda i: (i, 0, 0))],
        out_shape=[
            jax.ShapeDtypeStruct((length, features), half),
            jax.ShapeDtypeStruct((pairs, 2, length), single),
        ],
        compiler_params=pltpu.CompilerParams(vmem_limit_bytes=56 << 20),
        cost_estimate=estimate(16 * length * length * features, 8 * length * features),
        name="attend_forward",
    )(packed, packed, packed, bias)


def attend_grad_kernel(
    query_ref,
    key_ref,
    value_ref,
    bias_ref,
    upstream_ref,
    total_ref,
    attended_ref,
    out_ref,
    key_sum,
    value_sum,
    *,
    rows,
):
    pair = pl.program_id(0)
    features = out_ref.shape[1] // 3
    keys = key_ref[...]
    values = value_ref[...]
    scale = HEAD_SIZE ** (-0.5)
    for start in range(0, keys.shape[0], rows):
        window = pl.ds(start, rows)
        queries = query_ref[window, :] * jnp.asarray(scale, half)
        upstream = upstream_ref[window, :]
        product = (upstream.astype(single) * attended_ref[window, :].astype(single)).T
        bias = bias_ref[:, window]
        query_grads, key_grad, value_grad = [], 0.0, 0.0
        for head in range(2):
            head_queries = one_head_of(queries, head)
            head_upstream = one_head_of(upstream, head)
            inner = jnp.sum(
                product[HEAD_SIZE * head : HEAD_SIZE * (head + 1)], axis=0, keepdims=True
            )
            scores = contract(keys, head_queries, 1, 1) + bias
            weights = jnp.exp(scores - total_ref[head : head + 1, window])
            weight_grads = contract(values, head_upstream, 1, 1)
            score_grads = (weights * (weight_grads - inner)).astype(half)
            value_grad = value_grad + contract(weights.astype(half), head_upstream, 1, 0)
            key_grad = key_grad + contract(score_grads, head_queries, 1, 0)
            query_grads.append(
                contract(keys, score_grads, 0, 0)[HEAD_SIZE * head : HEAD_SIZE * (head + 1)]
            )
        out_ref[window, pl.ds(pl.multiple_of(pair * PAIR, PAIR), PAIR)] = (
            jnp.concatenate(query_grads, 0).T * scale
        ).astype(half)
        if start == 0:
            key_sum[...] = key_grad
            value_sum[...] = value_grad
        else:
            key_sum[...] += key_grad
            value_sum[...] += value_grad
    out_ref[:, pl.ds(pl.multiple_of(features + pair * PAIR, PAIR), PAIR)] = key_sum[...].astype(
        half
    )
    out_ref[:, pl.ds(pl.multiple_of(2 * features + pair * PAIR, PAIR), PAIR)] = value_sum[
        ...
    ].astype(half)


def attend_backward(packed, bias, upstream, totals, attended):
    length = packed.shape[0]
    features = packed.shape[1] // 3
    pairs = features // PAIR
    columns = lambda part: pl.BlockSpec((length, PAIR), lambda i: (0, part * pairs + i))
    return pl.pallas_call(
        functools.partial(attend_grad_kernel, rows=BACKWARD_ROWS),
        grid=(pairs,),
        in_specs=[
            columns(0),
            columns(1),
            columns(2),
            pl.BlockSpec((length, length), lambda i: (0, 0)),
            columns(0),
            pl.BlockSpec((None, 2, length), lambda i: (i, 0, 0)),
            columns(0),
        ],
        out_specs=pl.BlockSpec((length, 3 * features), lambda i: (0, 0)),
        out_shape=jax.ShapeDtypeStruct((length, 3 * features), half),
        scratch_shapes=[pltpu.VMEM((length, PAIR), single)] * 2,
        compiler_params=pltpu.CompilerParams(vmem_limit_bytes=56 << 20),
        cost_estimate=estimate(40 * length * length * features, 16 * length * features),
        name="attend_backward",
    )(packed, packed, packed, bias, upstream, totals, attended)


def place_pieces(pieces, out_shape, targets, indices):
    def kernel(index_ref, *refs):
        sources, out_ref, semaphores = refs[: len(pieces)], refs[-2], refs[-1]
        copies = [
            pltpu.make_async_copy(
                source, out_ref.at[target(index_ref)], semaphores.at[number]
            )
            for number, (source, target) in enumerate(zip(sources, targets))
        ]
        for copy in copies:
            copy.start()
        for copy in copies:
            copy.wait()

    size = 2 * 2
    for extent in out_shape:
        size *= extent
    anywhere = pl.BlockSpec(memory_space=pl.ANY)
    return pl.pallas_call(
        kernel,
        in_specs=[pl.BlockSpec(memory_space=pltpu.SMEM)] + [anywhere] * len(pieces),
        out_specs=pl.BlockSpec(memory_space=pltpu.VMEM),
        out_shape=jax.ShapeDtypeStruct(out_shape, pieces[0].dtype),
        scratch_shapes=[pltpu.SemaphoreType.DMA((len(pieces),))],
        compiler_params=pltpu.CompilerParams(vmem_limit_bytes=32 << 20),
        cost_estimate=estimate(0, size),
        name="place_pieces",
    )(indices, *pieces)


def normal_of(hidden):
    center = hidden - jnp.mean(hidden, axis=-1, keepdims=True)
    inverse = lax.rsqrt(jnp.mean(center * center, axis=-1, keepdims=True) + epsilon)
    return center * inverse, inverse


def norm_pull(normal, inverse, gain, upstream):
    scaled = upstream * gain
    slope = jnp.mean(scaled, axis=-1, keepdims=True)
    tilt = jnp.mean(scaled * normal, axis=-1, keepdims=True)
    return inverse * (scaled - slope - normal * tilt)


def column_sum(array):
    return jnp.sum(array, axis=0, keepdims=True)


def tile_of(columns):
    return pl.BlockSpec((ROW_TILE, columns), lambda i: (i, 0))


def resident(shape, *index):
    place = index or (0,) * len(shape)
    return pl.BlockSpec(shape, lambda i: place, pipeline_mode=pl.Buffered(1))


def row_tiled(kernel, name, length, in_specs, out_specs, out_shape, operands, flops):
    size = sum(operand.size * operand.dtype.itemsize for operand in operands)
    size += sum(shape.size * jnp.dtype(shape.dtype).itemsize for shape in out_shape)
    return pl.pallas_call(
        kernel,
        grid=(length // ROW_TILE,),
        in_specs=in_specs,
        out_specs=out_specs,
        out_shape=out_shape,
        compiler_params=pltpu.CompilerParams(vmem_limit_bytes=56 << 20),
        cost_estimate=estimate(flops, size),
        name=name,
    )(*operands)


def project_kernel(hidden_ref, gains_ref, offsets_ref, weight_ref, normed_ref, packed_ref):
    features = hidden_ref.shape[1]
    normal, _ = normal_of(hidden_ref[...])
    normed = (normal * gains_ref[0:1] + offsets_ref[0:1]).astype(half)
    normed_ref[...] = normed
    for part in range(3):
        window = slice(part * features, (part + 1) * features)
        product = contract(normed, weight_ref[:, window], 1, 0)
        if part != 1:
            row = 1 if part == 0 else 2
            product = product + offsets_ref[row : row + 1]
        packed_ref[:, window] = product.astype(half)


def project(hidden, gains, offsets, joined):
    length, features = hidden.shape
    return row_tiled(
        project_kernel,
        "project",
        length,
        [
            tile_of(features),
            resident(gains.shape),
            resident(offsets.shape),
            resident((features, 3 * features)),
        ],
        [tile_of(features), tile_of(3 * features)],
        [
            jax.ShapeDtypeStruct((length, features), half),
            jax.ShapeDtypeStruct((length, 3 * features), half),
        ],
        (hidden, gains, offsets, joined),
        6 * length * features * features,
    )


def feed_kernel(
    attended_ref,
    hidden_ref,
    gains_ref,
    offsets_ref,
    up_bias_ref,
    out_weight_ref,
    up_ref,
    down_ref,
    middle_ref,
    second_ref,
    activated_ref,
    slope_ref,
    result_ref,
):
    hidden_units = up_ref.shape[1]
    middle = hidden_ref[...] + (
        contract(attended_ref[...], out_weight_ref[...], 1, 0) + offsets_ref[3:4]
    )
    middle_ref[...] = middle
    normal, _ = normal_of(middle)
    second = (normal * gains_ref[1:2] + offsets_ref[4:5]).astype(half)
    second_ref[...] = second
    result = middle + offsets_ref[5:6]
    rate = 0.7978845608028654
    for start in range(0, hidden_units, FF_CHUNK):
        window = slice(start, start + FF_CHUNK)
        value = contract(second, up_ref[:, window], 1, 0) + up_bias_ref[:, window]
        square = value * value
        bent = jnp.tanh(value * (rate + (rate * 0.044715) * square))
        opened = 0.5 + 0.5 * bent
        activated = (value * opened).astype(half)
        activated_ref[:, window] = activated
        curve = (value * (0.5 * rate + (1.5 * rate * 0.044715) * square)) * (1.0 - bent * bent)
        slope_ref[:, window] = (opened + curve).astype(half)
        result = result + contract(activated, down_ref[window, :], 1, 0)
    result_ref[...] = result.astype(result_ref.dtype)


def feed(attended, hidden, gains, offsets, up_bias, joined, up, down, result_type):
    length, features = hidden.shape
    units = down.shape[0]
    up_array, up_place = up
    shape = jax.ShapeDtypeStruct
    return row_tiled(
        feed_kernel,
        "feed",
        length,
        [
            tile_of(features),
            tile_of(features),
            resident(gains.shape),
            resident(offsets.shape),
            resident(up_bias.shape),
            resident((features, features), 0, 3),
            resident((features, units), 0, up_place),
            resident(down.shape),
        ],
        [tile_of(features), tile_of(features), tile_of(units), tile_of(units), tile_of(features)],
        [
            shape((length, features), single),
            shape((length, features), half),
            shape((length, units), half),
            shape((length, units), half),
            shape((length, features), result_type),
        ],
        (attended, hidden, gains, offsets, up_bias, joined, up_array, down),
        2 * length * features * (features + 2 * units),
    )


def feed_grad_kernel(
    gradient_ref,
    slope_ref,
    middle_ref,
    gains_ref,
    out_weight_ref,
    up_ref,
    down_ref,
    branch_ref,
    upper_ref,
    middle_grad_ref,
    attention_grad_ref,
    upstream_ref,
    sums_ref,
    unit_sums_ref,
):
    units = up_ref.shape[1]

    @pl.when(pl.program_id(0) == 0)
    def _():
        sums_ref[...] = jnp.zeros_like(sums_ref)
        unit_sums_ref[...] = jnp.zeros_like(unit_sums_ref)

    gradient = gradient_ref[...].astype(single)
    branch = gradient.astype(half)
    branch_ref[...] = branch
    sums_ref[0:1] += column_sum(branch.astype(single))
    second_grad = jnp.zeros(gradient.shape, single)
    for start in range(0, units, FF_CHUNK):
        window = slice(start, start + FF_CHUNK)
        pulled = contract(branch, down_ref[window, :], 1, 1) * slope_ref[:, window].astype(single)
        upper = pulled.astype(half)
        upper_ref[:, window] = upper
        unit_sums_ref[:, window] += column_sum(upper.astype(single))
        second_grad = second_grad + contract(upper, up_ref[:, window], 1, 1)
    normal, inverse = normal_of(middle_ref[...])
    middle_grad = gradient + norm_pull(normal, inverse, gains_ref[1:2], second_grad)
    sums_ref[1:2] += column_sum(second_grad * normal)
    sums_ref[2:3] += column_sum(second_grad)
    middle_grad_ref[...] = middle_grad
    attention_grad = middle_grad.astype(half)
    attention_grad_ref[...] = attention_grad
    sums_ref[3:4] += column_sum(attention_grad.astype(single))
    upstream_ref[...] = contract(attention_grad, out_weight_ref[...], 1, 1).astype(half)


def feed_grad(gradient, slope, middle, gains, joined, up, down):
    up_array, up_place = up
    length, features = middle.shape
    units = down.shape[0]
    shape = jax.ShapeDtypeStruct
    return row_tiled(
        feed_grad_kernel,
        "feed_grad",
        length,
        [
            tile_of(features),
            tile_of(units),
            tile_of(features),
            resident(gains.shape),
            resident((features, features), 0, 3),
            resident((features, units), 0, up_place),
            resident(down.shape),
        ],
        [
            tile_of(features),
            tile_of(units),
            tile_of(features),
            tile_of(features),
            tile_of(features),
            resident((8, features)),
            resident((1, units)),
        ],
        [
            shape((length, features), half),
            shape((length, units), half),
            shape((length, features), single),
            shape((length, features), half),
            shape((length, features), half),
            shape((8, features), single),
            shape((1, units), single),
        ],
        (gradient, slope, middle, gains, joined, up_array, down),
        2 * length * features * (features + 2 * units),
    )


def project_grad_kernel(
    packed_grad_ref, hidden_ref, middle_grad_ref, gains_ref, weight_ref, *out_refs
):
    sums_ref = out_refs[-1]
    features = hidden_ref.shape[1]

    @pl.when(pl.program_id(0) == 0)
    def _():
        sums_ref[...] = jnp.zeros_like(sums_ref)

    packed_grad = packed_grad_ref[...]
    normed_grad = contract(packed_grad, weight_ref[...], 1, 1)
    normal, inverse = normal_of(hidden_ref[...])
    result = middle_grad_ref[...] + norm_pull(normal, inverse, gains_ref[0:1], normed_grad)
    for result_ref in out_refs[:-1]:
        result_ref[...] = result.astype(result_ref.dtype)
    sums_ref[0:1] += column_sum(normed_grad * normal)
    sums_ref[1:2] += column_sum(normed_grad)
    sums_ref[2:3] += column_sum(packed_grad[:, :features].astype(single))
    sums_ref[3:4] += column_sum(packed_grad[:, 2 * features :].astype(single))


def project_grad(packed_grad, hidden, middle_grad, gains, joined, result_types):
    length, features = hidden.shape
    shape = jax.ShapeDtypeStruct
    return row_tiled(
        project_grad_kernel,
        "project_grad",
        length,
        [
            tile_of(3 * features),
            tile_of(features),
            tile_of(features),
            resident(gains.shape),
            resident((features, 3 * features)),
        ],
        [tile_of(features) for _ in result_types] + [resident((8, features))],
        [shape((length, features), result_type) for result_type in result_types]
        + [shape((8, features), single)],
        (packed_grad, hidden, middle_grad, gains, joined),
        6 * length * features * features,
    )


def term_blocks(terms, core, groups, row_unit, by_core):
    pieces = [left.shape[1] // (groups * row_unit) for left, _ in terms]
    widths = [right.shape[1] // (2 if by_core else 1) for _, right in terms]
    total = sum(count * width for count, width in zip(pieces, widths))
    chips = groups // 2
    out_shape = (chips, 2, row_unit, total) if by_core else (groups, row_unit, total)
    outputs = 2 if by_core else 1
    if row_unit % 16:
        columns = []
        for (left, right), count, width in zip(terms, pieces, widths):
            part = contract(left, right, 0, 0).astype(half)
            part = part.reshape(chips, 2, count, row_unit, -1, width).transpose(2, 1, 0, 4, 3, 5)
            columns += [part[piece] for piece in range(count)]
        whole = jnp.concatenate(columns, axis=-1)
        if not by_core:
            return [whole[:, :, 0].swapaxes(0, 1).reshape(out_shape)]
        return [
            lax.dynamic_index_in_dim(whole, which, 0, keepdims=False) for which in (1 - core, core)
        ]
    number = len(terms)

    def kernel(core_ref, *refs):
        sources = refs[: 2 * number]
        outs = refs[2 * number : 2 * number + outputs]
        buffers = refs[2 * number + outputs : 4 * number + outputs]
        semaphores = refs[4 * number + outputs]
        first_core = core_ref[0] == 0
        copies = [
            pltpu.make_async_copy(source, buffer, semaphores.at[index])
            for index, (source, buffer) in enumerate(zip(sources, buffers))
        ]
        for copy in copies:
            copy.start()
        start = 0
        for index, (count, width) in enumerate(zip(pieces, widths)):
            copies[2 * index].wait()
            copies[2 * index + 1].wait()
            left, right = buffers[2 * index], buffers[2 * index + 1]
            rows = groups * row_unit
            step = max(size for size in (768, 640, 512, 384, 256, 128) if width % size == 0)
            held = chips // count
            for turn in range(count):
                turned = left[:, turn * rows : (turn + 1) * rows].T
                some = slice(turn * held, (turn + 1) * held)
                for low in range(0, right.shape[1], step):
                    product = contract(turned, right[:, low : low + step], 1, 0).astype(half)
                    product = product.reshape(held, 2, count, row_unit, step)
                    side, inside = divmod(low, width)
                    for piece in range(count):
                        lanes = start + piece * width + inside
                        lanes = slice(lanes, lanes + step)
                        even, odd = product[:, 0, piece], product[:, 1, piece]
                        if by_core:
                            outs[0][some, side, :, lanes] = jnp.where(first_core, odd, even)
                            outs[1][some, side, :, lanes] = jnp.where(first_core, even, odd)
                        else:
                            for chip in range(held):
                                owner = 2 * (turn * held + chip)
                                outs[0][owner, :, lanes] = even[chip]
                                outs[0][owner + 1, :, lanes] = odd[chip]
            start += count * width

    anywhere = pl.BlockSpec(memory_space=pl.ANY)
    operands = [operand for term in terms for operand in term]
    size = sum(operand.size for operand in operands) * 2
    flops = sum(2 * left.size * right.shape[1] for left, right in terms)
    shape = jax.ShapeDtypeStruct(out_shape, half)
    return pl.pallas_call(
        kernel,
        in_specs=[pl.BlockSpec(memory_space=pltpu.SMEM)] + [anywhere] * len(operands),
        out_specs=[pl.BlockSpec(memory_space=pltpu.VMEM)] * outputs,
        out_shape=[shape] * outputs,
        scratch_shapes=[pltpu.VMEM(operand.shape, half) for operand in operands]
        + [pltpu.SemaphoreType.DMA((len(operands),))],
        compiler_params=pltpu.CompilerParams(vmem_limit_bytes=60 << 20),
        cost_estimate=estimate(flops, size + 2 * outputs * shape.size),
        name="term_blocks",
    )(core.reshape(1).astype(jnp.int32), *operands)


def per_device(
    tokens,
    time_embed,
    segment_ids,
    pad_mask,
    out_grad,
    qkv_weight,
    out_weight,
    up_weight,
    down_weight,
    norm_gains,
    bias_rows,
    up_bias,
):
    layers = qkv_weight.shape[0]
    features = tokens.shape[2]
    groups = lax.axis_size("wide")
    swap = [(0, 1), (1, 0)]

    def whole_sequence(part):
        return lax.all_to_all(part, "seq", split_axis=0, concat_axis=1, tiled=True)[0]

    core = lax.axis_index("wide") & 1
    place = lax.axis_index("seq")
    indices = jnp.stack([core, place]).astype(jnp.int32)
    row_unit = qkv_weight.shape[1]

    def across(bit):
        pairs = [(index, index ^ bit) for index in range(groups)]
        return lambda part: lax.ppermute(part, "wide", pairs)

    def beside_seq(part):
        return lax.ppermute(part, "seq", swap)

    def to_owners(part):
        return lax.psum_scatter(part, "wide", scatter_dimension=0, tiled=True)

    bit_of = lambda bit: (lax.axis_index("wide") >> (bit.bit_length() - 1)) & 1
    running = []

    def begin(steps, finish):
        entry = [steps, finish, next(steps), None]
        running.append(entry)
        return entry

    def launch(main, entries):
        fresh = [entry for entry in entries if entry in running and entry[3] is None]
        if fresh:
            sends = [[sent for sent, _ in entry[2]] for entry in fresh]
            main, sends = lax.optimization_barrier((main, sends))
            for entry, sent in zip(fresh, sends):
                entry[3] = [pass_on(part) for part, (_, pass_on) in zip(sent, entry[2])]
        return main

    def advance(main, *only):
        chosen = [entry for entry in only or list(running) if entry in running]
        main = launch(main, chosen)
        if not chosen:
            return main
        main, flying = lax.optimization_barrier((main, [entry[3] for entry in chosen]))
        for entry, arrived in zip(chosen, flying):
            entry[3] = None
            try:
                entry[2] = entry[0].send(arrived)
            except StopIteration as stop:
                entry[1](stop.value)
                running.remove(entry)
        return launch(main, chosen)

    def side_of(array, which, axis):
        return lax.dynamic_index_in_dim(array, which, axis, keepdims=False)

    chip_bits = [1 << number for number in range(groups.bit_length() - 2, 0, -1)]

    def join(current, received, which):
        lead = current.shape[0]
        joined = place_pieces(
            [current, received],
            (lead, 2) + current.shape[1:],
            [lambda ref: (slice(None), ref[0]), lambda ref: (slice(None), 1 - ref[0])],
            which.reshape(1).astype(jnp.int32),
        )
        return joined.reshape((2 * lead,) + current.shape[1:])

    def gather_columns(shard):
        rows, columns = shard.shape[0], shard.shape[1] // 2
        current = lax.dynamic_slice_in_dim(shard, place * columns, columns, axis=1)[None]
        for bit in chip_bits:
            (received,) = yield [(current, across(bit))]
            current = join(current, received, bit_of(bit))
        (aside,) = yield [(current, beside_seq)]
        passed = yield [(part, across(1)) for part in (current, aside)]

        def target(own_core, own_place):
            def where(ref):
                which_core = ref[0] if own_core else 1 - ref[0]
                which_place = ref[1] if own_place else 1 - ref[1]
                start = pl.multiple_of(which_place * columns, columns)
                return (slice(None), which_core, slice(None), pl.ds(start, columns))

            return where

        return place_pieces(
            [current, aside, *passed],
            (current.shape[0], 2, rows, 2 * columns),
            [target(True, True), target(True, False), target(False, True), target(False, False)],
            indices,
        ).reshape(-1, 2 * columns)

    def gather_rows(shard):
        rows, columns = shard.shape[0] // 2, shard.shape[1]
        current = side_of(shard.reshape(2, rows, columns), place, 0)[None]
        for bit in chip_bits[:-1]:
            (received,) = yield [(current, across(bit))]
            current = join(current, received, bit_of(bit))
        (received,) = yield [(current, beside_seq)]
        current = join(current, received, place).reshape(-1, 2 * rows, columns)
        for bit in chip_bits[-1:] + [1]:
            (received,) = yield [(current, across(bit))]
            current = join(current, received, bit_of(bit))
        return current.reshape(-1, columns)

    my_tokens = whole_sequence(tokens)

    small = jnp.concatenate(
        [norm_gains.reshape(-1), bias_rows.reshape(-1), up_bias.reshape(-1)]
    )
    side = small.reshape(row_unit, -1)
    side_width = side.shape[1]
    side = jnp.pad(side, ((0, 0), (0, -side_width % PAIR)))
    joined_parts = [jnp.concatenate([qkv_weight[0], out_weight[0], side], axis=1)]
    for layer in range(1, layers):
        parts = [qkv_weight[layer], out_weight[layer], up_weight[layer]]
        joined_parts.append(jnp.concatenate(parts, axis=1))
    joined = [lax.all_gather(part, "wide", axis=0, tiled=True) for part in joined_parts]
    downs = {
        layer: lax.all_gather(down_weight[layer], "wide", axis=0, tiled=True)
        for layer in range(1, layers)
    }
    small_whole = joined[0][:, -side.shape[1] :][:, :side_width].reshape(groups, -1)
    cut_gains = norm_gains.size
    cut_rows = cut_gains + bias_rows.size

    def whole_rows(part, count):
        parts = part.reshape(groups, layers, count, -1)
        return parts.transpose(1, 2, 0, 3).reshape(layers, count, -1).astype(single)

    all_gains = whole_rows(small_whole[:, :cut_gains], norm_gains.shape[1])
    all_offsets = whole_rows(small_whole[:, cut_gains:cut_rows], bias_rows.shape[1])
    all_up_bias = whole_rows(small_whole[:, cut_rows:], 1)[:, 0]

    matrices = [None] * layers
    ups = {}
    fetches = [
        begin(gather_columns(up_weight[0]), functools.partial(ups.__setitem__, 0)),
        begin(gather_rows(down_weight[0]), functools.partial(downs.__setitem__, 0)),
    ]
    marks = jnp.stack([segment_ids, pad_mask], axis=2)
    time_embed, marks = advance((time_embed, marks), *fetches)
    marks = whole_sequence(marks)
    for _ in chip_bits[2:]:
        time_embed, marks = advance((time_embed, marks), *fetches)
    doc, pad = marks[:, 0], marks[:, 1]
    positions = jnp.arange(doc.shape[0])
    allowed = (doc[:, None] == doc[None, :]) & (
        (pad[:, None] == 1) | (positions[:, None] == positions[None, :])
    )
    bias = jnp.where(allowed, 0.0, masked_bias)

    my_time = lax.dynamic_index_in_dim(time_embed, place, 0, keepdims=True)
    hidden = my_tokens.astype(single) + my_time
    saved = []
    for layer in range(layers):
        whole = joined[layer]
        gains, offsets = all_gains[layer], all_offsets[layer]
        before = hidden
        normed, packed = project(hidden, gains, offsets, whole)
        if layer == layers - 1:
            packed, out_grad = lax.optimization_barrier((packed, out_grad))
            my_upstream = whole_sequence(out_grad)
        packed = advance(packed, *fetches)
        attended, totals = attend_forward(packed, bias)
        attended = advance(attended, *fetches)
        while running:
            attended = advance(attended, *fetches)
        up = (whole, 4 * features // up_bias.shape[1] // groups) if layer else (ups[0], 0)
        matrices[layer] = (whole, up, downs[layer])
        fetches = []
        middle, second, activated, slope, hidden = feed(
            attended,
            hidden,
            gains,
            offsets,
            all_up_bias[layer][None],
            whole,
            up,
            downs[layer],
            single if layer < layers - 1 else half,
        )
        saved.append((before, normed, packed, totals, attended, middle, second, activated, slope))

    def split_back(result):
        parts = result.reshape(2, -1, features).astype(half)
        return lax.all_to_all(parts, "seq", split_axis=0, concat_axis=0, tiled=True)

    output = split_back(hidden)

    def total_of(addends):
        return functools.reduce(jnp.add, [addend.astype(single) for addend in addends])

    def shares_of(terms, low, high):
        shares, start = [], 0
        for left, right in terms:
            rows, each = [], right.shape[1] // 2
            if high is None:
                each *= 2
            for _ in range(left.shape[1] // (groups * row_unit)):
                window = slice(start, start + each)
                if high is None:
                    rows.append(low[:, window])
                else:
                    rows.append(jnp.concatenate([low[:, window], high[:, window]], axis=1))
                start += each
            shares.append(jnp.concatenate(rows, axis=0))
        return shares

    def scatter_group(terms):
        (whole,) = term_blocks(terms, core, groups, row_unit, False)
        whole = whole.reshape(groups * row_unit, -1)
        (share,) = yield [(whole, to_owners)]
        (received,) = yield [(share, beside_seq)]
        return shares_of(terms, share.astype(single) + received.astype(single), None)

    def reduce_group(terms):
        other, own = term_blocks(terms, core, groups, row_unit, True)
        (received,) = yield [(other, across(1))]
        shape = (2,) * len(chip_bits) + (2, row_unit, own.shape[-1])
        addends = [part.reshape(shape) for part in (own, received)]
        axis = len(chip_bits)
        for bit in [0] + chip_bits[:1:-1]:
            mine, pass_on = (bit_of(bit), across(bit)) if bit else (place, beside_seq)
            sent = total_of([side_of(part, 1 - mine, axis) for part in addends]).astype(half)
            (received,) = yield [(sent, pass_on)]
            addends = [side_of(part, mine, axis) for part in addends] + [received]
            axis -= 1
        far, near = chip_bits[:2]

        def corner(part, bits):
            part = side_of(part, bit_of(far) ^ (1 if bits & far else 0), 0)
            return side_of(part, bit_of(near) ^ (1 if bits & near else 0), 0)

        received = yield [
            (total_of([corner(part, bits) for part in addends]).astype(half), across(bits))
            for bits in (near, far, near | far)
        ]
        addends = [corner(part, 0) for part in addends] + received
        current = total_of(addends).astype(half)
        (received,) = yield [(current, beside_seq)]
        low = jnp.where(place == 0, current, received).astype(single)
        high = jnp.where(place == 0, received, current).astype(single)
        return shares_of(terms, low, high)

    def reduce_small(array):
        parts = [array.reshape((2,) * (len(chip_bits) + 1) + array.shape[1:])]
        pairs = [(2, 1, len(chip_bits) - 1)]
        pairs += [(bit, None, chip_bits.index(bit)) for bit in chip_bits[-2:1:-1]]
        pairs += [(chip_bits[0], chip_bits[1], 0)]
        for high, low, axis in pairs:

            def chosen(bits):
                def pick(part):
                    if low is not None:
                        part = side_of(part, bit_of(low) ^ (1 if bits & low else 0), axis + 1)
                    return side_of(part, bit_of(high) ^ (1 if bits & high else 0), axis)

                return total_of([pick(part) for part in parts])

            masks = [high] if low is None else [low, high, low | high]
            received = yield [(chosen(bits), across(bits)) for bits in masks]
            parts = [chosen(0)] + received
        current = total_of(parts)
        (received,) = yield [(current, beside_seq)]
        return current + received

    weight_grads = [[None] * 4 for _ in range(layers)]

    def begin_group(steps, layer, named):
        def finish(shares):
            for (part, _), share in zip(named, shares):
                weight_grads[layer][part] = share

        return begin(steps([term for _, term in named]), finish)

    gradient = my_upstream
    small_grads = [None] * layers
    held = []
    for layer in range(layers - 1, -1, -1):
        whole, up, down = matrices[layer]
        gains = all_gains[layer]
        hidden, normed, packed, totals, attended, middle, second, activated, slope = saved[layer]
        steps = scatter_group if layer else reduce_group
        branch, upper, middle_grad, attention_grad, upstream, sums, unit_sums = feed_grad(
            gradient, slope, middle, gains, whole, up, down
        )
        named = [(2, (second, upper)), (1, (attended, attention_grad))]
        if layer:
            held.append(begin_group(steps, layer, [(3, (activated, branch))] + named))
            upstream = launch(upstream, held[-1:])
        else:
            upstream = advance(upstream, first_group)
            upper, attention_grad, upstream = lax.optimization_barrier(
                (upper, attention_grad, upstream)
            )
            named = [(2, (second, upper)), (1, (attended, attention_grad))]
            second_group = begin_group(steps, layer, named)
            upstream = launch(upstream, [second_group])
            upstream = advance(upstream, second_group)
            upstream = advance(upstream, *held[:1])
        packed_grad = attend_backward(packed, bias, upstream, totals, attended)
        if layer == layers - 1:
            packed_grad, output = lax.optimization_barrier((packed_grad, output))
            output = output.astype(single)
        named = [(0, (normed, packed_grad))]
        if not layer:
            packed_grad = advance(packed_grad, first_group, second_group, *held[:1])
            last_group = begin_group(steps, layer, named)
            packed_grad = launch(packed_grad, [last_group])
            packed_grad = advance(packed_grad, last_group)
        gradient, *rounded, more_sums = project_grad(
            packed_grad, hidden, middle_grad, gains, whole, (single, half) if layer else (half,)
        )
        if layer == 1:
            below = (saved[0][7], rounded[0])
            first_group = begin_group(reduce_group, 0, [(3, below)])
            gradient = launch(gradient, [first_group])
        if layer:
            held.append(begin_group(steps, layer, named))
            gradient = launch(gradient, held[-1:])
        if layer == 1:
            gradient = advance(gradient, first_group)
        if not layer:
            gradient = advance(gradient, last_group)
        small_grads[layer] = (
            jnp.stack([more_sums[0], sums[1]]),
            jnp.stack([more_sums[1], more_sums[2], more_sums[3], sums[3], sums[2], sums[0]]),
            unit_sums[0],
        )

    def by_owner(parts):
        stacked = jnp.stack(parts)
        stacked = stacked.reshape(layers, -1, groups, stacked.shape[-1] // groups)
        return stacked.transpose(2, 0, 1, 3).reshape(groups, -1)

    owned = jnp.concatenate(
        [by_owner([small_grads[layer][part] for layer in range(layers)]) for part in range(3)],
        axis=1,
    )
    small_result = []
    begin(reduce_small(owned), small_result.append)
    output = launch(output, running[-1:])
    output = advance(output, first_group, second_group, *held)
    input_grad = split_back(gradient)
    while running:
        output = advance(output, last_group)
        output = advance(output, *[entry for entry in running if entry is not last_group])
    owned = small_result[0]
    input_grad = input_grad.astype(single)
    stacked = [
        jnp.stack([weight_grads[layer][part] for layer in range(layers)]) for part in range(4)
    ]
    return (
        output,
        input_grad,
        *stacked,
        owned[:cut_gains].reshape(norm_gains.shape),
        owned[cut_gains:cut_rows].reshape(bias_rows.shape),
        owned[cut_rows:].reshape(up_bias.shape),
    )


def solution(mesh):
    tokens_spec = P("wide", "seq", None)
    matrix_spec = P(None, "wide", None)
    rows_spec = P(None, None, "wide")
    return jax.shard_map(
        per_device,
        mesh=mesh,
        in_specs=(
            tokens_spec,
            P("wide", None),
            P("wide", "seq"),
            P("wide", "seq"),
            tokens_spec,
            matrix_spec,
            matrix_spec,
            matrix_spec,
            matrix_spec,
            rows_spec,
            rows_spec,
            P(None, "wide"),
        ),
        out_specs=(
            tokens_spec,
            tokens_spec,
            matrix_spec,
            matrix_spec,
            matrix_spec,
            matrix_spec,
            rows_spec,
            rows_spec,
            P(None, "wide"),
        ),
        check_vma=False,
    )
```

```python
import functools

import jax
import jax.numpy as jnp
from jax import lax
from jax.experimental import pallas as pl
from jax.experimental.pallas import tpu as pltpu
from jax.sharding import PartitionSpec as P

HEAD_SIZE = 64
PAIR = 2 * HEAD_SIZE
FORWARD_ROWS = 1024
BACKWARD_ROWS = 256
ROW_TILE = 256
FF_CHUNK = 1024

epsilon = 1e-05
masked_bias = -1e30
half = jnp.bfloat16
single = jnp.float32


def estimate(flops, size):
    return pl.CostEstimate(flops=flops // 16, bytes_accessed=size // 16, transcendentals=0)


def contract(left, right, left_dim, right_dim):
    return lax.dot_general(
        left, right, (((left_dim,), (right_dim,)), ((), ())), preferred_element_type=jnp.float32
    )


def first_head_lanes():
    return lax.broadcasted_iota(jnp.int32, (1, PAIR), 1) < HEAD_SIZE


def one_head_of(pair, head):
    lanes = first_head_lanes()
    keep = lanes if head == 0 else jnp.logical_not(lanes)
    return jnp.where(keep, pair, jnp.zeros_like(pair))


def attend_kernel(query_ref, key_ref, value_ref, bias_ref, out_ref, total_ref, *, rows):
    keys = key_ref[...]
    values = value_ref[...]
    scale = jnp.asarray(HEAD_SIZE ** (-0.5), half)
    for start in range(0, keys.shape[0], rows):
        window = pl.ds(start, rows)
        queries = query_ref[window, :] * scale
        bias = bias_ref[:, window]
        attended = []
        for head in range(2):
            scores = contract(keys, one_head_of(queries, head), 1, 1) + bias
            top = jnp.max(scores, axis=0, keepdims=True)
            weights = jnp.exp(scores - top)
            total = jnp.sum(weights, axis=0, keepdims=True)
            mixed = contract(values, weights.astype(half), 0, 0) * (1.0 / total)
            attended.append(mixed[HEAD_SIZE * head : HEAD_SIZE * (head + 1)])
            total_ref[head : head + 1, window] = top + jnp.log(total)
        out_ref[window, :] = jnp.concatenate(attended, 0).T.astype(half)


def attend_forward(packed, bias):
    length = packed.shape[0]
    features = packed.shape[1] // 3
    pairs = features // PAIR
    columns = lambda part: pl.BlockSpec((length, PAIR), lambda i: (0, part * pairs + i))
    return pl.pallas_call(
        functools.partial(attend_kernel, rows=FORWARD_ROWS),
        grid=(pairs,),
        in_specs=[
            columns(0),
            columns(1),
            columns(2),
            pl.BlockSpec((length, length), lambda i: (0, 0)),
        ],
        out_specs=[columns(0), pl.BlockSpec((None, 2, length), lambda i: (i, 0, 0))],
        out_shape=[
            jax.ShapeDtypeStruct((length, features), half),
            jax.ShapeDtypeStruct((pairs, 2, length), single),
        ],
        compiler_params=pltpu.CompilerParams(vmem_limit_bytes=56 << 20),
        cost_estimate=estimate(16 * length * length * features, 8 * length * features),
        name="attend_forward",
    )(packed, packed, packed, bias)


def attend_grad_kernel(
    query_ref,
    key_ref,
    value_ref,
    bias_ref,
    upstream_ref,
    total_ref,
    attended_ref,
    out_ref,
    key_sum,
    value_sum,
    *,
    rows,
):
    pair = pl.program_id(0)
    features = out_ref.shape[1] // 3
    keys = key_ref[...]
    values = value_ref[...]
    scale = HEAD_SIZE ** (-0.5)
    for start in range(0, keys.shape[0], rows):
        window = pl.ds(start, rows)
        queries = query_ref[window, :] * jnp.asarray(scale, half)
        upstream = upstream_ref[window, :]
        product = (upstream.astype(single) * attended_ref[window, :].astype(single)).T
        bias = bias_ref[:, window]
        query_grads, key_grad, value_grad = [], 0.0, 0.0
        for head in range(2):
            head_queries = one_head_of(queries, head)
            head_upstream = one_head_of(upstream, head)
            inner = jnp.sum(
                product[HEAD_SIZE * head : HEAD_SIZE * (head + 1)], axis=0, keepdims=True
            )
            scores = contract(keys, head_queries, 1, 1) + bias
            weights = jnp.exp(scores - total_ref[head : head + 1, window])
            weight_grads = contract(values, head_upstream, 1, 1)
            score_grads = (weights * (weight_grads - inner)).astype(half)
            value_grad = value_grad + contract(weights.astype(half), head_upstream, 1, 0)
            key_grad = key_grad + contract(score_grads, head_queries, 1, 0)
            query_grads.append(
                contract(keys, score_grads, 0, 0)[HEAD_SIZE * head : HEAD_SIZE * (head + 1)]
            )
        out_ref[window, pl.ds(pl.multiple_of(pair * PAIR, PAIR), PAIR)] = (
            jnp.concatenate(query_grads, 0).T * scale
        ).astype(half)
        if start == 0:
            key_sum[...] = key_grad
            value_sum[...] = value_grad
        else:
            key_sum[...] += key_grad
            value_sum[...] += value_grad
    out_ref[:, pl.ds(pl.multiple_of(features + pair * PAIR, PAIR), PAIR)] = key_sum[...].astype(
        half
    )
    out_ref[:, pl.ds(pl.multiple_of(2 * features + pair * PAIR, PAIR), PAIR)] = value_sum[
        ...
    ].astype(half)


def attend_backward(packed, bias, upstream, totals, attended):
    length = packed.shape[0]
    features = packed.shape[1] // 3
    pairs = features // PAIR
    columns = lambda part: pl.BlockSpec((length, PAIR), lambda i: (0, part * pairs + i))
    return pl.pallas_call(
        functools.partial(attend_grad_kernel, rows=BACKWARD_ROWS),
        grid=(pairs,),
        in_specs=[
            columns(0),
            columns(1),
            columns(2),
            pl.BlockSpec((length, length), lambda i: (0, 0)),
            columns(0),
            pl.BlockSpec((None, 2, length), lambda i: (i, 0, 0)),
            columns(0),
        ],
        out_specs=pl.BlockSpec((length, 3 * features), lambda i: (0, 0)),
        out_shape=jax.ShapeDtypeStruct((length, 3 * features), half),
        scratch_shapes=[pltpu.VMEM((length, PAIR), single)] * 2,
        compiler_params=pltpu.CompilerParams(vmem_limit_bytes=56 << 20),
        cost_estimate=estimate(40 * length * length * features, 16 * length * features),
        name="attend_backward",
    )(packed, packed, packed, bias, upstream, totals, attended)


def place_pieces(pieces, out_shape, targets, indices):
    def kernel(index_ref, *refs):
        sources, out_ref, semaphores = refs[: len(pieces)], refs[-2], refs[-1]
        copies = [
            pltpu.make_async_copy(
                source, out_ref.at[target(index_ref)], semaphores.at[number]
            )
            for number, (source, target) in enumerate(zip(sources, targets))
        ]
        for copy in copies:
            copy.start()
        for copy in copies:
            copy.wait()

    size = 2 * 2
    for extent in out_shape:
        size *= extent
    anywhere = pl.BlockSpec(memory_space=pl.ANY)
    return pl.pallas_call(
        kernel,
        in_specs=[pl.BlockSpec(memory_space=pltpu.SMEM)] + [anywhere] * len(pieces),
        out_specs=pl.BlockSpec(memory_space=pltpu.VMEM),
        out_shape=jax.ShapeDtypeStruct(out_shape, pieces[0].dtype),
        scratch_shapes=[pltpu.SemaphoreType.DMA((len(pieces),))],
        compiler_params=pltpu.CompilerParams(vmem_limit_bytes=32 << 20),
        cost_estimate=estimate(0, size),
        name="place_pieces",
    )(indices, *pieces)


def normal_of(hidden):
    center = hidden - jnp.mean(hidden, axis=-1, keepdims=True)
    inverse = lax.rsqrt(jnp.mean(center * center, axis=-1, keepdims=True) + epsilon)
    return center * inverse, inverse


def norm_pull(normal, inverse, gain, upstream):
    scaled = upstream * gain
    slope = jnp.mean(scaled, axis=-1, keepdims=True)
    tilt = jnp.mean(scaled * normal, axis=-1, keepdims=True)
    return inverse * (scaled - slope - normal * tilt)


def column_sum(array):
    return jnp.sum(array, axis=0, keepdims=True)


def tile_of(columns):
    return pl.BlockSpec((ROW_TILE, columns), lambda i: (i, 0))


def resident(shape, *index):
    place = index or (0,) * len(shape)
    return pl.BlockSpec(shape, lambda i: place, pipeline_mode=pl.Buffered(1))


def row_tiled(kernel, name, length, in_specs, out_specs, out_shape, operands, flops):
    size = sum(operand.size * operand.dtype.itemsize for operand in operands)
    size += sum(shape.size * jnp.dtype(shape.dtype).itemsize for shape in out_shape)
    return pl.pallas_call(
        kernel,
        grid=(length // ROW_TILE,),
        in_specs=in_specs,
        out_specs=out_specs,
        out_shape=out_shape,
        compiler_params=pltpu.CompilerParams(vmem_limit_bytes=56 << 20),
        cost_estimate=estimate(flops, size),
        name=name,
    )(*operands)


def project_kernel(hidden_ref, gains_ref, offsets_ref, weight_ref, normed_ref, packed_ref):
    features = hidden_ref.shape[1]
    normal, _ = normal_of(hidden_ref[...])
    normed = (normal * gains_ref[0:1] + offsets_ref[0:1]).astype(half)
    normed_ref[...] = normed
    for part in range(3):
        window = slice(part * features, (part + 1) * features)
        product = contract(normed, weight_ref[:, window], 1, 0)
        if part != 1:
            row = 1 if part == 0 else 2
            product = product + offsets_ref[row : row + 1]
        packed_ref[:, window] = product.astype(half)


def project(hidden, gains, offsets, joined):
    length, features = hidden.shape
    return row_tiled(
        project_kernel,
        "project",
        length,
        [
            tile_of(features),
            resident(gains.shape),
            resident(offsets.shape),
            resident((features, 3 * features)),
        ],
        [tile_of(features), tile_of(3 * features)],
        [
            jax.ShapeDtypeStruct((length, features), half),
            jax.ShapeDtypeStruct((length, 3 * features), half),
        ],
        (hidden, gains, offsets, joined),
        6 * length * features * features,
    )


def feed_kernel(
    attended_ref,
    hidden_ref,
    gains_ref,
    offsets_ref,
    up_bias_ref,
    out_weight_ref,
    up_ref,
    down_ref,
    middle_ref,
    second_ref,
    activated_ref,
    slope_ref,
    result_ref,
):
    hidden_units = up_ref.shape[1]
    middle = hidden_ref[...] + (
        contract(attended_ref[...], out_weight_ref[...], 1, 0) + offsets_ref[3:4]
    )
    middle_ref[...] = middle
    normal, _ = normal_of(middle)
    second = (normal * gains_ref[1:2] + offsets_ref[4:5]).astype(half)
    second_ref[...] = second
    result = middle + offsets_ref[5:6]
    rate = 0.7978845608028654
    for start in range(0, hidden_units, FF_CHUNK):
        window = slice(start, start + FF_CHUNK)
        value = contract(second, up_ref[:, window], 1, 0) + up_bias_ref[:, window]
        square = value * value
        bent = jnp.tanh(value * (rate + (rate * 0.044715) * square))
        opened = 0.5 + 0.5 * bent
        activated = (value * opened).astype(half)
        activated_ref[:, window] = activated
        curve = (value * (0.5 * rate + (1.5 * rate * 0.044715) * square)) * (1.0 - bent * bent)
        slope_ref[:, window] = (opened + curve).astype(half)
        result = result + contract(activated, down_ref[window, :], 1, 0)
    result_ref[...] = result.astype(result_ref.dtype)


def feed(attended, hidden, gains, offsets, up_bias, joined, up, down, result_type):
    length, features = hidden.shape
    units = down.shape[0]
    up_array, up_place = up
    shape = jax.ShapeDtypeStruct
    return row_tiled(
        feed_kernel,
        "feed",
        length,
        [
            tile_of(features),
            tile_of(features),
            resident(gains.shape),
            resident(offsets.shape),
            resident(up_bias.shape),
            resident((features, features), 0, 3),
            resident((features, units), 0, up_place),
            resident(down.shape),
        ],
        [tile_of(features), tile_of(features), tile_of(units), tile_of(units), tile_of(features)],
        [
            shape((length, features), single),
            shape((length, features), half),
            shape((length, units), half),
            shape((length, units), half),
            shape((length, features), result_type),
        ],
        (attended, hidden, gains, offsets, up_bias, joined, up_array, down),
        2 * length * features * (features + 2 * units),
    )


def feed_grad_kernel(
    gradient_ref,
    slope_ref,
    middle_ref,
    gains_ref,
    out_weight_ref,
    up_ref,
    down_ref,
    branch_ref,
    upper_ref,
    middle_grad_ref,
    attention_grad_ref,
    upstream_ref,
    sums_ref,
    unit_sums_ref,
):
    units = up_ref.shape[1]

    @pl.when(pl.program_id(0) == 0)
    def _():
        sums_ref[...] = jnp.zeros_like(sums_ref)
        unit_sums_ref[...] = jnp.zeros_like(unit_sums_ref)

    gradient = gradient_ref[...].astype(single)
    branch = gradient.astype(half)
    branch_ref[...] = branch
    sums_ref[0:1] += column_sum(branch.astype(single))
    second_grad = jnp.zeros(gradient.shape, single)
    for start in range(0, units, FF_CHUNK):
        window = slice(start, start + FF_CHUNK)
        pulled = contract(branch, down_ref[window, :], 1, 1) * slope_ref[:, window].astype(single)
        upper = pulled.astype(half)
        upper_ref[:, window] = upper
        unit_sums_ref[:, window] += column_sum(upper.astype(single))
        second_grad = second_grad + contract(upper, up_ref[:, window], 1, 1)
    normal, inverse = normal_of(middle_ref[...])
    middle_grad = gradient + norm_pull(normal, inverse, gains_ref[1:2], second_grad)
    sums_ref[1:2] += column_sum(second_grad * normal)
    sums_ref[2:3] += column_sum(second_grad)
    middle_grad_ref[...] = middle_grad
    attention_grad = middle_grad.astype(half)
    attention_grad_ref[...] = attention_grad
    sums_ref[3:4] += column_sum(attention_grad.astype(single))
    upstream_ref[...] = contract(attention_grad, out_weight_ref[...], 1, 1).astype(half)


def feed_grad(gradient, slope, middle, gains, joined, up, down):
    up_array, up_place = up
    length, features = middle.shape
    units = down.shape[0]
    shape = jax.ShapeDtypeStruct
    return row_tiled(
        feed_grad_kernel,
        "feed_grad",
        length,
        [
            tile_of(features),
            tile_of(units),
            tile_of(features),
            resident(gains.shape),
            resident((features, features), 0, 3),
            resident((features, units), 0, up_place),
            resident(down.shape),
        ],
        [
            tile_of(features),
            tile_of(units),
            tile_of(features),
            tile_of(features),
            tile_of(features),
            resident((8, features)),
            resident((1, units)),
        ],
        [
            shape((length, features), half),
            shape((length, units), half),
            shape((length, features), single),
            shape((length, features), half),
            shape((length, features), half),
            shape((8, features), single),
            shape((1, units), single),
        ],
        (gradient, slope, middle, gains, joined, up_array, down),
        2 * length * features * (features + 2 * units),
    )


def project_grad_kernel(
    packed_grad_ref, hidden_ref, middle_grad_ref, gains_ref, weight_ref, *out_refs
):
    sums_ref = out_refs[-1]
    features = hidden_ref.shape[1]

    @pl.when(pl.program_id(0) == 0)
    def _():
        sums_ref[...] = jnp.zeros_like(sums_ref)

    packed_grad = packed_grad_ref[...]
    normed_grad = contract(packed_grad, weight_ref[...], 1, 1)
    normal, inverse = normal_of(hidden_ref[...])
    result = middle_grad_ref[...] + norm_pull(normal, inverse, gains_ref[0:1], normed_grad)
    for result_ref in out_refs[:-1]:
        result_ref[...] = result.astype(result_ref.dtype)
    sums_ref[0:1] += column_sum(normed_grad * normal)
    sums_ref[1:2] += column_sum(normed_grad)
    sums_ref[2:3] += column_sum(packed_grad[:, :features].astype(single))
    sums_ref[3:4] += column_sum(packed_grad[:, 2 * features :].astype(single))


def project_grad(packed_grad, hidden, middle_grad, gains, joined, result_types):
    length, features = hidden.shape
    shape = jax.ShapeDtypeStruct
    return row_tiled(
        project_grad_kernel,
        "project_grad",
        length,
        [
            tile_of(3 * features),
            tile_of(features),
            tile_of(features),
            resident(gains.shape),
            resident((features, 3 * features)),
        ],
        [tile_of(features) for _ in result_types] + [resident((8, features))],
        [shape((length, features), result_type) for result_type in result_types]
        + [shape((8, features), single)],
        (packed_grad, hidden, middle_grad, gains, joined),
        6 * length * features * features,
    )


def term_blocks(terms, core, groups, row_unit, by_core):
    pieces = [left.shape[1] // (groups * row_unit) for left, _ in terms]
    widths = [right.shape[1] // (2 if by_core else 1) for _, right in terms]
    total = sum(count * width for count, width in zip(pieces, widths))
    chips = groups // 2
    out_shape = (chips, 2, row_unit, total) if by_core else (groups, row_unit, total)
    outputs = 2 if by_core else 1
    if row_unit % 16:
        columns = []
        for (left, right), count, width in zip(terms, pieces, widths):
            part = contract(left, right, 0, 0).astype(half)
            part = part.reshape(chips, 2, count, row_unit, -1, width).transpose(2, 1, 0, 4, 3, 5)
            columns += [part[piece] for piece in range(count)]
        whole = jnp.concatenate(columns, axis=-1)
        if not by_core:
            return [whole[:, :, 0].swapaxes(0, 1).reshape(out_shape)]
        return [
            lax.dynamic_index_in_dim(whole, which, 0, keepdims=False) for which in (1 - core, core)
        ]
    number = len(terms)

    def kernel(core_ref, *refs):
        sources = refs[: 2 * number]
        outs = refs[2 * number : 2 * number + outputs]
        buffers = refs[2 * number + outputs : 4 * number + outputs]
        semaphores = refs[4 * number + outputs]
        first_core = core_ref[0] == 0
        copies = [
            pltpu.make_async_copy(source, buffer, semaphores.at[index])
            for index, (source, buffer) in enumerate(zip(sources, buffers))
        ]
        for copy in copies:
            copy.start()
        start = 0
        for index, (count, width) in enumerate(zip(pieces, widths)):
            copies[2 * index].wait()
            copies[2 * index + 1].wait()
            left, right = buffers[2 * index], buffers[2 * index + 1]
            rows = groups * row_unit
            step = max(size for size in (768, 640, 512, 384, 256, 128) if width % size == 0)
            held = chips // count
            for turn in range(count):
                turned = left[:, turn * rows : (turn + 1) * rows].T
                some = slice(turn * held, (turn + 1) * held)
                for low in range(0, right.shape[1], step):
                    product = contract(turned, right[:, low : low + step], 1, 0).astype(half)
                    product = product.reshape(held, 2, count, row_unit, step)
                    side, inside = divmod(low, width)
                    for piece in range(count):
                        lanes = start + piece * width + inside
                        lanes = slice(lanes, lanes + step)
                        even, odd = product[:, 0, piece], product[:, 1, piece]
                        if by_core:
                            outs[0][some, side, :, lanes] = jnp.where(first_core, odd, even)
                            outs[1][some, side, :, lanes] = jnp.where(first_core, even, odd)
                        else:
                            for chip in range(held):
                                owner = 2 * (turn * held + chip)
                                outs[0][owner, :, lanes] = even[chip]
                                outs[0][owner + 1, :, lanes] = odd[chip]
            start += count * width

    anywhere = pl.BlockSpec(memory_space=pl.ANY)
    operands = [operand for term in terms for operand in term]
    size = sum(operand.size for operand in operands) * 2
    flops = sum(2 * left.size * right.shape[1] for left, right in terms)
    shape = jax.ShapeDtypeStruct(out_shape, half)
    return pl.pallas_call(
        kernel,
        in_specs=[pl.BlockSpec(memory_space=pltpu.SMEM)] + [anywhere] * len(operands),
        out_specs=[pl.BlockSpec(memory_space=pltpu.VMEM)] * outputs,
        out_shape=[shape] * outputs,
        scratch_shapes=[pltpu.VMEM(operand.shape, half) for operand in operands]
        + [pltpu.SemaphoreType.DMA((len(operands),))],
        compiler_params=pltpu.CompilerParams(vmem_limit_bytes=60 << 20),
        cost_estimate=estimate(flops, size + 2 * outputs * shape.size),
        name="term_blocks",
    )(core.reshape(1).astype(jnp.int32), *operands)


def per_device(
    tokens,
    time_embed,
    segment_ids,
    pad_mask,
    out_grad,
    qkv_weight,
    out_weight,
    up_weight,
    down_weight,
    norm_gains,
    bias_rows,
    up_bias,
):
    layers = qkv_weight.shape[0]
    features = tokens.shape[2]
    groups = lax.axis_size("wide")
    swap = [(0, 1), (1, 0)]

    def whole_sequence(part):
        return lax.all_to_all(part, "seq", split_axis=0, concat_axis=1, tiled=True)[0]

    core = lax.axis_index("wide") & 1
    place = lax.axis_index("seq")
    indices = jnp.stack([core, place]).astype(jnp.int32)
    row_unit = qkv_weight.shape[1]

    def across(bit):
        pairs = [(index, index ^ bit) for index in range(groups)]
        return lambda part: lax.ppermute(part, "wide", pairs)

    def beside_seq(part):
        return lax.ppermute(part, "seq", swap)

    def to_owners(part):
        return lax.psum_scatter(part, "wide", scatter_dimension=0, tiled=True)

    bit_of = lambda bit: (lax.axis_index("wide") >> (bit.bit_length() - 1)) & 1
    running = []

    def begin(steps, finish):
        entry = [steps, finish, next(steps), None]
        running.append(entry)
        return entry

    def launch(main, entries):
        fresh = [entry for entry in entries if entry in running and entry[3] is None]
        if fresh:
            sends = [[sent for sent, _ in entry[2]] for entry in fresh]
            main, sends = lax.optimization_barrier((main, sends))
            for entry, sent in zip(fresh, sends):
                entry[3] = [pass_on(part) for part, (_, pass_on) in zip(sent, entry[2])]
        return main

    def advance(main, *only):
        chosen = [entry for entry in only or list(running) if entry in running]
        main = launch(main, chosen)
        if not chosen:
            return main
        main, flying = lax.optimization_barrier((main, [entry[3] for entry in chosen]))
        for entry, arrived in zip(chosen, flying):
            entry[3] = None
            try:
                entry[2] = entry[0].send(arrived)
            except StopIteration as stop:
                entry[1](stop.value)
                running.remove(entry)
        return launch(main, chosen)

    def side_of(array, which, axis):
        return lax.dynamic_index_in_dim(array, which, axis, keepdims=False)

    chip_bits = [1 << number for number in range(groups.bit_length() - 2, 0, -1)]

    def join(current, received, which):
        lead = current.shape[0]
        joined = place_pieces(
            [current, received],
            (lead, 2) + current.shape[1:],
            [lambda ref: (slice(None), ref[0]), lambda ref: (slice(None), 1 - ref[0])],
            which.reshape(1).astype(jnp.int32),
        )
        return joined.reshape((2 * lead,) + current.shape[1:])

    def gather_columns(shard):
        rows, columns = shard.shape[0], shard.shape[1] // 2
        current = lax.dynamic_slice_in_dim(shard, place * columns, columns, axis=1)[None]
        for bit in chip_bits:
            (received,) = yield [(current, across(bit))]
            current = join(current, received, bit_of(bit))
        (aside,) = yield [(current, beside_seq)]
        passed = yield [(part, across(1)) for part in (current, aside)]

        def target(own_core, own_place):
            def where(ref):
                which_core = ref[0] if own_core else 1 - ref[0]
                which_place = ref[1] if own_place else 1 - ref[1]
                start = pl.multiple_of(which_place * columns, columns)
                return (slice(None), which_core, slice(None), pl.ds(start, columns))

            return where

        return place_pieces(
            [current, aside, *passed],
            (current.shape[0], 2, rows, 2 * columns),
            [target(True, True), target(True, False), target(False, True), target(False, False)],
            indices,
        ).reshape(-1, 2 * columns)

    def gather_rows(shard):
        rows, columns = shard.shape[0] // 2, shard.shape[1]
        current = side_of(shard.reshape(2, rows, columns), place, 0)[None]
        for bit in chip_bits[:-1]:
            (received,) = yield [(current, across(bit))]
            current = join(current, received, bit_of(bit))
        (received,) = yield [(current, beside_seq)]
        current = join(current, received, place).reshape(-1, 2 * rows, columns)
        for bit in chip_bits[-1:] + [1]:
            (received,) = yield [(current, across(bit))]
            current = join(current, received, bit_of(bit))
        return current.reshape(-1, columns)

    marks = whole_sequence(jnp.stack([segment_ids, pad_mask], axis=2))
    tokens, marks = lax.optimization_barrier((tokens, marks))
    my_tokens = whole_sequence(tokens)

    small = jnp.concatenate(
        [norm_gains.reshape(-1), bias_rows.reshape(-1), up_bias.reshape(-1)]
    )
    side = small.reshape(row_unit, -1)
    side_width = side.shape[1]
    side = jnp.pad(side, ((0, 0), (0, -side_width % PAIR)))
    joined_parts = [jnp.concatenate([qkv_weight[0], out_weight[0], side], axis=1)]
    for layer in range(1, layers):
        parts = [qkv_weight[layer], out_weight[layer], up_weight[layer]]
        joined_parts.append(jnp.concatenate(parts, axis=1))
    joined = [lax.all_gather(part, "wide", axis=0, tiled=True) for part in joined_parts]
    downs = {
        layer: lax.all_gather(down_weight[layer], "wide", axis=0, tiled=True)
        for layer in range(1, layers)
    }
    small_whole = joined[0][:, -side.shape[1] :][:, :side_width].reshape(groups, -1)
    cut_gains = norm_gains.size
    cut_rows = cut_gains + bias_rows.size

    def whole_rows(part, count):
        parts = part.reshape(groups, layers, count, -1)
        return parts.transpose(1, 2, 0, 3).reshape(layers, count, -1).astype(single)

    all_gains = whole_rows(small_whole[:, :cut_gains], norm_gains.shape[1])
    all_offsets = whole_rows(small_whole[:, cut_gains:cut_rows], bias_rows.shape[1])
    all_up_bias = whole_rows(small_whole[:, cut_rows:], 1)[:, 0]

    matrices = [None] * layers
    ups = {}
    fetches = [
        begin(gather_columns(up_weight[0]), functools.partial(ups.__setitem__, 0)),
        begin(gather_rows(down_weight[0]), functools.partial(downs.__setitem__, 0)),
    ]
    for _ in chip_bits[1:]:
        time_embed = advance(time_embed, *fetches)
    doc, pad = marks[:, 0], marks[:, 1]
    positions = jnp.arange(doc.shape[0])
    allowed = (doc[:, None] == doc[None, :]) & (
        (pad[:, None] == 1) | (positions[:, None] == positions[None, :])
    )
    bias = jnp.where(allowed, 0.0, masked_bias)

    my_time = lax.dynamic_index_in_dim(time_embed, place, 0, keepdims=True)
    hidden = my_tokens.astype(single) + my_time
    saved = []
    for layer in range(layers):
        whole = joined[layer]
        gains, offsets = all_gains[layer], all_offsets[layer]
        before = hidden
        normed, packed = project(hidden, gains, offsets, whole)
        if layer == layers - 1:
            packed, out_grad = lax.optimization_barrier((packed, out_grad))
            my_upstream = whole_sequence(out_grad)
        packed = advance(packed, *fetches)
        attended, totals = attend_forward(packed, bias)
        attended = advance(attended, *fetches)
        while running:
            attended = advance(attended, *fetches)
        up = (whole, 4 * features // up_bias.shape[1] // groups) if layer else (ups[0], 0)
        matrices[layer] = (whole, up, downs[layer])
        fetches = []
        middle, second, activated, slope, hidden = feed(
            attended,
            hidden,
            gains,
            offsets,
            all_up_bias[layer][None],
            whole,
            up,
            downs[layer],
            single if layer < layers - 1 else half,
        )
        saved.append((before, normed, packed, totals, attended, middle, second, activated, slope))

    def split_back(result):
        parts = result.reshape(2, -1, features).astype(half)
        return lax.all_to_all(parts, "seq", split_axis=0, concat_axis=0, tiled=True)

    output = split_back(hidden)

    def total_of(addends):
        return functools.reduce(jnp.add, [addend.astype(single) for addend in addends])

    def shares_of(terms, low, high):
        shares, start = [], 0
        for left, right in terms:
            rows, each = [], right.shape[1] // 2
            if high is None:
                each *= 2
            for _ in range(left.shape[1] // (groups * row_unit)):
                window = slice(start, start + each)
                if high is None:
                    rows.append(low[:, window])
                else:
                    rows.append(jnp.concatenate([low[:, window], high[:, window]], axis=1))
                start += each
            shares.append(jnp.concatenate(rows, axis=0))
        return shares

    def scatter_group(terms):
        (whole,) = term_blocks(terms, core, groups, row_unit, False)
        whole = whole.reshape(groups * row_unit, -1)
        (share,) = yield [(whole, to_owners)]
        (received,) = yield [(share, beside_seq)]
        return shares_of(terms, share.astype(single) + received.astype(single), None)

    def reduce_group(terms):
        other, own = term_blocks(terms, core, groups, row_unit, True)
        (received,) = yield [(other, across(1))]
        shape = (2,) * len(chip_bits) + (2, row_unit, own.shape[-1])
        addends = [part.reshape(shape) for part in (own, received)]
        axis = len(chip_bits)
        for bit in [0] + chip_bits[:1:-1]:
            mine, pass_on = (bit_of(bit), across(bit)) if bit else (place, beside_seq)
            sent = total_of([side_of(part, 1 - mine, axis) for part in addends]).astype(half)
            (received,) = yield [(sent, pass_on)]
            addends = [side_of(part, mine, axis) for part in addends] + [received]
            axis -= 1
        far, near = chip_bits[:2]

        def corner(part, bits):
            part = side_of(part, bit_of(far) ^ (1 if bits & far else 0), 0)
            return side_of(part, bit_of(near) ^ (1 if bits & near else 0), 0)

        received = yield [
            (total_of([corner(part, bits) for part in addends]).astype(half), across(bits))
            for bits in (near, far, near | far)
        ]
        addends = [corner(part, 0) for part in addends] + received
        current = total_of(addends).astype(half)
        (received,) = yield [(current, beside_seq)]
        low = jnp.where(place == 0, current, received).astype(single)
        high = jnp.where(place == 0, received, current).astype(single)
        return shares_of(terms, low, high)

    def reduce_small(array):
        parts = [array.reshape((2,) * (len(chip_bits) + 1) + array.shape[1:])]
        pairs = [(2, 1, len(chip_bits) - 1)]
        pairs += [(bit, None, chip_bits.index(bit)) for bit in chip_bits[-2:1:-1]]
        pairs += [(chip_bits[0], chip_bits[1], 0)]
        for high, low, axis in pairs:

            def chosen(bits):
                def pick(part):
                    if low is not None:
                        part = side_of(part, bit_of(low) ^ (1 if bits & low else 0), axis + 1)
                    return side_of(part, bit_of(high) ^ (1 if bits & high else 0), axis)

                return total_of([pick(part) for part in parts])

            masks = [high] if low is None else [low, high, low | high]
            received = yield [(chosen(bits), across(bits)) for bits in masks]
            parts = [chosen(0)] + received
        current = total_of(parts)
        (received,) = yield [(current, beside_seq)]
        return current + received

    weight_grads = [[None] * 4 for _ in range(layers)]

    def begin_group(steps, layer, named):
        def finish(shares):
            for (part, _), share in zip(named, shares):
                weight_grads[layer][part] = share

        return begin(steps([term for _, term in named]), finish)

    gradient = my_upstream
    small_grads = [None] * layers
    held = []
    for layer in range(layers - 1, -1, -1):
        whole, up, down = matrices[layer]
        gains = all_gains[layer]
        hidden, normed, packed, totals, attended, middle, second, activated, slope = saved[layer]
        steps = scatter_group if layer else reduce_group
        branch, upper, middle_grad, attention_grad, upstream, sums, unit_sums = feed_grad(
            gradient, slope, middle, gains, whole, up, down
        )
        named = [(2, (second, upper)), (1, (attended, attention_grad))]
        if layer:
            held.append(begin_group(steps, layer, [(3, (activated, branch))] + named))
            upstream = launch(upstream, held[-1:])
        else:
            upstream = advance(upstream, first_group)
            upper, attention_grad, upstream = lax.optimization_barrier(
                (upper, attention_grad, upstream)
            )
            named = [(2, (second, upper)), (1, (attended, attention_grad))]
            second_group = begin_group(steps, layer, named)
            upstream = launch(upstream, [second_group])
            upstream = advance(upstream, second_group)
            upstream = advance(upstream, *held[:1])
        packed_grad = attend_backward(packed, bias, upstream, totals, attended)
        if layer == layers - 1:
            packed_grad, output = lax.optimization_barrier((packed_grad, output))
            output = output.astype(single)
        named = [(0, (normed, packed_grad))]
        if not layer:
            packed_grad = advance(packed_grad, first_group, second_group, *held[:1])
            last_group = begin_group(steps, layer, named)
            packed_grad = launch(packed_grad, [last_group])
            packed_grad = advance(packed_grad, last_group)
        gradient, *rounded, more_sums = project_grad(
            packed_grad, hidden, middle_grad, gains, whole, (single, half) if layer else (half,)
        )
        if layer == 1:
            below = (saved[0][7], rounded[0])
            first_group = begin_group(reduce_group, 0, [(3, below)])
            gradient = launch(gradient, [first_group])
        if layer:
            held.append(begin_group(steps, layer, named))
            gradient = launch(gradient, held[-1:])
        if layer == 1:
            gradient = advance(gradient, first_group)
        if not layer:
            gradient = advance(gradient, last_group)
        small_grads[layer] = (
            jnp.stack([more_sums[0], sums[1]]),
            jnp.stack([more_sums[1], more_sums[2], more_sums[3], sums[3], sums[2], sums[0]]),
            unit_sums[0],
        )

    def by_owner(parts):
        stacked = jnp.stack(parts)
        stacked = stacked.reshape(layers, -1, groups, stacked.shape[-1] // groups)
        return stacked.transpose(2, 0, 1, 3).reshape(groups, -1)

    owned = jnp.concatenate(
        [by_owner([small_grads[layer][part] for layer in range(layers)]) for part in range(3)],
        axis=1,
    )
    small_result = []
    begin(reduce_small(owned), small_result.append)
    output = launch(output, running[-1:])
    output = advance(output, first_group, second_group, *held)
    input_grad = split_back(gradient)
    while running:
        output = advance(output, last_group)
        output = advance(output, *[entry for entry in running if entry is not last_group])
    owned = small_result[0]
    input_grad = input_grad.astype(single)
    stacked = [
        jnp.stack([weight_grads[layer][part] for layer in range(layers)]) for part in range(4)
    ]
    return (
        output,
        input_grad,
        *stacked,
        owned[:cut_gains].reshape(norm_gains.shape),
        owned[cut_gains:cut_rows].reshape(bias_rows.shape),
        owned[cut_rows:].reshape(up_bias.shape),
    )


def solution(mesh):
    tokens_spec = P("wide", "seq", None)
    matrix_spec = P(None, "wide", None)
    rows_spec = P(None, None, "wide")
    return jax.shard_map(
        per_device,
        mesh=mesh,
        in_specs=(
            tokens_spec,
            P("wide", None),
            P("wide", "seq"),
            P("wide", "seq"),
            tokens_spec,
            matrix_spec,
            matrix_spec,
            matrix_spec,
            matrix_spec,
            rows_spec,
            rows_spec,
            P(None, "wide"),
        ),
        out_specs=(
            tokens_spec,
            tokens_spec,
            matrix_spec,
            matrix_spec,
            matrix_spec,
            matrix_spec,
            rows_spec,
            rows_spec,
            P(None, "wide"),
        ),
        check_vma=False,
    )
```

```python
import functools

import jax
import jax.numpy as jnp
from jax import lax
from jax.experimental import pallas as pl
from jax.experimental.pallas import tpu as pltpu
from jax.sharding import PartitionSpec as P

HEAD_SIZE = 64
PAIR = 2 * HEAD_SIZE
FORWARD_ROWS = 512
BACKWARD_ROWS = 256
ROW_TILE = 256
FF_CHUNK = 1024

epsilon = 1e-05
masked_bias = -1e30
half = jnp.bfloat16
single = jnp.float32


def estimate(flops, size):
    return pl.CostEstimate(flops=flops // 16, bytes_accessed=size // 16, transcendentals=0)


def contract(left, right, left_dim, right_dim):
    return lax.dot_general(
        left, right, (((left_dim,), (right_dim,)), ((), ())), preferred_element_type=jnp.float32
    )


def first_head_lanes():
    return lax.broadcasted_iota(jnp.int32, (1, PAIR), 1) < HEAD_SIZE


def one_head_of(pair, head):
    lanes = first_head_lanes()
    keep = lanes if head == 0 else jnp.logical_not(lanes)
    return jnp.where(keep, pair, jnp.zeros_like(pair))


def attend_kernel(query_ref, key_ref, value_ref, bias_ref, out_ref, total_ref, *, rows):
    keys = key_ref[...]
    values = value_ref[...]
    scale = jnp.asarray(HEAD_SIZE ** (-0.5), half)
    for start in range(0, keys.shape[0], rows):
        window = pl.ds(start, rows)
        queries = query_ref[window, :] * scale
        bias = bias_ref[:, window]
        attended = []
        for head in range(2):
            scores = contract(keys, one_head_of(queries, head), 1, 1) + bias
            top = jnp.max(scores, axis=0, keepdims=True)
            weights = jnp.exp(scores - top)
            total = jnp.sum(weights, axis=0, keepdims=True)
            mixed = contract(values, weights.astype(half), 0, 0) * (1.0 / total)
            attended.append(mixed[HEAD_SIZE * head : HEAD_SIZE * (head + 1)])
            total_ref[head : head + 1, window] = top + jnp.log(total)
        out_ref[window, :] = jnp.concatenate(attended, 0).T.astype(half)


def attend_forward(packed, bias):
    length = packed.shape[0]
    features = packed.shape[1] // 3
    pairs = features // PAIR
    columns = lambda part: pl.BlockSpec((length, PAIR), lambda i: (0, part * pairs + i))
    return pl.pallas_call(
        functools.partial(attend_kernel, rows=FORWARD_ROWS),
        grid=(pairs,),
        in_specs=[
            columns(0),
            columns(1),
            columns(2),
            pl.BlockSpec((length, length), lambda i: (0, 0)),
        ],
        out_specs=[columns(0), pl.BlockSpec((None, 2, length), lambda i: (i, 0, 0))],
        out_shape=[
            jax.ShapeDtypeStruct((length, features), half),
            jax.ShapeDtypeStruct((pairs, 2, length), single),
        ],
        compiler_params=pltpu.CompilerParams(vmem_limit_bytes=56 << 20),
        cost_estimate=estimate(16 * length * length * features, 8 * length * features),
        name="attend_forward",
    )(packed, packed, packed, bias)


def attend_grad_kernel(
    query_ref,
    key_ref,
    value_ref,
    bias_ref,
    upstream_ref,
    total_ref,
    attended_ref,
    out_ref,
    key_sum,
    value_sum,
    *,
    rows,
):
    pair = pl.program_id(0)
    features = out_ref.shape[1] // 3
    keys = key_ref[...]
    values = value_ref[...]
    scale = HEAD_SIZE ** (-0.5)
    for start in range(0, keys.shape[0], rows):
        window = pl.ds(start, rows)
        queries = query_ref[window, :] * jnp.asarray(scale, half)
        upstream = upstream_ref[window, :]
        product = (upstream.astype(single) * attended_ref[window, :].astype(single)).T
        bias = bias_ref[:, window]
        query_grads, key_grad, value_grad = [], 0.0, 0.0
        for head in range(2):
            head_queries = one_head_of(queries, head)
            head_upstream = one_head_of(upstream, head)
            inner = jnp.sum(
                product[HEAD_SIZE * head : HEAD_SIZE * (head + 1)], axis=0, keepdims=True
            )
            scores = contract(keys, head_queries, 1, 1) + bias
            weights = jnp.exp(scores - total_ref[head : head + 1, window])
            weight_grads = contract(values, head_upstream, 1, 1)
            score_grads = (weights * (weight_grads - inner)).astype(half)
            value_grad = value_grad + contract(weights.astype(half), head_upstream, 1, 0)
            key_grad = key_grad + contract(score_grads, head_queries, 1, 0)
            query_grads.append(
                contract(keys, score_grads, 0, 0)[HEAD_SIZE * head : HEAD_SIZE * (head + 1)]
            )
        out_ref[window, pl.ds(pl.multiple_of(pair * PAIR, PAIR), PAIR)] = (
            jnp.concatenate(query_grads, 0).T * scale
        ).astype(half)
        if start == 0:
            key_sum[...] = key_grad
            value_sum[...] = value_grad
        else:
            key_sum[...] += key_grad
            value_sum[...] += value_grad
    out_ref[:, pl.ds(pl.multiple_of(features + pair * PAIR, PAIR), PAIR)] = key_sum[...].astype(
        half
    )
    out_ref[:, pl.ds(pl.multiple_of(2 * features + pair * PAIR, PAIR), PAIR)] = value_sum[
        ...
    ].astype(half)


def attend_backward(packed, bias, upstream, totals, attended):
    length = packed.shape[0]
    features = packed.shape[1] // 3
    pairs = features // PAIR
    columns = lambda part: pl.BlockSpec((length, PAIR), lambda i: (0, part * pairs + i))
    return pl.pallas_call(
        functools.partial(attend_grad_kernel, rows=BACKWARD_ROWS),
        grid=(pairs,),
        in_specs=[
            columns(0),
            columns(1),
            columns(2),
            pl.BlockSpec((length, length), lambda i: (0, 0)),
            columns(0),
            pl.BlockSpec((None, 2, length), lambda i: (i, 0, 0)),
            columns(0),
        ],
        out_specs=pl.BlockSpec((length, 3 * features), lambda i: (0, 0)),
        out_shape=jax.ShapeDtypeStruct((length, 3 * features), half),
        scratch_shapes=[pltpu.VMEM((length, PAIR), single)] * 2,
        compiler_params=pltpu.CompilerParams(vmem_limit_bytes=56 << 20),
        cost_estimate=estimate(40 * length * length * features, 16 * length * features),
        name="attend_backward",
    )(packed, packed, packed, bias, upstream, totals, attended)


def place_pieces(pieces, out_shape, targets, indices):
    def kernel(index_ref, *refs):
        sources, out_ref, semaphores = refs[: len(pieces)], refs[-2], refs[-1]
        copies = [
            pltpu.make_async_copy(
                source, out_ref.at[target(index_ref)], semaphores.at[number]
            )
            for number, (source, target) in enumerate(zip(sources, targets))
        ]
        for copy in copies:
            copy.start()
        for copy in copies:
            copy.wait()

    size = 2 * 2
    for extent in out_shape:
        size *= extent
    anywhere = pl.BlockSpec(memory_space=pl.ANY)
    return pl.pallas_call(
        kernel,
        in_specs=[pl.BlockSpec(memory_space=pltpu.SMEM)] + [anywhere] * len(pieces),
        out_specs=pl.BlockSpec(memory_space=pltpu.VMEM),
        out_shape=jax.ShapeDtypeStruct(out_shape, pieces[0].dtype),
        scratch_shapes=[pltpu.SemaphoreType.DMA((len(pieces),))],
        compiler_params=pltpu.CompilerParams(vmem_limit_bytes=32 << 20),
        cost_estimate=estimate(0, size),
        name="place_pieces",
    )(indices, *pieces)


def normal_of(hidden):
    center = hidden - jnp.mean(hidden, axis=-1, keepdims=True)
    inverse = lax.rsqrt(jnp.mean(center * center, axis=-1, keepdims=True) + epsilon)
    return center * inverse, inverse


def norm_pull(normal, inverse, gain, upstream):
    scaled = upstream * gain
    slope = jnp.mean(scaled, axis=-1, keepdims=True)
    tilt = jnp.mean(scaled * normal, axis=-1, keepdims=True)
    return inverse * (scaled - slope - normal * tilt)


def column_sum(array):
    return jnp.sum(array, axis=0, keepdims=True)


def tile_of(columns):
    return pl.BlockSpec((ROW_TILE, columns), lambda i: (i, 0))


def resident(shape, *index):
    place = index or (0,) * len(shape)
    return pl.BlockSpec(shape, lambda i: place, pipeline_mode=pl.Buffered(1))


def row_tiled(kernel, name, length, in_specs, out_specs, out_shape, operands, flops):
    size = sum(operand.size * operand.dtype.itemsize for operand in operands)
    size += sum(shape.size * jnp.dtype(shape.dtype).itemsize for shape in out_shape)
    return pl.pallas_call(
        kernel,
        grid=(length // ROW_TILE,),
        in_specs=in_specs,
        out_specs=out_specs,
        out_shape=out_shape,
        compiler_params=pltpu.CompilerParams(vmem_limit_bytes=56 << 20),
        cost_estimate=estimate(flops, size),
        name=name,
    )(*operands)


def project_kernel(hidden_ref, gains_ref, offsets_ref, weight_ref, normed_ref, packed_ref):
    features = hidden_ref.shape[1]
    normal, _ = normal_of(hidden_ref[...])
    normed = (normal * gains_ref[0:1] + offsets_ref[0:1]).astype(half)
    normed_ref[...] = normed
    for part in range(3):
        window = slice(part * features, (part + 1) * features)
        product = contract(normed, weight_ref[:, window], 1, 0)
        if part != 1:
            row = 1 if part == 0 else 2
            product = product + offsets_ref[row : row + 1]
        packed_ref[:, window] = product.astype(half)


def project(hidden, gains, offsets, joined):
    length, features = hidden.shape
    return row_tiled(
        project_kernel,
        "project",
        length,
        [
            tile_of(features),
            resident(gains.shape),
            resident(offsets.shape),
            resident((features, 3 * features)),
        ],
        [tile_of(features), tile_of(3 * features)],
        [
            jax.ShapeDtypeStruct((length, features), half),
            jax.ShapeDtypeStruct((length, 3 * features), half),
        ],
        (hidden, gains, offsets, joined),
        6 * length * features * features,
    )


def feed_kernel(
    attended_ref,
    hidden_ref,
    gains_ref,
    offsets_ref,
    up_bias_ref,
    out_weight_ref,
    up_ref,
    down_ref,
    middle_ref,
    second_ref,
    activated_ref,
    slope_ref,
    result_ref,
):
    hidden_units = up_ref.shape[1]
    middle = hidden_ref[...] + (
        contract(attended_ref[...], out_weight_ref[...], 1, 0) + offsets_ref[3:4]
    )
    middle_ref[...] = middle
    normal, _ = normal_of(middle)
    second = (normal * gains_ref[1:2] + offsets_ref[4:5]).astype(half)
    second_ref[...] = second
    result = middle + offsets_ref[5:6]
    rate = 0.7978845608028654
    for start in range(0, hidden_units, FF_CHUNK):
        window = slice(start, start + FF_CHUNK)
        value = contract(second, up_ref[:, window], 1, 0) + up_bias_ref[:, window]
        square = value * value
        bent = jnp.tanh(value * (rate + (rate * 0.044715) * square))
        opened = 0.5 + 0.5 * bent
        activated = (value * opened).astype(half)
        activated_ref[:, window] = activated
        curve = (value * (0.5 * rate + (1.5 * rate * 0.044715) * square)) * (1.0 - bent * bent)
        slope_ref[:, window] = (opened + curve).astype(half)
        result = result + contract(activated, down_ref[window, :], 1, 0)
    result_ref[...] = result.astype(result_ref.dtype)


def feed(attended, hidden, gains, offsets, up_bias, joined, up, down, result_type):
    length, features = hidden.shape
    units = down.shape[0]
    up_array, up_place = up
    shape = jax.ShapeDtypeStruct
    return row_tiled(
        feed_kernel,
        "feed",
        length,
        [
            tile_of(features),
            tile_of(features),
            resident(gains.shape),
            resident(offsets.shape),
            resident(up_bias.shape),
            resident((features, features), 0, 3),
            resident((features, units), 0, up_place),
            resident(down.shape),
        ],
        [tile_of(features), tile_of(features), tile_of(units), tile_of(units), tile_of(features)],
        [
            shape((length, features), single),
            shape((length, features), half),
            shape((length, units), half),
            shape((length, units), half),
            shape((length, features), result_type),
        ],
        (attended, hidden, gains, offsets, up_bias, joined, up_array, down),
        2 * length * features * (features + 2 * units),
    )


def feed_grad_kernel(
    gradient_ref,
    slope_ref,
    middle_ref,
    gains_ref,
    out_weight_ref,
    up_ref,
    down_ref,
    branch_ref,
    upper_ref,
    middle_grad_ref,
    attention_grad_ref,
    upstream_ref,
    sums_ref,
    unit_sums_ref,
):
    units = up_ref.shape[1]

    @pl.when(pl.program_id(0) == 0)
    def _():
        sums_ref[...] = jnp.zeros_like(sums_ref)
        unit_sums_ref[...] = jnp.zeros_like(unit_sums_ref)

    gradient = gradient_ref[...].astype(single)
    branch = gradient.astype(half)
    branch_ref[...] = branch
    sums_ref[0:1] += column_sum(branch.astype(single))
    second_grad = jnp.zeros(gradient.shape, single)
    for start in range(0, units, FF_CHUNK):
        window = slice(start, start + FF_CHUNK)
        pulled = contract(branch, down_ref[window, :], 1, 1) * slope_ref[:, window].astype(single)
        upper = pulled.astype(half)
        upper_ref[:, window] = upper
        unit_sums_ref[:, window] += column_sum(upper.astype(single))
        second_grad = second_grad + contract(upper, up_ref[:, window], 1, 1)
    normal, inverse = normal_of(middle_ref[...])
    middle_grad = gradient + norm_pull(normal, inverse, gains_ref[1:2], second_grad)
    sums_ref[1:2] += column_sum(second_grad * normal)
    sums_ref[2:3] += column_sum(second_grad)
    middle_grad_ref[...] = middle_grad
    attention_grad = middle_grad.astype(half)
    attention_grad_ref[...] = attention_grad
    sums_ref[3:4] += column_sum(attention_grad.astype(single))
    upstream_ref[...] = contract(attention_grad, out_weight_ref[...], 1, 1).astype(half)


def feed_grad(gradient, slope, middle, gains, joined, up, down):
    up_array, up_place = up
    length, features = middle.shape
    units = down.shape[0]
    shape = jax.ShapeDtypeStruct
    return row_tiled(
        feed_grad_kernel,
        "feed_grad",
        length,
        [
            tile_of(features),
            tile_of(units),
            tile_of(features),
            resident(gains.shape),
            resident((features, features), 0, 3),
            resident((features, units), 0, up_place),
            resident(down.shape),
        ],
        [
            tile_of(features),
            tile_of(units),
            tile_of(features),
            tile_of(features),
            tile_of(features),
            resident((8, features)),
            resident((1, units)),
        ],
        [
            shape((length, features), half),
            shape((length, units), half),
            shape((length, features), single),
            shape((length, features), half),
            shape((length, features), half),
            shape((8, features), single),
            shape((1, units), single),
        ],
        (gradient, slope, middle, gains, joined, up_array, down),
        2 * length * features * (features + 2 * units),
    )


def project_grad_kernel(
    packed_grad_ref, hidden_ref, middle_grad_ref, gains_ref, weight_ref, *out_refs
):
    sums_ref = out_refs[-1]
    features = hidden_ref.shape[1]

    @pl.when(pl.program_id(0) == 0)
    def _():
        sums_ref[...] = jnp.zeros_like(sums_ref)

    packed_grad = packed_grad_ref[...]
    normed_grad = contract(packed_grad, weight_ref[...], 1, 1)
    normal, inverse = normal_of(hidden_ref[...])
    result = middle_grad_ref[...] + norm_pull(normal, inverse, gains_ref[0:1], normed_grad)
    for result_ref in out_refs[:-1]:
        result_ref[...] = result.astype(result_ref.dtype)
    sums_ref[0:1] += column_sum(normed_grad * normal)
    sums_ref[1:2] += column_sum(normed_grad)
    sums_ref[2:3] += column_sum(packed_grad[:, :features].astype(single))
    sums_ref[3:4] += column_sum(packed_grad[:, 2 * features :].astype(single))


def project_grad(packed_grad, hidden, middle_grad, gains, joined, result_types):
    length, features = hidden.shape
    shape = jax.ShapeDtypeStruct
    return row_tiled(
        project_grad_kernel,
        "project_grad",
        length,
        [
            tile_of(3 * features),
            tile_of(features),
            tile_of(features),
            resident(gains.shape),
            resident((features, 3 * features)),
        ],
        [tile_of(features) for _ in result_types] + [resident((8, features))],
        [shape((length, features), result_type) for result_type in result_types]
        + [shape((8, features), single)],
        (packed_grad, hidden, middle_grad, gains, joined),
        6 * length * features * features,
    )


def term_blocks(terms, core, groups, row_unit, by_core):
    pieces = [left.shape[1] // (groups * row_unit) for left, _ in terms]
    widths = [right.shape[1] // (2 if by_core else 1) for _, right in terms]
    total = sum(count * width for count, width in zip(pieces, widths))
    chips = groups // 2
    out_shape = (chips, 2, row_unit, total) if by_core else (groups, row_unit, total)
    outputs = 2 if by_core else 1
    if row_unit % 16:
        columns = []
        for (left, right), count, width in zip(terms, pieces, widths):
            part = contract(left, right, 0, 0).astype(half)
            part = part.reshape(chips, 2, count, row_unit, -1, width).transpose(2, 1, 0, 4, 3, 5)
            columns += [part[piece] for piece in range(count)]
        whole = jnp.concatenate(columns, axis=-1)
        if not by_core:
            return [whole[:, :, 0].swapaxes(0, 1).reshape(out_shape)]
        return [
            lax.dynamic_index_in_dim(whole, which, 0, keepdims=False) for which in (1 - core, core)
        ]
    number = len(terms)

    def kernel(core_ref, *refs):
        sources = refs[: 2 * number]
        outs = refs[2 * number : 2 * number + outputs]
        buffers = refs[2 * number + outputs : 4 * number + outputs]
        semaphores = refs[4 * number + outputs]
        first_core = core_ref[0] == 0
        copies = [
            pltpu.make_async_copy(source, buffer, semaphores.at[index])
            for index, (source, buffer) in enumerate(zip(sources, buffers))
        ]
        for copy in copies:
            copy.start()
        start = 0
        for index, (count, width) in enumerate(zip(pieces, widths)):
            copies[2 * index].wait()
            copies[2 * index + 1].wait()
            left, right = buffers[2 * index], buffers[2 * index + 1]
            rows = groups * row_unit
            step = max(size for size in (768, 640, 512, 384, 256, 128) if width % size == 0)
            held = chips // count
            for turn in range(count):
                turned = left[:, turn * rows : (turn + 1) * rows].T
                some = slice(turn * held, (turn + 1) * held)
                for low in range(0, right.shape[1], step):
                    product = contract(turned, right[:, low : low + step], 1, 0).astype(half)
                    product = product.reshape(held, 2, count, row_unit, step)
                    side, inside = divmod(low, width)
                    for piece in range(count):
                        lanes = start + piece * width + inside
                        lanes = slice(lanes, lanes + step)
                        even, odd = product[:, 0, piece], product[:, 1, piece]
                        if by_core:
                            outs[0][some, side, :, lanes] = jnp.where(first_core, odd, even)
                            outs[1][some, side, :, lanes] = jnp.where(first_core, even, odd)
                        else:
                            for chip in range(held):
                                owner = 2 * (turn * held + chip)
                                outs[0][owner, :, lanes] = even[chip]
                                outs[0][owner + 1, :, lanes] = odd[chip]
            start += count * width

    anywhere = pl.BlockSpec(memory_space=pl.ANY)
    operands = [operand for term in terms for operand in term]
    size = sum(operand.size for operand in operands) * 2
    flops = sum(2 * left.size * right.shape[1] for left, right in terms)
    shape = jax.ShapeDtypeStruct(out_shape, half)
    return pl.pallas_call(
        kernel,
        in_specs=[pl.BlockSpec(memory_space=pltpu.SMEM)] + [anywhere] * len(operands),
        out_specs=[pl.BlockSpec(memory_space=pltpu.VMEM)] * outputs,
        out_shape=[shape] * outputs,
        scratch_shapes=[pltpu.VMEM(operand.shape, half) for operand in operands]
        + [pltpu.SemaphoreType.DMA((len(operands),))],
        compiler_params=pltpu.CompilerParams(vmem_limit_bytes=60 << 20),
        cost_estimate=estimate(flops, size + 2 * outputs * shape.size),
        name="term_blocks",
    )(core.reshape(1).astype(jnp.int32), *operands)


def per_device(
    tokens,
    time_embed,
    segment_ids,
    pad_mask,
    out_grad,
    qkv_weight,
    out_weight,
    up_weight,
    down_weight,
    norm_gains,
    bias_rows,
    up_bias,
):
    layers = qkv_weight.shape[0]
    features = tokens.shape[2]
    groups = lax.axis_size("wide")
    swap = [(0, 1), (1, 0)]

    def whole_sequence(part):
        return lax.all_to_all(part, "seq", split_axis=0, concat_axis=1, tiled=True)[0]

    core = lax.axis_index("wide") & 1
    place = lax.axis_index("seq")
    indices = jnp.stack([core, place]).astype(jnp.int32)
    row_unit = qkv_weight.shape[1]

    def across(bit):
        pairs = [(index, index ^ bit) for index in range(groups)]
        return lambda part: lax.ppermute(part, "wide", pairs)

    def beside_seq(part):
        return lax.ppermute(part, "seq", swap)

    def to_owners(part):
        return lax.psum_scatter(part, "wide", scatter_dimension=0, tiled=True)

    bit_of = lambda bit: (lax.axis_index("wide") >> (bit.bit_length() - 1)) & 1
    running = []

    def begin(steps, finish):
        entry = [steps, finish, next(steps), None]
        running.append(entry)
        return entry

    def launch(main, entries):
        fresh = [entry for entry in entries if entry in running and entry[3] is None]
        if fresh:
            sends = [[sent for sent, _ in entry[2]] for entry in fresh]
            main, sends = lax.optimization_barrier((main, sends))
            for entry, sent in zip(fresh, sends):
                entry[3] = [pass_on(part) for part, (_, pass_on) in zip(sent, entry[2])]
        return main

    def advance(main, *only):
        chosen = [entry for entry in only or list(running) if entry in running]
        main = launch(main, chosen)
        if not chosen:
            return main
        main, flying = lax.optimization_barrier((main, [entry[3] for entry in chosen]))
        for entry, arrived in zip(chosen, flying):
            entry[3] = None
            try:
                entry[2] = entry[0].send(arrived)
            except StopIteration as stop:
                entry[1](stop.value)
                running.remove(entry)
        return launch(main, chosen)

    def side_of(array, which, axis):
        return lax.dynamic_index_in_dim(array, which, axis, keepdims=False)

    chip_bits = [1 << number for number in range(groups.bit_length() - 2, 0, -1)]

    def join(current, received, which):
        lead = current.shape[0]
        joined = place_pieces(
            [current, received],
            (lead, 2) + current.shape[1:],
            [lambda ref: (slice(None), ref[0]), lambda ref: (slice(None), 1 - ref[0])],
            which.reshape(1).astype(jnp.int32),
        )
        return joined.reshape((2 * lead,) + current.shape[1:])

    def gather_columns(shard):
        rows, columns = shard.shape[0], shard.shape[1] // 2
        current = lax.dynamic_slice_in_dim(shard, place * columns, columns, axis=1)[None]
        for bit in chip_bits:
            (received,) = yield [(current, across(bit))]
            current = join(current, received, bit_of(bit))
        (aside,) = yield [(current, beside_seq)]
        passed = yield [(part, across(1)) for part in (current, aside)]

        def target(own_core, own_place):
            def where(ref):
                which_core = ref[0] if own_core else 1 - ref[0]
                which_place = ref[1] if own_place else 1 - ref[1]
                start = pl.multiple_of(which_place * columns, columns)
                return (slice(None), which_core, slice(None), pl.ds(start, columns))

            return where

        return place_pieces(
            [current, aside, *passed],
            (current.shape[0], 2, rows, 2 * columns),
            [target(True, True), target(True, False), target(False, True), target(False, False)],
            indices,
        ).reshape(-1, 2 * columns)

    def gather_rows(shard):
        rows, columns = shard.shape[0] // 2, shard.shape[1]
        current = side_of(shard.reshape(2, rows, columns), place, 0)[None]
        for bit in chip_bits[:-1]:
            (received,) = yield [(current, across(bit))]
            current = join(current, received, bit_of(bit))
        (received,) = yield [(current, beside_seq)]
        current = join(current, received, place).reshape(-1, 2 * rows, columns)
        for bit in chip_bits[-1:] + [1]:
            (received,) = yield [(current, across(bit))]
            current = join(current, received, bit_of(bit))
        return current.reshape(-1, columns)

    marks = whole_sequence(jnp.stack([segment_ids, pad_mask], axis=2))
    tokens, marks = lax.optimization_barrier((tokens, marks))
    my_tokens = whole_sequence(tokens)

    small = jnp.concatenate(
        [norm_gains.reshape(-1), bias_rows.reshape(-1), up_bias.reshape(-1)]
    )
    side = small.reshape(row_unit, -1)
    side_width = side.shape[1]
    side = jnp.pad(side, ((0, 0), (0, -side_width % PAIR)))
    joined_parts = [jnp.concatenate([qkv_weight[0], out_weight[0], side], axis=1)]
    for layer in range(1, layers):
        parts = [qkv_weight[layer], out_weight[layer], up_weight[layer]]
        joined_parts.append(jnp.concatenate(parts, axis=1))
    joined = [lax.all_gather(part, "wide", axis=0, tiled=True) for part in joined_parts]
    downs = {
        layer: lax.all_gather(down_weight[layer], "wide", axis=0, tiled=True)
        for layer in range(1, layers)
    }
    small_whole = joined[0][:, -side.shape[1] :][:, :side_width].reshape(groups, -1)
    cut_gains = norm_gains.size
    cut_rows = cut_gains + bias_rows.size

    def whole_rows(part, count):
        parts = part.reshape(groups, layers, count, -1)
        return parts.transpose(1, 2, 0, 3).reshape(layers, count, -1).astype(single)

    all_gains = whole_rows(small_whole[:, :cut_gains], norm_gains.shape[1])
    all_offsets = whole_rows(small_whole[:, cut_gains:cut_rows], bias_rows.shape[1])
    all_up_bias = whole_rows(small_whole[:, cut_rows:], 1)[:, 0]

    matrices = [None] * layers
    ups = {}
    fetches = [
        begin(gather_columns(up_weight[0]), functools.partial(ups.__setitem__, 0)),
        begin(gather_rows(down_weight[0]), functools.partial(downs.__setitem__, 0)),
    ]
    for _ in chip_bits[1:]:
        time_embed = advance(time_embed, *fetches)
    doc, pad = marks[:, 0], marks[:, 1]
    positions = jnp.arange(doc.shape[0])
    allowed = (doc[:, None] == doc[None, :]) & (
        (pad[:, None] == 1) | (positions[:, None] == positions[None, :])
    )
    bias = jnp.where(allowed, 0.0, masked_bias)

    my_time = lax.dynamic_index_in_dim(time_embed, place, 0, keepdims=True)
    hidden = my_tokens.astype(single) + my_time
    saved = []
    for layer in range(layers):
        whole = joined[layer]
        gains, offsets = all_gains[layer], all_offsets[layer]
        before = hidden
        normed, packed = project(hidden, gains, offsets, whole)
        if layer == layers - 1:
            packed, out_grad = lax.optimization_barrier((packed, out_grad))
            my_upstream = whole_sequence(out_grad)
        packed = advance(packed, *fetches)
        attended, totals = attend_forward(packed, bias)
        attended = advance(attended, *fetches)
        while running:
            attended = advance(attended, *fetches)
        up = (whole, 4 * features // up_bias.shape[1] // groups) if layer else (ups[0], 0)
        matrices[layer] = (whole, up, downs[layer])
        fetches = []
        middle, second, activated, slope, hidden = feed(
            attended,
            hidden,
            gains,
            offsets,
            all_up_bias[layer][None],
            whole,
            up,
            downs[layer],
            single if layer < layers - 1 else half,
        )
        saved.append((before, normed, packed, totals, attended, middle, second, activated, slope))

    def split_back(result):
        parts = result.reshape(2, -1, features).astype(half)
        return lax.all_to_all(parts, "seq", split_axis=0, concat_axis=0, tiled=True)

    output = split_back(hidden)

    def total_of(addends):
        return functools.reduce(jnp.add, [addend.astype(single) for addend in addends])

    def shares_of(terms, low, high):
        shares, start = [], 0
        for left, right in terms:
            rows, each = [], right.shape[1] // 2
            if high is None:
                each *= 2
            for _ in range(left.shape[1] // (groups * row_unit)):
                window = slice(start, start + each)
                if high is None:
                    rows.append(low[:, window])
                else:
                    rows.append(jnp.concatenate([low[:, window], high[:, window]], axis=1))
                start += each
            shares.append(jnp.concatenate(rows, axis=0))
        return shares

    def scatter_group(terms):
        (whole,) = term_blocks(terms, core, groups, row_unit, False)
        whole = whole.reshape(groups * row_unit, -1)
        (share,) = yield [(whole, to_owners)]
        (received,) = yield [(share, beside_seq)]
        return shares_of(terms, share.astype(single) + received.astype(single), None)

    def reduce_group(terms):
        other, own = term_blocks(terms, core, groups, row_unit, True)
        (received,) = yield [(other, across(1))]
        shape = (2,) * len(chip_bits) + (2, row_unit, own.shape[-1])
        addends = [part.reshape(shape) for part in (own, received)]
        axis = len(chip_bits)
        for bit in [0] + chip_bits[:1:-1]:
            mine, pass_on = (bit_of(bit), across(bit)) if bit else (place, beside_seq)
            sent = total_of([side_of(part, 1 - mine, axis) for part in addends]).astype(half)
            (received,) = yield [(sent, pass_on)]
            addends = [side_of(part, mine, axis) for part in addends] + [received]
            axis -= 1
        far, near = chip_bits[:2]

        def corner(part, bits):
            part = side_of(part, bit_of(far) ^ (1 if bits & far else 0), 0)
            return side_of(part, bit_of(near) ^ (1 if bits & near else 0), 0)

        received = yield [
            (total_of([corner(part, bits) for part in addends]).astype(half), across(bits))
            for bits in (near, far, near | far)
        ]
        addends = [corner(part, 0) for part in addends] + received
        current = total_of(addends).astype(half)
        (received,) = yield [(current, beside_seq)]
        low = jnp.where(place == 0, current, received).astype(single)
        high = jnp.where(place == 0, received, current).astype(single)
        return shares_of(terms, low, high)

    def reduce_small(array):
        parts = [array.reshape((2,) * (len(chip_bits) + 1) + array.shape[1:])]
        pairs = [(2, 1, len(chip_bits) - 1)]
        pairs += [(bit, None, chip_bits.index(bit)) for bit in chip_bits[-2:1:-1]]
        pairs += [(chip_bits[0], chip_bits[1], 0)]
        for high, low, axis in pairs:

            def chosen(bits):
                def pick(part):
                    if low is not None:
                        part = side_of(part, bit_of(low) ^ (1 if bits & low else 0), axis + 1)
                    return side_of(part, bit_of(high) ^ (1 if bits & high else 0), axis)

                return total_of([pick(part) for part in parts])

            masks = [high] if low is None else [low, high, low | high]
            received = yield [(chosen(bits), across(bits)) for bits in masks]
            parts = [chosen(0)] + received
        current = total_of(parts)
        (received,) = yield [(current, beside_seq)]
        return current + received

    weight_grads = [[None] * 4 for _ in range(layers)]

    def begin_group(steps, layer, named):
        def finish(shares):
            for (part, _), share in zip(named, shares):
                weight_grads[layer][part] = share

        return begin(steps([term for _, term in named]), finish)

    gradient = my_upstream
    small_grads = [None] * layers
    held = []
    for layer in range(layers - 1, -1, -1):
        whole, up, down = matrices[layer]
        gains = all_gains[layer]
        hidden, normed, packed, totals, attended, middle, second, activated, slope = saved[layer]
        steps = scatter_group if layer else reduce_group
        branch, upper, middle_grad, attention_grad, upstream, sums, unit_sums = feed_grad(
            gradient, slope, middle, gains, whole, up, down
        )
        named = [(2, (second, upper)), (1, (attended, attention_grad))]
        if layer:
            held.append(begin_group(steps, layer, [(3, (activated, branch))] + named))
            upstream = launch(upstream, held[-1:])
        else:
            upstream = advance(upstream, first_group)
            upper, attention_grad, upstream = lax.optimization_barrier(
                (upper, attention_grad, upstream)
            )
            named = [(2, (second, upper)), (1, (attended, attention_grad))]
            second_group = begin_group(steps, layer, named)
            upstream = launch(upstream, [second_group])
            upstream = advance(upstream, second_group)
            upstream = advance(upstream, *held[:1])
        packed_grad = attend_backward(packed, bias, upstream, totals, attended)
        if layer == layers - 1:
            packed_grad, output = lax.optimization_barrier((packed_grad, output))
            output = output.astype(single)
        named = [(0, (normed, packed_grad))]
        if not layer:
            packed_grad = advance(packed_grad, first_group, second_group, *held[:1])
            last_group = begin_group(steps, layer, named)
            packed_grad = launch(packed_grad, [last_group])
            packed_grad = advance(packed_grad, last_group)
        gradient, *rounded, more_sums = project_grad(
            packed_grad, hidden, middle_grad, gains, whole, (single, half) if layer else (half,)
        )
        if layer == 1:
            below = (saved[0][7], rounded[0])
            first_group = begin_group(reduce_group, 0, [(3, below)])
            gradient = launch(gradient, [first_group])
        if layer:
            held.append(begin_group(steps, layer, named))
            gradient = launch(gradient, held[-1:])
        if layer == 1:
            gradient = advance(gradient, first_group)
        if not layer:
            gradient = advance(gradient, last_group)
        small_grads[layer] = (
            jnp.stack([more_sums[0], sums[1]]),
            jnp.stack([more_sums[1], more_sums[2], more_sums[3], sums[3], sums[2], sums[0]]),
            unit_sums[0],
        )

    def by_owner(parts):
        stacked = jnp.stack(parts)
        stacked = stacked.reshape(layers, -1, groups, stacked.shape[-1] // groups)
        return stacked.transpose(2, 0, 1, 3).reshape(groups, -1)

    owned = jnp.concatenate(
        [by_owner([small_grads[layer][part] for layer in range(layers)]) for part in range(3)],
        axis=1,
    )
    small_result = []
    begin(reduce_small(owned), small_result.append)
    output = launch(output, running[-1:])
    output = advance(output, first_group, second_group, *held)
    input_grad = split_back(gradient)
    while running:
        output = advance(output, last_group)
        output = advance(output, *[entry for entry in running if entry is not last_group])
    owned = small_result[0]
    input_grad = input_grad.astype(single)
    stacked = [
        jnp.stack([weight_grads[layer][part] for layer in range(layers)]) for part in range(4)
    ]
    return (
        output,
        input_grad,
        *stacked,
        owned[:cut_gains].reshape(norm_gains.shape),
        owned[cut_gains:cut_rows].reshape(bias_rows.shape),
        owned[cut_rows:].reshape(up_bias.shape),
    )


def solution(mesh):
    tokens_spec = P("wide", "seq", None)
    matrix_spec = P(None, "wide", None)
    rows_spec = P(None, None, "wide")
    return jax.shard_map(
        per_device,
        mesh=mesh,
        in_specs=(
            tokens_spec,
            P("wide", None),
            P("wide", "seq"),
            P("wide", "seq"),
            tokens_spec,
            matrix_spec,
            matrix_spec,
            matrix_spec,
            matrix_spec,
            rows_spec,
            rows_spec,
            P(None, "wide"),
        ),
        out_specs=(
            tokens_spec,
            tokens_spec,
            matrix_spec,
            matrix_spec,
            matrix_spec,
            matrix_spec,
            rows_spec,
            rows_spec,
            P(None, "wide"),
        ),
        check_vma=False,
    )
```

```python
import functools

import jax
import jax.numpy as jnp
from jax import lax
from jax.experimental import pallas as pl
from jax.experimental.pallas import tpu as pltpu
from jax.sharding import PartitionSpec as P

HEAD_SIZE = 64
PAIR = 2 * HEAD_SIZE
FORWARD_ROWS = 1024
BACKWARD_ROWS = 256
ROW_TILE = 256
FF_CHUNK = 768

epsilon = 1e-05
masked_bias = -1e30
half = jnp.bfloat16
single = jnp.float32


def estimate(flops, size):
    return pl.CostEstimate(flops=flops // 16, bytes_accessed=size // 16, transcendentals=0)


def contract(left, right, left_dim, right_dim):
    return lax.dot_general(
        left, right, (((left_dim,), (right_dim,)), ((), ())), preferred_element_type=jnp.float32
    )


def first_head_lanes():
    return lax.broadcasted_iota(jnp.int32, (1, PAIR), 1) < HEAD_SIZE


def one_head_of(pair, head):
    lanes = first_head_lanes()
    keep = lanes if head == 0 else jnp.logical_not(lanes)
    return jnp.where(keep, pair, jnp.zeros_like(pair))


def attend_kernel(query_ref, key_ref, value_ref, bias_ref, out_ref, total_ref, *, rows):
    keys = key_ref[...]
    values = value_ref[...]
    scale = jnp.asarray(HEAD_SIZE ** (-0.5), half)
    for start in range(0, keys.shape[0], rows):
        window = pl.ds(start, rows)
        queries = query_ref[window, :] * scale
        bias = bias_ref[:, window]
        attended = []
        for head in range(2):
            scores = contract(keys, one_head_of(queries, head), 1, 1) + bias
            top = jnp.max(scores, axis=0, keepdims=True)
            weights = jnp.exp(scores - top)
            total = jnp.sum(weights, axis=0, keepdims=True)
            mixed = contract(values, weights.astype(half), 0, 0) * (1.0 / total)
            attended.append(mixed[HEAD_SIZE * head : HEAD_SIZE * (head + 1)])
            total_ref[head : head + 1, window] = top + jnp.log(total)
        out_ref[window, :] = jnp.concatenate(attended, 0).T.astype(half)


def attend_forward(packed, bias):
    length = packed.shape[0]
    features = packed.shape[1] // 3
    pairs = features // PAIR
    columns = lambda part: pl.BlockSpec((length, PAIR), lambda i: (0, part * pairs + i))
    return pl.pallas_call(
        functools.partial(attend_kernel, rows=FORWARD_ROWS),
        grid=(pairs,),
        in_specs=[
            columns(0),
            columns(1),
            columns(2),
            pl.BlockSpec((length, length), lambda i: (0, 0)),
        ],
        out_specs=[columns(0), pl.BlockSpec((None, 2, length), lambda i: (i, 0, 0))],
        out_shape=[
            jax.ShapeDtypeStruct((length, features), half),
            jax.ShapeDtypeStruct((pairs, 2, length), single),
        ],
        compiler_params=pltpu.CompilerParams(vmem_limit_bytes=56 << 20),
        cost_estimate=estimate(16 * length * length * features, 8 * length * features),
        name="attend_forward",
    )(packed, packed, packed, bias)


def attend_grad_kernel(
    query_ref,
    key_ref,
    value_ref,
    bias_ref,
    upstream_ref,
    total_ref,
    attended_ref,
    out_ref,
    key_sum,
    value_sum,
    *,
    rows,
):
    pair = pl.program_id(0)
    features = out_ref.shape[1] // 3
    keys = key_ref[...]
    values = value_ref[...]
    scale = HEAD_SIZE ** (-0.5)
    for start in range(0, keys.shape[0], rows):
        window = pl.ds(start, rows)
        queries = query_ref[window, :] * jnp.asarray(scale, half)
        upstream = upstream_ref[window, :]
        product = (upstream.astype(single) * attended_ref[window, :].astype(single)).T
        bias = bias_ref[:, window]
        query_grads, key_grad, value_grad = [], 0.0, 0.0
        for head in range(2):
            head_queries = one_head_of(queries, head)
            head_upstream = one_head_of(upstream, head)
            inner = jnp.sum(
                product[HEAD_SIZE * head : HEAD_SIZE * (head + 1)], axis=0, keepdims=True
            )
            scores = contract(keys, head_queries, 1, 1) + bias
            weights = jnp.exp(scores - total_ref[head : head + 1, window])
            weight_grads = contract(values, head_upstream, 1, 1)
            score_grads = (weights * (weight_grads - inner)).astype(half)
            value_grad = value_grad + contract(weights.astype(half), head_upstream, 1, 0)
            key_grad = key_grad + contract(score_grads, head_queries, 1, 0)
            query_grads.append(
                contract(keys, score_grads, 0, 0)[HEAD_SIZE * head : HEAD_SIZE * (head + 1)]
            )
        out_ref[window, pl.ds(pl.multiple_of(pair * PAIR, PAIR), PAIR)] = (
            jnp.concatenate(query_grads, 0).T * scale
        ).astype(half)
        if start == 0:
            key_sum[...] = key_grad
            value_sum[...] = value_grad
        else:
            key_sum[...] += key_grad
            value_sum[...] += value_grad
    out_ref[:, pl.ds(pl.multiple_of(features + pair * PAIR, PAIR), PAIR)] = key_sum[...].astype(
        half
    )
    out_ref[:, pl.ds(pl.multiple_of(2 * features + pair * PAIR, PAIR), PAIR)] = value_sum[
        ...
    ].astype(half)


def attend_backward(packed, bias, upstream, totals, attended):
    length = packed.shape[0]
    features = packed.shape[1] // 3
    pairs = features // PAIR
    columns = lambda part: pl.BlockSpec((length, PAIR), lambda i: (0, part * pairs + i))
    return pl.pallas_call(
        functools.partial(attend_grad_kernel, rows=BACKWARD_ROWS),
        grid=(pairs,),
        in_specs=[
            columns(0),
            columns(1),
            columns(2),
            pl.BlockSpec((length, length), lambda i: (0, 0)),
            columns(0),
            pl.BlockSpec((None, 2, length), lambda i: (i, 0, 0)),
            columns(0),
        ],
        out_specs=pl.BlockSpec((length, 3 * features), lambda i: (0, 0)),
        out_shape=jax.ShapeDtypeStruct((length, 3 * features), half),
        scratch_shapes=[pltpu.VMEM((length, PAIR), single)] * 2,
        compiler_params=pltpu.CompilerParams(vmem_limit_bytes=56 << 20),
        cost_estimate=estimate(40 * length * length * features, 16 * length * features),
        name="attend_backward",
    )(packed, packed, packed, bias, upstream, totals, attended)


def place_pieces(pieces, out_shape, targets, indices):
    def kernel(index_ref, *refs):
        sources, out_ref, semaphores = refs[: len(pieces)], refs[-2], refs[-1]
        copies = [
            pltpu.make_async_copy(
                source, out_ref.at[target(index_ref)], semaphores.at[number]
            )
            for number, (source, target) in enumerate(zip(sources, targets))
        ]
        for copy in copies:
            copy.start()
        for copy in copies:
            copy.wait()

    size = 2 * 2
    for extent in out_shape:
        size *= extent
    anywhere = pl.BlockSpec(memory_space=pl.ANY)
    return pl.pallas_call(
        kernel,
        in_specs=[pl.BlockSpec(memory_space=pltpu.SMEM)] + [anywhere] * len(pieces),
        out_specs=pl.BlockSpec(memory_space=pltpu.VMEM),
        out_shape=jax.ShapeDtypeStruct(out_shape, pieces[0].dtype),
        scratch_shapes=[pltpu.SemaphoreType.DMA((len(pieces),))],
        compiler_params=pltpu.CompilerParams(vmem_limit_bytes=32 << 20),
        cost_estimate=estimate(0, size),
        name="place_pieces",
    )(indices, *pieces)


def normal_of(hidden):
    center = hidden - jnp.mean(hidden, axis=-1, keepdims=True)
    inverse = lax.rsqrt(jnp.mean(center * center, axis=-1, keepdims=True) + epsilon)
    return center * inverse, inverse


def norm_pull(normal, inverse, gain, upstream):
    scaled = upstream * gain
    slope = jnp.mean(scaled, axis=-1, keepdims=True)
    tilt = jnp.mean(scaled * normal, axis=-1, keepdims=True)
    return inverse * (scaled - slope - normal * tilt)


def column_sum(array):
    return jnp.sum(array, axis=0, keepdims=True)


def tile_of(columns):
    return pl.BlockSpec((ROW_TILE, columns), lambda i: (i, 0))


def resident(shape, *index):
    place = index or (0,) * len(shape)
    return pl.BlockSpec(shape, lambda i: place, pipeline_mode=pl.Buffered(1))


def row_tiled(kernel, name, length, in_specs, out_specs, out_shape, operands, flops):
    size = sum(operand.size * operand.dtype.itemsize for operand in operands)
    size += sum(shape.size * jnp.dtype(shape.dtype).itemsize for shape in out_shape)
    return pl.pallas_call(
        kernel,
        grid=(length // ROW_TILE,),
        in_specs=in_specs,
        out_specs=out_specs,
        out_shape=out_shape,
        compiler_params=pltpu.CompilerParams(vmem_limit_bytes=56 << 20),
        cost_estimate=estimate(flops, size),
        name=name,
    )(*operands)


def project_kernel(hidden_ref, gains_ref, offsets_ref, weight_ref, normed_ref, packed_ref):
    features = hidden_ref.shape[1]
    normal, _ = normal_of(hidden_ref[...])
    normed = (normal * gains_ref[0:1] + offsets_ref[0:1]).astype(half)
    normed_ref[...] = normed
    for part in range(3):
        window = slice(part * features, (part + 1) * features)
        product = contract(normed, weight_ref[:, window], 1, 0)
        if part != 1:
            row = 1 if part == 0 else 2
            product = product + offsets_ref[row : row + 1]
        packed_ref[:, window] = product.astype(half)


def project(hidden, gains, offsets, joined):
    length, features = hidden.shape
    return row_tiled(
        project_kernel,
        "project",
        length,
        [
            tile_of(features),
            resident(gains.shape),
            resident(offsets.shape),
            resident((features, 3 * features)),
        ],
        [tile_of(features), tile_of(3 * features)],
        [
            jax.ShapeDtypeStruct((length, features), half),
            jax.ShapeDtypeStruct((length, 3 * features), half),
        ],
        (hidden, gains, offsets, joined),
        6 * length * features * features,
    )


def feed_kernel(
    attended_ref,
    hidden_ref,
    gains_ref,
    offsets_ref,
    up_bias_ref,
    out_weight_ref,
    up_ref,
    down_ref,
    middle_ref,
    second_ref,
    activated_ref,
    slope_ref,
    result_ref,
):
    hidden_units = up_ref.shape[1]
    middle = hidden_ref[...] + (
        contract(attended_ref[...], out_weight_ref[...], 1, 0) + offsets_ref[3:4]
    )
    middle_ref[...] = middle
    normal, _ = normal_of(middle)
    second = (normal * gains_ref[1:2] + offsets_ref[4:5]).astype(half)
    second_ref[...] = second
    result = middle + offsets_ref[5:6]
    rate = 0.7978845608028654
    for start in range(0, hidden_units, FF_CHUNK):
        window = slice(start, start + FF_CHUNK)
        value = contract(second, up_ref[:, window], 1, 0) + up_bias_ref[:, window]
        square = value * value
        bent = jnp.tanh(value * (rate + (rate * 0.044715) * square))
        opened = 0.5 + 0.5 * bent
        activated = (value * opened).astype(half)
        activated_ref[:, window] = activated
        curve = (value * (0.5 * rate + (1.5 * rate * 0.044715) * square)) * (1.0 - bent * bent)
        slope_ref[:, window] = (opened + curve).astype(half)
        result = result + contract(activated, down_ref[window, :], 1, 0)
    result_ref[...] = result.astype(result_ref.dtype)


def feed(attended, hidden, gains, offsets, up_bias, joined, up, down, result_type):
    length, features = hidden.shape
    units = down.shape[0]
    up_array, up_place = up
    shape = jax.ShapeDtypeStruct
    return row_tiled(
        feed_kernel,
        "feed",
        length,
        [
            tile_of(features),
            tile_of(features),
            resident(gains.shape),
            resident(offsets.shape),
            resident(up_bias.shape),
            resident((features, features), 0, 3),
            resident((features, units), 0, up_place),
            resident(down.shape),
        ],
        [tile_of(features), tile_of(features), tile_of(units), tile_of(units), tile_of(features)],
        [
            shape((length, features), single),
            shape((length, features), half),
            shape((length, units), half),
            shape((length, units), half),
            shape((length, features), result_type),
        ],
        (attended, hidden, gains, offsets, up_bias, joined, up_array, down),
        2 * length * features * (features + 2 * units),
    )


def feed_grad_kernel(
    gradient_ref,
    slope_ref,
    middle_ref,
    gains_ref,
    out_weight_ref,
    up_ref,
    down_ref,
    branch_ref,
    upper_ref,
    middle_grad_ref,
    attention_grad_ref,
    upstream_ref,
    sums_ref,
    unit_sums_ref,
):
    units = up_ref.shape[1]

    @pl.when(pl.program_id(0) == 0)
    def _():
        sums_ref[...] = jnp.zeros_like(sums_ref)
        unit_sums_ref[...] = jnp.zeros_like(unit_sums_ref)

    gradient = gradient_ref[...].astype(single)
    branch = gradient.astype(half)
    branch_ref[...] = branch
    sums_ref[0:1] += column_sum(branch.astype(single))
    second_grad = jnp.zeros(gradient.shape, single)
    for start in range(0, units, FF_CHUNK):
        window = slice(start, start + FF_CHUNK)
        pulled = contract(branch, down_ref[window, :], 1, 1) * slope_ref[:, window].astype(single)
        upper = pulled.astype(half)
        upper_ref[:, window] = upper
        unit_sums_ref[:, window] += column_sum(upper.astype(single))
        second_grad = second_grad + contract(upper, up_ref[:, window], 1, 1)
    normal, inverse = normal_of(middle_ref[...])
    middle_grad = gradient + norm_pull(normal, inverse, gains_ref[1:2], second_grad)
    sums_ref[1:2] += column_sum(second_grad * normal)
    sums_ref[2:3] += column_sum(second_grad)
    middle_grad_ref[...] = middle_grad
    attention_grad = middle_grad.astype(half)
    attention_grad_ref[...] = attention_grad
    sums_ref[3:4] += column_sum(attention_grad.astype(single))
    upstream_ref[...] = contract(attention_grad, out_weight_ref[...], 1, 1).astype(half)


def feed_grad(gradient, slope, middle, gains, joined, up, down):
    up_array, up_place = up
    length, features = middle.shape
    units = down.shape[0]
    shape = jax.ShapeDtypeStruct
    return row_tiled(
        feed_grad_kernel,
        "feed_grad",
        length,
        [
            tile_of(features),
            tile_of(units),
            tile_of(features),
            resident(gains.shape),
            resident((features, features), 0, 3),
            resident((features, units), 0, up_place),
            resident(down.shape),
        ],
        [
            tile_of(features),
            tile_of(units),
            tile_of(features),
            tile_of(features),
            tile_of(features),
            resident((8, features)),
            resident((1, units)),
        ],
        [
            shape((length, features), half),
            shape((length, units), half),
            shape((length, features), single),
            shape((length, features), half),
            shape((length, features), half),
            shape((8, features), single),
            shape((1, units), single),
        ],
        (gradient, slope, middle, gains, joined, up_array, down),
        2 * length * features * (features + 2 * units),
    )


def project_grad_kernel(
    packed_grad_ref, hidden_ref, middle_grad_ref, gains_ref, weight_ref, *out_refs
):
    sums_ref = out_refs[-1]
    features = hidden_ref.shape[1]

    @pl.when(pl.program_id(0) == 0)
    def _():
        sums_ref[...] = jnp.zeros_like(sums_ref)

    packed_grad = packed_grad_ref[...]
    normed_grad = contract(packed_grad, weight_ref[...], 1, 1)
    normal, inverse = normal_of(hidden_ref[...])
    result = middle_grad_ref[...] + norm_pull(normal, inverse, gains_ref[0:1], normed_grad)
    for result_ref in out_refs[:-1]:
        result_ref[...] = result.astype(result_ref.dtype)
    sums_ref[0:1] += column_sum(normed_grad * normal)
    sums_ref[1:2] += column_sum(normed_grad)
    sums_ref[2:3] += column_sum(packed_grad[:, :features].astype(single))
    sums_ref[3:4] += column_sum(packed_grad[:, 2 * features :].astype(single))


def project_grad(packed_grad, hidden, middle_grad, gains, joined, result_types):
    length, features = hidden.shape
    shape = jax.ShapeDtypeStruct
    return row_tiled(
        project_grad_kernel,
        "project_grad",
        length,
        [
            tile_of(3 * features),
            tile_of(features),
            tile_of(features),
            resident(gains.shape),
            resident((features, 3 * features)),
        ],
        [tile_of(features) for _ in result_types] + [resident((8, features))],
        [shape((length, features), result_type) for result_type in result_types]
        + [shape((8, features), single)],
        (packed_grad, hidden, middle_grad, gains, joined),
        6 * length * features * features,
    )


def term_blocks(terms, core, groups, row_unit, by_core):
    pieces = [left.shape[1] // (groups * row_unit) for left, _ in terms]
    widths = [right.shape[1] // (2 if by_core else 1) for _, right in terms]
    total = sum(count * width for count, width in zip(pieces, widths))
    chips = groups // 2
    out_shape = (chips, 2, row_unit, total) if by_core else (groups, row_unit, total)
    outputs = 2 if by_core else 1
    if row_unit % 16:
        columns = []
        for (left, right), count, width in zip(terms, pieces, widths):
            part = contract(left, right, 0, 0).astype(half)
            part = part.reshape(chips, 2, count, row_unit, -1, width).transpose(2, 1, 0, 4, 3, 5)
            columns += [part[piece] for piece in range(count)]
        whole = jnp.concatenate(columns, axis=-1)
        if not by_core:
            return [whole[:, :, 0].swapaxes(0, 1).reshape(out_shape)]
        return [
            lax.dynamic_index_in_dim(whole, which, 0, keepdims=False) for which in (1 - core, core)
        ]
    number = len(terms)

    def kernel(core_ref, *refs):
        sources = refs[: 2 * number]
        outs = refs[2 * number : 2 * number + outputs]
        buffers = refs[2 * number + outputs : 4 * number + outputs]
        semaphores = refs[4 * number + outputs]
        first_core = core_ref[0] == 0
        copies = [
            pltpu.make_async_copy(source, buffer, semaphores.at[index])
            for index, (source, buffer) in enumerate(zip(sources, buffers))
        ]
        for copy in copies:
            copy.start()
        start = 0
        for index, (count, width) in enumerate(zip(pieces, widths)):
            copies[2 * index].wait()
            copies[2 * index + 1].wait()
            left, right = buffers[2 * index], buffers[2 * index + 1]
            rows = groups * row_unit
            step = max(size for size in (768, 640, 512, 384, 256, 128) if width % size == 0)
            held = chips // count
            for turn in range(count):
                turned = left[:, turn * rows : (turn + 1) * rows].T
                some = slice(turn * held, (turn + 1) * held)
                for low in range(0, right.shape[1], step):
                    product = contract(turned, right[:, low : low + step], 1, 0).astype(half)
                    product = product.reshape(held, 2, count, row_unit, step)
                    side, inside = divmod(low, width)
                    for piece in range(count):
                        lanes = start + piece * width + inside
                        lanes = slice(lanes, lanes + step)
                        even, odd = product[:, 0, piece], product[:, 1, piece]
                        if by_core:
                            outs[0][some, side, :, lanes] = jnp.where(first_core, odd, even)
                            outs[1][some, side, :, lanes] = jnp.where(first_core, even, odd)
                        else:
                            for chip in range(held):
                                owner = 2 * (turn * held + chip)
                                outs[0][owner, :, lanes] = even[chip]
                                outs[0][owner + 1, :, lanes] = odd[chip]
            start += count * width

    anywhere = pl.BlockSpec(memory_space=pl.ANY)
    operands = [operand for term in terms for operand in term]
    size = sum(operand.size for operand in operands) * 2
    flops = sum(2 * left.size * right.shape[1] for left, right in terms)
    shape = jax.ShapeDtypeStruct(out_shape, half)
    return pl.pallas_call(
        kernel,
        in_specs=[pl.BlockSpec(memory_space=pltpu.SMEM)] + [anywhere] * len(operands),
        out_specs=[pl.BlockSpec(memory_space=pltpu.VMEM)] * outputs,
        out_shape=[shape] * outputs,
        scratch_shapes=[pltpu.VMEM(operand.shape, half) for operand in operands]
        + [pltpu.SemaphoreType.DMA((len(operands),))],
        compiler_params=pltpu.CompilerParams(vmem_limit_bytes=60 << 20),
        cost_estimate=estimate(flops, size + 2 * outputs * shape.size),
        name="term_blocks",
    )(core.reshape(1).astype(jnp.int32), *operands)


def per_device(
    tokens,
    time_embed,
    segment_ids,
    pad_mask,
    out_grad,
    qkv_weight,
    out_weight,
    up_weight,
    down_weight,
    norm_gains,
    bias_rows,
    up_bias,
):
    layers = qkv_weight.shape[0]
    features = tokens.shape[2]
    groups = lax.axis_size("wide")
    swap = [(0, 1), (1, 0)]

    def whole_sequence(part):
        return lax.all_to_all(part, "seq", split_axis=0, concat_axis=1, tiled=True)[0]

    core = lax.axis_index("wide") & 1
    place = lax.axis_index("seq")
    indices = jnp.stack([core, place]).astype(jnp.int32)
    row_unit = qkv_weight.shape[1]

    def across(bit):
        pairs = [(index, index ^ bit) for index in range(groups)]
        return lambda part: lax.ppermute(part, "wide", pairs)

    def beside_seq(part):
        return lax.ppermute(part, "seq", swap)

    def to_owners(part):
        return lax.psum_scatter(part, "wide", scatter_dimension=0, tiled=True)

    bit_of = lambda bit: (lax.axis_index("wide") >> (bit.bit_length() - 1)) & 1
    running = []

    def begin(steps, finish):
        entry = [steps, finish, next(steps), None]
        running.append(entry)
        return entry

    def launch(main, entries):
        fresh = [entry for entry in entries if entry in running and entry[3] is None]
        if fresh:
            sends = [[sent for sent, _ in entry[2]] for entry in fresh]
            main, sends = lax.optimization_barrier((main, sends))
            for entry, sent in zip(fresh, sends):
                entry[3] = [pass_on(part) for part, (_, pass_on) in zip(sent, entry[2])]
        return main

    def advance(main, *only):
        chosen = [entry for entry in only or list(running) if entry in running]
        main = launch(main, chosen)
        if not chosen:
            return main
        main, flying = lax.optimization_barrier((main, [entry[3] for entry in chosen]))
        for entry, arrived in zip(chosen, flying):
            entry[3] = None
            try:
                entry[2] = entry[0].send(arrived)
            except StopIteration as stop:
                entry[1](stop.value)
                running.remove(entry)
        return launch(main, chosen)

    def side_of(array, which, axis):
        return lax.dynamic_index_in_dim(array, which, axis, keepdims=False)

    chip_bits = [1 << number for number in range(groups.bit_length() - 2, 0, -1)]

    def join(current, received, which):
        lead = current.shape[0]
        joined = place_pieces(
            [current, received],
            (lead, 2) + current.shape[1:],
            [lambda ref: (slice(None), ref[0]), lambda ref: (slice(None), 1 - ref[0])],
            which.reshape(1).astype(jnp.int32),
        )
        return joined.reshape((2 * lead,) + current.shape[1:])

    def gather_columns(shard):
        rows, columns = shard.shape[0], shard.shape[1] // 2
        current = lax.dynamic_slice_in_dim(shard, place * columns, columns, axis=1)[None]
        for bit in chip_bits:
            (received,) = yield [(current, across(bit))]
            current = join(current, received, bit_of(bit))
        (aside,) = yield [(current, beside_seq)]
        passed = yield [(part, across(1)) for part in (current, aside)]

        def target(own_core, own_place):
            def where(ref):
                which_core = ref[0] if own_core else 1 - ref[0]
                which_place = ref[1] if own_place else 1 - ref[1]
                start = pl.multiple_of(which_place * columns, columns)
                return (slice(None), which_core, slice(None), pl.ds(start, columns))

            return where

        return place_pieces(
            [current, aside, *passed],
            (current.shape[0], 2, rows, 2 * columns),
            [target(True, True), target(True, False), target(False, True), target(False, False)],
            indices,
        ).reshape(-1, 2 * columns)

    def gather_rows(shard):
        rows, columns = shard.shape[0] // 2, shard.shape[1]
        current = side_of(shard.reshape(2, rows, columns), place, 0)[None]
        for bit in chip_bits[:-1]:
            (received,) = yield [(current, across(bit))]
            current = join(current, received, bit_of(bit))
        (received,) = yield [(current, beside_seq)]
        current = join(current, received, place).reshape(-1, 2 * rows, columns)
        for bit in chip_bits[-1:] + [1]:
            (received,) = yield [(current, across(bit))]
            current = join(current, received, bit_of(bit))
        return current.reshape(-1, columns)

    my_tokens = whole_sequence(tokens)

    small = jnp.concatenate(
        [norm_gains.reshape(-1), bias_rows.reshape(-1), up_bias.reshape(-1)]
    )
    side = small.reshape(row_unit, -1)
    side_width = side.shape[1]
    side = jnp.pad(side, ((0, 0), (0, -side_width % PAIR)))
    joined_parts = [jnp.concatenate([qkv_weight[0], out_weight[0], side], axis=1)]
    for layer in range(1, layers):
        parts = [qkv_weight[layer], out_weight[layer], up_weight[layer]]
        joined_parts.append(jnp.concatenate(parts, axis=1))
    joined = [lax.all_gather(part, "wide", axis=0, tiled=True) for part in joined_parts]
    downs = {
        layer: lax.all_gather(down_weight[layer], "wide", axis=0, tiled=True)
        for layer in range(1, layers)
    }
    small_whole = joined[0][:, -side.shape[1] :][:, :side_width].reshape(groups, -1)
    cut_gains = norm_gains.size
    cut_rows = cut_gains + bias_rows.size

    def whole_rows(part, count):
        parts = part.reshape(groups, layers, count, -1)
        return parts.transpose(1, 2, 0, 3).reshape(layers, count, -1).astype(single)

    all_gains = whole_rows(small_whole[:, :cut_gains], norm_gains.shape[1])
    all_offsets = whole_rows(small_whole[:, cut_gains:cut_rows], bias_rows.shape[1])
    all_up_bias = whole_rows(small_whole[:, cut_rows:], 1)[:, 0]

    matrices = [None] * layers
    ups = {}
    fetches = [
        begin(gather_columns(up_weight[0]), functools.partial(ups.__setitem__, 0)),
        begin(gather_rows(down_weight[0]), functools.partial(downs.__setitem__, 0)),
    ]
    marks = jnp.stack([segment_ids, pad_mask], axis=2)
    time_embed, marks = advance((time_embed, marks), *fetches)
    marks = whole_sequence(marks)
    for _ in chip_bits[2:]:
        time_embed, marks = advance((time_embed, marks), *fetches)
    doc, pad = marks[:, 0], marks[:, 1]
    positions = jnp.arange(doc.shape[0])
    allowed = (doc[:, None] == doc[None, :]) & (
        (pad[:, None] == 1) | (positions[:, None] == positions[None, :])
    )
    bias = jnp.where(allowed, 0.0, masked_bias)

    my_time = lax.dynamic_index_in_dim(time_embed, place, 0, keepdims=True)
    hidden = my_tokens.astype(single) + my_time
    saved = []
    for layer in range(layers):
        whole = joined[layer]
        gains, offsets = all_gains[layer], all_offsets[layer]
        before = hidden
        normed, packed = project(hidden, gains, offsets, whole)
        if layer == layers - 1:
            packed, out_grad = lax.optimization_barrier((packed, out_grad))
            my_upstream = whole_sequence(out_grad)
        packed = advance(packed, *fetches)
        attended, totals = attend_forward(packed, bias)
        attended = advance(attended, *fetches)
        while running:
            attended = advance(attended, *fetches)
        up = (whole, 4 * features // up_bias.shape[1] // groups) if layer else (ups[0], 0)
        matrices[layer] = (whole, up, downs[layer])
        fetches = []
        middle, second, activated, slope, hidden = feed(
            attended,
            hidden,
            gains,
            offsets,
            all_up_bias[layer][None],
            whole,
            up,
            downs[layer],
            single if layer < layers - 1 else half,
        )
        saved.append((before, normed, packed, totals, attended, middle, second, activated, slope))

    def split_back(result):
        parts = result.reshape(2, -1, features).astype(half)
        return lax.all_to_all(parts, "seq", split_axis=0, concat_axis=0, tiled=True)

    output = split_back(hidden)

    def total_of(addends):
        return functools.reduce(jnp.add, [addend.astype(single) for addend in addends])

    def shares_of(terms, low, high):
        shares, start = [], 0
        for left, right in terms:
            rows, each = [], right.shape[1] // 2
            if high is None:
                each *= 2
            for _ in range(left.shape[1] // (groups * row_unit)):
                window = slice(start, start + each)
                if high is None:
                    rows.append(low[:, window])
                else:
                    rows.append(jnp.concatenate([low[:, window], high[:, window]], axis=1))
                start += each
            shares.append(jnp.concatenate(rows, axis=0))
        return shares

    def scatter_group(terms):
        (whole,) = term_blocks(terms, core, groups, row_unit, False)
        whole = whole.reshape(groups * row_unit, -1)
        (share,) = yield [(whole, to_owners)]
        (received,) = yield [(share, beside_seq)]
        return shares_of(terms, share.astype(single) + received.astype(single), None)

    def reduce_group(terms):
        other, own = term_blocks(terms, core, groups, row_unit, True)
        (received,) = yield [(other, across(1))]
        shape = (2,) * len(chip_bits) + (2, row_unit, own.shape[-1])
        addends = [part.reshape(shape) for part in (own, received)]
        axis = len(chip_bits)
        for bit in [0] + chip_bits[:1:-1]:
            mine, pass_on = (bit_of(bit), across(bit)) if bit else (place, beside_seq)
            sent = total_of([side_of(part, 1 - mine, axis) for part in addends]).astype(half)
            (received,) = yield [(sent, pass_on)]
            addends = [side_of(part, mine, axis) for part in addends] + [received]
            axis -= 1
        far, near = chip_bits[:2]

        def corner(part, bits):
            part = side_of(part, bit_of(far) ^ (1 if bits & far else 0), 0)
            return side_of(part, bit_of(near) ^ (1 if bits & near else 0), 0)

        received = yield [
            (total_of([corner(part, bits) for part in addends]).astype(half), across(bits))
            for bits in (near, far, near | far)
        ]
        addends = [corner(part, 0) for part in addends] + received
        current = total_of(addends).astype(half)
        (received,) = yield [(current, beside_seq)]
        low = jnp.where(place == 0, current, received).astype(single)
        high = jnp.where(place == 0, received, current).astype(single)
        return shares_of(terms, low, high)

    def reduce_small(array):
        parts = [array.reshape((2,) * (len(chip_bits) + 1) + array.shape[1:])]
        pairs = [(2, 1, len(chip_bits) - 1)]
        pairs += [(bit, None, chip_bits.index(bit)) for bit in chip_bits[-2:1:-1]]
        pairs += [(chip_bits[0], chip_bits[1], 0)]
        for high, low, axis in pairs:

            def chosen(bits):
                def pick(part):
                    if low is not None:
                        part = side_of(part, bit_of(low) ^ (1 if bits & low else 0), axis + 1)
                    return side_of(part, bit_of(high) ^ (1 if bits & high else 0), axis)

                return total_of([pick(part) for part in parts])

            masks = [high] if low is None else [low, high, low | high]
            received = yield [(chosen(bits), across(bits)) for bits in masks]
            parts = [chosen(0)] + received
        current = total_of(parts)
        (received,) = yield [(current, beside_seq)]
        return current + received

    weight_grads = [[None] * 4 for _ in range(layers)]

    def begin_group(steps, layer, named):
        def finish(shares):
            for (part, _), share in zip(named, shares):
                weight_grads[layer][part] = share

        return begin(steps([term for _, term in named]), finish)

    gradient = my_upstream
    small_grads = [None] * layers
    held = []
    for layer in range(layers - 1, -1, -1):
        whole, up, down = matrices[layer]
        gains = all_gains[layer]
        hidden, normed, packed, totals, attended, middle, second, activated, slope = saved[layer]
        steps = scatter_group if layer else reduce_group
        branch, upper, middle_grad, attention_grad, upstream, sums, unit_sums = feed_grad(
            gradient, slope, middle, gains, whole, up, down
        )
        named = [(2, (second, upper)), (1, (attended, attention_grad))]
        if layer:
            held.append(begin_group(steps, layer, [(3, (activated, branch))] + named))
            upstream = launch(upstream, held[-1:])
        else:
            upstream = advance(upstream, first_group)
            upper, attention_grad, upstream = lax.optimization_barrier(
                (upper, attention_grad, upstream)
            )
            named = [(2, (second, upper)), (1, (attended, attention_grad))]
            second_group = begin_group(steps, layer, named)
            upstream = launch(upstream, [second_group])
            upstream = advance(upstream, second_group)
            upstream = advance(upstream, *held[:1])
        packed_grad = attend_backward(packed, bias, upstream, totals, attended)
        if layer == layers - 1:
            packed_grad, output = lax.optimization_barrier((packed_grad, output))
            output = output.astype(single)
        named = [(0, (normed, packed_grad))]
        if not layer:
            packed_grad = advance(packed_grad, first_group, second_group, *held[:1])
            last_group = begin_group(steps, layer, named)
            packed_grad = launch(packed_grad, [last_group])
            packed_grad = advance(packed_grad, last_group)
        gradient, *rounded, more_sums = project_grad(
            packed_grad, hidden, middle_grad, gains, whole, (single, half) if layer else (half,)
        )
        if layer == 1:
            below = (saved[0][7], rounded[0])
            first_group = begin_group(reduce_group, 0, [(3, below)])
            gradient = launch(gradient, [first_group])
        if layer:
            held.append(begin_group(steps, layer, named))
            gradient = launch(gradient, held[-1:])
        if layer == 1:
            gradient = advance(gradient, first_group)
        if not layer:
            gradient = advance(gradient, last_group)
        small_grads[layer] = (
            jnp.stack([more_sums[0], sums[1]]),
            jnp.stack([more_sums[1], more_sums[2], more_sums[3], sums[3], sums[2], sums[0]]),
            unit_sums[0],
        )

    def by_owner(parts):
        stacked = jnp.stack(parts)
        stacked = stacked.reshape(layers, -1, groups, stacked.shape[-1] // groups)
        return stacked.transpose(2, 0, 1, 3).reshape(groups, -1)

    owned = jnp.concatenate(
        [by_owner([small_grads[layer][part] for layer in range(layers)]) for part in range(3)],
        axis=1,
    )
    small_result = []
    begin(reduce_small(owned), small_result.append)
    output = launch(output, running[-1:])
    output = advance(output, first_group, second_group, *held)
    input_grad = split_back(gradient)
    while running:
        output = advance(output, last_group)
        output = advance(output, *[entry for entry in running if entry is not last_group])
    owned = small_result[0]
    input_grad = input_grad.astype(single)
    stacked = [
        jnp.stack([weight_grads[layer][part] for layer in range(layers)]) for part in range(4)
    ]
    return (
        output,
        input_grad,
        *stacked,
        owned[:cut_gains].reshape(norm_gains.shape),
        owned[cut_gains:cut_rows].reshape(bias_rows.shape),
        owned[cut_rows:].reshape(up_bias.shape),
    )


def solution(mesh):
    tokens_spec = P("wide", "seq", None)
    matrix_spec = P(None, "wide", None)
    rows_spec = P(None, None, "wide")
    return jax.shard_map(
        per_device,
        mesh=mesh,
        in_specs=(
            tokens_spec,
            P("wide", None),
            P("wide", "seq"),
            P("wide", "seq"),
            tokens_spec,
            matrix_spec,
            matrix_spec,
            matrix_spec,
            matrix_spec,
            rows_spec,
            rows_spec,
            P(None, "wide"),
        ),
        out_specs=(
            tokens_spec,
            tokens_spec,
            matrix_spec,
            matrix_spec,
            matrix_spec,
            matrix_spec,
            rows_spec,
            rows_spec,
            P(None, "wide"),
        ),
        check_vma=False,
    )
```

```python
import functools

import jax
import jax.numpy as jnp
from jax import lax
from jax.experimental import pallas as pl
from jax.experimental.pallas import tpu as pltpu
from jax.sharding import PartitionSpec as P

HEAD_SIZE = 64
PAIR = 2 * HEAD_SIZE
FORWARD_ROWS = 1024
BACKWARD_ROWS = 256
ROW_TILE = 256
FF_CHUNK = 768

epsilon = 1e-05
masked_bias = -1e30
half = jnp.bfloat16
single = jnp.float32


def estimate(flops, size):
    return pl.CostEstimate(flops=flops // 16, bytes_accessed=size // 16, transcendentals=0)


def contract(left, right, left_dim, right_dim):
    return lax.dot_general(
        left, right, (((left_dim,), (right_dim,)), ((), ())), preferred_element_type=jnp.float32
    )


def first_head_lanes():
    return lax.broadcasted_iota(jnp.int32, (1, PAIR), 1) < HEAD_SIZE


def one_head_of(pair, head):
    lanes = first_head_lanes()
    keep = lanes if head == 0 else jnp.logical_not(lanes)
    return jnp.where(keep, pair, jnp.zeros_like(pair))


def attend_kernel(query_ref, key_ref, value_ref, bias_ref, out_ref, total_ref, *, rows):
    keys = key_ref[...]
    values = value_ref[...]
    scale = jnp.asarray(HEAD_SIZE ** (-0.5), half)
    for start in range(0, keys.shape[0], rows):
        window = pl.ds(start, rows)
        queries = query_ref[window, :] * scale
        bias = bias_ref[:, window]
        attended = []
        for head in range(2):
            scores = contract(keys, one_head_of(queries, head), 1, 1) + bias
            top = jnp.max(scores, axis=0, keepdims=True)
            weights = jnp.exp(scores - top)
            total = jnp.sum(weights, axis=0, keepdims=True)
            mixed = contract(values, weights.astype(half), 0, 0) * (1.0 / total)
            attended.append(mixed[HEAD_SIZE * head : HEAD_SIZE * (head + 1)])
            total_ref[head : head + 1, window] = top + jnp.log(total)
        out_ref[window, :] = jnp.concatenate(attended, 0).T.astype(half)


def attend_forward(packed, bias):
    length = packed.shape[0]
    features = packed.shape[1] // 3
    pairs = features // PAIR
    columns = lambda part: pl.BlockSpec((length, PAIR), lambda i: (0, part * pairs + i))
    return pl.pallas_call(
        functools.partial(attend_kernel, rows=FORWARD_ROWS),
        grid=(pairs,),
        in_specs=[
            columns(0),
            columns(1),
            columns(2),
            pl.BlockSpec((length, length), lambda i: (0, 0)),
        ],
        out_specs=[columns(0), pl.BlockSpec((None, 2, length), lambda i: (i, 0, 0))],
        out_shape=[
            jax.ShapeDtypeStruct((length, features), half),
            jax.ShapeDtypeStruct((pairs, 2, length), single),
        ],
        compiler_params=pltpu.CompilerParams(vmem_limit_bytes=56 << 20),
        cost_estimate=estimate(16 * length * length * features, 8 * length * features),
        name="attend_forward",
    )(packed, packed, packed, bias)


def attend_grad_kernel(
    query_ref,
    key_ref,
    value_ref,
    bias_ref,
    upstream_ref,
    total_ref,
    attended_ref,
    out_ref,
    key_sum,
    value_sum,
    *,
    rows,
):
    pair = pl.program_id(0)
    features = out_ref.shape[1] // 3
    keys = key_ref[...]
    values = value_ref[...]
    scale = HEAD_SIZE ** (-0.5)
    for start in range(0, keys.shape[0], rows):
        window = pl.ds(start, rows)
        queries = query_ref[window, :] * jnp.asarray(scale, half)
        upstream = upstream_ref[window, :]
        product = (upstream.astype(single) * attended_ref[window, :].astype(single)).T
        bias = bias_ref[:, window]
        query_grads, key_grad, value_grad = [], 0.0, 0.0
        for head in range(2):
            head_queries = one_head_of(queries, head)
            head_upstream = one_head_of(upstream, head)
            inner = jnp.sum(
                product[HEAD_SIZE * head : HEAD_SIZE * (head + 1)], axis=0, keepdims=True
            )
            scores = contract(keys, head_queries, 1, 1) + bias
            weights = jnp.exp(scores - total_ref[head : head + 1, window])
            weight_grads = contract(values, head_upstream, 1, 1)
            score_grads = (weights * (weight_grads - inner)).astype(half)
            value_grad = value_grad + contract(weights.astype(half), head_upstream, 1, 0)
            key_grad = key_grad + contract(score_grads, head_queries, 1, 0)
            query_grads.append(
                contract(keys, score_grads, 0, 0)[HEAD_SIZE * head : HEAD_SIZE * (head + 1)]
            )
        out_ref[window, pl.ds(pl.multiple_of(pair * PAIR, PAIR), PAIR)] = (
            jnp.concatenate(query_grads, 0).T * scale
        ).astype(half)
        if start == 0:
            key_sum[...] = key_grad
            value_sum[...] = value_grad
        else:
            key_sum[...] += key_grad
            value_sum[...] += value_grad
    out_ref[:, pl.ds(pl.multiple_of(features + pair * PAIR, PAIR), PAIR)] = key_sum[...].astype(
        half
    )
    out_ref[:, pl.ds(pl.multiple_of(2 * features + pair * PAIR, PAIR), PAIR)] = value_sum[
        ...
    ].astype(half)


def attend_backward(packed, bias, upstream, totals, attended):
    length = packed.shape[0]
    features = packed.shape[1] // 3
    pairs = features // PAIR
    columns = lambda part: pl.BlockSpec((length, PAIR), lambda i: (0, part * pairs + i))
    return pl.pallas_call(
        functools.partial(attend_grad_kernel, rows=BACKWARD_ROWS),
        grid=(pairs,),
        in_specs=[
            columns(0),
            columns(1),
            columns(2),
            pl.BlockSpec((length, length), lambda i: (0, 0)),
            columns(0),
            pl.BlockSpec((None, 2, length), lambda i: (i, 0, 0)),
            columns(0),
        ],
        out_specs=pl.BlockSpec((length, 3 * features), lambda i: (0, 0)),
        out_shape=jax.ShapeDtypeStruct((length, 3 * features), half),
        scratch_shapes=[pltpu.VMEM((length, PAIR), single)] * 2,
        compiler_params=pltpu.CompilerParams(vmem_limit_bytes=56 << 20),
        cost_estimate=estimate(40 * length * length * features, 16 * length * features),
        name="attend_backward",
    )(packed, packed, packed, bias, upstream, totals, attended)


def place_pieces(pieces, out_shape, targets, indices):
    def kernel(index_ref, *refs):
        sources, out_ref, semaphores = refs[: len(pieces)], refs[-2], refs[-1]
        copies = [
            pltpu.make_async_copy(
                source, out_ref.at[target(index_ref)], semaphores.at[number]
            )
            for number, (source, target) in enumerate(zip(sources, targets))
        ]
        for copy in copies:
            copy.start()
        for copy in copies:
            copy.wait()

    size = 2 * 2
    for extent in out_shape:
        size *= extent
    anywhere = pl.BlockSpec(memory_space=pl.ANY)
    return pl.pallas_call(
        kernel,
        in_specs=[pl.BlockSpec(memory_space=pltpu.SMEM)] + [anywhere] * len(pieces),
        out_specs=pl.BlockSpec(memory_space=pltpu.VMEM),
        out_shape=jax.ShapeDtypeStruct(out_shape, pieces[0].dtype),
        scratch_shapes=[pltpu.SemaphoreType.DMA((len(pieces),))],
        compiler_params=pltpu.CompilerParams(vmem_limit_bytes=32 << 20),
        cost_estimate=estimate(0, size),
        name="place_pieces",
    )(indices, *pieces)


def normal_of(hidden):
    center = hidden - jnp.mean(hidden, axis=-1, keepdims=True)
    inverse = lax.rsqrt(jnp.mean(center * center, axis=-1, keepdims=True) + epsilon)
    return center * inverse, inverse


def norm_pull(normal, inverse, gain, upstream):
    scaled = upstream * gain
    slope = jnp.mean(scaled, axis=-1, keepdims=True)
    tilt = jnp.mean(scaled * normal, axis=-1, keepdims=True)
    return inverse * (scaled - slope - normal * tilt)


def column_sum(array):
    return jnp.sum(array, axis=0, keepdims=True)


def tile_of(columns):
    return pl.BlockSpec((ROW_TILE, columns), lambda i: (i, 0))


def resident(shape, *index):
    place = index or (0,) * len(shape)
    return pl.BlockSpec(shape, lambda i: place, pipeline_mode=pl.Buffered(1))


def row_tiled(kernel, name, length, in_specs, out_specs, out_shape, operands, flops):
    size = sum(operand.size * operand.dtype.itemsize for operand in operands)
    size += sum(shape.size * jnp.dtype(shape.dtype).itemsize for shape in out_shape)
    return pl.pallas_call(
        kernel,
        grid=(length // ROW_TILE,),
        in_specs=in_specs,
        out_specs=out_specs,
        out_shape=out_shape,
        compiler_params=pltpu.CompilerParams(vmem_limit_bytes=56 << 20),
        cost_estimate=estimate(flops, size),
        name=name,
    )(*operands)


def project_kernel(hidden_ref, gains_ref, offsets_ref, weight_ref, normed_ref, packed_ref):
    features = hidden_ref.shape[1]
    normal, _ = normal_of(hidden_ref[...])
    normed = (normal * gains_ref[0:1] + offsets_ref[0:1]).astype(half)
    normed_ref[...] = normed
    for part in range(3):
        window = slice(part * features, (part + 1) * features)
        product = contract(normed, weight_ref[:, window], 1, 0)
        if part != 1:
            row = 1 if part == 0 else 2
            product = product + offsets_ref[row : row + 1]
        packed_ref[:, window] = product.astype(half)


def project(hidden, gains, offsets, joined):
    length, features = hidden.shape
    return row_tiled(
        project_kernel,
        "project",
        length,
        [
            tile_of(features),
            resident(gains.shape),
            resident(offsets.shape),
            resident((features, 3 * features)),
        ],
        [tile_of(features), tile_of(3 * features)],
        [
            jax.ShapeDtypeStruct((length, features), half),
            jax.ShapeDtypeStruct((length, 3 * features), half),
        ],
        (hidden, gains, offsets, joined),
        6 * length * features * features,
    )


def feed_kernel(
    attended_ref,
    hidden_ref,
    gains_ref,
    offsets_ref,
    up_bias_ref,
    out_weight_ref,
    up_ref,
    down_ref,
    middle_ref,
    second_ref,
    activated_ref,
    slope_ref,
    result_ref,
):
    hidden_units = up_ref.shape[1]
    middle = hidden_ref[...] + (
        contract(attended_ref[...], out_weight_ref[...], 1, 0) + offsets_ref[3:4]
    )
    middle_ref[...] = middle
    normal, _ = normal_of(middle)
    second = (normal * gains_ref[1:2] + offsets_ref[4:5]).astype(half)
    second_ref[...] = second
    result = middle + offsets_ref[5:6]
    rate = 0.7978845608028654
    for start in range(0, hidden_units, FF_CHUNK):
        window = slice(start, start + FF_CHUNK)
        value = contract(second, up_ref[:, window], 1, 0) + up_bias_ref[:, window]
        square = value * value
        bent = jnp.tanh(value * (rate + (rate * 0.044715) * square))
        opened = 0.5 + 0.5 * bent
        activated = (value * opened).astype(half)
        activated_ref[:, window] = activated
        curve = (value * (0.5 * rate + (1.5 * rate * 0.044715) * square)) * (1.0 - bent * bent)
        slope_ref[:, window] = (opened + curve).astype(half)
        result = result + contract(activated, down_ref[window, :], 1, 0)
    result_ref[...] = result.astype(result_ref.dtype)


def feed(attended, hidden, gains, offsets, up_bias, joined, up, down, result_type):
    length, features = hidden.shape
    units = down.shape[0]
    up_array, up_place = up
    shape = jax.ShapeDtypeStruct
    return row_tiled(
        feed_kernel,
        "feed",
        length,
        [
            tile_of(features),
            tile_of(features),
            resident(gains.shape),
            resident(offsets.shape),
            resident(up_bias.shape),
            resident((features, features), 0, 3),
            resident((features, units), 0, up_place),
            resident(down.shape),
        ],
        [tile_of(features), tile_of(features), tile_of(units), tile_of(units), tile_of(features)],
        [
            shape((length, features), single),
            shape((length, features), half),
            shape((length, units), half),
            shape((length, units), half),
            shape((length, features), result_type),
        ],
        (attended, hidden, gains, offsets, up_bias, joined, up_array, down),
        2 * length * features * (features + 2 * units),
    )


def feed_grad_kernel(
    gradient_ref,
    slope_ref,
    middle_ref,
    gains_ref,
    out_weight_ref,
    up_ref,
    down_ref,
    branch_ref,
    upper_ref,
    middle_grad_ref,
    attention_grad_ref,
    upstream_ref,
    sums_ref,
    unit_sums_ref,
):
    units = up_ref.shape[1]

    @pl.when(pl.program_id(0) == 0)
    def _():
        sums_ref[...] = jnp.zeros_like(sums_ref)
        unit_sums_ref[...] = jnp.zeros_like(unit_sums_ref)

    gradient = gradient_ref[...].astype(single)
    branch = gradient.astype(half)
    branch_ref[...] = branch
    sums_ref[0:1] += column_sum(branch.astype(single))
    second_grad = jnp.zeros(gradient.shape, single)
    for start in range(0, units, FF_CHUNK):
        window = slice(start, start + FF_CHUNK)
        pulled = contract(branch, down_ref[window, :], 1, 1) * slope_ref[:, window].astype(single)
        upper = pulled.astype(half)
        upper_ref[:, window] = upper
        unit_sums_ref[:, window] += column_sum(upper.astype(single))
        second_grad = second_grad + contract(upper, up_ref[:, window], 1, 1)
    normal, inverse = normal_of(middle_ref[...])
    middle_grad = gradient + norm_pull(normal, inverse, gains_ref[1:2], second_grad)
    sums_ref[1:2] += column_sum(second_grad * normal)
    sums_ref[2:3] += column_sum(second_grad)
    middle_grad_ref[...] = middle_grad
    attention_grad = middle_grad.astype(half)
    attention_grad_ref[...] = attention_grad
    sums_ref[3:4] += column_sum(attention_grad.astype(single))
    upstream_ref[...] = contract(attention_grad, out_weight_ref[...], 1, 1).astype(half)


def feed_grad(gradient, slope, middle, gains, joined, up, down):
    up_array, up_place = up
    length, features = middle.shape
    units = down.shape[0]
    shape = jax.ShapeDtypeStruct
    return row_tiled(
        feed_grad_kernel,
        "feed_grad",
        length,
        [
            tile_of(features),
            tile_of(units),
            tile_of(features),
            resident(gains.shape),
            resident((features, features), 0, 3),
            resident((features, units), 0, up_place),
            resident(down.shape),
        ],
        [
            tile_of(features),
            tile_of(units),
            tile_of(features),
            tile_of(features),
            tile_of(features),
            resident((8, features)),
            resident((1, units)),
        ],
        [
            shape((length, features), half),
            shape((length, units), half),
            shape((length, features), single),
            shape((length, features), half),
            shape((length, features), half),
            shape((8, features), single),
            shape((1, units), single),
        ],
        (gradient, slope, middle, gains, joined, up_array, down),
        2 * length * features * (features + 2 * units),
    )


def project_grad_kernel(
    packed_grad_ref, hidden_ref, middle_grad_ref, gains_ref, weight_ref, *out_refs
):
    sums_ref = out_refs[-1]
    features = hidden_ref.shape[1]

    @pl.when(pl.program_id(0) == 0)
    def _():
        sums_ref[...] = jnp.zeros_like(sums_ref)

    packed_grad = packed_grad_ref[...]
    normed_grad = contract(packed_grad, weight_ref[...], 1, 1)
    normal, inverse = normal_of(hidden_ref[...])
    result = middle_grad_ref[...] + norm_pull(normal, inverse, gains_ref[0:1], normed_grad)
    for result_ref in out_refs[:-1]:
        result_ref[...] = result.astype(result_ref.dtype)
    sums_ref[0:1] += column_sum(normed_grad * normal)
    sums_ref[1:2] += column_sum(normed_grad)
    sums_ref[2:3] += column_sum(packed_grad[:, :features].astype(single))
    sums_ref[3:4] += column_sum(packed_grad[:, 2 * features :].astype(single))


def project_grad(packed_grad, hidden, middle_grad, gains, joined, result_types):
    length, features = hidden.shape
    shape = jax.ShapeDtypeStruct
    return row_tiled(
        project_grad_kernel,
        "project_grad",
        length,
        [
            tile_of(3 * features),
            tile_of(features),
            tile_of(features),
            resident(gains.shape),
            resident((features, 3 * features)),
        ],
        [tile_of(features) for _ in result_types] + [resident((8, features))],
        [shape((length, features), result_type) for result_type in result_types]
        + [shape((8, features), single)],
        (packed_grad, hidden, middle_grad, gains, joined),
        6 * length * features * features,
    )


def term_blocks(terms, core, groups, row_unit, by_core):
    pieces = [left.shape[1] // (groups * row_unit) for left, _ in terms]
    widths = [right.shape[1] // (2 if by_core else 1) for _, right in terms]
    total = sum(count * width for count, width in zip(pieces, widths))
    chips = groups // 2
    out_shape = (chips, 2, row_unit, total) if by_core else (groups, row_unit, total)
    outputs = 2 if by_core else 1
    if row_unit % 16:
        columns = []
        for (left, right), count, width in zip(terms, pieces, widths):
            part = contract(left, right, 0, 0).astype(half)
            part = part.reshape(chips, 2, count, row_unit, -1, width).transpose(2, 1, 0, 4, 3, 5)
            columns += [part[piece] for piece in range(count)]
        whole = jnp.concatenate(columns, axis=-1)
        if not by_core:
            return [whole[:, :, 0].swapaxes(0, 1).reshape(out_shape)]
        return [
            lax.dynamic_index_in_dim(whole, which, 0, keepdims=False) for which in (1 - core, core)
        ]
    number = len(terms)

    def kernel(core_ref, *refs):
        sources = refs[: 2 * number]
        outs = refs[2 * number : 2 * number + outputs]
        buffers = refs[2 * number + outputs : 4 * number + outputs]
        semaphores = refs[4 * number + outputs]
        first_core = core_ref[0] == 0
        copies = [
            pltpu.make_async_copy(source, buffer, semaphores.at[index])
            for index, (source, buffer) in enumerate(zip(sources, buffers))
        ]
        for copy in copies:
            copy.start()
        start = 0
        for index, (count, width) in enumerate(zip(pieces, widths)):
            copies[2 * index].wait()
            copies[2 * index + 1].wait()
            left, right = buffers[2 * index], buffers[2 * index + 1]
            rows = groups * row_unit
            columns = right.shape[1]
            step = max(size for size in (768, 640, 512, 384, 256, 128) if columns % size == 0)
            held = chips // count
            for turn in range(count):
                turned = left[:, turn * rows : (turn + 1) * rows].T
                some = slice(turn * held, (turn + 1) * held)
                for low in range(0, columns, step):
                    product = contract(turned, right[:, low : low + step], 1, 0).astype(half)
                    product = product.reshape(held, 2, count, row_unit, step)
                    for side in range(columns // width):
                        first = max(low, side * width)
                        last = min(low + step, (side + 1) * width)
                        if first >= last:
                            continue
                        for piece in range(count):
                            lanes = start + piece * width + first - side * width
                            lanes = slice(lanes, lanes + last - first)
                            even = product[:, 0, piece, :, first - low : last - low]
                            odd = product[:, 1, piece, :, first - low : last - low]
                            if by_core:
                                outs[0][some, side, :, lanes] = jnp.where(first_core, odd, even)
                                outs[1][some, side, :, lanes] = jnp.where(first_core, even, odd)
                            else:
                                for chip in range(held):
                                    owner = 2 * (turn * held + chip)
                                    outs[0][owner, :, lanes] = even[chip]
                                    outs[0][owner + 1, :, lanes] = odd[chip]
            start += count * width

    anywhere = pl.BlockSpec(memory_space=pl.ANY)
    operands = [operand for term in terms for operand in term]
    size = sum(operand.size for operand in operands) * 2
    flops = sum(2 * left.size * right.shape[1] for left, right in terms)
    shape = jax.ShapeDtypeStruct(out_shape, half)
    return pl.pallas_call(
        kernel,
        in_specs=[pl.BlockSpec(memory_space=pltpu.SMEM)] + [anywhere] * len(operands),
        out_specs=[pl.BlockSpec(memory_space=pltpu.VMEM)] * outputs,
        out_shape=[shape] * outputs,
        scratch_shapes=[pltpu.VMEM(operand.shape, half) for operand in operands]
        + [pltpu.SemaphoreType.DMA((len(operands),))],
        compiler_params=pltpu.CompilerParams(vmem_limit_bytes=60 << 20),
        cost_estimate=estimate(flops, size + 2 * outputs * shape.size),
        name="term_blocks",
    )(core.reshape(1).astype(jnp.int32), *operands)


def per_device(
    tokens,
    time_embed,
    segment_ids,
    pad_mask,
    out_grad,
    qkv_weight,
    out_weight,
    up_weight,
    down_weight,
    norm_gains,
    bias_rows,
    up_bias,
):
    layers = qkv_weight.shape[0]
    features = tokens.shape[2]
    groups = lax.axis_size("wide")
    swap = [(0, 1), (1, 0)]

    def whole_sequence(part):
        return lax.all_to_all(part, "seq", split_axis=0, concat_axis=1, tiled=True)[0]

    core = lax.axis_index("wide") & 1
    place = lax.axis_index("seq")
    indices = jnp.stack([core, place]).astype(jnp.int32)
    row_unit = qkv_weight.shape[1]

    def across(bit):
        pairs = [(index, index ^ bit) for index in range(groups)]
        return lambda part: lax.ppermute(part, "wide", pairs)

    def beside_seq(part):
        return lax.ppermute(part, "seq", swap)

    def to_owners(part):
        return lax.psum_scatter(part, "wide", scatter_dimension=0, tiled=True)

    bit_of = lambda bit: (lax.axis_index("wide") >> (bit.bit_length() - 1)) & 1
    running = []

    def begin(steps, finish):
        entry = [steps, finish, next(steps), None]
        running.append(entry)
        return entry

    def launch(main, entries):
        fresh = [entry for entry in entries if entry in running and entry[3] is None]
        if fresh:
            sends = [[sent for sent, _ in entry[2]] for entry in fresh]
            main, sends = lax.optimization_barrier((main, sends))
            for entry, sent in zip(fresh, sends):
                entry[3] = [pass_on(part) for part, (_, pass_on) in zip(sent, entry[2])]
        return main

    def advance(main, *only):
        chosen = [entry for entry in only or list(running) if entry in running]
        main = launch(main, chosen)
        if not chosen:
            return main
        main, flying = lax.optimization_barrier((main, [entry[3] for entry in chosen]))
        for entry, arrived in zip(chosen, flying):
            entry[3] = None
            try:
                entry[2] = entry[0].send(arrived)
            except StopIteration as stop:
                entry[1](stop.value)
                running.remove(entry)
        return launch(main, chosen)

    def side_of(array, which, axis):
        return lax.dynamic_index_in_dim(array, which, axis, keepdims=False)

    chip_bits = [1 << number for number in range(groups.bit_length() - 2, 0, -1)]

    def join(current, received, which):
        lead = current.shape[0]
        joined = place_pieces(
            [current, received],
            (lead, 2) + current.shape[1:],
            [lambda ref: (slice(None), ref[0]), lambda ref: (slice(None), 1 - ref[0])],
            which.reshape(1).astype(jnp.int32),
        )
        return joined.reshape((2 * lead,) + current.shape[1:])

    def gather_columns(shard):
        rows, columns = shard.shape[0], shard.shape[1] // 2
        current = lax.dynamic_slice_in_dim(shard, place * columns, columns, axis=1)[None]
        for bit in chip_bits:
            (received,) = yield [(current, across(bit))]
            current = join(current, received, bit_of(bit))
        (aside,) = yield [(current, beside_seq)]
        passed = yield [(part, across(1)) for part in (current, aside)]

        def target(own_core, own_place):
            def where(ref):
                which_core = ref[0] if own_core else 1 - ref[0]
                which_place = ref[1] if own_place else 1 - ref[1]
                start = pl.multiple_of(which_place * columns, columns)
                return (slice(None), which_core, slice(None), pl.ds(start, columns))

            return where

        return place_pieces(
            [current, aside, *passed],
            (current.shape[0], 2, rows, 2 * columns),
            [target(True, True), target(True, False), target(False, True), target(False, False)],
            indices,
        ).reshape(-1, 2 * columns)

    def gather_rows(shard):
        rows, columns = shard.shape[0] // 2, shard.shape[1]
        current = side_of(shard.reshape(2, rows, columns), place, 0)[None]
        for bit in chip_bits[:-1]:
            (received,) = yield [(current, across(bit))]
            current = join(current, received, bit_of(bit))
        (received,) = yield [(current, beside_seq)]
        current = join(current, received, place).reshape(-1, 2 * rows, columns)
        for bit in chip_bits[-1:] + [1]:
            (received,) = yield [(current, across(bit))]
            current = join(current, received, bit_of(bit))
        return current.reshape(-1, columns)

    my_tokens = whole_sequence(tokens)

    small = jnp.concatenate(
        [norm_gains.reshape(-1), bias_rows.reshape(-1), up_bias.reshape(-1)]
    )
    side = small.reshape(row_unit, -1)
    side_width = side.shape[1]
    side = jnp.pad(side, ((0, 0), (0, -side_width % PAIR)))
    joined_parts = [jnp.concatenate([qkv_weight[0], out_weight[0], side], axis=1)]
    for layer in range(1, layers):
        parts = [qkv_weight[layer], out_weight[layer], up_weight[layer]]
        joined_parts.append(jnp.concatenate(parts, axis=1))
    joined = [lax.all_gather(part, "wide", axis=0, tiled=True) for part in joined_parts]
    downs = {
        layer: lax.all_gather(down_weight[layer], "wide", axis=0, tiled=True)
        for layer in range(1, layers)
    }
    small_whole = joined[0][:, -side.shape[1] :][:, :side_width].reshape(groups, -1)
    cut_gains = norm_gains.size
    cut_rows = cut_gains + bias_rows.size

    def whole_rows(part, count):
        parts = part.reshape(groups, layers, count, -1)
        return parts.transpose(1, 2, 0, 3).reshape(layers, count, -1).astype(single)

    all_gains = whole_rows(small_whole[:, :cut_gains], norm_gains.shape[1])
    all_offsets = whole_rows(small_whole[:, cut_gains:cut_rows], bias_rows.shape[1])
    all_up_bias = whole_rows(small_whole[:, cut_rows:], 1)[:, 0]

    matrices = [None] * layers
    ups = {}
    fetches = [
        begin(gather_columns(up_weight[0]), functools.partial(ups.__setitem__, 0)),
        begin(gather_rows(down_weight[0]), functools.partial(downs.__setitem__, 0)),
    ]
    marks = jnp.stack([segment_ids, pad_mask], axis=2)
    time_embed, marks = advance((time_embed, marks), *fetches)
    marks = whole_sequence(marks)
    for _ in chip_bits[2:]:
        time_embed, marks = advance((time_embed, marks), *fetches)
    doc, pad = marks[:, 0], marks[:, 1]
    positions = jnp.arange(doc.shape[0])
    allowed = (doc[:, None] == doc[None, :]) & (
        (pad[:, None] == 1) | (positions[:, None] == positions[None, :])
    )
    bias = jnp.where(allowed, 0.0, masked_bias)

    my_time = lax.dynamic_index_in_dim(time_embed, place, 0, keepdims=True)
    hidden = my_tokens.astype(single) + my_time
    saved = []
    for layer in range(layers):
        whole = joined[layer]
        gains, offsets = all_gains[layer], all_offsets[layer]
        before = hidden
        normed, packed = project(hidden, gains, offsets, whole)
        if layer == layers - 1:
            packed, out_grad = lax.optimization_barrier((packed, out_grad))
            my_upstream = whole_sequence(out_grad)
        packed = advance(packed, *fetches)
        attended, totals = attend_forward(packed, bias)
        attended = advance(attended, *fetches)
        while running:
            attended = advance(attended, *fetches)
        up = (whole, 4 * features // up_bias.shape[1] // groups) if layer else (ups[0], 0)
        matrices[layer] = (whole, up, downs[layer])
        fetches = []
        middle, second, activated, slope, hidden = feed(
            attended,
            hidden,
            gains,
            offsets,
            all_up_bias[layer][None],
            whole,
            up,
            downs[layer],
            single if layer < layers - 1 else half,
        )
        saved.append((before, normed, packed, totals, attended, middle, second, activated, slope))

    def split_back(result):
        parts = result.reshape(2, -1, features).astype(half)
        return lax.all_to_all(parts, "seq", split_axis=0, concat_axis=0, tiled=True)

    output = split_back(hidden)

    def total_of(addends):
        return functools.reduce(jnp.add, [addend.astype(single) for addend in addends])

    def shares_of(terms, low, high):
        shares, start = [], 0
        for left, right in terms:
            rows, each = [], right.shape[1] // 2
            if high is None:
                each *= 2
            for _ in range(left.shape[1] // (groups * row_unit)):
                window = slice(start, start + each)
                if high is None:
                    rows.append(low[:, window])
                else:
                    rows.append(jnp.concatenate([low[:, window], high[:, window]], axis=1))
                start += each
            shares.append(jnp.concatenate(rows, axis=0))
        return shares

    def scatter_group(terms):
        (whole,) = term_blocks(terms, core, groups, row_unit, False)
        whole = whole.reshape(groups * row_unit, -1)
        (share,) = yield [(whole, to_owners)]
        (received,) = yield [(share, beside_seq)]
        return shares_of(terms, share.astype(single) + received.astype(single), None)

    def reduce_group(terms):
        other, own = term_blocks(terms, core, groups, row_unit, True)
        (received,) = yield [(other, across(1))]
        shape = (2,) * len(chip_bits) + (2, row_unit, own.shape[-1])
        addends = [part.reshape(shape) for part in (own, received)]
        axis = len(chip_bits)
        for bit in [0] + chip_bits[:1:-1]:
            mine, pass_on = (bit_of(bit), across(bit)) if bit else (place, beside_seq)
            sent = total_of([side_of(part, 1 - mine, axis) for part in addends]).astype(half)
            (received,) = yield [(sent, pass_on)]
            addends = [side_of(part, mine, axis) for part in addends] + [received]
            axis -= 1
        far, near = chip_bits[:2]

        def corner(part, bits):
            part = side_of(part, bit_of(far) ^ (1 if bits & far else 0), 0)
            return side_of(part, bit_of(near) ^ (1 if bits & near else 0), 0)

        received = yield [
            (total_of([corner(part, bits) for part in addends]).astype(half), across(bits))
            for bits in (near, far, near | far)
        ]
        addends = [corner(part, 0) for part in addends] + received
        current = total_of(addends).astype(half)
        (received,) = yield [(current, beside_seq)]
        low = jnp.where(place == 0, current, received).astype(single)
        high = jnp.where(place == 0, received, current).astype(single)
        return shares_of(terms, low, high)

    def reduce_small(array):
        parts = [array.reshape((2,) * (len(chip_bits) + 1) + array.shape[1:])]
        pairs = [(2, 1, len(chip_bits) - 1)]
        pairs += [(bit, None, chip_bits.index(bit)) for bit in chip_bits[-2:1:-1]]
        pairs += [(chip_bits[0], chip_bits[1], 0)]
        for high, low, axis in pairs:

            def chosen(bits):
                def pick(part):
                    if low is not None:
                        part = side_of(part, bit_of(low) ^ (1 if bits & low else 0), axis + 1)
                    return side_of(part, bit_of(high) ^ (1 if bits & high else 0), axis)

                return total_of([pick(part) for part in parts])

            masks = [high] if low is None else [low, high, low | high]
            received = yield [(chosen(bits), across(bits)) for bits in masks]
            parts = [chosen(0)] + received
        current = total_of(parts)
        (received,) = yield [(current, beside_seq)]
        return current + received

    weight_grads = [[None] * 4 for _ in range(layers)]

    def begin_group(steps, layer, named):
        def finish(shares):
            for (part, _), share in zip(named, shares):
                weight_grads[layer][part] = share

        return begin(steps([term for _, term in named]), finish)

    gradient = my_upstream
    small_grads = [None] * layers
    held = []
    for layer in range(layers - 1, -1, -1):
        whole, up, down = matrices[layer]
        gains = all_gains[layer]
        hidden, normed, packed, totals, attended, middle, second, activated, slope = saved[layer]
        steps = scatter_group if layer else reduce_group
        branch, upper, middle_grad, attention_grad, upstream, sums, unit_sums = feed_grad(
            gradient, slope, middle, gains, whole, up, down
        )
        named = [(2, (second, upper)), (1, (attended, attention_grad))]
        if layer:
            held.append(begin_group(steps, layer, [(3, (activated, branch))] + named))
            upstream = launch(upstream, held[-1:])
        else:
            upstream = advance(upstream, first_group)
            upper, attention_grad, upstream = lax.optimization_barrier(
                (upper, attention_grad, upstream)
            )
            named = [(2, (second, upper)), (1, (attended, attention_grad))]
            second_group = begin_group(steps, layer, named)
            upstream = launch(upstream, [second_group])
            upstream = advance(upstream, second_group)
            upstream = advance(upstream, *held[:1])
        packed_grad = attend_backward(packed, bias, upstream, totals, attended)
        if layer == layers - 1:
            packed_grad, output = lax.optimization_barrier((packed_grad, output))
            output = output.astype(single)
        named = [(0, (normed, packed_grad))]
        if not layer:
            packed_grad = advance(packed_grad, first_group, second_group, *held[:1])
            last_group = begin_group(steps, layer, named)
            packed_grad = launch(packed_grad, [last_group])
            packed_grad = advance(packed_grad, last_group)
        gradient, *rounded, more_sums = project_grad(
            packed_grad, hidden, middle_grad, gains, whole, (single, half) if layer else (half,)
        )
        if layer == 1:
            below = (saved[0][7], rounded[0])
            first_group = begin_group(reduce_group, 0, [(3, below)])
            gradient = launch(gradient, [first_group])
        if layer:
            held.append(begin_group(steps, layer, named))
            gradient = launch(gradient, held[-1:])
        if layer == 1:
            gradient = advance(gradient, first_group)
        if not layer:
            gradient = advance(gradient, last_group)
        small_grads[layer] = (
            jnp.stack([more_sums[0], sums[1]]),
            jnp.stack([more_sums[1], more_sums[2], more_sums[3], sums[3], sums[2], sums[0]]),
            unit_sums[0],
        )

    def by_owner(parts):
        stacked = jnp.stack(parts)
        stacked = stacked.reshape(layers, -1, groups, stacked.shape[-1] // groups)
        return stacked.transpose(2, 0, 1, 3).reshape(groups, -1)

    owned = jnp.concatenate(
        [by_owner([small_grads[layer][part] for layer in range(layers)]) for part in range(3)],
        axis=1,
    )
    small_result = []
    begin(reduce_small(owned), small_result.append)
    output = launch(output, running[-1:])
    output = advance(output, first_group, second_group, *held)
    input_grad = split_back(gradient)
    while running:
        output = advance(output, last_group)
        output = advance(output, *[entry for entry in running if entry is not last_group])
    owned = small_result[0]
    input_grad = input_grad.astype(single)
    stacked = [
        jnp.stack([weight_grads[layer][part] for layer in range(layers)]) for part in range(4)
    ]
    return (
        output,
        input_grad,
        *stacked,
        owned[:cut_gains].reshape(norm_gains.shape),
        owned[cut_gains:cut_rows].reshape(bias_rows.shape),
        owned[cut_rows:].reshape(up_bias.shape),
    )


def solution(mesh):
    tokens_spec = P("wide", "seq", None)
    matrix_spec = P(None, "wide", None)
    rows_spec = P(None, None, "wide")
    return jax.shard_map(
        per_device,
        mesh=mesh,
        in_specs=(
            tokens_spec,
            P("wide", None),
            P("wide", "seq"),
            P("wide", "seq"),
            tokens_spec,
            matrix_spec,
            matrix_spec,
            matrix_spec,
            matrix_spec,
            rows_spec,
            rows_spec,
            P(None, "wide"),
        ),
        out_specs=(
            tokens_spec,
            tokens_spec,
            matrix_spec,
            matrix_spec,
            matrix_spec,
            matrix_spec,
            rows_spec,
            rows_spec,
            P(None, "wide"),
        ),
        check_vma=False,
    )
```
